32 devices in a mesh: pack: 2 (over core), seq: 16 (over z, y, x).
Axes of the slice: x: 2, y: 2, z: 4, core: 2. Of those that a mesh axis runs over, the one named last changes fastest.
Arguments:
- hidden: bfloat16 [2, 8192, 1024], P('pack', 'seq'), may hold values from -6 to 6
- cotangent: bfloat16 [2, 8192, 1024], P('pack', 'seq'), may hold values from -6 to 6
- levels: int32 [2, 32], P('pack', 'seq'), may hold values from 0 to 999
- segments: int32 [2, 32], P('pack'), may hold values from 0 to 3, never falling along the last dimension, each value on 1 to 16 neighbouring positions
- live_frames: int32 [2, 32], P('pack'), may hold values 0 or 1
- noise_table: float32 [1000, 1024], replicated, may hold values from -6 to 6
- mod_weight: bfloat16 [1024, 6144], replicated, may hold values from -0.1875 to 0.1875
- mod_bias: float32 [6144], replicated, may hold values from -3 to 3
- qkv_weight: bfloat16 [1024, 3072], replicated, may hold values from -0.1875 to 0.1875
- qkv_bias: float32 [3072], replicated, may hold values from -3 to 3
- out_weight: bfloat16 [1024, 1024], replicated, may hold values from -3 to 3
- out_bias: float32 [1024], replicated, may hold values from -3 to 3
- up_weight: bfloat16 [1024, 4096], replicated, may hold values from -0.1875 to 0.1875
- up_bias: float32 [4096], replicated, may hold values from -3 to 3
- down_weight: bfloat16 [4096, 1024], replicated, may hold values from -0.09375 to 0.09375
- down_bias: float32 [1024], replicated, may hold values from -3 to 3
Outputs:
- layer_out: bfloat16 [2, 8192, 1024], P('pack', 'seq')
- hidden_grad: bfloat16 [2, 8192, 1024], P('pack', 'seq')
- table_grad: float32 [1000, 1024], P(None, 'seq')
- mod_weight_grad: float32 [1024, 6144], P('seq')
- mod_bias_grad: float32 [6144], P('seq')
- qkv_weight_grad: float32 [1024, 3072], P('seq')
- qkv_bias_grad: float32 [3072], P('seq')
- out_weight_grad: float32 [1024, 1024], P('seq')
- out_bias_grad: float32 [1024], P('seq')
- up_weight_grad: float32 [1024, 4096], P('seq')
- up_bias_grad: float32 [4096], P('seq')
- down_weight_grad: float32 [4096, 1024], P('seq')
- down_bias_grad: float32 [1024], P('seq')
The draws below stay inside these ranges and needn't reach their ends.
Inputs may be any that keep to these rules, and one draw needn't show every extreme that they name: `segments`: in each pack, clip numbers never fall along the frames; each clip has at most 16 frames and one has exactly 16.
All inputs are finite; a program needn't handle non-finite values. No bound on the sum of `live_frames` on one device may be relied on, other than what follows from the above.
Results may differ from the reference program's by a relative error of at most 0.02.
Values may be sent and summed in bfloat16 or wider, within the bound.
No kernel may reach another device: no remote copies, remote signals or barrier semaphores. Data moves between devices by JAX's collectives and lax.ppermute only.
A program may use at most 320 MiB of HBM per device.

```python
import math
import jax
import jax.numpy as jnp
import numpy as np
from jax import lax

D = 1024
HEAD = 64
FF = 4096
LEVELS = 1000
PATCHES = 256
SIDE = 16
TOK_DEV = 512
FRAMES = 32
PACK_TOK = 8192
PACKS = 2
CLIPS = 4
MAXC = 16


def touch_ends(drawn, key, low, high):
    longest = drawn.shape.index(max(drawn.shape))
    spots = []
    for shift in (0, 1):
        where = [jax.random.randint(jax.random.fold_in(key, axis), (), 0, length) for axis, length in enumerate(drawn.shape)]
        where[longest] = (where[longest] + shift) % drawn.shape[longest]
        spots.append(tuple(where))
    return drawn.at[spots[0]].set(low).at[spots[1]].set(high)


def strengthened(values, rng, source, target, blocks, factor):
    def block_of(axis_at):
        return (jnp.arange(values.shape[axis_at]) // (values.shape[axis_at] // blocks)).reshape((-1,) + (1,) * (values.ndim - 1 - axis_at))

    first = jax.random.permutation(rng, blocks)[block_of(target)]
    far = (block_of(target) + blocks // 2) % blocks
    return jnp.where((block_of(source) == first) | (block_of(source) == far), factor * values, values)


def block_scale(key, shape, cuts, smallest, high):
    loudness, own = 1.0, jax.random.fold_in(key, 6)
    for axis_at, blocks in cuts:
        heights = jnp.exp(jax.random.uniform(jax.random.fold_in(own, axis_at), (blocks,), jnp.float32, smallest / len(cuts), high / len(cuts)))
        loudness = loudness * jnp.repeat(heights, shape[axis_at] // blocks).reshape([-1 if axis == axis_at else 1 for axis in range(len(shape))])
    return loudness


def profile(number_of, total, reach, lean):
    loads = [(1 << 20) // math.isqrt(standing ** lean) + 1 for standing in range(2, number_of + 1)]
    surplus, holding = total - reach - (number_of - 1), [1] * (number_of - 1)
    while surplus > 0:
        free = [i for i in range(number_of - 1) if holding[i] < reach]
        pool, left = sum([loads[i] for i in free]), surplus
        for i in free:
            more = min(reach - holding[i], max(1, left * loads[i] // pool), surplus)
            holding[i] = holding[i] + more
            surplus = surplus - more
    return np.array([reach] + holding)


def ragged(own_key, number_of, total, reach, lean):
    if number_of == 2:
        one = jax.random.randint(own_key, (), max(1, total - reach), min(reach, total - 1) + 1)
        return jnp.stack([one, total - one])
    lengths = jnp.asarray(profile(number_of, total, reach, lean), jnp.int32)
    couples = (number_of - 1) // 2
    source_of, sink = lengths[1:1 + 2 * couples:2], lengths[2:2 + 2 * couples:2]
    room = jnp.minimum(source_of - 1, reach - sink)
    moved = jax.random.randint(jax.random.fold_in(own_key, 1), (couples,), 0, 1 << 20) % (room + 1)
    lengths = lengths.at[1:1 + 2 * couples:2].set(source_of - moved).at[2:2 + 2 * couples:2].set(sink + moved)
    return lengths[jax.random.permutation(jax.random.fold_in(own_key, 2), number_of)]


def scatter_about(stream_key, shape, scale, limit, cuts=(), held_as=jnp.bfloat16):
    factor_of = block_scale(stream_key, shape, cuts, -0.22, 0.18) if cuts else 1.0
    array = jax.random.normal(stream_key, shape, jnp.float32) * scale * factor_of
    return jnp.minimum(jnp.maximum(array, -limit), limit).astype(held_as)


def heavy_noise(own_key, extent, width, most, cuts, heavy, kind=jnp.bfloat16):
    values = width * jax.random.normal(own_key, extent, jnp.float32)
    if cuts:
        values = values * block_scale(own_key, extent, cuts, -0.22, 0.18)
    return jnp.clip(strengthened(values, jax.random.fold_in(own_key, 3), *heavy), -most, most).astype(kind)


def setup_inputs(seed: int = 0) -> dict:
    seeds = jax.random.split(jax.random.key(seed), 17)
    return {
        "hidden": scatter_about(seeds[0], (PACKS, PACK_TOK, D), 1.0, 6.0, ((0, 2), (1, 16))),
        "cotangent": heavy_noise(seeds[1], (PACKS, PACK_TOK, D), 1.0, 6.0, ((0, 2), (1, 16)), (1, 2, 16, 2.0)),
        "levels": touch_ends(jax.random.randint(seeds[2], (PACKS, FRAMES), 0, LEVELS), jax.random.fold_in(seeds[2], 1), 0, LEVELS - 1).astype(jnp.int32),
        "segments": jax.vmap(lambda own: jnp.searchsorted(jnp.cumsum(ragged(own, CLIPS, FRAMES, MAXC, 2)), jnp.arange(FRAMES), side="right"))(jax.random.split(seeds[3], PACKS)).reshape((PACKS, FRAMES)).astype(jnp.int32),
        "live_frames": touch_ends((jax.random.randint(seeds[4], (PACKS, FRAMES), 0, 4) < 3).astype(jnp.int32), jax.random.fold_in(seeds[4], 1), 0, 1),
        "noise_table": scatter_about(seeds[5], (LEVELS, D), 1.0, 6.0, (), jnp.float32),
        "mod_weight": scatter_about(seeds[6], (D, 6 * D), D ** -0.5, 0.1875),
        "mod_bias": scatter_about(seeds[7], (6 * D,), 0.5, 3.0, (), jnp.float32),
        "qkv_weight": scatter_about(seeds[8], (D, 3 * D), D ** -0.5, 0.1875),
        "qkv_bias": scatter_about(seeds[9], (3 * D,), 0.5, 3.0, (), jnp.float32),
        "out_weight": scatter_about(seeds[10], (D, D), 4 ** -0.5, 3.0),
        "out_bias": scatter_about(seeds[11], (D,), 0.5, 3.0, (), jnp.float32),
        "up_weight": scatter_about(seeds[12], (D, FF), D ** -0.5, 0.1875),
        "up_bias": scatter_about(seeds[13], (FF,), 0.5, 3.0, (), jnp.float32),
        "down_weight": scatter_about(seeds[14], (FF, D), FF ** -0.5, 0.09375),
        "down_bias": scatter_about(seeds[15], (D,), 0.5, 3.0, (), jnp.float32),
    }


EPSILON = 1e-06
NEGATIVE = -1e+30
PRECISE = lax.Precision.HIGHEST

@jax.custom_vjp
def low(v):
    return lax.optimization_barrier(v.astype(jnp.bfloat16)).astype(jnp.float32)

@jax.custom_vjp
def low_back(v):
    return v

def low_keep(v):
    return (low(v), None)

def low_pass(kept, grad):
    return (grad,)

def back_keep(v):
    return (v, None)

def back_low(kept, grad):
    return (low(grad),)
low.defvjp(low_keep, low_pass)
low_back.defvjp(back_keep, back_low)

def modulate_norm(rows, shift, scale):
    center = lax.optimization_barrier(jnp.mean(rows, axis=-1, keepdims=True))
    centered = rows - center
    spread = lax.optimization_barrier(jnp.mean(centered * centered, axis=-1, keepdims=True))
    normed = centered * lax.rsqrt(spread + EPSILON)
    return normed * (1.0 + scale[:, None, :]) + shift[:, None, :]

def rotary_tables(time_tok, count, half_dim):
    time_pairs = half_dim // 4
    space_pairs = (half_dim - time_pairs) // 2
    patch = jnp.arange(count, dtype=jnp.int32) % PATCHES
    row_pos = (patch // SIDE).astype(jnp.float32)
    col_pos = (patch % SIDE).astype(jnp.float32)
    time_freq = 10000.0 ** (-jnp.arange(time_pairs, dtype=jnp.float32) / time_pairs)
    space_freq = 10000.0 ** (-jnp.arange(space_pairs, dtype=jnp.float32) / space_pairs)
    angles = jnp.concatenate([time_tok[:, None] * time_freq[None, :], row_pos[:, None] * space_freq[None, :], col_pos[:, None] * space_freq[None, :]], axis=1)
    return (jnp.cos(angles), jnp.sin(angles))

def rotate_pairs(values, cos_table, sin_table, sign):
    half_dim = values.shape[2] // 2
    lower = values[:, :, :half_dim]
    upper = values[:, :, half_dim:]
    cosine = cos_table[:, None, :]
    signed_sine = sign * sin_table[:, None, :]
    return jnp.concatenate([lower * cosine - upper * signed_sine, upper * cosine + lower * signed_sine], axis=2)

def gelu_tanh(values):
    return jax.nn.gelu(values, approximate=True)

def layer_pack(hidden_rows, level_row, clip_row, live_row, noise_table, mod_weight, mod_bias, qkv_weight, qkv_bias, out_weight, out_bias, up_weight, up_bias, down_weight, down_bias):
    frames = clip_row.shape[0]
    count = hidden_rows.shape[0]
    model_width = hidden_rows.shape[1]
    head_count = model_width // HEAD
    score_scale = HEAD ** (-0.5)
    embed = noise_table[level_row]
    cond = low(jax.nn.silu(embed))
    modulation = low_back(jnp.dot(cond, mod_weight, precision=PRECISE, preferred_element_type=jnp.float32) + mod_bias)
    attn_shift, attn_scale, attn_gate, feed_shift, feed_scale, feed_gate = jnp.split(modulation, 6, axis=1)
    frame_rows = hidden_rows.reshape(frames, PATCHES, model_width)
    attn_in = low(modulate_norm(frame_rows, attn_shift, attn_scale).reshape(count, model_width))
    qkv = low_back(jnp.dot(attn_in, qkv_weight, precision=PRECISE, preferred_element_type=jnp.float32) + qkv_bias)
    query_raw, key_raw, value_raw = jnp.split(qkv, 3, axis=1)
    frame_ids = jnp.arange(frames, dtype=jnp.int32)
    same_clip = clip_row[:, None] == clip_row[None, :]
    clip_starts = lax.optimization_barrier(jnp.min(jnp.where(same_clip, frame_ids[None, :], frames), axis=1))
    time_frames = (frame_ids - clip_starts).astype(jnp.float32)
    cos_table, sin_table = rotary_tables(jnp.repeat(time_frames, PATCHES), count, HEAD // 2)
    query_heads = low(rotate_pairs(query_raw.reshape(count, head_count, HEAD), cos_table, sin_table, 1.0))
    key_heads = low(rotate_pairs(key_raw.reshape(count, head_count, HEAD), cos_table, sin_table, 1.0))
    value_heads = low(value_raw.reshape(count, head_count, HEAD))
    allowed = same_clip & (frame_ids[None, :] <= frame_ids[:, None]) & ((live_row[None, :] == 1) | (frame_ids[None, :] == frame_ids[:, None]))
    key_frames = jnp.arange(count, dtype=jnp.int32) // PATCHES

    def attend_block(entry):
        query_block, start = entry
        query_frames = (start + jnp.arange(TOK_DEV, dtype=jnp.int32)) // PATCHES
        token_mask = allowed[query_frames][:, key_frames]
        raw = low_back(jnp.einsum('qhd,khd->hqk', query_block, key_heads, precision=PRECISE)) * score_scale
        masked = jnp.where(token_mask[None, :, :], raw, NEGATIVE)
        weights = low(jax.nn.softmax(masked, axis=-1))
        return jnp.einsum('hqk,khd->qhd', weights, value_heads, precision=PRECISE)
    block_count = count // TOK_DEV
    starts = jnp.arange(block_count, dtype=jnp.int32) * TOK_DEV
    attended = lax.map(jax.checkpoint(attend_block), (query_heads.reshape(block_count, TOK_DEV, head_count, HEAD), starts))
    attn_mix = low(low_back(attended.reshape(count, model_width)))
    attn_out = low_back(jnp.dot(attn_mix, out_weight, precision=PRECISE, preferred_element_type=jnp.float32) + out_bias)
    middle = frame_rows + attn_gate[:, None, :] * attn_out.reshape(frames, PATCHES, model_width)
    feed_in = low(modulate_norm(middle, feed_shift, feed_scale).reshape(count, model_width))
    pre = low_back(jnp.dot(feed_in, up_weight, precision=PRECISE, preferred_element_type=jnp.float32) + up_bias)
    act = low(gelu_tanh(pre))
    feed_out = low_back(jnp.dot(act, down_weight, precision=PRECISE, preferred_element_type=jnp.float32) + down_bias)
    result = middle + feed_gate[:, None, :] * feed_out.reshape(frames, PATCHES, model_width)
    return result.reshape(count, model_width)

def reference(hidden, cotangent, levels, segments, live_frames, noise_table, mod_weight, mod_bias, qkv_weight, qkv_bias, out_weight, out_bias, up_weight, up_bias, down_weight, down_bias):

    def forward(hidden_f, table_f, mod_w, mod_b, qkv_w, qkv_b, out_w, out_b, up_w, up_b, down_w, down_b):

        def one_pack(entry):
            return layer_pack(entry[0], entry[1], entry[2], entry[3], table_f, mod_w, mod_b, qkv_w, qkv_b, out_w, out_b, up_w, up_b, down_w, down_b)
        return lax.map(one_pack, (hidden_f, levels, segments, live_frames))
    result, pullback = jax.vjp(forward, hidden.astype(jnp.float32), noise_table, mod_weight.astype(jnp.float32), mod_bias, qkv_weight.astype(jnp.float32), qkv_bias, out_weight.astype(jnp.float32), out_bias, up_weight.astype(jnp.float32), up_bias, down_weight.astype(jnp.float32), down_bias)
    grads = pullback(cotangent.astype(jnp.float32))
    return (result.astype(jnp.bfloat16), grads[0].astype(jnp.bfloat16), grads[1], grads[2], grads[3], grads[4], grads[5], grads[6], grads[7], grads[8], grads[9], grads[10], grads[11])
```

```python
import functools

import jax
import jax.numpy as jnp
from jax import lax
from jax.experimental import pallas as pl
from jax.experimental.pallas import tpu as pltpu
from jax.sharding import PartitionSpec as P

HEAD = 64
PATCHES = 256
SIDE = 16
EPSILON = 1e-06
PRECISE = lax.Precision.HIGHEST
HALF = HEAD // 2
F32 = jnp.float32
BF16 = jnp.bfloat16


def modulate_norm(rows, shift, scale):
    center = jnp.mean(rows, axis=-1, keepdims=True)
    centered = rows - center
    spread = jnp.mean(centered * centered, axis=-1, keepdims=True)
    normed = centered * lax.rsqrt(spread + EPSILON)
    return normed * (1.0 + scale[:, None, :]) + shift[:, None, :]


def gelu_tanh(values):
    return jax.nn.gelu(values, approximate=True)


def dot_over(first, second, first_dim, second_dim):
    return lax.dot_general(
        first, second, (((first_dim,), (second_dim,)), ((), ())), preferred_element_type=F32
    )


def spatial_angles():
    time_pairs = HALF // 4
    space_pairs = (HALF - time_pairs) // 2
    patch = jnp.arange(PATCHES, dtype=jnp.int32)
    row_pos = (patch // SIDE).astype(F32)
    col_pos = (patch % SIDE).astype(F32)
    time_freq = 10000.0 ** (-jnp.arange(time_pairs, dtype=F32) / time_pairs)
    space_freq = 10000.0 ** (-jnp.arange(space_pairs, dtype=F32) / space_pairs)
    space = jnp.concatenate(
        [space_freq[:, None] * row_pos[None, :], space_freq[:, None] * col_pos[None, :]], axis=0
    )
    return time_freq, space


def rotary_tables(time_frames):
    time_freq, space = spatial_angles()
    count = time_frames.shape[0]
    time_angle = time_frames[:, None] * time_freq[None, :]

    def whole(function):
        return jnp.concatenate(
            [
                jnp.broadcast_to(
                    function(time_angle)[:, :, None], (count, time_freq.shape[0], PATCHES)
                ),
                jnp.broadcast_to(function(space)[None], (count,) + space.shape),
            ],
            axis=1,
        )

    return whole(jnp.cos), whole(jnp.sin)


def place(frame, per_device):
    return lax.div(frame, per_device), pl.multiple_of(
        lax.rem(frame, per_device) * PATCHES, PATCHES
    )


def walk_frames(frames, segments_ref, live_ref, list_ref, visit):
    def step(frame, held):
        before = jnp.maximum(frame - 1, 0)
        fresh = (frame == 0) | (segments_ref[frame] != segments_ref[before])
        held = jnp.where(fresh, 0, held)
        list_ref[held] = frame
        visit(frame, held + 1)
        return held + jnp.where(live_ref[frame] == 1, 1, 0)

    lax.fori_loop(0, frames, step, jnp.int32(0))


def attend_kernel(per_device, segments_ref, live_ref, x_ref, mix_ref, wide_ref, lse_ref, key_ref, list_ref):
    frames = key_ref.shape[0]

    def turn(frame, carry):
        source, start = place(frame, per_device)
        block = x_ref[source, 1, :, pl.ds(start, PATCHES)].astype(F32)
        key_ref[frame] = block.T.astype(BF16)
        return carry

    lax.fori_loop(0, frames, turn, 0)

    def visit(frame, count):
        source, start = place(frame, per_device)
        query = x_ref[source, 0, :, pl.ds(start, PATCHES)]

        def scores_of(other):
            return jnp.dot(key_ref[other], query, preferred_element_type=F32)

        def mixed(other, weights):
            other_source, other_start = place(other, per_device)
            value = x_ref[other_source, 2, :, pl.ds(other_start, PATCHES)]
            return jnp.dot(value, weights.astype(BF16), preferred_element_type=F32)

        def first(other):
            scores = scores_of(other)
            top = jnp.max(scores, axis=0, keepdims=True)
            weights = jnp.exp(scores - top)
            return top, jnp.sum(weights, axis=0, keepdims=True), mixed(other, weights)

        def pair(index, carry):
            top, total, accum = carry
            one = list_ref[2 * index]
            two = list_ref[2 * index + 1]
            scores_one = scores_of(one)
            scores_two = scores_of(two)
            new_top = jnp.maximum(
                top,
                jnp.maximum(
                    jnp.max(scores_one, axis=0, keepdims=True),
                    jnp.max(scores_two, axis=0, keepdims=True),
                ),
            )
            shrink = jnp.exp(top - new_top)
            weights_one = jnp.exp(scores_one - new_top)
            weights_two = jnp.exp(scores_two - new_top)
            total = (
                total * shrink
                + jnp.sum(weights_one, axis=0, keepdims=True)
                + jnp.sum(weights_two, axis=0, keepdims=True)
            )
            accum = accum * shrink + mixed(one, weights_one) + mixed(two, weights_two)
            return new_top, total, accum

        others = count - 1
        carry = first(frame)
        carry = lax.fori_loop(0, lax.div(others, 2), pair, carry)

        def single(carry):
            top, total, accum = carry
            other = list_ref[others - 1]
            scores = scores_of(other)
            new_top = jnp.maximum(top, jnp.max(scores, axis=0, keepdims=True))
            shrink = jnp.exp(top - new_top)
            weights = jnp.exp(scores - new_top)
            return (
                new_top,
                total * shrink + jnp.sum(weights, axis=0, keepdims=True),
                accum * shrink + mixed(other, weights),
            )

        top, total, accum = lax.fori_loop(
            0, lax.rem(others, 2), lambda unused, state: single(state), carry
        )
        result = accum * (1.0 / total)
        wide_ref[source, :, pl.ds(start, PATCHES)] = result
        mix_ref[source, :, pl.ds(start, PATCHES)] = result.astype(BF16)
        lse_ref[pl.ds(frame, 1), :] = top + jnp.log(total)

    walk_frames(frames, segments_ref, live_ref, list_ref, visit)


def whole_spec():
    return pl.BlockSpec(memory_space=pltpu.VMEM)


def scalar_spec():
    return pl.BlockSpec(memory_space=pltpu.SMEM)


def attend(segments, live, x):
    sources, _, _, tokens = x.shape
    per_device = tokens // PATCHES
    frames = sources * per_device
    pairs = frames * 6
    return pl.pallas_call(
        functools.partial(attend_kernel, per_device),
        out_shape=(
            jax.ShapeDtypeStruct((sources, HEAD, tokens), BF16),
            jax.ShapeDtypeStruct((sources, HEAD, tokens), F32),
            jax.ShapeDtypeStruct((frames, PATCHES), F32),
        ),
        in_specs=[scalar_spec(), scalar_spec(), whole_spec()],
        out_specs=(whole_spec(), whole_spec(), whole_spec()),
        scratch_shapes=[pltpu.VMEM((frames, PATCHES, HEAD), BF16), pltpu.SMEM((frames,), jnp.int32)],
        cost_estimate=pl.CostEstimate(
            flops=pairs * 4 * PATCHES * PATCHES * 256,
            bytes_accessed=x.size * 2 * 3,
            transcendentals=pairs * PATCHES * PATCHES,
        ),
        compiler_params=pltpu.CompilerParams(vmem_limit_bytes=40 << 20),
        name="attend",
    )(segments, live, x)


def attend_back_kernel(
    per_device,
    segments_ref,
    live_ref,
    x_ref,
    wide_ref,
    lse_ref,
    d_mix_ref,
    cos_ref,
    sin_ref,
    out_ref,
    kv_ref,
    qd_ref,
    dkv_ref,
    delta_ref,
    list_ref,
):
    frames = kv_ref.shape[0]

    def turn(frame, carry):
        source, start = place(frame, per_device)
        lanes = pl.ds(start, PATCHES)
        d_mix = d_mix_ref[source, :, lanes].astype(F32)
        key_value = jnp.concatenate(
            [x_ref[source, 1, :, lanes].astype(F32), x_ref[source, 2, :, lanes].astype(F32)], axis=0
        )
        kv_ref[frame] = key_value.T.astype(BF16)
        query = x_ref[source, 0, :, lanes].astype(F32)
        blank = jnp.zeros_like(query)
        qd_ref[frame, pl.ds(0, PATCHES), :] = jnp.concatenate([query, blank], axis=0).T.astype(BF16)
        qd_ref[frame, pl.ds(PATCHES, PATCHES), :] = jnp.concatenate([blank, d_mix], axis=0).T.astype(
            BF16
        )
        delta_ref[pl.ds(frame, 1), :] = jnp.sum(
            d_mix * wide_ref[source, :, lanes], axis=0, keepdims=True
        )
        dkv_ref[frame] = jnp.zeros((PATCHES, 2 * HEAD), F32)
        return carry

    lax.fori_loop(0, frames, turn, 0)

    def unturn(frame, values):
        lower = values[:HALF]
        upper = values[HALF:]
        cosine = cos_ref[frame]
        sine = sin_ref[frame]
        return jnp.concatenate([lower * cosine + upper * sine, upper * cosine - lower * sine], axis=0)

    def visit(frame, count):
        source, start = place(frame, per_device)
        lanes = pl.ds(start, PATCHES)
        query = x_ref[source, 0, :, lanes]
        d_mix = d_mix_ref[source, :, lanes]
        blank = jnp.zeros_like(query)
        query_side = jnp.concatenate([query, blank], axis=0)
        d_mix_side = jnp.concatenate([blank, d_mix], axis=0)
        lse = lse_ref[pl.ds(frame, 1), :]
        delta = delta_ref[pl.ds(frame, 1), :]
        both = qd_ref[frame]

        def block(other):
            other_source, other_start = place(other, per_device)
            key_value = kv_ref[other]
            scores = jnp.dot(key_value, query_side, preferred_element_type=F32)
            d_weights = jnp.dot(key_value, d_mix_side, preferred_element_type=F32)
            weights = jnp.exp(scores - lse)
            d_scores = (weights * (d_weights - delta)).astype(BF16)
            sides = jnp.concatenate([d_scores, weights.astype(BF16)], axis=1)
            dkv_ref[other] += jnp.dot(sides, both, preferred_element_type=F32)
            key = x_ref[other_source, 1, :, pl.ds(other_start, PATCHES)]
            return jnp.dot(key, d_scores, preferred_element_type=F32)

        def pair(index, d_query):
            return d_query + block(list_ref[2 * index]) + block(list_ref[2 * index + 1])

        d_query = lax.fori_loop(
            0, lax.div(count, 2), pair, jnp.zeros((HEAD, PATCHES), F32)
        )
        d_query = lax.fori_loop(
            0,
            lax.rem(count, 2),
            lambda unused, state: state + block(list_ref[count - 1]),
            d_query,
        )
        out_ref[source, 0, :, lanes] = unturn(frame, d_query * (HEAD**-0.5)).astype(BF16)

    walk_frames(frames, segments_ref, live_ref, list_ref, visit)

    def finish(frame, carry):
        source, start = place(frame, per_device)
        lanes = pl.ds(start, PATCHES)
        both = dkv_ref[frame].T
        out_ref[source, 1, :, lanes] = unturn(frame, both[:HEAD]).astype(BF16)
        out_ref[source, 2, :, lanes] = both[HEAD:].astype(BF16)
        return carry

    lax.fori_loop(0, frames, finish, 0)


def attend_back(segments, live, x, wide, lse, d_mix, cosine, sine):
    sources, _, _, tokens = x.shape
    per_device = tokens // PATCHES
    frames = sources * per_device
    pairs = frames * 6
    return pl.pallas_call(
        functools.partial(attend_back_kernel, per_device),
        out_shape=jax.ShapeDtypeStruct(x.shape, BF16),
        in_specs=[scalar_spec(), scalar_spec()] + [whole_spec()] * 6,
        out_specs=whole_spec(),
        scratch_shapes=[
            pltpu.VMEM((frames, PATCHES, 2 * HEAD), BF16),
            pltpu.VMEM((frames, 2 * PATCHES, 2 * HEAD), BF16),
            pltpu.VMEM((frames, PATCHES, 2 * HEAD), F32),
            pltpu.VMEM((frames, PATCHES), F32),
            pltpu.SMEM((frames,), jnp.int32),
        ],
        cost_estimate=pl.CostEstimate(
            flops=pairs * 10 * PATCHES * PATCHES * 256,
            bytes_accessed=x.size * 2 * 5,
            transcendentals=pairs * PATCHES * PATCHES,
        ),
        compiler_params=pltpu.CompilerParams(vmem_limit_bytes=60 << 20),
        name="attend_back",
    )(segments, live, x, wide, lse, d_mix, cosine, sine)


def exchange(value, axis, bit):
    count = lax.axis_size(axis)
    return lax.ppermute(value, axis, [(source, source ^ bit) for source in range(count)])


def gather_all(value):
    bit = lax.axis_size("seq") // 2
    while bit:
        value = jnp.concatenate([value, exchange(value, "seq", bit)], axis=0)
        bit //= 2
    packs = lax.axis_size("pack")
    bit = packs // 2
    while bit:
        value = jnp.concatenate([value, exchange(value, "pack", bit)], axis=0)
        bit //= 2
    return value


def sum_rows(term_of, rows, columns, order):
    count = lax.axis_size("seq")
    packs = lax.axis_size("pack")
    if packs != 2 or count != 16:
        whole = term_of(0, columns)
        part = lax.psum_scatter(whole.astype(BF16), "seq", scatter_dimension=0, tiled=True)
        return lax.psum(part, "pack").astype(F32)
    pack = lax.axis_index("pack")
    index = lax.axis_index("seq")
    width = columns // 2
    theirs = term_of((1 - pack) * width, width).astype(BF16)
    came = exchange(theirs, "pack", 1)
    mine = term_of(pack * width, width)
    shape = [2, 2, 2, 2, rows // count, width]
    parts = [mine.reshape(shape), came.reshape(shape)]
    for bit in order:
        axis = {8: 0, 4: 1, 2: 2, 1: 3}[bit]
        own_bit = lax.rem(lax.div(index, bit), 2)

        def pick(which):
            pieces = [lax.dynamic_slice_in_dim(part, which, 1, axis) for part in parts]
            return (pieces[0].astype(F32) + pieces[1].astype(F32)).astype(BF16)

        sent = exchange(pick(1 - own_bit), "seq", bit)
        parts = [pick(own_bit), sent]
    own = (parts[0].astype(F32) + parts[1].astype(F32)).astype(BF16).reshape(rows // count, width)
    other = exchange(own, "pack", 1)
    left = jnp.where(pack == 0, own, other)
    right = jnp.where(pack == 0, other, own)
    return jnp.concatenate([left, right], axis=1).astype(F32)


def columns_of(matrix, start, width, axis=1):
    if isinstance(start, int) and start == 0 and width == matrix.shape[axis]:
        return matrix
    return lax.dynamic_slice_in_dim(matrix, start, width, axis)


def local(
    hidden,
    cotangent,
    levels,
    segments,
    live_frames,
    noise_table,
    mod_weight,
    mod_bias,
    qkv_weight,
    qkv_bias,
    out_weight,
    out_bias,
    up_weight,
    up_bias,
    down_weight,
    down_bias,
):
    seq_index = lax.axis_index("seq")
    seq_count = lax.axis_size("seq")
    tokens = hidden.shape[1]
    width = hidden.shape[2]
    per_device = tokens // PATCHES
    frames = segments.shape[1]
    heads = width // HEAD
    copies = seq_count // heads
    hidden_units = up_weight.shape[1]
    level_count = noise_table.shape[0]
    share = width // seq_count
    clip_ids = segments[0]
    live = live_frames[0]

    frame_ids = jnp.arange(frames, dtype=jnp.int32)
    same_clip = clip_ids[:, None] == clip_ids[None, :]
    clip_starts = jnp.min(jnp.where(same_clip, frame_ids[None, :], frames), axis=1)
    cos_all, sin_all = rotary_tables((frame_ids - clip_starts).astype(F32))
    first_frame = seq_index * per_device
    own_cos = lax.dynamic_slice_in_dim(cos_all, first_frame, per_device)
    own_sin = lax.dynamic_slice_in_dim(sin_all, first_frame, per_device)
    own_cos = own_cos.transpose(1, 0, 2).reshape(HALF, tokens)
    own_sin = own_sin.transpose(1, 0, 2).reshape(HALF, tokens)

    embed = jnp.concatenate(
        [
            lax.dynamic_slice_in_dim(noise_table, levels[0, frame], 1, 0)
            for frame in range(per_device)
        ],
        axis=0,
    )
    cond = jax.nn.silu(embed).astype(BF16)
    modulation = jnp.dot(cond, mod_weight, preferred_element_type=F32) + mod_bias
    attn_shift, attn_scale, attn_gate, feed_shift, feed_scale, feed_gate = jnp.split(
        modulation, 6, axis=1
    )
    frame_rows = hidden[0].astype(F32).reshape(per_device, PATCHES, width)
    attn_value, attn_norm_back = jax.vjp(modulate_norm, frame_rows, attn_shift, attn_scale)
    attn_in = attn_value.reshape(tokens, width).astype(BF16)

    qkv = dot_over(qkv_weight, attn_in, 0, 1) + qkv_bias[:, None]
    qkv = qkv.reshape(3, heads, 2, HALF, tokens)
    turned = qkv[:2]
    lower = turned[:, :, 0] * own_cos - turned[:, :, 1] * own_sin
    upper = turned[:, :, 1] * own_cos + turned[:, :, 0] * own_sin
    turned = jnp.stack([lower, upper], axis=2)
    query = (turned[0] * (HEAD**-0.5)).astype(BF16).reshape(heads, HEAD, tokens)
    key = turned[1].astype(BF16).reshape(heads, HEAD, tokens)
    value = qkv[2].astype(BF16).reshape(heads, HEAD, tokens)
    sent = jnp.stack([query, key, value], axis=1)

    def to_heads(array):
        if copies > 1:
            array = jnp.concatenate([array] * copies, axis=0)
        return lax.all_to_all(array, "seq", 0, 0, tiled=True)

    def to_tokens(array):
        return lax.all_to_all(array, "seq", 0, 0, tiled=True)[:heads]

    x = to_heads(sent)
    mix, wide, lse = attend(clip_ids, live, x)
    attn_mix = to_tokens(mix).reshape(width, tokens)

    attn_out = dot_over(attn_mix, out_weight, 0, 0) + out_bias
    attn_rows = attn_out.reshape(per_device, PATCHES, width)
    middle = frame_rows + attn_gate[:, None, :] * attn_rows
    feed_value, feed_norm_back = jax.vjp(modulate_norm, middle, feed_shift, feed_scale)
    feed_in = feed_value.reshape(tokens, width).astype(BF16)
    pre = jnp.dot(feed_in, up_weight, preferred_element_type=F32) + up_bias
    act_value, act_back = jax.vjp(gelu_tanh, pre)
    act = act_value.astype(BF16)
    grad_rows = cotangent[0].astype(F32).reshape(per_device, PATCHES, width)
    d_feed_out = (feed_gate[:, None, :] * grad_rows).reshape(tokens, width).astype(BF16)
    down_weight_grad = sum_rows(
        lambda start, size: dot_over(act, columns_of(d_feed_out, start, size), 0, 0),
        hidden_units,
        width,
        (1, 2, 8, 4),
    )
    down_bias_term = jnp.sum(d_feed_out.astype(F32), axis=0)
    d_pre = act_back(dot_over(d_feed_out, down_weight, 1, 1))[0].astype(BF16)
    up_weight_grad = sum_rows(
        lambda start, size: dot_over(feed_in, columns_of(d_pre, start, size), 0, 0),
        width,
        hidden_units,
        (2, 1, 8, 4),
    )
    up_bias_term = jnp.sum(d_pre.astype(F32), axis=0)
    d_feed_in = dot_over(d_pre, up_weight, 1, 1).reshape(per_device, PATCHES, width)
    d_middle_norm, d_feed_shift, d_feed_scale = feed_norm_back(d_feed_in)
    d_middle = grad_rows + d_middle_norm
    d_attn_gate = jnp.sum(d_middle * attn_rows, axis=1)
    d_attn_out = (attn_gate[:, None, :] * d_middle).reshape(tokens, width).astype(BF16)
    d_mix = dot_over(out_weight, d_attn_out, 1, 1).astype(BF16).reshape(heads, HEAD, tokens)
    d_mix_heads = to_heads(d_mix)
    out_weight_grad = sum_rows(
        lambda start, size: dot_over(attn_mix, columns_of(d_attn_out, start, size), 1, 0),
        width,
        width,
        (1, 2, 8, 4),
    )
    out_bias_term = jnp.sum(d_attn_out.astype(F32), axis=0)

    feed_out = jnp.dot(act, down_weight, preferred_element_type=F32) + down_bias
    feed_rows = feed_out.reshape(per_device, PATCHES, width)
    layer_out = (middle + feed_gate[:, None, :] * feed_rows).reshape(1, tokens, width).astype(BF16)
    d_feed_gate = jnp.sum(grad_rows * feed_rows, axis=1)

    early_mod = jnp.concatenate([d_attn_gate, d_feed_shift, d_feed_scale, d_feed_gate], axis=1)
    own_levels = levels[0]
    early_bias = jnp.concatenate([out_bias_term, up_bias_term, down_bias_term])
    bias_rows = early_bias.reshape(per_device, early_bias.shape[0] // per_device)
    early = jnp.concatenate(
        [
            early_mod.astype(BF16),
            bias_rows.astype(BF16),
            jnp.broadcast_to(lax.div(own_levels, 32)[:, None], (per_device, 128)).astype(BF16),
            jnp.broadcast_to(lax.rem(own_levels, 32)[:, None], (per_device, 128)).astype(BF16),
        ],
        axis=1,
    )
    early_all = gather_all(early)

    d_x = attend_back(clip_ids, live, x, wide, lse, d_mix_heads, cos_all, sin_all)
    d_qkv = to_tokens(d_x).transpose(1, 0, 2, 3).reshape(3 * width, tokens)
    d_attn_in = dot_over(d_qkv, qkv_weight, 0, 1).reshape(per_device, PATCHES, width)
    d_hidden_norm, d_attn_shift, d_attn_scale = attn_norm_back(d_attn_in)
    hidden_grad = (d_middle + d_hidden_norm).reshape(1, tokens, width).astype(BF16)
    qkv_weight_grad = sum_rows(
        lambda start, size: dot_over(attn_in, columns_of(d_qkv, start, size, 0), 0, 1),
        width,
        3 * width,
        (1, 2, 8, 4),
    )
    qkv_bias_term = jnp.sum(d_qkv.astype(F32), axis=1)
    late = jnp.concatenate(
        [
            d_attn_shift.astype(BF16),
            d_attn_scale.astype(BF16),
            qkv_bias_term.reshape(per_device, 3 * width // per_device).astype(BF16),
        ],
        axis=1,
    )
    late_all = gather_all(late)

    devices = late_all.shape[0] // per_device

    def bias_share(rows, sizes):
        flat = rows.reshape(devices, sum(sizes))
        shares = []
        at = 0
        for size in sizes:
            piece = size // seq_count
            own = lax.dynamic_slice_in_dim(flat, at + seq_index * piece, piece, 1)
            shares.append(jnp.sum(own.astype(F32), axis=0))
            at += size
        return shares

    early_width = 4 * width
    bias_width = early_bias.shape[0] // per_device
    out_bias_grad, up_bias_grad, down_bias_grad = bias_share(
        early_all[:, early_width : early_width + bias_width], (width, hidden_units, width)
    )
    (qkv_bias_grad,) = bias_share(late_all[:, 2 * width :], (3 * width,))
    coarse = early_all[:, early_width + bias_width].astype(jnp.int32)
    fine = early_all[:, early_width + bias_width + 128].astype(jnp.int32)
    all_levels = coarse * 32 + fine
    picks = (all_levels[:, None] == jnp.arange(level_count, dtype=jnp.int32)[None, :]).astype(F32)
    own_table = lax.dynamic_slice_in_dim(noise_table, seq_index * share, share, 1)
    all_embed = jnp.dot(picks, own_table, precision=PRECISE, preferred_element_type=F32)
    silu_value, silu_back = jax.vjp(jax.nn.silu, all_embed)
    all_cond = silu_value.astype(BF16)
    d_mod_early = early_all[:, :early_width]
    d_mod_late = late_all[:, : 2 * width]
    own_mod = lax.dynamic_slice_in_dim(mod_weight, seq_index * share, share, 0)
    d_cond_early = dot_over(d_mod_early, own_mod[:, 2 * width :], 1, 1)
    d_cond = d_cond_early + dot_over(d_mod_late, own_mod[:, : 2 * width], 1, 1)
    d_embed = silu_back(d_cond)[0]
    table_grad = lax.dot_general(
        picks, d_embed, (((0,), (0,)), ((), ())), precision=PRECISE, preferred_element_type=F32
    )
    mod_weight_grad = jnp.concatenate(
        [dot_over(all_cond, d_mod_late, 0, 0), dot_over(all_cond, d_mod_early, 0, 0)], axis=1
    )
    bias_piece = mod_bias.shape[0] // seq_count
    d_mod_sum = jnp.concatenate(
        [jnp.sum(d_mod_late.astype(F32), axis=0), jnp.sum(d_mod_early.astype(F32), axis=0)]
    )
    mod_bias_grad = lax.dynamic_slice_in_dim(d_mod_sum, seq_index * bias_piece, bias_piece)
    return (
        layer_out,
        hidden_grad,
        table_grad,
        mod_weight_grad,
        mod_bias_grad,
        qkv_weight_grad,
        qkv_bias_grad,
        out_weight_grad,
        out_bias_grad,
        up_weight_grad,
        up_bias_grad,
        down_weight_grad,
        down_bias_grad,
    )


def solution(mesh):
    in_specs = (
        P("pack", "seq", None),
        P("pack", "seq", None),
        P("pack", "seq"),
        P("pack", None),
        P("pack", None),
    ) + (P(),) * 11
    out_specs = (
        P("pack", "seq", None),
        P("pack", "seq", None),
        P(None, "seq"),
        P("seq", None),
        P("seq"),
        P("seq", None),
        P("seq"),
        P("seq", None),
        P("seq"),
        P("seq", None),
        P("seq"),
        P("seq", None),
        P("seq"),
    )
    return jax.shard_map(local, mesh=mesh, in_specs=in_specs, out_specs=out_specs, check_vma=False)
```

```python
import functools

import jax
import jax.numpy as jnp
from jax import lax
from jax.experimental import pallas as pl
from jax.experimental.pallas import tpu as pltpu
from jax.sharding import PartitionSpec as P

HEAD = 64
PATCHES = 256
SIDE = 16
EPSILON = 1e-06
PRECISE = lax.Precision.HIGHEST
HALF = HEAD // 2
F32 = jnp.float32
BF16 = jnp.bfloat16


def modulate_norm(rows, shift, scale):
    center = jnp.mean(rows, axis=-1, keepdims=True)
    centered = rows - center
    spread = jnp.mean(centered * centered, axis=-1, keepdims=True)
    normed = centered * lax.rsqrt(spread + EPSILON)
    return normed * (1.0 + scale[:, None, :]) + shift[:, None, :]


def gelu_tanh(values):
    return jax.nn.gelu(values, approximate=True)


def dot_over(first, second, first_dim, second_dim):
    return lax.dot_general(
        first, second, (((first_dim,), (second_dim,)), ((), ())), preferred_element_type=F32
    )


def spatial_angles():
    time_pairs = HALF // 4
    space_pairs = (HALF - time_pairs) // 2
    patch = jnp.arange(PATCHES, dtype=jnp.int32)
    row_pos = (patch // SIDE).astype(F32)
    col_pos = (patch % SIDE).astype(F32)
    time_freq = 10000.0 ** (-jnp.arange(time_pairs, dtype=F32) / time_pairs)
    space_freq = 10000.0 ** (-jnp.arange(space_pairs, dtype=F32) / space_pairs)
    space = jnp.concatenate(
        [space_freq[:, None] * row_pos[None, :], space_freq[:, None] * col_pos[None, :]], axis=0
    )
    return time_freq, space


def rotary_tables(time_frames):
    time_freq, space = spatial_angles()
    count = time_frames.shape[0]
    time_angle = time_frames[:, None] * time_freq[None, :]

    def whole(function):
        return jnp.concatenate(
            [
                jnp.broadcast_to(
                    function(time_angle)[:, :, None], (count, time_freq.shape[0], PATCHES)
                ),
                jnp.broadcast_to(function(space)[None], (count,) + space.shape),
            ],
            axis=1,
        )

    return whole(jnp.cos), whole(jnp.sin)


def walk_frames(frames, per_device, part, segments_ref, live_ref, list_ref, visit):
    def step(source, held):
        for place in range(per_device):
            frame = source * per_device + place
            before = jnp.maximum(frame - 1, 0)
            fresh = (frame == 0) | (segments_ref[frame] != segments_ref[before])
            held = jnp.where(fresh, 0, held)
            list_ref[held] = frame
            if place == part:
                visit(source, frame, held + 1)
            held = held + jnp.where(live_ref[frame] == 1, 1, 0)
        return held

    lax.fori_loop(0, frames // per_device, step, jnp.int32(0))


def attend_kernel(per_device, part, slot, segments_ref, live_ref, x_ref, q_ref, *refs):
    if part == 0:
        mix_ref, wide_ref, lse_ref, kv_ref, list_ref = refs
    else:
        kv_ref, mix_ref, wide_ref, lse_ref, list_ref = refs
    frames = kv_ref.shape[0]

    def turn(source, carry):
        for place in range(per_device):
            both = jnp.concatenate(
                [x_ref[source, place], x_ref[source, per_device + place]], axis=0
            )
            kv_ref[source * per_device + place] = both.astype(F32).T.astype(BF16)
        return carry

    if part == 0:
        lax.fori_loop(0, frames // per_device, turn, 0)

    def visit(source, frame, count):
        query = q_ref[source, slot]
        query_side = jnp.concatenate([query, jnp.zeros_like(query)], axis=0)

        def scores_of(other):
            return jnp.dot(kv_ref[other], query_side, preferred_element_type=F32)

        def mixed(other, weights):
            value = x_ref[lax.div(other, per_device), per_device + lax.rem(other, per_device)]
            return jnp.dot(value, weights.astype(BF16), preferred_element_type=F32)

        def join(others, carry):
            scores = [scores_of(other) for other in others]
            tops = [jnp.max(score, axis=0, keepdims=True) for score in scores]
            new_top = functools.reduce(jnp.maximum, tops)
            if carry is not None:
                top, total, accum = carry
                new_top = jnp.maximum(top, new_top)
                shrink = jnp.exp(top - new_top)
                total = total * shrink
                accum = accum * shrink
            for index, score in enumerate(scores):
                weights = jnp.exp(score - new_top)
                added = jnp.sum(weights, axis=0, keepdims=True)
                product = mixed(others[index], weights)
                if carry is None and index == 0:
                    total, accum = added, product
                else:
                    total, accum = total + added, accum + product
            return new_top, total, accum

        others = count - 1
        carry = join([frame], None)
        carry = lax.fori_loop(
            0,
            lax.div(others, 2),
            lambda index, state: join([list_ref[2 * index], list_ref[2 * index + 1]], state),
            carry,
        )
        top, total, accum = lax.fori_loop(
            0,
            lax.rem(others, 2),
            lambda unused, state: join([list_ref[others - 1]], state),
            carry,
        )
        result = accum * (1.0 / total)
        wide_ref[source] = result
        mix_ref[source] = result.astype(BF16)
        lse_ref[pl.ds(source, 1), :] = top + jnp.log(total)

    walk_frames(frames, per_device, part, segments_ref, live_ref, list_ref, visit)


def whole_spec():
    return pl.BlockSpec(memory_space=pltpu.VMEM)


def scalar_spec():
    return pl.BlockSpec(memory_space=pltpu.SMEM)


def attend(part, per_device, slot, segments, live, x, query, kv):
    sources = x.shape[0]
    frames = sources * per_device
    pairs = sources * 6
    outs = [
        jax.ShapeDtypeStruct((sources, HEAD, PATCHES), BF16),
        jax.ShapeDtypeStruct((sources, HEAD, PATCHES), F32),
        jax.ShapeDtypeStruct((sources, PATCHES), F32),
    ]
    args = [segments, live, x, query]
    if part == 0:
        outs.append(jax.ShapeDtypeStruct((frames, PATCHES, 2 * HEAD), BF16))
    else:
        args.append(kv)
    result = pl.pallas_call(
        functools.partial(attend_kernel, per_device, part, slot),
        out_shape=tuple(outs),
        in_specs=[scalar_spec(), scalar_spec()] + [whole_spec()] * (len(args) - 2),
        out_specs=(whole_spec(),) * len(outs),
        scratch_shapes=[pltpu.SMEM((frames,), jnp.int32)],
        cost_estimate=pl.CostEstimate(
            flops=pairs * 4 * PATCHES * PATCHES * 256,
            bytes_accessed=x.size * 2 * 3,
            transcendentals=pairs * PATCHES * PATCHES,
        ),
        compiler_params=pltpu.CompilerParams(vmem_limit_bytes=40 << 20),
        name="attend%d" % part,
    )(*args)
    return result if part == 0 else tuple(result) + (kv,)


def attend_back_kernel(
    per_device,
    part,
    slot,
    last,
    segments_ref,
    live_ref,
    x_ref,
    q_ref,
    kv_ref,
    wide_ref,
    lse_ref,
    d_mix_ref,
    cos_ref,
    sin_ref,
    *refs
):
    if last:
        before_ref, out_ref, dkv_ref, list_ref = refs
    else:
        out_ref, dkv_ref, list_ref = refs
    frames = kv_ref.shape[0]

    def clear(frame, carry):
        dkv_ref[frame] = jnp.zeros((PATCHES, 2 * HEAD), F32)
        return carry

    lax.fori_loop(0, frames, clear, 0)

    def unturn(frame, values):
        lower = values[:HALF]
        upper = values[HALF:]
        cosine = cos_ref[frame]
        sine = sin_ref[frame]
        return jnp.concatenate([lower * cosine + upper * sine, upper * cosine - lower * sine], axis=0)

    def visit(source, frame, count):
        query = q_ref[source, slot]
        d_mix = d_mix_ref[source]
        blank = jnp.zeros_like(query)
        query_side = jnp.concatenate([query, blank], axis=0)
        d_mix_side = jnp.concatenate([blank, d_mix], axis=0)
        both = jnp.concatenate(
            [query_side.astype(F32).T.astype(BF16), d_mix_side.astype(F32).T.astype(BF16)], axis=0
        )
        lse = lse_ref[pl.ds(source, 1), :]
        delta = jnp.sum(d_mix.astype(F32) * wide_ref[source], axis=0, keepdims=True)

        def block(other):
            key_value = kv_ref[other]
            scores = jnp.dot(key_value, query_side, preferred_element_type=F32)
            d_weights = jnp.dot(key_value, d_mix_side, preferred_element_type=F32)
            weights = jnp.exp(scores - lse)
            d_scores = (weights * (d_weights - delta)).astype(BF16)
            sides = jnp.concatenate([d_scores, weights.astype(BF16)], axis=1)
            dkv_ref[other] += jnp.dot(sides, both, preferred_element_type=F32)
            key = x_ref[lax.div(other, per_device), lax.rem(other, per_device)]
            return jnp.dot(key, d_scores, preferred_element_type=F32)

        d_query = lax.fori_loop(
            0,
            lax.div(count, 2),
            lambda index, state: state
            + block(list_ref[2 * index])
            + block(list_ref[2 * index + 1]),
            jnp.zeros((HEAD, PATCHES), F32),
        )
        d_query = lax.fori_loop(
            0,
            lax.rem(count, 2),
            lambda unused, state: state + block(list_ref[count - 1]),
            d_query,
        )
        d_query = unturn(frame, d_query * (HEAD**-0.5)).astype(BF16)
        if last:
            out_ref[source, 2 * per_device] = d_query
        else:
            out_ref[source] = d_query

    walk_frames(frames, per_device, part, segments_ref, live_ref, list_ref, visit)

    def finish(source, carry):
        for place in range(per_device):
            frame = source * per_device + place
            both = (dkv_ref[frame] + before_ref[frame]).T
            out_ref[source, place] = unturn(frame, both[:HEAD]).astype(BF16)
            out_ref[source, per_device + place] = both[HEAD:].astype(BF16)
        return carry

    if last:
        lax.fori_loop(0, frames // per_device, finish, 0)


def attend_back(
    part, per_device, slot, segments, live, x, query, kv, wide, lse, d_mix, cosine, sine, before
):
    sources = x.shape[0]
    frames = sources * per_device
    pairs = sources * 6
    last = part == per_device - 1
    args = [segments, live, x, query, kv, wide, lse, d_mix, cosine, sine]
    dkv = (frames, PATCHES, 2 * HEAD)
    lists = pltpu.SMEM((frames,), jnp.int32)
    if last:
        args.append(before)
        outs = jax.ShapeDtypeStruct((sources, 2 * per_device + 1, HEAD, PATCHES), BF16)
        out_specs = whole_spec()
        scratch = [pltpu.VMEM(dkv, F32), lists]
    else:
        outs = (
            jax.ShapeDtypeStruct((sources, HEAD, PATCHES), BF16),
            jax.ShapeDtypeStruct(dkv, F32),
        )
        out_specs = (whole_spec(), whole_spec())
        scratch = [lists]
    return pl.pallas_call(
        functools.partial(attend_back_kernel, per_device, part, slot, last),
        out_shape=outs,
        in_specs=[scalar_spec(), scalar_spec()] + [whole_spec()] * (len(args) - 2),
        out_specs=out_specs,
        scratch_shapes=scratch,
        cost_estimate=pl.CostEstimate(
            flops=pairs * 10 * PATCHES * PATCHES * 256,
            bytes_accessed=x.size * 2 * 5,
            transcendentals=pairs * PATCHES * PATCHES,
        ),
        compiler_params=pltpu.CompilerParams(vmem_limit_bytes=60 << 20),
        name="attend_back%d" % part,
    )(*args)


def exchange(value, axis, bit):
    count = lax.axis_size(axis)
    return lax.ppermute(value, axis, [(source, source ^ bit) for source in range(count)])


def after(value, *earlier):
    return lax.optimization_barrier((value,) + earlier)[0]


def gather_all(value):
    bit = lax.axis_size("seq") // 2
    while bit:
        value = jnp.concatenate([value, exchange(value, "seq", bit)], axis=0)
        bit //= 2
    bit = lax.axis_size("pack") // 2
    while bit:
        value = jnp.concatenate([value, exchange(value, "pack", bit)], axis=0)
        bit //= 2
    return value


def halving_fits():
    return lax.axis_size("pack") == 2 and lax.axis_size("seq") == 16


class RowSum:
    def __init__(self, term_of, rows, columns, order):
        self.direct = not halving_fits()
        self.rows, self.columns, self.order = rows, columns, list(order)
        if self.direct:
            part = lax.psum_scatter(
                term_of(0, columns).astype(BF16), "seq", scatter_dimension=0, tiled=True
            )
            self.value = lax.psum(part, "pack").astype(F32)
            return
        self.pack = lax.axis_index("pack")
        self.index = lax.axis_index("seq")
        self.width = columns // 2
        theirs = term_of((1 - self.pack) * self.width, self.width).astype(BF16)
        came = exchange(theirs, "pack", 1)
        mine = term_of(self.pack * self.width, self.width).astype(BF16)
        shape = [2, 2, 2, 2, rows // 16, self.width]
        self.parts = [mine.reshape(shape), came.reshape(shape)]

    def pick(self, bit, which):
        axis = {8: 0, 4: 1, 2: 2, 1: 3}[bit]
        pieces = [lax.dynamic_slice_in_dim(part, which, 1, axis) for part in self.parts]
        return (pieces[0].astype(F32) + pieces[1].astype(F32)).astype(BF16)

    def stage(self):
        if self.direct:
            return ()
        bit = self.order.pop(0)
        own_bit = lax.rem(lax.div(self.index, bit), 2)
        send = self.pick(bit, 1 - own_bit)
        came = exchange(send, "seq", bit)
        self.parts = [self.pick(bit, own_bit), came]
        return (send,)

    def finish(self):
        if self.direct:
            return self.value
        while self.order:
            self.stage()
        own = (self.parts[0].astype(F32) + self.parts[1].astype(F32)).astype(BF16)
        own = own.reshape(self.rows // 16, self.width)
        other = exchange(own, "pack", 1)
        left = jnp.where(self.pack == 0, own, other)
        right = jnp.where(self.pack == 0, other, own)
        return jnp.concatenate([left, right], axis=1).astype(F32)


def columns_of(matrix, start, width, axis=1):
    if isinstance(start, int) and start == 0 and width == matrix.shape[axis]:
        return matrix
    return lax.dynamic_slice_in_dim(matrix, start, width, axis)


def local(
    hidden,
    cotangent,
    levels,
    segments,
    live_frames,
    noise_table,
    mod_weight,
    mod_bias,
    qkv_weight,
    qkv_bias,
    out_weight,
    out_bias,
    up_weight,
    up_bias,
    down_weight,
    down_bias,
):
    seq_index = lax.axis_index("seq")
    seq_count = lax.axis_size("seq")
    tokens = hidden.shape[1]
    width = hidden.shape[2]
    per_device = tokens // PATCHES
    frames = segments.shape[1]
    heads = width // HEAD
    copies = seq_count // heads
    hidden_units = up_weight.shape[1]
    level_count = noise_table.shape[0]
    share = width // seq_count
    clip_ids = segments[0]
    live = live_frames[0]

    frame_ids = jnp.arange(frames, dtype=jnp.int32)
    same_clip = clip_ids[:, None] == clip_ids[None, :]
    clip_starts = jnp.min(jnp.where(same_clip, frame_ids[None, :], frames), axis=1)
    cos_all, sin_all = rotary_tables((frame_ids - clip_starts).astype(F32))
    first_frame = seq_index * per_device
    own_cos = lax.dynamic_slice_in_dim(cos_all, first_frame, per_device)
    own_sin = lax.dynamic_slice_in_dim(sin_all, first_frame, per_device)
    own_cos = own_cos.transpose(1, 0, 2).reshape(HALF, tokens)
    own_sin = own_sin.transpose(1, 0, 2).reshape(HALF, tokens)

    embed = jnp.concatenate(
        [
            lax.dynamic_slice_in_dim(noise_table, levels[0, frame], 1, 0)
            for frame in range(per_device)
        ],
        axis=0,
    )
    cond = jax.nn.silu(embed).astype(BF16)
    modulation = jnp.dot(cond, mod_weight, preferred_element_type=F32) + mod_bias
    attn_shift, attn_scale, attn_gate, feed_shift, feed_scale, feed_gate = jnp.split(
        modulation, 6, axis=1
    )
    frame_rows = hidden[0].astype(F32).reshape(per_device, PATCHES, width)
    attn_value, attn_norm_back = jax.vjp(modulate_norm, frame_rows, attn_shift, attn_scale)
    attn_in = attn_value.reshape(tokens, width).astype(BF16)

    qkv = dot_over(qkv_weight, attn_in, 0, 1) + qkv_bias[:, None]
    qkv = qkv.reshape(3, heads, 2, HALF, tokens)
    turned = qkv[:2]
    lower = turned[:, :, 0] * own_cos - turned[:, :, 1] * own_sin
    upper = turned[:, :, 1] * own_cos + turned[:, :, 0] * own_sin
    turned = jnp.stack([lower, upper], axis=2)

    def by_frame(array):
        split = array.astype(BF16).reshape(heads, HEAD, per_device, PATCHES)
        return [split[:, :, place] for place in range(per_device)]

    queries = by_frame(turned[0] * (HEAD**-0.5))
    keys = by_frame(turned[1])
    values = by_frame(qkv[2])
    sent = jnp.stack(keys + values + queries[:1], axis=1)

    def to_heads(array):
        if copies > 1:
            array = jnp.concatenate([array] * copies, axis=0)
        return lax.all_to_all(array, "seq", 0, 0, tiled=True)

    def to_tokens(array):
        return lax.all_to_all(array, "seq", 0, 0, tiled=True)[:heads]

    x = to_heads(sent)
    head_queries = [x] + [
        to_heads(after(query, x[0, 0, :8]).reshape(heads, 1, HEAD, PATCHES)) for query in queries[1:]
    ]
    slots = [2 * per_device] + [0] * (per_device - 1)
    kv = None
    attended = []
    mixes = []
    for part in range(per_device):
        mix, wide, lse, kv = attend(
            part, per_device, slots[part], clip_ids, live, x, head_queries[part], kv
        )
        attended.append((wide, lse))
        mixes.append(to_tokens(mix).reshape(width, PATCHES))
    attn_rows = jnp.stack([dot_over(mix, out_weight, 0, 0) for mix in mixes]) + out_bias
    attn_mix = jnp.concatenate(mixes, axis=1)

    middle = frame_rows + attn_gate[:, None, :] * attn_rows
    feed_value, feed_norm_back = jax.vjp(modulate_norm, middle, feed_shift, feed_scale)
    feed_in = feed_value.reshape(tokens, width).astype(BF16)
    pre = jnp.dot(feed_in, up_weight, preferred_element_type=F32) + up_bias
    act_value, act_back = jax.vjp(gelu_tanh, pre)
    act = act_value.astype(BF16)
    grad_rows = cotangent[0].astype(F32).reshape(per_device, PATCHES, width)
    d_feed_out = (feed_gate[:, None, :] * grad_rows).reshape(tokens, width).astype(BF16)
    d_pre = act_back(dot_over(d_feed_out, down_weight, 1, 1))[0].astype(BF16)
    down_sum = RowSum(
        lambda start, size: dot_over(act, columns_of(d_feed_out, start, size), 0, 0),
        hidden_units,
        width,
        (1, 2, 8, 4),
    )
    down_bias_term = jnp.sum(d_feed_out.astype(F32), axis=0)
    d_feed_in = dot_over(d_pre, up_weight, 1, 1).reshape(per_device, PATCHES, width)
    up_sum = RowSum(
        lambda start, size: dot_over(feed_in, columns_of(d_pre, start, size), 0, 0),
        width,
        hidden_units,
        (2, 1, 8, 4),
    )
    up_bias_term = jnp.sum(d_pre.astype(F32), axis=0)
    d_middle_norm, d_feed_shift, d_feed_scale = feed_norm_back(d_feed_in)
    d_middle = grad_rows + d_middle_norm
    d_attn_gate = jnp.sum(d_middle * attn_rows, axis=1)
    d_attn_rows = (attn_gate[:, None, :] * d_middle).astype(BF16)
    d_attn_out = d_attn_rows.reshape(tokens, width)
    d_mixes = []
    for part in range(per_device):
        d_mix = dot_over(out_weight, d_attn_rows[part], 1, 1).astype(BF16)
        d_mixes.append(to_heads(d_mix.reshape(heads, HEAD, PATCHES)))
    out_sum = RowSum(
        lambda start, size: dot_over(attn_mix, columns_of(d_attn_out, start, size), 1, 0),
        width,
        width,
        (1, 2, 8, 4),
    )
    out_bias_term = jnp.sum(d_attn_out.astype(F32), axis=0)

    feed_out = jnp.dot(act, down_weight, preferred_element_type=F32) + down_bias
    feed_rows = feed_out.reshape(per_device, PATCHES, width)
    layer_out = (middle + feed_gate[:, None, :] * feed_rows).reshape(1, tokens, width).astype(BF16)
    d_feed_gate = jnp.sum(grad_rows * feed_rows, axis=1)

    early_mod = jnp.concatenate([d_attn_gate, d_feed_shift, d_feed_scale, d_feed_gate], axis=1)
    own_levels = levels[0]
    early_bias = jnp.concatenate([out_bias_term, up_bias_term, down_bias_term])
    bias_rows = early_bias.reshape(per_device, early_bias.shape[0] // per_device)
    early = jnp.concatenate(
        [
            early_mod.astype(BF16),
            bias_rows.astype(BF16),
            jnp.broadcast_to(lax.div(own_levels, 32)[:, None], (per_device, 128)).astype(BF16),
            jnp.broadcast_to(lax.rem(own_levels, 32)[:, None], (per_device, 128)).astype(BF16),
        ],
        axis=1,
    )
    early_all = gather_all(early)

    before = None
    d_queries = []
    sums = (down_sum, up_sum, out_sum)
    for part in range(per_device):
        d_mix = after(d_mixes[part], *[send for each in sums for send in each.stage()])
        result = attend_back(
            part,
            per_device,
            slots[part],
            clip_ids,
            live,
            x,
            head_queries[part],
            kv,
            attended[part][0],
            attended[part][1],
            d_mix,
            cos_all,
            sin_all,
            before,
        )
        if part < per_device - 1:
            d_query, before = result
            d_queries.append(to_tokens(d_query))
    result = after(result, *[send for each in sums for send in each.stage()])
    back = to_tokens(result)
    d_queries.append(back[:, 2 * per_device])

    def joined(blocks):
        return jnp.stack(blocks, axis=2).reshape(width, tokens)

    d_qkv = jnp.concatenate(
        [
            joined(d_queries),
            joined([back[:, place] for place in range(per_device)]),
            joined([back[:, per_device + place] for place in range(per_device)]),
        ],
        axis=0,
    )
    d_attn_in = dot_over(d_qkv, qkv_weight, 0, 1).reshape(per_device, PATCHES, width)
    qkv_sum = RowSum(
        lambda start, size: dot_over(attn_in, columns_of(d_qkv, start, size, 0), 0, 1),
        width,
        3 * width,
        (1, 2, 8, 4),
    )
    d_hidden_norm, d_attn_shift, d_attn_scale = attn_norm_back(d_attn_in)
    hidden_grad = (d_middle + d_hidden_norm).reshape(1, tokens, width).astype(BF16)
    qkv_bias_term = jnp.sum(d_qkv.astype(F32), axis=1)
    late = jnp.concatenate(
        [
            d_attn_shift.astype(BF16),
            d_attn_scale.astype(BF16),
            qkv_bias_term.reshape(per_device, 3 * width // per_device).astype(BF16),
        ],
        axis=1,
    )
    late_all = gather_all(late)
    down_weight_grad = down_sum.finish()
    up_weight_grad = up_sum.finish()
    out_weight_grad = out_sum.finish()
    qkv_weight_grad = qkv_sum.finish()

    devices = late_all.shape[0] // per_device

    def bias_share(rows, sizes):
        flat = rows.reshape(devices, sum(sizes))
        shares = []
        at = 0
        for size in sizes:
            piece = size // seq_count
            own = lax.dynamic_slice_in_dim(flat, at + seq_index * piece, piece, 1)
            shares.append(jnp.sum(own.astype(F32), axis=0))
            at += size
        return shares

    early_width = 4 * width
    bias_width = early_bias.shape[0] // per_device
    out_bias_grad, up_bias_grad, down_bias_grad = bias_share(
        early_all[:, early_width : early_width + bias_width], (width, hidden_units, width)
    )
    (qkv_bias_grad,) = bias_share(late_all[:, 2 * width :], (3 * width,))
    coarse = early_all[:, early_width + bias_width].astype(jnp.int32)
    fine = early_all[:, early_width + bias_width + 128].astype(jnp.int32)
    all_levels = coarse * 32 + fine
    picks = (all_levels[:, None] == jnp.arange(level_count, dtype=jnp.int32)[None, :]).astype(F32)
    own_table = lax.dynamic_slice_in_dim(noise_table, seq_index * share, share, 1)
    all_embed = jnp.dot(picks, own_table, precision=PRECISE, preferred_element_type=F32)
    silu_value, silu_back = jax.vjp(jax.nn.silu, all_embed)
    all_cond = silu_value.astype(BF16)
    d_mod_early = early_all[:, :early_width]
    d_mod_late = late_all[:, : 2 * width]
    own_mod = lax.dynamic_slice_in_dim(mod_weight, seq_index * share, share, 0)
    d_cond_early = dot_over(d_mod_early, own_mod[:, 2 * width :], 1, 1)
    d_cond = d_cond_early + dot_over(d_mod_late, own_mod[:, : 2 * width], 1, 1)
    d_embed = silu_back(d_cond)[0]
    table_grad = lax.dot_general(
        picks, d_embed, (((0,), (0,)), ((), ())), precision=PRECISE, preferred_element_type=F32
    )
    mod_weight_grad = jnp.concatenate(
        [dot_over(all_cond, d_mod_late, 0, 0), dot_over(all_cond, d_mod_early, 0, 0)], axis=1
    )
    bias_piece = mod_bias.shape[0] // seq_count
    d_mod_sum = jnp.concatenate(
        [jnp.sum(d_mod_late.astype(F32), axis=0), jnp.sum(d_mod_early.astype(F32), axis=0)]
    )
    mod_bias_grad = lax.dynamic_slice_in_dim(d_mod_sum, seq_index * bias_piece, bias_piece)
    return (
        layer_out,
        hidden_grad,
        table_grad,
        mod_weight_grad,
        mod_bias_grad,
        qkv_weight_grad,
        qkv_bias_grad,
        out_weight_grad,
        out_bias_grad,
        up_weight_grad,
        up_bias_grad,
        down_weight_grad,
        down_bias_grad,
    )


def solution(mesh):
    in_specs = (
        P("pack", "seq", None),
        P("pack", "seq", None),
        P("pack", "seq"),
        P("pack", None),
        P("pack", None),
    ) + (P(),) * 11
    out_specs = (
        P("pack", "seq", None),
        P("pack", "seq", None),
        P(None, "seq"),
        P("seq", None),
        P("seq"),
        P("seq", None),
        P("seq"),
        P("seq", None),
        P("seq"),
        P("seq", None),
        P("seq"),
        P("seq", None),
        P("seq"),
    )
    return jax.shard_map(local, mesh=mesh, in_specs=in_specs, out_specs=out_specs, check_vma=False)
```

```python
import functools

import jax
import jax.numpy as jnp
from jax import lax
from jax.experimental import pallas as pl
from jax.experimental.pallas import tpu as pltpu
from jax.sharding import PartitionSpec as P

HEAD = 64
PATCHES = 256
SIDE = 16
EPSILON = 1e-06
PRECISE = lax.Precision.HIGHEST
HALF = HEAD // 2
F32 = jnp.float32
BF16 = jnp.bfloat16


def modulate_norm(rows, shift, scale):
    center = jnp.mean(rows, axis=-1, keepdims=True)
    centered = rows - center
    spread = jnp.mean(centered * centered, axis=-1, keepdims=True)
    normed = centered * lax.rsqrt(spread + EPSILON)
    return normed * (1.0 + scale[:, None, :]) + shift[:, None, :]


def gelu_tanh(values):
    return jax.nn.gelu(values, approximate=True)


def dot_over(first, second, first_dim, second_dim):
    return lax.dot_general(
        first, second, (((first_dim,), (second_dim,)), ((), ())), preferred_element_type=F32
    )


def spatial_angles():
    time_pairs = HALF // 4
    space_pairs = (HALF - time_pairs) // 2
    patch = jnp.arange(PATCHES, dtype=jnp.int32)
    row_pos = (patch // SIDE).astype(F32)
    col_pos = (patch % SIDE).astype(F32)
    time_freq = 10000.0 ** (-jnp.arange(time_pairs, dtype=F32) / time_pairs)
    space_freq = 10000.0 ** (-jnp.arange(space_pairs, dtype=F32) / space_pairs)
    space = jnp.concatenate(
        [space_freq[:, None] * row_pos[None, :], space_freq[:, None] * col_pos[None, :]], axis=0
    )
    return time_freq, space


def rotary_tables(time_frames):
    time_freq, space = spatial_angles()
    count = time_frames.shape[0]
    time_angle = time_frames[:, None] * time_freq[None, :]

    def whole(function):
        return jnp.concatenate(
            [
                jnp.broadcast_to(
                    function(time_angle)[:, :, None], (count, time_freq.shape[0], PATCHES)
                ),
                jnp.broadcast_to(function(space)[None], (count,) + space.shape),
            ],
            axis=1,
        )

    return whole(jnp.cos), whole(jnp.sin)


def walk_frames(frames, per_device, part, segments_ref, live_ref, list_ref, visit):
    def step(source, held):
        for place in range(per_device):
            frame = source * per_device + place
            before = jnp.maximum(frame - 1, 0)
            fresh = (frame == 0) | (segments_ref[frame] != segments_ref[before])
            held = jnp.where(fresh, 0, held)
            list_ref[held] = frame
            if place == part:
                visit(source, frame, held + 1)
            held = held + jnp.where(live_ref[frame] == 1, 1, 0)
        return held

    lax.fori_loop(0, frames // per_device, step, jnp.int32(0))


def attend_kernel(per_device, part, slot, segments_ref, live_ref, x_ref, q_ref, *refs):
    if part == 0:
        mix_ref, wide_ref, lse_ref, kv_ref, list_ref = refs
    else:
        kv_ref, mix_ref, wide_ref, lse_ref, list_ref = refs
    frames = kv_ref.shape[0]

    def turn(source, carry):
        for place in range(per_device):
            both = jnp.concatenate(
                [x_ref[source, place], x_ref[source, per_device + place]], axis=0
            )
            kv_ref[source * per_device + place] = both.astype(F32).T.astype(BF16)
        return carry

    if part == 0:
        lax.fori_loop(0, frames // per_device, turn, 0)

    def visit(source, frame, count):
        query = q_ref[source, slot]
        query_side = jnp.concatenate([query, jnp.zeros_like(query)], axis=0)

        def scores_of(other):
            return jnp.dot(kv_ref[other], query_side, preferred_element_type=F32)

        def mixed(other, weights):
            value = x_ref[lax.div(other, per_device), per_device + lax.rem(other, per_device)]
            return jnp.dot(value, weights.astype(BF16), preferred_element_type=F32)

        def join(others, carry):
            scores = [scores_of(other) for other in others]
            tops = [jnp.max(score, axis=0, keepdims=True) for score in scores]
            new_top = functools.reduce(jnp.maximum, tops)
            if carry is not None:
                top, total, accum = carry
                new_top = jnp.maximum(top, new_top)
                shrink = jnp.exp(top - new_top)
                total = total * shrink
                accum = accum * shrink
            for index, score in enumerate(scores):
                weights = jnp.exp(score - new_top)
                added = jnp.sum(weights, axis=0, keepdims=True)
                product = mixed(others[index], weights)
                if carry is None and index == 0:
                    total, accum = added, product
                else:
                    total, accum = total + added, accum + product
            return new_top, total, accum

        others = count - 1
        carry = join([frame], None)
        carry = lax.fori_loop(
            0,
            lax.div(others, 2),
            lambda index, state: join([list_ref[2 * index], list_ref[2 * index + 1]], state),
            carry,
        )
        top, total, accum = lax.fori_loop(
            0,
            lax.rem(others, 2),
            lambda unused, state: join([list_ref[others - 1]], state),
            carry,
        )
        result = accum * (1.0 / total)
        wide_ref[source] = result
        mix_ref[source] = result.astype(BF16)
        lse_ref[pl.ds(source, 1), :] = top + jnp.log(total)

    walk_frames(frames, per_device, part, segments_ref, live_ref, list_ref, visit)


def whole_spec():
    return pl.BlockSpec(memory_space=pltpu.VMEM)


def scalar_spec():
    return pl.BlockSpec(memory_space=pltpu.SMEM)


def attend(part, per_device, slot, segments, live, x, query, kv):
    sources = x.shape[0]
    frames = sources * per_device
    pairs = sources * 6
    outs = [
        jax.ShapeDtypeStruct((sources, HEAD, PATCHES), BF16),
        jax.ShapeDtypeStruct((sources, HEAD, PATCHES), F32),
        jax.ShapeDtypeStruct((sources, PATCHES), F32),
    ]
    args = [segments, live, x, query]
    if part == 0:
        outs.append(jax.ShapeDtypeStruct((frames, PATCHES, 2 * HEAD), BF16))
    else:
        args.append(kv)
    result = pl.pallas_call(
        functools.partial(attend_kernel, per_device, part, slot),
        out_shape=tuple(outs),
        in_specs=[scalar_spec(), scalar_spec()] + [whole_spec()] * (len(args) - 2),
        out_specs=(whole_spec(),) * len(outs),
        scratch_shapes=[pltpu.SMEM((frames,), jnp.int32)],
        cost_estimate=pl.CostEstimate(
            flops=pairs * 4 * PATCHES * PATCHES * 256,
            bytes_accessed=x.size * 2 * 3,
            transcendentals=pairs * PATCHES * PATCHES,
        ),
        compiler_params=pltpu.CompilerParams(vmem_limit_bytes=40 << 20),
        name="attend%d" % part,
    )(*args)
    return result if part == 0 else tuple(result) + (kv,)


def attend_back_kernel(
    per_device,
    part,
    slot,
    last,
    segments_ref,
    live_ref,
    x_ref,
    q_ref,
    kv_ref,
    wide_ref,
    lse_ref,
    d_mix_ref,
    cos_ref,
    sin_ref,
    *refs
):
    if last:
        before_ref, out_ref, dkv_ref, list_ref = refs
    else:
        out_ref, dkv_ref, list_ref = refs
    frames = kv_ref.shape[0]

    def clear(frame, carry):
        dkv_ref[frame] = jnp.zeros((PATCHES, 2 * HEAD), F32)
        return carry

    lax.fori_loop(0, frames, clear, 0)

    def unturn(frame, values):
        lower = values[:HALF]
        upper = values[HALF:]
        cosine = cos_ref[frame]
        sine = sin_ref[frame]
        return jnp.concatenate([lower * cosine + upper * sine, upper * cosine - lower * sine], axis=0)

    def visit(source, frame, count):
        query = q_ref[source, slot]
        d_mix = d_mix_ref[source]
        blank = jnp.zeros_like(query)
        query_side = jnp.concatenate([query, blank], axis=0)
        d_mix_side = jnp.concatenate([blank, d_mix], axis=0)
        both = jnp.concatenate(
            [query_side.astype(F32).T.astype(BF16), d_mix_side.astype(F32).T.astype(BF16)], axis=0
        )
        lse = lse_ref[pl.ds(source, 1), :]
        delta = jnp.sum(d_mix.astype(F32) * wide_ref[source], axis=0, keepdims=True)

        def block(other):
            key_value = kv_ref[other]
            scores = jnp.dot(key_value, query_side, preferred_element_type=F32)
            d_weights = jnp.dot(key_value, d_mix_side, preferred_element_type=F32)
            weights = jnp.exp(scores - lse)
            d_scores = (weights * (d_weights - delta)).astype(BF16)
            sides = jnp.concatenate([d_scores, weights.astype(BF16)], axis=1)
            dkv_ref[other] += jnp.dot(sides, both, preferred_element_type=F32)
            key = x_ref[lax.div(other, per_device), lax.rem(other, per_device)]
            return jnp.dot(key, d_scores, preferred_element_type=F32)

        d_query = lax.fori_loop(
            0,
            lax.div(count, 2),
            lambda index, state: state
            + block(list_ref[2 * index])
            + block(list_ref[2 * index + 1]),
            jnp.zeros((HEAD, PATCHES), F32),
        )
        d_query = lax.fori_loop(
            0,
            lax.rem(count, 2),
            lambda unused, state: state + block(list_ref[count - 1]),
            d_query,
        )
        d_query = unturn(frame, d_query * (HEAD**-0.5)).astype(BF16)
        if last:
            out_ref[source, 2 * per_device] = d_query
        else:
            out_ref[source] = d_query

    walk_frames(frames, per_device, part, segments_ref, live_ref, list_ref, visit)

    def finish(source, carry):
        for place in range(per_device):
            frame = source * per_device + place
            both = (dkv_ref[frame] + before_ref[frame]).T
            out_ref[source, place] = unturn(frame, both[:HEAD]).astype(BF16)
            out_ref[source, per_device + place] = both[HEAD:].astype(BF16)
        return carry

    if last:
        lax.fori_loop(0, frames // per_device, finish, 0)


def attend_back(
    part, per_device, slot, segments, live, x, query, kv, wide, lse, d_mix, cosine, sine, before
):
    sources = x.shape[0]
    frames = sources * per_device
    pairs = sources * 6
    last = part == per_device - 1
    args = [segments, live, x, query, kv, wide, lse, d_mix, cosine, sine]
    dkv = (frames, PATCHES, 2 * HEAD)
    lists = pltpu.SMEM((frames,), jnp.int32)
    if last:
        args.append(before)
        outs = jax.ShapeDtypeStruct((sources, 2 * per_device + 1, HEAD, PATCHES), BF16)
        out_specs = whole_spec()
        scratch = [pltpu.VMEM(dkv, F32), lists]
    else:
        outs = (
            jax.ShapeDtypeStruct((sources, HEAD, PATCHES), BF16),
            jax.ShapeDtypeStruct(dkv, F32),
        )
        out_specs = (whole_spec(), whole_spec())
        scratch = [lists]
    return pl.pallas_call(
        functools.partial(attend_back_kernel, per_device, part, slot, last),
        out_shape=outs,
        in_specs=[scalar_spec(), scalar_spec()] + [whole_spec()] * (len(args) - 2),
        out_specs=out_specs,
        scratch_shapes=scratch,
        cost_estimate=pl.CostEstimate(
            flops=pairs * 10 * PATCHES * PATCHES * 256,
            bytes_accessed=x.size * 2 * 5,
            transcendentals=pairs * PATCHES * PATCHES,
        ),
        compiler_params=pltpu.CompilerParams(vmem_limit_bytes=60 << 20),
        name="attend_back%d" % part,
    )(*args)


def exchange(value, axis, bit):
    count = lax.axis_size(axis)
    return lax.ppermute(value, axis, [(source, source ^ bit) for source in range(count)])


def after(value, *earlier):
    return lax.optimization_barrier((value,) + earlier)[0]


def gather_all(value):
    bit = lax.axis_size("seq") // 2
    while bit:
        value = jnp.concatenate([value, exchange(value, "seq", bit)], axis=0)
        bit //= 2
    bit = lax.axis_size("pack") // 2
    while bit:
        value = jnp.concatenate([value, exchange(value, "pack", bit)], axis=0)
        bit //= 2
    return value


def halving_fits():
    return lax.axis_size("pack") == 2 and lax.axis_size("seq") == 16


class RowSum:
    def __init__(self, mine, came, order):
        self.order = list(order)
        self.index = lax.axis_index("seq")
        rows = mine.shape[-2]
        self.tail = (rows // 16, mine.shape[-1])
        self.lead = mine.shape[:-2]
        shape = self.lead + (2, 2, 2, 2) + self.tail
        self.parts = [mine.reshape(shape), came.reshape(shape)]

    def pick(self, bit, which):
        axis = len(self.lead) + {8: 0, 4: 1, 2: 2, 1: 3}[bit]
        pieces = [lax.dynamic_slice_in_dim(part, which, 1, axis) for part in self.parts]
        return (pieces[0].astype(F32) + pieces[1].astype(F32)).astype(BF16)

    def stage(self):
        bit = self.order.pop(0)
        own_bit = lax.rem(lax.div(self.index, bit), 2)
        send = self.pick(bit, 1 - own_bit)
        came = exchange(send, "seq", bit)
        self.parts = [self.pick(bit, own_bit), came]
        return send

    def finish(self):
        while self.order:
            self.stage()
        own = (self.parts[0].astype(F32) + self.parts[1].astype(F32)).astype(BF16)
        own = own.reshape(self.lead + self.tail)
        other = exchange(own, "pack", 1)
        first = lax.axis_index("pack") == 0
        return jnp.where(first, own, other), jnp.where(first, other, own)


def row_sum_direct(term):
    part = lax.psum_scatter(term.astype(BF16), "seq", scatter_dimension=0, tiled=True)
    return lax.psum(part, "pack").astype(F32)


def project_kernel(
    per_device,
    hidden_ref,
    shift_ref,
    scale_ref,
    wq_ref,
    wk_ref,
    wv_ref,
    bq_ref,
    bk_ref,
    bv_ref,
    cos_ref,
    sin_ref,
    in_ref,
    first_ref,
    rest_ref,
):
    @pl.when(pl.program_id(0) == 0)
    def _():
        for place in range(per_device):
            rows = pl.ds(place * PATCHES, PATCHES)
            values = hidden_ref[rows, :].astype(F32)
            centered = values - jnp.mean(values, axis=-1, keepdims=True)
            spread = jnp.mean(centered * centered, axis=-1, keepdims=True)
            normed = centered * lax.rsqrt(spread + EPSILON)
            scale = scale_ref[pl.ds(place, 1), :]
            in_ref[rows, :] = (normed * (1.0 + scale) + shift_ref[pl.ds(place, 1), :]).astype(BF16)

    rows = in_ref[...]
    group = wq_ref.shape[1] // HEAD

    def turned(values, place):
        lower = values[:HALF]
        upper = values[HALF:]
        cosine = cos_ref[place]
        sine = sin_ref[place]
        return jnp.concatenate([lower * cosine - upper * sine, upper * cosine + lower * sine], axis=0)

    for kind, (weight_ref, bias_ref) in enumerate(
        ((wq_ref, bq_ref), (wk_ref, bk_ref), (wv_ref, bv_ref))
    ):
        flat = jnp.dot(rows, weight_ref[...], preferred_element_type=F32) + bias_ref[...]
        for place in range(per_device):
            block = flat[place * PATCHES : (place + 1) * PATCHES].T
            for head in range(group):
                values = block[head * HEAD : (head + 1) * HEAD]
                if kind == 0:
                    values = (turned(values, place) * (HEAD**-0.5)).astype(BF16)
                    if place == 0:
                        first_ref[head, 2 * per_device] = values
                    else:
                        rest_ref[head, place - 1] = values
                elif kind == 1:
                    first_ref[head, place] = turned(values, place).astype(BF16)
                else:
                    first_ref[head, per_device + place] = values.astype(BF16)


def project(per_device, hidden, shift, scale, weight, bias, cosine, sine):
    tokens, width = hidden.shape
    heads = width // HEAD
    group = 2
    lanes = group * HEAD
    steps = heads // group
    bias_row = bias[None, :]

    def whole(shape):
        return pl.BlockSpec(shape, lambda step: (0,) * len(shape))

    def part(kind, rows):
        return pl.BlockSpec((rows, lanes), lambda step: (0, kind * steps + step))

    first = (heads, 2 * per_device + 1, HEAD, PATCHES)
    rest = (heads, per_device - 1, HEAD, PATCHES)
    return pl.pallas_call(
        functools.partial(project_kernel, per_device),
        grid=(steps,),
        out_shape=(
            jax.ShapeDtypeStruct((tokens, width), BF16),
            jax.ShapeDtypeStruct(first, BF16),
            jax.ShapeDtypeStruct(rest, BF16),
        ),
        in_specs=[whole((tokens, width)), whole(shift.shape), whole(scale.shape)]
        + [part(kind, width) for kind in range(3)]
        + [part(kind, 1) for kind in range(3)]
        + [whole(cosine.shape), whole(sine.shape)],
        out_specs=(
            whole((tokens, width)),
            pl.BlockSpec((group,) + first[1:], lambda step: (step, 0, 0, 0)),
            pl.BlockSpec((group,) + rest[1:], lambda step: (step, 0, 0, 0)),
        ),
        cost_estimate=pl.CostEstimate(
            flops=2 * tokens * width * 3 * width,
            bytes_accessed=2 * (weight.size + 5 * tokens * width),
            transcendentals=0,
        ),
        compiler_params=pltpu.CompilerParams(vmem_limit_bytes=40 << 20),
        name="project",
    )(hidden, shift, scale, weight, weight, weight, bias_row, bias_row, bias_row, cosine, sine)


GELU_SLOPE = 0.7978845608028654
GELU_CUBE = 0.044715


def feed_kernel(
    carried,
    which_ref,
    in_ref,
    d_out_ref,
    up_a_ref,
    up_b_ref,
    bias_a_ref,
    bias_b_ref,
    down_a_ref,
    down_b_ref,
    *refs
):
    if carried:
        out_before_ref, d_in_before_ref = refs[:2]
        refs = refs[2:]
    out_ref, d_in_ref, d_up_ref, d_down_ref, d_bias_ref, turned_ref = refs

    @pl.when(pl.program_id(0) == 0)
    def _():
        turned_ref[...] = in_ref[...].astype(F32).T.astype(BF16)
        if carried:
            out_ref[...] = out_before_ref[...]
            d_in_ref[...] = d_in_before_ref[...]
        else:
            out_ref[...] = jnp.zeros_like(out_ref)
            d_in_ref[...] = jnp.zeros_like(d_in_ref)

    up = jnp.concatenate([up_a_ref[...], up_b_ref[...]], axis=1)
    down = jnp.concatenate([down_a_ref[...], down_b_ref[...]], axis=0)
    bias = jnp.concatenate([bias_a_ref[...], bias_b_ref[...]], axis=1)
    d_out = d_out_ref[...]
    pre = jnp.dot(in_ref[...], up, preferred_element_type=F32) + bias
    d_act = dot_over(d_out, down, 1, 1)
    square = pre * pre
    bend = jnp.tanh(GELU_SLOPE * pre * (1.0 + GELU_CUBE * square))
    half = 0.5 * (1.0 + bend)
    act = (pre * half).astype(BF16)
    slope = half + (0.5 * GELU_SLOPE) * pre * (1.0 - bend * bend) * (
        1.0 + (3.0 * GELU_CUBE) * square
    )
    d_pre = (d_act * slope).astype(BF16)
    out_ref[...] += jnp.dot(act, down, preferred_element_type=F32)
    d_in_ref[...] += dot_over(d_pre, up, 1, 1)
    d_up_ref[...] = jnp.dot(turned_ref[...], d_pre, preferred_element_type=F32).astype(BF16)
    d_down_ref[...] = jnp.dot(
        act.astype(F32).T.astype(BF16), d_out, preferred_element_type=F32
    ).astype(BF16)
    d_bias_ref[...] = jnp.sum(d_pre.astype(F32), axis=0, keepdims=True)


def feed(which, feed_in, d_feed_out, up_weight, up_bias, down_weight, before):
    tokens, width = feed_in.shape
    hidden_units = up_weight.shape[1]
    small = 128
    steps = hidden_units // (4 * small)
    own = hidden_units // 2

    def whole(shape):
        return pl.BlockSpec(shape, lambda step, which: (0,) * len(shape))

    def group(nth):
        return lambda step, which: 2 * (2 * step + nth) + which[0]

    def columns(nth, rows):
        return pl.BlockSpec((rows, small), lambda step, which: (0, group(nth)(step, which)))

    def rows_of(nth):
        return pl.BlockSpec((small, width), lambda step, which: (group(nth)(step, which), 0))

    args = [feed_in, d_feed_out, up_weight, up_weight, up_bias[None], up_bias[None]]
    args += [down_weight, down_weight]
    specs = [whole((tokens, width)), whole((tokens, width)), columns(0, width), columns(1, width)]
    specs += [columns(0, 1), columns(1, 1), rows_of(0), rows_of(1)]
    if before is not None:
        args += list(before)
        specs += [whole((tokens, width)), whole((tokens, width))]
    return pl.pallas_call(
        functools.partial(feed_kernel, before is not None),
        grid_spec=pltpu.PrefetchScalarGridSpec(
            num_scalar_prefetch=1,
            grid=(steps,),
            in_specs=specs,
            out_specs=(
                whole((tokens, width)),
                whole((tokens, width)),
                pl.BlockSpec((width, 2 * small), lambda step, which: (0, step)),
                pl.BlockSpec((2 * small, width), lambda step, which: (step, 0)),
                pl.BlockSpec((1, 2 * small), lambda step, which: (0, step)),
            ),
            scratch_shapes=[pltpu.VMEM((width, tokens), BF16)],
        ),
        out_shape=(
            jax.ShapeDtypeStruct((tokens, width), F32),
            jax.ShapeDtypeStruct((tokens, width), F32),
            jax.ShapeDtypeStruct((width, own), BF16),
            jax.ShapeDtypeStruct((own, width), BF16),
            jax.ShapeDtypeStruct((1, own), F32),
        ),
        cost_estimate=pl.CostEstimate(
            flops=12 * tokens * width * own,
            bytes_accessed=2 * (4 * own * width + 8 * tokens * width),
            transcendentals=tokens * own,
        ),
        compiler_params=pltpu.CompilerParams(vmem_limit_bytes=56 << 20),
        name="feed%d" % (before is not None),
    )(which.reshape(1), *args)


def unproject_kernel(
    per_device, carried, which_ref, in_ref, first_ref, back_ref, wq_ref, wk_ref, wv_ref, *refs
):
    if carried:
        before_ref = refs[0]
        refs = refs[1:]
    d_in_ref, d_weight_ref, d_bias_ref, turned_ref = refs

    @pl.when(pl.program_id(0) == 0)
    def _():
        turned_ref[...] = in_ref[...].astype(F32).T.astype(BF16)
        if carried:
            d_in_ref[...] = before_ref[...]
        else:
            d_in_ref[...] = jnp.zeros_like(d_in_ref)

    group = wq_ref.shape[1] // HEAD

    def token_major(block_of):
        rows = []
        for place in range(per_device):
            block = jnp.concatenate([block_of(head, place) for head in range(group)], axis=0)
            rows.append(block.astype(F32).T.astype(BF16))
        return jnp.concatenate(rows, axis=0)

    def query_block(head, place):
        if place == per_device - 1:
            return back_ref[head, 2 * per_device]
        return first_ref[head, place]

    sides = jnp.concatenate(
        [
            token_major(query_block),
            token_major(lambda head, place: back_ref[head, place]),
            token_major(lambda head, place: back_ref[head, per_device + place]),
        ],
        axis=1,
    )
    weights = jnp.concatenate([wq_ref[...], wk_ref[...], wv_ref[...]], axis=1)
    d_in_ref[...] += dot_over(sides, weights, 1, 1)
    d_weight = jnp.dot(turned_ref[...], sides, preferred_element_type=F32).astype(BF16)
    d_bias = jnp.sum(sides.astype(F32), axis=0, keepdims=True)
    lanes = group * HEAD
    for kind in range(3):
        d_weight_ref[kind] = d_weight[:, kind * lanes : (kind + 1) * lanes]
        d_bias_ref[kind] = d_bias[:, kind * lanes : (kind + 1) * lanes]


def unproject(per_device, which, attn_in, first, back, weight, before):
    tokens, width = attn_in.shape
    heads = width // HEAD
    group = 2
    lanes = group * HEAD
    groups = heads // group
    steps = groups // 2

    def whole(shape):
        return pl.BlockSpec(shape, lambda step, which: (0,) * len(shape))

    def blocks(array):
        return pl.BlockSpec(
            (group,) + array.shape[1:], lambda step, which: (which[0] * steps + step, 0, 0, 0)
        )

    def part(kind):
        return pl.BlockSpec(
            (width, lanes), lambda step, which: (0, kind * groups + which[0] * steps + step)
        )

    args = [attn_in, first, back, weight, weight, weight]
    specs = [whole((tokens, width)), blocks(first), blocks(back), part(0), part(1), part(2)]
    if before is not None:
        args.append(before)
        specs.append(whole((tokens, width)))
    return pl.pallas_call(
        functools.partial(unproject_kernel, per_device, before is not None),
        grid_spec=pltpu.PrefetchScalarGridSpec(
            num_scalar_prefetch=1,
            grid=(steps,),
            in_specs=specs,
            out_specs=(
                whole((tokens, width)),
                pl.BlockSpec((3, width, lanes), lambda step, which: (0, 0, step)),
                pl.BlockSpec((3, 1, lanes), lambda step, which: (0, 0, step)),
            ),
            scratch_shapes=[pltpu.VMEM((width, tokens), BF16)],
        ),
        out_shape=(
            jax.ShapeDtypeStruct((tokens, width), F32),
            jax.ShapeDtypeStruct((3, width, width // 2), BF16),
            jax.ShapeDtypeStruct((3, 1, width // 2), F32),
        ),
        cost_estimate=pl.CostEstimate(
            flops=6 * tokens * width * width,
            bytes_accessed=2 * (3 * width * width + 6 * tokens * width),
            transcendentals=0,
        ),
        compiler_params=pltpu.CompilerParams(vmem_limit_bytes=40 << 20),
        name="unproject%d" % (before is not None),
    )(which.reshape(1), *args)


def columns_of(matrix, start, width, axis=1):
    if isinstance(start, int) and start == 0 and width == matrix.shape[axis]:
        return matrix
    return lax.dynamic_slice_in_dim(matrix, start, width, axis)


def local(
    hidden,
    cotangent,
    levels,
    segments,
    live_frames,
    noise_table,
    mod_weight,
    mod_bias,
    qkv_weight,
    qkv_bias,
    out_weight,
    out_bias,
    up_weight,
    up_bias,
    down_weight,
    down_bias,
):
    seq_index = lax.axis_index("seq")
    seq_count = lax.axis_size("seq")
    tokens = hidden.shape[1]
    width = hidden.shape[2]
    per_device = tokens // PATCHES
    frames = segments.shape[1]
    heads = width // HEAD
    copies = seq_count // heads
    hidden_units = up_weight.shape[1]
    level_count = noise_table.shape[0]
    share = width // seq_count
    clip_ids = segments[0]
    live = live_frames[0]

    pack = lax.axis_index("pack")
    halves = halving_fits()
    frame_ids = jnp.arange(frames, dtype=jnp.int32)
    same_clip = clip_ids[:, None] == clip_ids[None, :]
    clip_starts = jnp.min(jnp.where(same_clip, frame_ids[None, :], frames), axis=1)
    frame_times = (frame_ids - clip_starts).astype(F32)
    own_cos, own_sin = rotary_tables(
        lax.dynamic_slice_in_dim(frame_times, seq_index * per_device, per_device)
    )

    embed = jnp.concatenate(
        [
            lax.dynamic_slice_in_dim(noise_table, levels[0, frame], 1, 0)
            for frame in range(per_device)
        ],
        axis=0,
    )
    cond = jax.nn.silu(embed).astype(BF16)
    modulation = jnp.dot(cond, mod_weight[:, : 2 * width], preferred_element_type=F32)
    attn_shift, attn_scale = jnp.split(modulation + mod_bias[: 2 * width], 2, axis=1)
    attn_in, sent, rest = project(
        per_device, hidden[0], attn_shift, attn_scale, qkv_weight, qkv_bias, own_cos, own_sin
    )

    def to_heads(array):
        if copies > 1:
            array = jnp.concatenate([array] * copies, axis=0)
        return lax.all_to_all(array, "seq", 0, 0, tiled=True)

    def to_tokens(array):
        return lax.all_to_all(array, "seq", 0, 0, tiled=True)[:heads]

    x = to_heads(sent)
    late_modulation = jnp.dot(
        after(cond, attn_in), mod_weight[:, 2 * width :], preferred_element_type=F32
    )
    attn_gate, feed_shift, feed_scale, feed_gate = jnp.split(
        late_modulation + mod_bias[2 * width :], 4, axis=1
    )
    cos_all, sin_all = rotary_tables(after(frame_times, attn_in))
    grad_rows = cotangent[0].astype(F32).reshape(per_device, PATCHES, width)
    d_feed_out = (feed_gate[:, None, :] * grad_rows).reshape(tokens, width).astype(BF16)
    head_queries = [x] + [
        to_heads(after(rest[:, place : place + 1], x[0, 0, :8])) for place in range(per_device - 1)
    ]
    slots = [2 * per_device] + [0] * (per_device - 1)
    kv = None
    attended = []
    mixes = []
    for part in range(per_device):
        mix, wide, lse, kv = attend(
            part, per_device, slots[part], clip_ids, live, x, head_queries[part], kv
        )
        attended.append((wide, lse))
        mixes.append(to_tokens(mix).reshape(width, PATCHES))
    attn_rows = jnp.stack([dot_over(mix, out_weight, 0, 0) for mix in mixes]) + out_bias
    attn_mix = jnp.concatenate(mixes, axis=1)

    frame_rows = hidden[0].astype(F32).reshape(per_device, PATCHES, width)
    middle = frame_rows + attn_gate[:, None, :] * attn_rows
    feed_value, feed_norm_back = jax.vjp(modulate_norm, middle, feed_shift, feed_scale)
    feed_in = feed_value.reshape(tokens, width).astype(BF16)
    feed_args = (feed_in, d_feed_out, up_weight, up_bias, down_weight)
    theirs = feed(1 - pack if halves else pack * 0 + 1, *feed_args, None)
    mine = feed(pack if halves else pack * 0, *feed_args, theirs[:2])
    feed_rows, d_feed_in = [each.reshape(per_device, PATCHES, width) for each in mine[:2]]
    small = 128

    def in_order(own, other):
        if halves:
            even, odd = jnp.where(pack == 0, own, other), jnp.where(pack == 0, other, own)
        else:
            even, odd = own, other
        rows = own.shape[0]
        return jnp.stack(
            [even.reshape(rows, -1, small), odd.reshape(rows, -1, small)], axis=2
        ).reshape(rows, -1)

    up_bias_term = in_order(mine[4], theirs[4])[0]
    down_bias_term = jnp.sum(d_feed_out.astype(F32), axis=0)
    d_middle_norm, d_feed_shift, d_feed_scale = feed_norm_back(d_feed_in)
    d_middle = grad_rows + d_middle_norm
    d_attn_gate = jnp.sum(d_middle * attn_rows, axis=1)
    d_attn_rows = (attn_gate[:, None, :] * d_middle).astype(BF16)
    d_attn_out = d_attn_rows.reshape(tokens, width)
    d_mixes = []
    for part in range(per_device):
        d_mix = dot_over(out_weight, d_attn_rows[part], 1, 1).astype(BF16)
        d_mixes.append(to_heads(d_mix.reshape(heads, HEAD, PATCHES)))

    def out_term(start, size):
        return dot_over(attn_mix, columns_of(d_attn_out, start, size), 1, 0).astype(BF16)

    sums = ()
    if halves:
        up_sum = RowSum(mine[2], exchange(theirs[2], "pack", 1), (2, 1, 4, 8))
        down_sum = RowSum(mine[3], exchange(theirs[3], "pack", 1), (1, 2, 4, 8))
        out_theirs = exchange(out_term((1 - pack) * (width // 2), width // 2), "pack", 1)
        out_sum = RowSum(out_term(pack * (width // 2), width // 2), out_theirs, (1, 2, 4, 8))
        sums = (down_sum, up_sum, out_sum)
    out_bias_term = jnp.sum(d_attn_out.astype(F32), axis=0)

    feed_rows = feed_rows + down_bias
    layer_out = (middle + feed_gate[:, None, :] * feed_rows).reshape(1, tokens, width).astype(BF16)
    d_feed_gate = jnp.sum(grad_rows * feed_rows, axis=1)

    early_mod = jnp.concatenate([d_attn_gate, d_feed_shift, d_feed_scale, d_feed_gate], axis=1)
    own_levels = levels[0]
    early_bias = jnp.concatenate([out_bias_term, up_bias_term, down_bias_term])
    bias_rows = early_bias.reshape(per_device, early_bias.shape[0] // per_device)
    early = jnp.concatenate(
        [
            early_mod.astype(BF16),
            bias_rows.astype(BF16),
            jnp.broadcast_to(lax.div(own_levels, 32)[:, None], (per_device, 128)).astype(BF16),
            jnp.broadcast_to(lax.rem(own_levels, 32)[:, None], (per_device, 128)).astype(BF16),
        ],
        axis=1,
    )
    early_all = gather_all(early)

    before = None
    d_queries = []
    for part in range(per_device):
        d_mix = after(d_mixes[part], *[each.stage() for each in sums])
        result = attend_back(
            part,
            per_device,
            slots[part],
            clip_ids,
            live,
            x,
            head_queries[part],
            kv,
            attended[part][0],
            attended[part][1],
            d_mix,
            cos_all,
            sin_all,
            before,
        )
        if part < per_device - 1:
            d_query, before = result
            d_queries.append(to_tokens(d_query))
    firsts = jnp.stack(d_queries, axis=1)
    result = after(result, firsts[0, 0, :8], *[each.stage() for each in sums])
    back = to_tokens(result)
    which = (1 - pack, pack) if halves else (pack * 0, pack * 0 + 1)
    qkv_theirs = unproject(per_device, which[0], attn_in, firsts, back, qkv_weight, None)
    qkv_mine = unproject(per_device, which[1], attn_in, firsts, back, qkv_weight, qkv_theirs[0])
    d_attn_in = qkv_mine[0].reshape(per_device, PATCHES, width)
    _, attn_norm_back = jax.vjp(modulate_norm, frame_rows, attn_shift, attn_scale)
    d_hidden_norm, d_attn_shift, d_attn_scale = attn_norm_back(d_attn_in)
    hidden_grad = (d_middle + d_hidden_norm).reshape(1, tokens, width).astype(BF16)

    def halves_in_order(own, other):
        if halves:
            return jnp.where(pack == 0, own, other), jnp.where(pack == 0, other, own)
        return other, own

    qkv_bias_term = jnp.concatenate(
        halves_in_order(qkv_mine[2][:, 0], qkv_theirs[2][:, 0]), axis=1
    ).reshape(3 * width)
    late = jnp.concatenate(
        [
            d_attn_shift.astype(BF16),
            d_attn_scale.astype(BF16),
            qkv_bias_term.reshape(per_device, 3 * width // per_device).astype(BF16),
        ],
        axis=1,
    )
    late_all = gather_all(late)
    if halves:
        came = exchange(qkv_theirs[1], "pack", 1)
        split = width // 4
        qkv_sums = [
            RowSum(qkv_mine[1][..., :split], came[..., :split], (1, 2, 4, 8)),
            RowSum(qkv_mine[1][..., split:], came[..., split:], (2, 1, 4, 8)),
        ]
        down_weight_grad = jnp.concatenate(down_sum.finish(), axis=0).astype(F32)
        even, odd = up_sum.finish()
        up_weight_grad = jnp.stack(
            [even.reshape(share, -1, small), odd.reshape(share, -1, small)], axis=2
        ).reshape(share, hidden_units)
        up_weight_grad = up_weight_grad.astype(F32)
        out_weight_grad = jnp.concatenate(out_sum.finish(), axis=1).astype(F32)
        done = [each.finish() for each in qkv_sums]
        qkv_weight_grad = jnp.concatenate(
            [done[0][0], done[1][0], done[0][1], done[1][1]], axis=-1
        )
        qkv_weight_grad = qkv_weight_grad.transpose(1, 0, 2).reshape(share, 3 * width).astype(F32)
    else:
        up_weight_grad = row_sum_direct(in_order(mine[2], theirs[2]))
        pairs = [each[3].reshape(-1, small, width) for each in (mine, theirs)]
        down_weight_grad = row_sum_direct(jnp.stack(pairs, axis=1).reshape(hidden_units, width))
        out_weight_grad = row_sum_direct(out_term(0, width))
        qkv_term = jnp.concatenate(halves_in_order(qkv_mine[1], qkv_theirs[1]), axis=-1)
        qkv_weight_grad = row_sum_direct(qkv_term.transpose(1, 0, 2).reshape(width, 3 * width))

    devices = late_all.shape[0] // per_device

    def bias_share(rows, sizes):
        flat = rows.reshape(devices, sum(sizes))
        shares = []
        at = 0
        for size in sizes:
            piece = size // seq_count
            own = lax.dynamic_slice_in_dim(flat, at + seq_index * piece, piece, 1)
            shares.append(jnp.sum(own.astype(F32), axis=0))
            at += size
        return shares

    early_width = 4 * width
    bias_width = early_bias.shape[0] // per_device
    out_bias_grad, up_bias_grad, down_bias_grad = bias_share(
        early_all[:, early_width : early_width + bias_width], (width, hidden_units, width)
    )
    (qkv_bias_grad,) = bias_share(late_all[:, 2 * width :], (3 * width,))
    coarse = early_all[:, early_width + bias_width].astype(jnp.int32)
    fine = early_all[:, early_width + bias_width + 128].astype(jnp.int32)
    all_levels = coarse * 32 + fine
    picks = (all_levels[:, None] == jnp.arange(level_count, dtype=jnp.int32)[None, :]).astype(F32)
    own_table = lax.dynamic_slice_in_dim(noise_table, seq_index * share, share, 1)
    all_embed = jnp.dot(picks, own_table, precision=PRECISE, preferred_element_type=F32)
    silu_value, silu_back = jax.vjp(jax.nn.silu, all_embed)
    all_cond = silu_value.astype(BF16)
    d_mod_early = early_all[:, :early_width]
    d_mod_late = late_all[:, : 2 * width]
    own_mod = lax.dynamic_slice_in_dim(mod_weight, seq_index * share, share, 0)
    d_cond_early = dot_over(d_mod_early, own_mod[:, 2 * width :], 1, 1)
    d_cond = d_cond_early + dot_over(d_mod_late, own_mod[:, : 2 * width], 1, 1)
    d_embed = silu_back(d_cond)[0]
    table_grad = lax.dot_general(
        picks, d_embed, (((0,), (0,)), ((), ())), precision=PRECISE, preferred_element_type=F32
    )
    mod_weight_grad = jnp.concatenate(
        [dot_over(all_cond, d_mod_late, 0, 0), dot_over(all_cond, d_mod_early, 0, 0)], axis=1
    )
    bias_piece = mod_bias.shape[0] // seq_count
    d_mod_sum = jnp.concatenate(
        [jnp.sum(d_mod_late.astype(F32), axis=0), jnp.sum(d_mod_early.astype(F32), axis=0)]
    )
    mod_bias_grad = lax.dynamic_slice_in_dim(d_mod_sum, seq_index * bias_piece, bias_piece)
    return (
        layer_out,
        hidden_grad,
        table_grad,
        mod_weight_grad,
        mod_bias_grad,
        qkv_weight_grad,
        qkv_bias_grad,
        out_weight_grad,
        out_bias_grad,
        up_weight_grad,
        up_bias_grad,
        down_weight_grad,
        down_bias_grad,
    )


def solution(mesh):
    in_specs = (
        P("pack", "seq", None),
        P("pack", "seq", None),
        P("pack", "seq"),
        P("pack", None),
        P("pack", None),
    ) + (P(),) * 11
    out_specs = (
        P("pack", "seq", None),
        P("pack", "seq", None),
        P(None, "seq"),
        P("seq", None),
        P("seq"),
        P("seq", None),
        P("seq"),
        P("seq", None),
        P("seq"),
        P("seq", None),
        P("seq"),
        P("seq", None),
        P("seq"),
    )
    return jax.shard_map(local, mesh=mesh, in_specs=in_specs, out_specs=out_specs, check_vma=False)
```

```python
import functools

import jax
import jax.numpy as jnp
from jax import lax
from jax.experimental import pallas as pl
from jax.experimental.pallas import tpu as pltpu
from jax.sharding import PartitionSpec as P

HEAD = 64
PATCHES = 256
SIDE = 16
EPSILON = 1e-06
PRECISE = lax.Precision.HIGHEST
HALF = HEAD // 2
F32 = jnp.float32
BF16 = jnp.bfloat16


def modulate_norm(rows, shift, scale):
    center = jnp.mean(rows, axis=-1, keepdims=True)
    centered = rows - center
    spread = jnp.mean(centered * centered, axis=-1, keepdims=True)
    normed = centered * lax.rsqrt(spread + EPSILON)
    return normed * (1.0 + scale[:, None, :]) + shift[:, None, :]


def gelu_tanh(values):
    return jax.nn.gelu(values, approximate=True)


def dot_over(first, second, first_dim, second_dim):
    return lax.dot_general(
        first, second, (((first_dim,), (second_dim,)), ((), ())), preferred_element_type=F32
    )


def spatial_angles():
    time_pairs = HALF // 4
    space_pairs = (HALF - time_pairs) // 2
    patch = jnp.arange(PATCHES, dtype=jnp.int32)
    row_pos = (patch // SIDE).astype(F32)
    col_pos = (patch % SIDE).astype(F32)
    time_freq = 10000.0 ** (-jnp.arange(time_pairs, dtype=F32) / time_pairs)
    space_freq = 10000.0 ** (-jnp.arange(space_pairs, dtype=F32) / space_pairs)
    space = jnp.concatenate(
        [space_freq[:, None] * row_pos[None, :], space_freq[:, None] * col_pos[None, :]], axis=0
    )
    return time_freq, space


def rotary_tables(time_frames):
    time_freq, space = spatial_angles()
    count = time_frames.shape[0]
    time_angle = time_frames[:, None] * time_freq[None, :]

    def whole(function):
        return jnp.concatenate(
            [
                jnp.broadcast_to(
                    function(time_angle)[:, :, None], (count, time_freq.shape[0], PATCHES)
                ),
                jnp.broadcast_to(function(space)[None], (count,) + space.shape),
            ],
            axis=1,
        )

    return whole(jnp.cos), whole(jnp.sin)


def walk_frames(frames, per_device, parts, segments_ref, live_ref, list_ref, visit):
    def step(source, held):
        for place in range(per_device):
            frame = source * per_device + place
            before = jnp.maximum(frame - 1, 0)
            fresh = (frame == 0) | (segments_ref[frame] != segments_ref[before])
            held = jnp.where(fresh, 0, held)
            list_ref[held] = frame
            if place in parts:
                visit(source, place, frame, held + 1)
            held = held + jnp.where(live_ref[frame] == 1, 1, 0)
        return held

    lax.fori_loop(0, frames // per_device, step, jnp.int32(0))


def attend_kernel(per_device, segments_ref, live_ref, x_ref, mix_ref, wide_ref, lse_ref, kv_ref, list_ref):
    frames = kv_ref.shape[0]

    def turn(source, carry):
        for place in range(per_device):
            both = jnp.concatenate(
                [x_ref[source, place], x_ref[source, per_device + place]], axis=0
            )
            kv_ref[source * per_device + place] = both.astype(F32).T.astype(BF16)
        return carry

    lax.fori_loop(0, frames // per_device, turn, 0)

    def visit(source, place, frame, count):
        query = x_ref[source, 2 * per_device + place]
        query_side = jnp.concatenate([query, jnp.zeros_like(query)], axis=0)

        def scores_of(other):
            return jnp.dot(kv_ref[other], query_side, preferred_element_type=F32)

        def mixed(other, weights):
            value = x_ref[lax.div(other, per_device), per_device + lax.rem(other, per_device)]
            return jnp.dot(value, weights.astype(BF16), preferred_element_type=F32)

        def join(others, carry):
            scores = [scores_of(other) for other in others]
            tops = [jnp.max(score, axis=0, keepdims=True) for score in scores]
            new_top = functools.reduce(jnp.maximum, tops)
            if carry is not None:
                top, total, accum = carry
                new_top = jnp.maximum(top, new_top)
                shrink = jnp.exp(top - new_top)
                total = total * shrink
                accum = accum * shrink
            for index, score in enumerate(scores):
                weights = jnp.exp(score - new_top)
                added = jnp.sum(weights, axis=0, keepdims=True)
                product = mixed(others[index], weights)
                if carry is None and index == 0:
                    total, accum = added, product
                else:
                    total, accum = total + added, accum + product
            return new_top, total, accum

        others = count - 1
        carry = join([frame], None)
        carry = lax.fori_loop(
            0,
            lax.div(others, 2),
            lambda index, state: join([list_ref[2 * index], list_ref[2 * index + 1]], state),
            carry,
        )
        top, total, accum = lax.fori_loop(
            0,
            lax.rem(others, 2),
            lambda unused, state: join([list_ref[others - 1]], state),
            carry,
        )
        result = accum * (1.0 / total)
        wide_ref[source, place] = result
        mix_ref[source, place] = result.astype(BF16)
        lse_ref[pl.ds(frame, 1), :] = top + jnp.log(total)

    walk_frames(frames, per_device, range(per_device), segments_ref, live_ref, list_ref, visit)


def whole_spec():
    return pl.BlockSpec(memory_space=pltpu.VMEM)


def scalar_spec():
    return pl.BlockSpec(memory_space=pltpu.SMEM)


def attend(per_device, segments, live, x):
    sources = x.shape[0]
    frames = sources * per_device
    pairs = frames * 6
    outs = (
        jax.ShapeDtypeStruct((sources, per_device, HEAD, PATCHES), BF16),
        jax.ShapeDtypeStruct((sources, per_device, HEAD, PATCHES), F32),
        jax.ShapeDtypeStruct((frames, PATCHES), F32),
        jax.ShapeDtypeStruct((frames, PATCHES, 2 * HEAD), BF16),
    )
    return pl.pallas_call(
        functools.partial(attend_kernel, per_device),
        out_shape=outs,
        in_specs=[scalar_spec(), scalar_spec(), whole_spec()],
        out_specs=(whole_spec(),) * len(outs),
        scratch_shapes=[pltpu.SMEM((frames,), jnp.int32)],
        cost_estimate=pl.CostEstimate(
            flops=pairs * 4 * PATCHES * PATCHES * 256,
            bytes_accessed=x.size * 2 * 3,
            transcendentals=pairs * PATCHES * PATCHES,
        ),
        compiler_params=pltpu.CompilerParams(vmem_limit_bytes=40 << 20),
        name="attend",
    )(segments, live, x)


def attend_back_kernel(
    per_device,
    part,
    last,
    segments_ref,
    live_ref,
    x_ref,
    kv_ref,
    wide_ref,
    lse_ref,
    d_mix_ref,
    cos_ref,
    sin_ref,
    *refs
):
    if last:
        before_ref, out_ref, dkv_ref, list_ref = refs
    else:
        out_ref, dkv_ref, list_ref = refs
    frames = kv_ref.shape[0]

    def clear(frame, carry):
        dkv_ref[frame] = jnp.zeros((PATCHES, 2 * HEAD), F32)
        return carry

    lax.fori_loop(0, frames, clear, 0)

    def unturn(frame, values):
        lower = values[:HALF]
        upper = values[HALF:]
        cosine = cos_ref[frame]
        sine = sin_ref[frame]
        return jnp.concatenate([lower * cosine + upper * sine, upper * cosine - lower * sine], axis=0)

    def visit(source, place, frame, count):
        query = x_ref[source, 2 * per_device + place]
        d_mix = d_mix_ref[source, place]
        blank = jnp.zeros_like(query)
        query_side = jnp.concatenate([query, blank], axis=0)
        d_mix_side = jnp.concatenate([blank, d_mix], axis=0)
        both = jnp.concatenate(
            [query_side.astype(F32).T.astype(BF16), d_mix_side.astype(F32).T.astype(BF16)], axis=0
        )
        lse = lse_ref[pl.ds(frame, 1), :]
        delta = jnp.sum(d_mix.astype(F32) * wide_ref[source, place], axis=0, keepdims=True)

        def block(other):
            key_value = kv_ref[other]
            scores = jnp.dot(key_value, query_side, preferred_element_type=F32)
            d_weights = jnp.dot(key_value, d_mix_side, preferred_element_type=F32)
            weights = jnp.exp(scores - lse)
            d_scores = (weights * (d_weights - delta)).astype(BF16)
            sides = jnp.concatenate([d_scores, weights.astype(BF16)], axis=1)
            dkv_ref[other] += jnp.dot(sides, both, preferred_element_type=F32)
            key = x_ref[lax.div(other, per_device), lax.rem(other, per_device)]
            return jnp.dot(key, d_scores, preferred_element_type=F32)

        d_query = lax.fori_loop(
            0,
            lax.div(count, 2),
            lambda index, state: state
            + block(list_ref[2 * index])
            + block(list_ref[2 * index + 1]),
            jnp.zeros((HEAD, PATCHES), F32),
        )
        d_query = lax.fori_loop(
            0,
            lax.rem(count, 2),
            lambda unused, state: state + block(list_ref[count - 1]),
            d_query,
        )
        d_query = unturn(frame, d_query * (HEAD**-0.5)).astype(BF16)
        if last:
            out_ref[source, 2 * per_device] = d_query
        else:
            out_ref[source] = d_query

    walk_frames(frames, per_device, (part,), segments_ref, live_ref, list_ref, visit)

    def finish(source, carry):
        for place in range(per_device):
            frame = source * per_device + place
            both = (dkv_ref[frame] + before_ref[frame]).T
            out_ref[source, place] = unturn(frame, both[:HEAD]).astype(BF16)
            out_ref[source, per_device + place] = both[HEAD:].astype(BF16)
        return carry

    if last:
        lax.fori_loop(0, frames // per_device, finish, 0)


def attend_back(
    part, per_device, segments, live, x, kv, wide, lse, d_mix, cosine, sine, before
):
    sources = x.shape[0]
    frames = sources * per_device
    pairs = sources * 6
    last = part == per_device - 1
    args = [segments, live, x, kv, wide, lse, d_mix, cosine, sine]
    dkv = (frames, PATCHES, 2 * HEAD)
    lists = pltpu.SMEM((frames,), jnp.int32)
    if last:
        args.append(before)
        outs = jax.ShapeDtypeStruct((sources, 2 * per_device + 1, HEAD, PATCHES), BF16)
        out_specs = whole_spec()
        scratch = [pltpu.VMEM(dkv, F32), lists]
    else:
        outs = (
            jax.ShapeDtypeStruct((sources, HEAD, PATCHES), BF16),
            jax.ShapeDtypeStruct(dkv, F32),
        )
        out_specs = (whole_spec(), whole_spec())
        scratch = [lists]
    return pl.pallas_call(
        functools.partial(attend_back_kernel, per_device, part, last),
        out_shape=outs,
        in_specs=[scalar_spec(), scalar_spec()] + [whole_spec()] * (len(args) - 2),
        out_specs=out_specs,
        scratch_shapes=scratch,
        cost_estimate=pl.CostEstimate(
            flops=pairs * 10 * PATCHES * PATCHES * 256,
            bytes_accessed=x.size * 2 * 5,
            transcendentals=pairs * PATCHES * PATCHES,
        ),
        compiler_params=pltpu.CompilerParams(vmem_limit_bytes=60 << 20),
        name="attend_back%d" % part,
    )(*args)


def exchange(value, axis, bit):
    count = lax.axis_size(axis)
    return lax.ppermute(value, axis, [(source, source ^ bit) for source in range(count)])


def after(value, *earlier):
    return lax.optimization_barrier((value,) + earlier)[0]


def gather_all(value):
    value = value[None]
    for axis in ("seq", "pack"):
        bit = lax.axis_size(axis) // 2
        while bit:
            value = jnp.concatenate([value, exchange(value, axis, bit)], axis=0)
            bit //= 2
    return value


def halving_fits():
    return lax.axis_size("pack") == 2 and lax.axis_size("seq") == 16


class RowSum:
    def __init__(self, mine, came, order):
        self.order = list(order)
        self.index = lax.axis_index("seq")
        rows = mine.shape[-2]
        self.tail = (rows // 16, mine.shape[-1])
        self.lead = mine.shape[:-2]
        shape = self.lead + (2, 2, 2, 2) + self.tail
        self.parts = [mine.reshape(shape), came.reshape(shape)]

    def pick(self, bit, which):
        axis = len(self.lead) + {8: 0, 4: 1, 2: 2, 1: 3}[bit]
        pieces = [lax.dynamic_slice_in_dim(part, which, 1, axis) for part in self.parts]
        return (pieces[0].astype(F32) + pieces[1].astype(F32)).astype(BF16)

    def hold(self, *earlier):
        self.parts = [after(part, *earlier) for part in self.parts]

    def stage(self):
        bit = self.order.pop(0)
        own_bit = lax.rem(lax.div(self.index, bit), 2)
        send = self.pick(bit, 1 - own_bit)
        came = exchange(send, "seq", bit)
        self.parts = [self.pick(bit, own_bit), came]
        return send

    def finish(self):
        while self.order:
            self.stage()
        own = (self.parts[0].astype(F32) + self.parts[1].astype(F32)).astype(BF16)
        own = own.reshape(self.lead + self.tail)
        other = exchange(own, "pack", 1)
        first = lax.axis_index("pack") == 0
        return jnp.where(first, own, other), jnp.where(first, other, own)


def row_sum_direct(term):
    part = lax.psum_scatter(term.astype(BF16), "seq", scatter_dimension=0, tiled=True)
    return lax.psum(part, "pack").astype(F32)


def project_kernel(
    per_device,
    hidden_ref,
    shift_ref,
    scale_ref,
    wq_ref,
    wk_ref,
    wv_ref,
    bq_ref,
    bk_ref,
    bv_ref,
    cos_ref,
    sin_ref,
    in_ref,
    x_ref,
):
    @pl.when(pl.program_id(0) == 0)
    def _():
        for place in range(per_device):
            rows = pl.ds(place * PATCHES, PATCHES)
            values = hidden_ref[rows, :].astype(F32)
            centered = values - jnp.mean(values, axis=-1, keepdims=True)
            spread = jnp.mean(centered * centered, axis=-1, keepdims=True)
            normed = centered * lax.rsqrt(spread + EPSILON)
            scale = scale_ref[pl.ds(place, 1), :]
            in_ref[rows, :] = (normed * (1.0 + scale) + shift_ref[pl.ds(place, 1), :]).astype(BF16)

    rows = in_ref[...]
    group = wq_ref.shape[1] // HEAD

    def turned(values, place):
        lower = values[:HALF]
        upper = values[HALF:]
        cosine = cos_ref[place]
        sine = sin_ref[place]
        return jnp.concatenate([lower * cosine - upper * sine, upper * cosine + lower * sine], axis=0)

    for kind, (weight_ref, bias_ref) in enumerate(
        ((wq_ref, bq_ref), (wk_ref, bk_ref), (wv_ref, bv_ref))
    ):
        flat = jnp.dot(rows, weight_ref[...], preferred_element_type=F32) + bias_ref[...]
        for place in range(per_device):
            block = flat[place * PATCHES : (place + 1) * PATCHES].T
            for head in range(group):
                values = block[head * HEAD : (head + 1) * HEAD]
                if kind == 0:
                    values = turned(values, place) * (HEAD**-0.5)
                    x_ref[head, 2 * per_device + place] = values.astype(BF16)
                elif kind == 1:
                    x_ref[head, place] = turned(values, place).astype(BF16)
                else:
                    x_ref[head, per_device + place] = values.astype(BF16)


def project(per_device, hidden, shift, scale, weight, bias, cosine, sine):
    tokens, width = hidden.shape
    heads = width // HEAD
    group = 2
    lanes = group * HEAD
    steps = heads // group
    bias_row = bias[None, :]

    def whole(shape):
        return pl.BlockSpec(shape, lambda step: (0,) * len(shape))

    def part(kind, rows):
        return pl.BlockSpec((rows, lanes), lambda step: (0, kind * steps + step))

    blocks = (heads, 3 * per_device, HEAD, PATCHES)
    return pl.pallas_call(
        functools.partial(project_kernel, per_device),
        grid=(steps,),
        out_shape=(
            jax.ShapeDtypeStruct((tokens, width), BF16),
            jax.ShapeDtypeStruct(blocks, BF16),
        ),
        in_specs=[whole((tokens, width)), whole(shift.shape), whole(scale.shape)]
        + [part(kind, width) for kind in range(3)]
        + [part(kind, 1) for kind in range(3)]
        + [whole(cosine.shape), whole(sine.shape)],
        out_specs=(
            whole((tokens, width)),
            pl.BlockSpec((group,) + blocks[1:], lambda step: (step, 0, 0, 0)),
        ),
        cost_estimate=pl.CostEstimate(
            flops=2 * tokens * width * 3 * width,
            bytes_accessed=2 * (weight.size + 5 * tokens * width),
            transcendentals=0,
        ),
        compiler_params=pltpu.CompilerParams(vmem_limit_bytes=40 << 20),
        name="project",
    )(hidden, shift, scale, weight, weight, weight, bias_row, bias_row, bias_row, cosine, sine)


GELU_SLOPE = 0.7978845608028654
GELU_CUBE = 0.044715


def feed_kernel(
    carried,
    which_ref,
    in_ref,
    d_out_ref,
    up_a_ref,
    up_b_ref,
    bias_a_ref,
    bias_b_ref,
    down_a_ref,
    down_b_ref,
    *refs
):
    if carried:
        out_before_ref, d_in_before_ref = refs[:2]
        refs = refs[2:]
    out_ref, d_in_ref, d_up_ref, d_down_ref, d_bias_ref, turned_ref = refs

    @pl.when(pl.program_id(0) == 0)
    def _():
        turned_ref[...] = in_ref[...].astype(F32).T.astype(BF16)
        if carried:
            out_ref[...] = out_before_ref[...]
            d_in_ref[...] = d_in_before_ref[...]
        else:
            out_ref[...] = jnp.zeros_like(out_ref)
            d_in_ref[...] = jnp.zeros_like(d_in_ref)

    up = jnp.concatenate([up_a_ref[...], up_b_ref[...]], axis=1)
    down = jnp.concatenate([down_a_ref[...], down_b_ref[...]], axis=0)
    bias = jnp.concatenate([bias_a_ref[...], bias_b_ref[...]], axis=1)
    d_out = d_out_ref[...]
    pre = jnp.dot(in_ref[...], up, preferred_element_type=F32) + bias
    d_act = dot_over(d_out, down, 1, 1)
    square = pre * pre
    bend = jnp.tanh(GELU_SLOPE * pre * (1.0 + GELU_CUBE * square))
    half = 0.5 * (1.0 + bend)
    act = (pre * half).astype(BF16)
    slope = half + (0.5 * GELU_SLOPE) * pre * (1.0 - bend * bend) * (
        1.0 + (3.0 * GELU_CUBE) * square
    )
    d_pre = (d_act * slope).astype(BF16)
    out_ref[...] += jnp.dot(act, down, preferred_element_type=F32)
    d_in_ref[...] += dot_over(d_pre, up, 1, 1)
    d_up_ref[...] = jnp.dot(turned_ref[...], d_pre, preferred_element_type=F32).astype(BF16)
    d_down_ref[...] = jnp.dot(
        act.astype(F32).T.astype(BF16), d_out, preferred_element_type=F32
    ).astype(BF16)
    d_bias_ref[...] = jnp.sum(d_pre.astype(F32), axis=0, keepdims=True)


def feed(which, feed_in, d_feed_out, up_weight, up_bias, down_weight, before):
    tokens, width = feed_in.shape
    hidden_units = up_weight.shape[1]
    small = 128
    steps = hidden_units // (4 * small)
    own = hidden_units // 2

    def whole(shape):
        return pl.BlockSpec(shape, lambda step, which: (0,) * len(shape))

    def group(nth):
        return lambda step, which: 2 * (2 * step + nth) + which[0]

    def columns(nth, rows):
        return pl.BlockSpec((rows, small), lambda step, which: (0, group(nth)(step, which)))

    def rows_of(nth):
        return pl.BlockSpec((small, width), lambda step, which: (group(nth)(step, which), 0))

    args = [feed_in, d_feed_out, up_weight, up_weight, up_bias[None], up_bias[None]]
    args += [down_weight, down_weight]
    specs = [whole((tokens, width)), whole((tokens, width)), columns(0, width), columns(1, width)]
    specs += [columns(0, 1), columns(1, 1), rows_of(0), rows_of(1)]
    if before is not None:
        args += list(before)
        specs += [whole((tokens, width)), whole((tokens, width))]
    return pl.pallas_call(
        functools.partial(feed_kernel, before is not None),
        grid_spec=pltpu.PrefetchScalarGridSpec(
            num_scalar_prefetch=1,
            grid=(steps,),
            in_specs=specs,
            out_specs=(
                whole((tokens, width)),
                whole((tokens, width)),
                pl.BlockSpec((width, 2 * small), lambda step, which: (0, step)),
                pl.BlockSpec((2 * small, width), lambda step, which: (step, 0)),
                pl.BlockSpec((1, 2 * small), lambda step, which: (0, step)),
            ),
            scratch_shapes=[pltpu.VMEM((width, tokens), BF16)],
        ),
        out_shape=(
            jax.ShapeDtypeStruct((tokens, width), F32),
            jax.ShapeDtypeStruct((tokens, width), F32),
            jax.ShapeDtypeStruct((width, own), BF16),
            jax.ShapeDtypeStruct((own, width), BF16),
            jax.ShapeDtypeStruct((1, own), F32),
        ),
        cost_estimate=pl.CostEstimate(
            flops=12 * tokens * width * own,
            bytes_accessed=2 * (4 * own * width + 8 * tokens * width),
            transcendentals=tokens * own,
        ),
        compiler_params=pltpu.CompilerParams(vmem_limit_bytes=56 << 20),
        name="feed%d" % (before is not None),
    )(which.reshape(1), *args)


def norm_back(values, d_in, scale):
    centered = values - jnp.mean(values, axis=-1, keepdims=True)
    spread = jnp.mean(centered * centered, axis=-1, keepdims=True)
    inverse = lax.rsqrt(spread + EPSILON)
    normed = centered * inverse
    product = d_in * normed
    d_shift = jnp.sum(d_in, axis=0, keepdims=True)
    d_scale = jnp.sum(product, axis=0, keepdims=True)
    scaled = 1.0 + scale
    mean_d = jnp.mean(d_in * scaled, axis=-1, keepdims=True)
    mean_p = jnp.mean(product * scaled, axis=-1, keepdims=True)
    return (d_in * scaled - mean_d - normed * mean_p) * inverse, d_shift, d_scale


def middle_back_kernel(
    d_in_ref,
    middle_ref,
    grad_ref,
    attn_ref,
    scale_ref,
    gate_ref,
    weight_ref,
    d_middle_ref,
    d_attn_ref,
    d_mix_ref,
    d_shift_ref,
    d_scale_ref,
    d_gate_ref,
    d_bias_ref,
):
    frame = pl.program_id(0)
    mine = pl.ds(frame, 1)
    back, d_shift, d_scale = norm_back(middle_ref[...], d_in_ref[...], scale_ref[mine, :])
    d_middle = grad_ref[...].astype(F32) + back
    d_middle_ref[...] = d_middle
    d_shift_ref[mine, :] = d_shift
    d_scale_ref[mine, :] = d_scale
    d_gate_ref[mine, :] = jnp.sum(d_middle * attn_ref[...], axis=0, keepdims=True)
    d_attn = (d_middle * gate_ref[mine, :]).astype(BF16)
    d_attn_ref[...] = d_attn
    d_bias_ref[mine, :] = jnp.sum(d_attn.astype(F32), axis=0, keepdims=True)
    d_mix = dot_over(weight_ref[...], d_attn, 1, 1).astype(BF16)
    for head in range(d_mix_ref.shape[0]):
        d_mix_ref[head, 0] = d_mix[head * HEAD : (head + 1) * HEAD]


def middle_back(per_device, d_in, middle, grads, attn_rows, scale, gate, weight):
    tokens, width = d_in.shape
    heads = width // HEAD
    rows = pl.BlockSpec((PATCHES, width), lambda frame: (frame, 0))

    def whole(shape):
        return pl.BlockSpec(shape, lambda frame: (0,) * len(shape))

    small = whole((per_device, width))
    small_shape = jax.ShapeDtypeStruct((per_device, width), F32)
    return pl.pallas_call(
        middle_back_kernel,
        grid=(per_device,),
        out_shape=(
            jax.ShapeDtypeStruct((tokens, width), F32),
            jax.ShapeDtypeStruct((tokens, width), BF16),
            jax.ShapeDtypeStruct((heads, per_device, HEAD, PATCHES), BF16),
        )
        + (small_shape,) * 4,
        in_specs=[rows] * 4 + [small, small, whole(weight.shape)],
        out_specs=(
            rows,
            rows,
            pl.BlockSpec((heads, 1, HEAD, PATCHES), lambda frame: (0, frame, 0, 0)),
        )
        + (small,) * 4,
        cost_estimate=pl.CostEstimate(
            flops=2 * tokens * width * width, bytes_accessed=24 * tokens * width, transcendentals=0
        ),
        compiler_params=pltpu.CompilerParams(vmem_limit_bytes=40 << 20),
        name="middle_back",
    )(d_in, middle, grads, attn_rows, scale, gate, weight)


def unproject_kernel(
    per_device, carried, which_ref, in_ref, first_ref, back_ref, wq_ref, wk_ref, wv_ref, *refs
):
    if carried:
        before_ref, hidden_ref, d_middle_ref, scale_ref = refs[:4]
        d_weight_ref, d_bias_ref, grad_ref, d_shift_ref, d_scale_ref, d_in_ref, turned_ref = refs[4:]
    else:
        d_in_ref, d_weight_ref, d_bias_ref, turned_ref = refs

    @pl.when(pl.program_id(0) == 0)
    def _():
        turned_ref[...] = in_ref[...].astype(F32).T.astype(BF16)
        if carried:
            d_in_ref[...] = before_ref[...]
        else:
            d_in_ref[...] = jnp.zeros_like(d_in_ref)

    group = wq_ref.shape[1] // HEAD

    def token_major(block_of):
        rows = []
        for place in range(per_device):
            block = jnp.concatenate([block_of(head, place) for head in range(group)], axis=0)
            rows.append(block.astype(F32).T.astype(BF16))
        return jnp.concatenate(rows, axis=0)

    def query_block(head, place):
        if place == per_device - 1:
            return back_ref[head, 2 * per_device]
        return first_ref[head, place]

    sides = jnp.concatenate(
        [
            token_major(query_block),
            token_major(lambda head, place: back_ref[head, place]),
            token_major(lambda head, place: back_ref[head, per_device + place]),
        ],
        axis=1,
    )
    weights = jnp.concatenate([wq_ref[...], wk_ref[...], wv_ref[...]], axis=1)
    d_in_ref[...] += dot_over(sides, weights, 1, 1)
    d_weight = jnp.dot(turned_ref[...], sides, preferred_element_type=F32).astype(BF16)
    d_bias = jnp.sum(sides.astype(F32), axis=0, keepdims=True)
    lanes = group * HEAD
    for kind in range(3):
        d_weight_ref[kind] = d_weight[:, kind * lanes : (kind + 1) * lanes]
        d_bias_ref[kind] = d_bias[:, kind * lanes : (kind + 1) * lanes]

    if carried:

        @pl.when(pl.program_id(0) == pl.num_programs(0) - 1)
        def _():
            for place in range(per_device):
                rows = pl.ds(place * PATCHES, PATCHES)
                mine = pl.ds(place, 1)
                back, d_shift, d_scale = norm_back(
                    hidden_ref[rows, :].astype(F32), d_in_ref[rows, :], scale_ref[mine, :]
                )
                grad_ref[rows, :] = (d_middle_ref[rows, :] + back).astype(BF16)
                d_shift_ref[mine, :] = d_shift
                d_scale_ref[mine, :] = d_scale


def unproject(per_device, which, attn_in, first, back, weight, before=None, norm_args=()):
    tokens, width = attn_in.shape
    heads = width // HEAD
    group = 2
    lanes = group * HEAD
    groups = heads // group
    steps = groups // 2

    def whole(shape):
        return pl.BlockSpec(shape, lambda step, which: (0,) * len(shape))

    def blocks(array):
        return pl.BlockSpec(
            (group,) + array.shape[1:], lambda step, which: (which[0] * steps + step, 0, 0, 0)
        )

    def part(kind):
        return pl.BlockSpec(
            (width, lanes), lambda step, which: (0, kind * groups + which[0] * steps + step)
        )

    args = [attn_in, first, back, weight, weight, weight]
    specs = [whole((tokens, width)), blocks(first), blocks(back), part(0), part(1), part(2)]
    weight_shape = (
        jax.ShapeDtypeStruct((3, width, width // 2), BF16),
        jax.ShapeDtypeStruct((3, 1, width // 2), F32),
    )
    weight_specs = (
        pl.BlockSpec((3, width, lanes), lambda step, which: (0, 0, step)),
        pl.BlockSpec((3, 1, lanes), lambda step, which: (0, 0, step)),
    )
    scratch = [pltpu.VMEM((width, tokens), BF16)]
    small = (per_device, width)
    if before is not None:
        args += [before] + list(norm_args)
        specs += [whole((tokens, width))] * 3 + [whole(small)]
        outs = weight_shape + (
            jax.ShapeDtypeStruct((tokens, width), BF16),
            jax.ShapeDtypeStruct(small, F32),
            jax.ShapeDtypeStruct(small, F32),
        )
        out_specs = weight_specs + (whole((tokens, width)), whole(small), whole(small))
        scratch = [pltpu.VMEM((tokens, width), F32)] + scratch
    else:
        outs = (jax.ShapeDtypeStruct((tokens, width), F32),) + weight_shape
        out_specs = (whole((tokens, width)),) + weight_specs
    return pl.pallas_call(
        functools.partial(unproject_kernel, per_device, before is not None),
        grid_spec=pltpu.PrefetchScalarGridSpec(
            num_scalar_prefetch=1,
            grid=(steps,),
            in_specs=specs,
            out_specs=out_specs,
            scratch_shapes=scratch,
        ),
        out_shape=outs,
        cost_estimate=pl.CostEstimate(
            flops=6 * tokens * width * width,
            bytes_accessed=2 * (3 * width * width + 6 * tokens * width),
            transcendentals=0,
        ),
        compiler_params=pltpu.CompilerParams(vmem_limit_bytes=48 << 20),
        name="unproject%d" % (before is not None),
    )(which.reshape(1), *args)


def columns_of(matrix, start, width, axis=1):
    if isinstance(start, int) and start == 0 and width == matrix.shape[axis]:
        return matrix
    return lax.dynamic_slice_in_dim(matrix, start, width, axis)


def local(
    hidden,
    cotangent,
    levels,
    segments,
    live_frames,
    noise_table,
    mod_weight,
    mod_bias,
    qkv_weight,
    qkv_bias,
    out_weight,
    out_bias,
    up_weight,
    up_bias,
    down_weight,
    down_bias,
):
    seq_index = lax.axis_index("seq")
    seq_count = lax.axis_size("seq")
    tokens = hidden.shape[1]
    width = hidden.shape[2]
    per_device = tokens // PATCHES
    frames = segments.shape[1]
    heads = width // HEAD
    copies = seq_count // heads
    hidden_units = up_weight.shape[1]
    level_count = noise_table.shape[0]
    share = width // seq_count
    clip_ids = segments[0]
    live = live_frames[0]

    pack = lax.axis_index("pack")
    halves = halving_fits()
    frame_ids = jnp.arange(frames, dtype=jnp.int32)
    same_clip = clip_ids[:, None] == clip_ids[None, :]
    clip_starts = jnp.min(jnp.where(same_clip, frame_ids[None, :], frames), axis=1)
    frame_times = (frame_ids - clip_starts).astype(F32)
    own_cos, own_sin = rotary_tables(
        lax.dynamic_slice_in_dim(frame_times, seq_index * per_device, per_device)
    )

    embed = jnp.concatenate(
        [
            lax.dynamic_slice_in_dim(noise_table, levels[0, frame], 1, 0)
            for frame in range(per_device)
        ],
        axis=0,
    )
    cond = jax.nn.silu(embed).astype(BF16)
    modulation = jnp.dot(cond, mod_weight[:, : 2 * width], preferred_element_type=F32)
    attn_shift, attn_scale = jnp.split(modulation + mod_bias[: 2 * width], 2, axis=1)
    attn_in, sent = project(
        per_device, hidden[0], attn_shift, attn_scale, qkv_weight, qkv_bias, own_cos, own_sin
    )

    def to_heads(array):
        if copies > 1:
            array = jnp.concatenate([array] * copies, axis=0)
        return lax.all_to_all(array, "seq", 0, 0, tiled=True)

    def to_tokens(array):
        return lax.all_to_all(array, "seq", 0, 0, tiled=True)[:heads]

    x = to_heads(sent)
    late_modulation = jnp.dot(
        after(cond, attn_in), mod_weight[:, 2 * width :], preferred_element_type=F32
    )
    attn_gate, feed_shift, feed_scale, feed_gate = jnp.split(
        late_modulation + mod_bias[2 * width :], 4, axis=1
    )
    cos_all, sin_all = rotary_tables(after(frame_times, attn_in))
    grad_rows = cotangent[0].astype(F32).reshape(per_device, PATCHES, width)
    d_feed_out = (feed_gate[:, None, :] * grad_rows).reshape(tokens, width).astype(BF16)
    down_bias_term = jnp.sum(d_feed_out.astype(F32), axis=0)
    x, d_feed_out, down_bias_term, cos_all, sin_all = lax.optimization_barrier(
        (x, d_feed_out, down_bias_term, cos_all, sin_all)
    )
    mix, wide, lse, kv = attend(per_device, clip_ids, live, x)
    mix = to_tokens(mix)
    mixes = [mix[:, place].reshape(width, PATCHES) for place in range(per_device)]
    attn_rows = jnp.stack([dot_over(each, out_weight, 0, 0) for each in mixes]) + out_bias
    attn_mix = jnp.concatenate(mixes, axis=1)

    frame_rows = hidden[0].astype(F32).reshape(per_device, PATCHES, width)
    middle = frame_rows + attn_gate[:, None, :] * attn_rows
    feed_in = modulate_norm(middle, feed_shift, feed_scale).reshape(tokens, width).astype(BF16)
    feed_args = (feed_in, d_feed_out, up_weight, up_bias, down_weight)
    theirs = feed(1 - pack if halves else pack * 0 + 1, *feed_args, None)
    mine = feed(pack if halves else pack * 0, *feed_args, theirs[:2])
    feed_rows = mine[0].reshape(per_device, PATCHES, width)
    small = 128

    def in_order(own, other):
        if halves:
            even, odd = jnp.where(pack == 0, own, other), jnp.where(pack == 0, other, own)
        else:
            even, odd = own, other
        rows = own.shape[0]
        return jnp.stack(
            [even.reshape(rows, -1, small), odd.reshape(rows, -1, small)], axis=2
        ).reshape(rows, -1)

    up_bias_term = in_order(mine[4], theirs[4])[0]
    d_middle, d_attn_out, d_mix, d_feed_shift, d_feed_scale, d_attn_gate, out_bias_rows = middle_back(
        per_device,
        mine[1],
        middle.reshape(tokens, width),
        cotangent[0],
        attn_rows.reshape(tokens, width),
        feed_scale,
        attn_gate,
        out_weight,
    )
    d_mix = to_heads(d_mix)
    out_bias_term = jnp.sum(out_bias_rows, axis=0)

    def out_term(start, size):
        return dot_over(attn_mix, columns_of(d_attn_out, start, size), 1, 0).astype(BF16)

    sums = ()
    if halves:
        up_sum = RowSum(mine[2], exchange(theirs[2], "pack", 1), (2, 1, 4, 8))
        down_sum = RowSum(mine[3], exchange(theirs[3], "pack", 1), (1, 2, 4, 8))
        out_theirs = exchange(out_term((1 - pack) * (width // 2), width // 2), "pack", 1)
        out_sum = RowSum(out_term(pack * (width // 2), width // 2), out_theirs, (1, 2, 4, 8))
        sums = (down_sum, up_sum, out_sum)
    feed_rows = feed_rows + down_bias
    layer_out = (middle + feed_gate[:, None, :] * feed_rows).reshape(1, tokens, width).astype(BF16)
    d_feed_gate = jnp.sum(grad_rows * feed_rows, axis=1)

    own_levels = levels[0]
    chunk = width
    early_bias = [out_bias_term, up_bias_term, down_bias_term]
    bias_sizes = [each.shape[0] for each in early_bias]
    rows = [
        each.astype(BF16) for each in (d_attn_gate, d_feed_shift, d_feed_scale, d_feed_gate)
    ] + [each.astype(BF16).reshape(-1, chunk) for each in early_bias]
    rows.append(
        jnp.broadcast_to(
            jnp.concatenate([lax.div(own_levels, 32), lax.rem(own_levels, 32)])[:, None],
            (2 * per_device, chunk),
        ).astype(BF16)
    )
    early = jnp.concatenate(rows, axis=0)
    early_all = gather_all(early)

    def bias_share(rows, size):
        flat = jnp.sum(rows.astype(F32), axis=0).reshape(size)
        piece = size // seq_count
        return lax.dynamic_slice_in_dim(flat, seq_index * piece, piece)

    def frames_of(rows):
        return rows.reshape(-1, rows.shape[-1])

    at = 4 * per_device
    early_bias_grads = []
    for size in bias_sizes:
        early_bias_grads.append(bias_share(early_all[:, at : at + size // chunk], size))
        at += size // chunk
    coarse = early_all[:, at : at + per_device, 0].astype(jnp.int32)
    fine = early_all[:, at + per_device : at + 2 * per_device, 0].astype(jnp.int32)
    all_levels = (coarse * 32 + fine).reshape(-1)
    picks = (all_levels[:, None] == jnp.arange(level_count, dtype=jnp.int32)[None, :]).astype(F32)
    own_table = lax.dynamic_slice_in_dim(noise_table, seq_index * share, share, 1)
    all_embed = jnp.dot(picks, own_table, precision=PRECISE, preferred_element_type=F32)
    silu_value, silu_back = jax.vjp(jax.nn.silu, all_embed)
    all_cond = silu_value.astype(BF16)
    d_mod_early = jnp.concatenate(
        [
            frames_of(early_all[:, kind * per_device : (kind + 1) * per_device])
            for kind in range(4)
        ],
        axis=1,
    )
    own_mod = lax.dynamic_slice_in_dim(mod_weight, seq_index * share, share, 0)
    d_cond_early = dot_over(d_mod_early, own_mod[:, 2 * width :], 1, 1)
    mod_grad_early = dot_over(all_cond, d_mod_early, 0, 0)
    mod_sum_early = jnp.sum(d_mod_early.astype(F32), axis=0)
    early_done = [d_cond_early, mod_grad_early, mod_sum_early, all_embed, layer_out]
    early_done += early_bias_grads

    before = None
    d_queries = []
    for part in range(per_device):
        sends = [each.stage() for each in sums]
        result = attend_back(
            part,
            per_device,
            clip_ids,
            live,
            x,
            kv,
            wide,
            lse,
            after(d_mix, *sends),
            cos_all,
            sin_all,
            before,
        )
        if part < per_device - 1:
            d_query, before = result
            d_queries.append(to_tokens(d_query))
    firsts = jnp.stack(d_queries, axis=1)
    result = after(result, firsts[0, 0, :8], *[each.stage() for each in sums])
    back = to_tokens(result)
    for each in sums:
        each.hold(back[0, 0, :8])
    back = after(back, *early_done)
    which = (1 - pack, pack) if halves else (pack * 0, pack * 0 + 1)
    d_in_theirs, qkv_theirs, bias_theirs = unproject(
        per_device, which[0], attn_in, firsts, back, qkv_weight
    )
    qkv_mine, bias_mine, hidden_grad, d_attn_shift, d_attn_scale = unproject(
        per_device,
        which[1],
        attn_in,
        firsts,
        back,
        qkv_weight,
        d_in_theirs,
        (hidden[0], d_middle, attn_scale),
    )
    hidden_grad = hidden_grad.reshape(1, tokens, width)

    def halves_in_order(own, other):
        if halves:
            return jnp.where(pack == 0, own, other), jnp.where(pack == 0, other, own)
        return other, own

    qkv_bias_term = jnp.concatenate(halves_in_order(bias_mine[:, 0], bias_theirs[:, 0]), axis=1)
    late = jnp.concatenate(
        [d_attn_shift.astype(BF16), d_attn_scale.astype(BF16), qkv_bias_term.astype(BF16)], axis=0
    )
    late_all = gather_all(late)
    if halves:
        came = exchange(qkv_theirs, "pack", 1)
        split = width // 4
        qkv_sums = [
            RowSum(qkv_mine[..., :split], came[..., :split], (1, 2, 4, 8)),
            RowSum(qkv_mine[..., split:], came[..., split:], (2, 1, 4, 8)),
        ]
        down_weight_grad = jnp.concatenate(down_sum.finish(), axis=0).astype(F32)
        even, odd = up_sum.finish()
        up_weight_grad = jnp.stack(
            [even.reshape(share, -1, small), odd.reshape(share, -1, small)], axis=2
        ).reshape(share, hidden_units)
        up_weight_grad = up_weight_grad.astype(F32)
        out_weight_grad = jnp.concatenate(out_sum.finish(), axis=1).astype(F32)
        done = [each.finish() for each in qkv_sums]
        qkv_weight_grad = jnp.concatenate(
            [done[0][0], done[1][0], done[0][1], done[1][1]], axis=-1
        )
        qkv_weight_grad = qkv_weight_grad.transpose(1, 0, 2).reshape(share, 3 * width).astype(F32)
    else:
        up_weight_grad = row_sum_direct(in_order(mine[2], theirs[2]))
        pairs = [each[3].reshape(-1, small, width) for each in (mine, theirs)]
        down_weight_grad = row_sum_direct(jnp.stack(pairs, axis=1).reshape(hidden_units, width))
        out_weight_grad = row_sum_direct(out_term(0, width))
        qkv_term = jnp.concatenate(halves_in_order(qkv_mine, qkv_theirs), axis=-1)
        qkv_weight_grad = row_sum_direct(qkv_term.transpose(1, 0, 2).reshape(width, 3 * width))

    out_bias_grad, up_bias_grad, down_bias_grad = early_bias_grads
    qkv_bias_grad = bias_share(late_all[:, 2 * per_device :], 3 * width)
    d_mod_late = jnp.concatenate(
        [
            frames_of(late_all[:, kind * per_device : (kind + 1) * per_device])
            for kind in range(2)
        ],
        axis=1,
    )
    d_cond = d_cond_early + dot_over(d_mod_late, own_mod[:, : 2 * width], 1, 1)
    d_embed = silu_back(d_cond)[0]
    table_grad = lax.dot_general(
        picks, d_embed, (((0,), (0,)), ((), ())), precision=PRECISE, preferred_element_type=F32
    )
    mod_weight_grad = jnp.concatenate([dot_over(all_cond, d_mod_late, 0, 0), mod_grad_early], axis=1)
    bias_piece = mod_bias.shape[0] // seq_count
    d_mod_sum = jnp.concatenate([jnp.sum(d_mod_late.astype(F32), axis=0), mod_sum_early])
    mod_bias_grad = lax.dynamic_slice_in_dim(d_mod_sum, seq_index * bias_piece, bias_piece)
    return (
        layer_out,
        hidden_grad,
        table_grad,
        mod_weight_grad,
        mod_bias_grad,
        qkv_weight_grad,
        qkv_bias_grad,
        out_weight_grad,
        out_bias_grad,
        up_weight_grad,
        up_bias_grad,
        down_weight_grad,
        down_bias_grad,
    )


def solution(mesh):
    in_specs = (
        P("pack", "seq", None),
        P("pack", "seq", None),
        P("pack", "seq"),
        P("pack", None),
        P("pack", None),
    ) + (P(),) * 11
    out_specs = (
        P("pack", "seq", None),
        P("pack", "seq", None),
        P(None, "seq"),
        P("seq", None),
        P("seq"),
        P("seq", None),
        P("seq"),
        P("seq", None),
        P("seq"),
        P("seq", None),
        P("seq"),
        P("seq", None),
        P("seq"),
    )
    return jax.shard_map(local, mesh=mesh, in_specs=in_specs, out_specs=out_specs, check_vma=False)
```

```python
import functools

import jax
import jax.numpy as jnp
from jax import lax
from jax.experimental import pallas as pl
from jax.experimental.pallas import tpu as pltpu
from jax.sharding import PartitionSpec as P

HEAD = 64
PATCHES = 256
SIDE = 16
EPSILON = 1e-06
PRECISE = lax.Precision.HIGHEST
HALF = HEAD // 2
F32 = jnp.float32
BF16 = jnp.bfloat16


def modulate_norm(rows, shift, scale):
    center = jnp.mean(rows, axis=-1, keepdims=True)
    centered = rows - center
    spread = jnp.mean(centered * centered, axis=-1, keepdims=True)
    normed = centered * lax.rsqrt(spread + EPSILON)
    return normed * (1.0 + scale[:, None, :]) + shift[:, None, :]


def gelu_tanh(values):
    return jax.nn.gelu(values, approximate=True)


def dot_over(first, second, first_dim, second_dim):
    return lax.dot_general(
        first, second, (((first_dim,), (second_dim,)), ((), ())), preferred_element_type=F32
    )


def spatial_angles():
    time_pairs = HALF // 4
    space_pairs = (HALF - time_pairs) // 2
    patch = jnp.arange(PATCHES, dtype=jnp.int32)
    row_pos = (patch // SIDE).astype(F32)
    col_pos = (patch % SIDE).astype(F32)
    time_freq = 10000.0 ** (-jnp.arange(time_pairs, dtype=F32) / time_pairs)
    space_freq = 10000.0 ** (-jnp.arange(space_pairs, dtype=F32) / space_pairs)
    space = jnp.concatenate(
        [space_freq[:, None] * row_pos[None, :], space_freq[:, None] * col_pos[None, :]], axis=0
    )
    return time_freq, space


def rotary_tables(time_frames):
    time_freq, space = spatial_angles()
    count = time_frames.shape[0]
    time_angle = time_frames[:, None] * time_freq[None, :]

    def whole(function):
        return jnp.concatenate(
            [
                jnp.broadcast_to(
                    function(time_angle)[:, :, None], (count, time_freq.shape[0], PATCHES)
                ),
                jnp.broadcast_to(function(space)[None], (count,) + space.shape),
            ],
            axis=1,
        )

    return whole(jnp.cos), whole(jnp.sin)


def walk_frames(frames, per_device, parts, segments_ref, live_ref, list_ref, visit):
    def step(source, held):
        for place in range(per_device):
            frame = source * per_device + place
            before = jnp.maximum(frame - 1, 0)
            fresh = (frame == 0) | (segments_ref[frame] != segments_ref[before])
            held = jnp.where(fresh, 0, held)
            list_ref[held] = frame
            if place in parts:
                visit(source, place, frame, held + 1)
            held = held + jnp.where(live_ref[frame] == 1, 1, 0)
        return held

    lax.fori_loop(0, frames // per_device, step, jnp.int32(0))


def attend_kernel(per_device, segments_ref, live_ref, x_ref, mix_ref, wide_ref, lse_ref, kv_ref, list_ref):
    frames = kv_ref.shape[0]

    def turn(source, carry):
        for place in range(per_device):
            both = jnp.concatenate(
                [x_ref[source, place], x_ref[source, per_device + place]], axis=0
            )
            kv_ref[source * per_device + place] = both.astype(F32).T.astype(BF16)
        return carry

    lax.fori_loop(0, frames // per_device, turn, 0)

    def visit(source, place, frame, count):
        query = x_ref[source, 2 * per_device + place]
        query_side = jnp.concatenate([query, jnp.zeros_like(query)], axis=0)

        def scores_of(other):
            return jnp.dot(kv_ref[other], query_side, preferred_element_type=F32)

        def mixed(other, weights):
            value = x_ref[lax.div(other, per_device), per_device + lax.rem(other, per_device)]
            return jnp.dot(value, weights.astype(BF16), preferred_element_type=F32)

        def join(others, carry):
            scores = [scores_of(other) for other in others]
            tops = [jnp.max(score, axis=0, keepdims=True) for score in scores]
            new_top = functools.reduce(jnp.maximum, tops)
            if carry is not None:
                top, total, accum = carry
                new_top = jnp.maximum(top, new_top)
                shrink = jnp.exp(top - new_top)
                total = total * shrink
                accum = accum * shrink
            for index, score in enumerate(scores):
                weights = jnp.exp(score - new_top)
                added = jnp.sum(weights, axis=0, keepdims=True)
                product = mixed(others[index], weights)
                if carry is None and index == 0:
                    total, accum = added, product
                else:
                    total, accum = total + added, accum + product
            return new_top, total, accum

        others = count - 1
        carry = join([frame], None)
        carry = lax.fori_loop(
            0,
            lax.div(others, 2),
            lambda index, state: join([list_ref[2 * index], list_ref[2 * index + 1]], state),
            carry,
        )
        top, total, accum = lax.fori_loop(
            0,
            lax.rem(others, 2),
            lambda unused, state: join([list_ref[others - 1]], state),
            carry,
        )
        result = accum * (1.0 / total)
        wide_ref[source, place] = result
        mix_ref[source, place] = result.astype(BF16)
        lse_ref[pl.ds(frame, 1), :] = top + jnp.log(total)

    walk_frames(frames, per_device, range(per_device), segments_ref, live_ref, list_ref, visit)


def whole_spec():
    return pl.BlockSpec(memory_space=pltpu.VMEM)


def scalar_spec():
    return pl.BlockSpec(memory_space=pltpu.SMEM)


def attend(per_device, segments, live, x):
    sources = x.shape[0]
    frames = sources * per_device
    pairs = frames * 6
    outs = (
        jax.ShapeDtypeStruct((sources, per_device, HEAD, PATCHES), BF16),
        jax.ShapeDtypeStruct((sources, per_device, HEAD, PATCHES), F32),
        jax.ShapeDtypeStruct((frames, PATCHES), F32),
        jax.ShapeDtypeStruct((frames, PATCHES, 2 * HEAD), BF16),
    )
    return pl.pallas_call(
        functools.partial(attend_kernel, per_device),
        out_shape=outs,
        in_specs=[scalar_spec(), scalar_spec(), whole_spec()],
        out_specs=(whole_spec(),) * len(outs),
        scratch_shapes=[pltpu.SMEM((frames,), jnp.int32)],
        cost_estimate=pl.CostEstimate(
            flops=pairs * 4 * PATCHES * PATCHES * 256,
            bytes_accessed=x.size * 2 * 3,
            transcendentals=pairs * PATCHES * PATCHES,
        ),
        compiler_params=pltpu.CompilerParams(vmem_limit_bytes=40 << 20),
        name="attend",
    )(segments, live, x)


def attend_back_kernel(
    per_device,
    part,
    last,
    segments_ref,
    live_ref,
    x_ref,
    kv_ref,
    wide_ref,
    lse_ref,
    d_mix_ref,
    cos_ref,
    sin_ref,
    *refs
):
    if last:
        before_ref, d_query_ref, out_ref, dkv_ref, list_ref = refs
    else:
        out_ref, dkv_ref, list_ref = refs
    frames = kv_ref.shape[0]

    def clear(frame, carry):
        dkv_ref[frame] = jnp.zeros((PATCHES, 2 * HEAD), F32)
        return carry

    lax.fori_loop(0, frames, clear, 0)

    def unturn(frame, values):
        lower = values[:HALF]
        upper = values[HALF:]
        cosine = cos_ref[frame]
        sine = sin_ref[frame]
        return jnp.concatenate([lower * cosine + upper * sine, upper * cosine - lower * sine], axis=0)

    def visit(source, place, frame, count):
        query = x_ref[source, 2 * per_device + place]
        d_mix = d_mix_ref[source, place]
        blank = jnp.zeros_like(query)
        query_side = jnp.concatenate([query, blank], axis=0)
        d_mix_side = jnp.concatenate([blank, d_mix], axis=0)
        both = jnp.concatenate(
            [query_side.astype(F32).T.astype(BF16), d_mix_side.astype(F32).T.astype(BF16)], axis=0
        )
        lse = lse_ref[pl.ds(frame, 1), :]
        delta = jnp.sum(d_mix.astype(F32) * wide_ref[source, place], axis=0, keepdims=True)

        def block(other):
            key_value = kv_ref[other]
            scores = jnp.dot(key_value, query_side, preferred_element_type=F32)
            d_weights = jnp.dot(key_value, d_mix_side, preferred_element_type=F32)
            weights = jnp.exp(scores - lse)
            d_scores = (weights * (d_weights - delta)).astype(BF16)
            sides = jnp.concatenate([d_scores, weights.astype(BF16)], axis=1)
            dkv_ref[other] += jnp.dot(sides, both, preferred_element_type=F32)
            key = x_ref[lax.div(other, per_device), lax.rem(other, per_device)]
            return jnp.dot(key, d_scores, preferred_element_type=F32)

        d_query = lax.fori_loop(
            0,
            lax.div(count, 2),
            lambda index, state: state
            + block(list_ref[2 * index])
            + block(list_ref[2 * index + 1]),
            jnp.zeros((HEAD, PATCHES), F32),
        )
        d_query = lax.fori_loop(
            0,
            lax.rem(count, 2),
            lambda unused, state: state + block(list_ref[count - 1]),
            d_query,
        )
        d_query = unturn(frame, d_query * (HEAD**-0.5)).astype(BF16)
        if last:
            out_ref[source, 2 * per_device + part] = d_query
        else:
            out_ref[source] = d_query

    walk_frames(frames, per_device, (part,), segments_ref, live_ref, list_ref, visit)

    def finish(source, carry):
        for place in range(per_device):
            frame = source * per_device + place
            both = (dkv_ref[frame] + before_ref[frame]).T
            out_ref[source, place] = unturn(frame, both[:HEAD]).astype(BF16)
            out_ref[source, per_device + place] = both[HEAD:].astype(BF16)
        for place in range(part):
            out_ref[source, 2 * per_device + place] = d_query_ref[source]
        return carry

    if last:
        lax.fori_loop(0, frames // per_device, finish, 0)


def attend_back(
    part, per_device, segments, live, x, kv, wide, lse, d_mix, cosine, sine, before
):
    sources = x.shape[0]
    frames = sources * per_device
    pairs = sources * 6
    last = part == per_device - 1
    args = [segments, live, x, kv, wide, lse, d_mix, cosine, sine]
    dkv = (frames, PATCHES, 2 * HEAD)
    lists = pltpu.SMEM((frames,), jnp.int32)
    if last:
        args += [before[1], before[0]]
        outs = jax.ShapeDtypeStruct(x.shape, BF16)
        out_specs = whole_spec()
        scratch = [pltpu.VMEM(dkv, F32), lists]
    else:
        outs = (
            jax.ShapeDtypeStruct((sources, HEAD, PATCHES), BF16),
            jax.ShapeDtypeStruct(dkv, F32),
        )
        out_specs = (whole_spec(), whole_spec())
        scratch = [lists]
    return pl.pallas_call(
        functools.partial(attend_back_kernel, per_device, part, last),
        out_shape=outs,
        in_specs=[scalar_spec(), scalar_spec()] + [whole_spec()] * (len(args) - 2),
        out_specs=out_specs,
        scratch_shapes=scratch,
        cost_estimate=pl.CostEstimate(
            flops=pairs * 10 * PATCHES * PATCHES * 256,
            bytes_accessed=x.size * 2 * 5,
            transcendentals=pairs * PATCHES * PATCHES,
        ),
        compiler_params=pltpu.CompilerParams(vmem_limit_bytes=60 << 20),
        name="attend_back%d" % part,
    )(*args)


def exchange(value, axis, bit):
    count = lax.axis_size(axis)
    return lax.ppermute(value, axis, [(source, source ^ bit) for source in range(count)])


def after(value, *earlier):
    return lax.optimization_barrier((value,) + earlier)[0]


def of_packs(value):
    values = [value]
    bit = lax.axis_size("pack") // 2
    while bit:
        values = values + [exchange(each, "pack", bit) for each in values]
        bit //= 2
    return values


def halving_fits():
    return lax.axis_size("pack") == 2 and lax.axis_size("seq") == 16


class RowSum:
    def __init__(self, mine, came, order):
        self.order = list(order)
        self.index = lax.axis_index("seq")
        rows = mine.shape[-2]
        self.tail = (rows // 16, mine.shape[-1])
        self.lead = mine.shape[:-2]
        shape = self.lead + (2, 2, 2, 2) + self.tail
        self.parts = [mine.reshape(shape), came.reshape(shape)]

    def pick(self, bit, which):
        axis = len(self.lead) + {8: 0, 4: 1, 2: 2, 1: 3}[bit]
        pieces = [lax.dynamic_slice_in_dim(part, which, 1, axis) for part in self.parts]
        return (pieces[0].astype(F32) + pieces[1].astype(F32)).astype(BF16)

    def hold(self, *earlier):
        self.parts = [after(part, *earlier) for part in self.parts]

    def stage(self):
        bit = self.order.pop(0)
        own_bit = lax.rem(lax.div(self.index, bit), 2)
        send = self.pick(bit, 1 - own_bit)
        came = exchange(send, "seq", bit)
        self.parts = [self.pick(bit, own_bit), came]
        return send

    def finish(self):
        while self.order:
            self.stage()
        own = (self.parts[0].astype(F32) + self.parts[1].astype(F32)).astype(BF16)
        own = own.reshape(self.lead + self.tail)
        other = exchange(own, "pack", 1)
        first = lax.axis_index("pack") == 0
        return jnp.where(first, own, other), jnp.where(first, other, own)


def row_sum_direct(term):
    part = lax.psum_scatter(term.astype(BF16), "seq", scatter_dimension=0, tiled=True)
    return lax.psum(part, "pack").astype(F32)


def project_kernel(
    per_device,
    hidden_ref,
    shift_ref,
    scale_ref,
    wq_ref,
    wk_ref,
    wv_ref,
    bq_ref,
    bk_ref,
    bv_ref,
    cos_ref,
    sin_ref,
    in_ref,
    x_ref,
):
    @pl.when(pl.program_id(0) == 0)
    def _():
        for place in range(per_device):
            rows = pl.ds(place * PATCHES, PATCHES)
            values = hidden_ref[rows, :].astype(F32)
            centered = values - jnp.mean(values, axis=-1, keepdims=True)
            spread = jnp.mean(centered * centered, axis=-1, keepdims=True)
            normed = centered * lax.rsqrt(spread + EPSILON)
            scale = scale_ref[pl.ds(place, 1), :]
            in_ref[rows, :] = (normed * (1.0 + scale) + shift_ref[pl.ds(place, 1), :]).astype(BF16)

    rows = in_ref[...]
    group = wq_ref.shape[1] // HEAD

    def turned(values, place):
        lower = values[:HALF]
        upper = values[HALF:]
        cosine = cos_ref[place]
        sine = sin_ref[place]
        return jnp.concatenate([lower * cosine - upper * sine, upper * cosine + lower * sine], axis=0)

    for kind, (weight_ref, bias_ref) in enumerate(
        ((wq_ref, bq_ref), (wk_ref, bk_ref), (wv_ref, bv_ref))
    ):
        flat = jnp.dot(rows, weight_ref[...], preferred_element_type=F32) + bias_ref[...]
        for place in range(per_device):
            block = flat[place * PATCHES : (place + 1) * PATCHES].T
            for head in range(group):
                values = block[head * HEAD : (head + 1) * HEAD]
                if kind == 0:
                    values = turned(values, place) * (HEAD**-0.5)
                    x_ref[head, 2 * per_device + place] = values.astype(BF16)
                elif kind == 1:
                    x_ref[head, place] = turned(values, place).astype(BF16)
                else:
                    x_ref[head, per_device + place] = values.astype(BF16)


def project(per_device, hidden, shift, scale, weight, bias, cosine, sine):
    tokens, width = hidden.shape
    heads = width // HEAD
    group = 2
    lanes = group * HEAD
    steps = heads // group
    bias_row = bias[None, :]

    def whole(shape):
        return pl.BlockSpec(shape, lambda step: (0,) * len(shape))

    def part(kind, rows):
        return pl.BlockSpec((rows, lanes), lambda step: (0, kind * steps + step))

    blocks = (heads, 3 * per_device, HEAD, PATCHES)
    return pl.pallas_call(
        functools.partial(project_kernel, per_device),
        grid=(steps,),
        out_shape=(
            jax.ShapeDtypeStruct((tokens, width), BF16),
            jax.ShapeDtypeStruct(blocks, BF16),
        ),
        in_specs=[whole((tokens, width)), whole(shift.shape), whole(scale.shape)]
        + [part(kind, width) for kind in range(3)]
        + [part(kind, 1) for kind in range(3)]
        + [whole(cosine.shape), whole(sine.shape)],
        out_specs=(
            whole((tokens, width)),
            pl.BlockSpec((group,) + blocks[1:], lambda step: (step, 0, 0, 0)),
        ),
        cost_estimate=pl.CostEstimate(
            flops=2 * tokens * width * 3 * width,
            bytes_accessed=2 * (weight.size + 5 * tokens * width),
            transcendentals=0,
        ),
        compiler_params=pltpu.CompilerParams(vmem_limit_bytes=40 << 20),
        name="project",
    )(hidden, shift, scale, weight, weight, weight, bias_row, bias_row, bias_row, cosine, sine)


GELU_SLOPE = 0.7978845608028654
GELU_CUBE = 0.044715


def feed_kernel(
    carried,
    which_ref,
    in_ref,
    d_out_ref,
    up_a_ref,
    up_b_ref,
    bias_a_ref,
    bias_b_ref,
    down_a_ref,
    down_b_ref,
    *refs
):
    if carried:
        out_before_ref, d_in_before_ref = refs[:2]
        refs = refs[2:]
    out_ref, d_in_ref, d_up_ref, d_down_ref, d_bias_ref, turned_ref = refs

    @pl.when(pl.program_id(0) == 0)
    def _():
        turned_ref[...] = in_ref[...].astype(F32).T.astype(BF16)
        if carried:
            out_ref[...] = out_before_ref[...]
            d_in_ref[...] = d_in_before_ref[...]
        else:
            out_ref[...] = jnp.zeros_like(out_ref)
            d_in_ref[...] = jnp.zeros_like(d_in_ref)

    up = jnp.concatenate([up_a_ref[...], up_b_ref[...]], axis=1)
    down = jnp.concatenate([down_a_ref[...], down_b_ref[...]], axis=0)
    bias = jnp.concatenate([bias_a_ref[...], bias_b_ref[...]], axis=1)
    d_out = d_out_ref[...]
    pre = jnp.dot(in_ref[...], up, preferred_element_type=F32) + bias
    d_act = dot_over(d_out, down, 1, 1)
    square = pre * pre
    bend = jnp.tanh(GELU_SLOPE * pre * (1.0 + GELU_CUBE * square))
    half = 0.5 * (1.0 + bend)
    act = (pre * half).astype(BF16)
    slope = half + (0.5 * GELU_SLOPE) * pre * (1.0 - bend * bend) * (
        1.0 + (3.0 * GELU_CUBE) * square
    )
    d_pre = (d_act * slope).astype(BF16)
    out_ref[...] += jnp.dot(act, down, preferred_element_type=F32)
    d_in_ref[...] += dot_over(d_pre, up, 1, 1)
    d_up_ref[...] = jnp.dot(turned_ref[...], d_pre, preferred_element_type=F32).astype(BF16)
    d_down_ref[...] = jnp.dot(
        act.astype(F32).T.astype(BF16), d_out, preferred_element_type=F32
    ).astype(BF16)
    d_bias_ref[...] = jnp.sum(d_pre.astype(F32), axis=0, keepdims=True)


def feed(which, feed_in, d_feed_out, up_weight, up_bias, down_weight, before):
    tokens, width = feed_in.shape
    hidden_units = up_weight.shape[1]
    small = 128
    steps = hidden_units // (4 * small)
    own = hidden_units // 2

    def whole(shape):
        return pl.BlockSpec(shape, lambda step, which: (0,) * len(shape))

    def group(nth):
        return lambda step, which: 2 * (2 * step + nth) + which[0]

    def columns(nth, rows):
        return pl.BlockSpec((rows, small), lambda step, which: (0, group(nth)(step, which)))

    def rows_of(nth):
        return pl.BlockSpec((small, width), lambda step, which: (group(nth)(step, which), 0))

    args = [feed_in, d_feed_out, up_weight, up_weight, up_bias[None], up_bias[None]]
    args += [down_weight, down_weight]
    specs = [whole((tokens, width)), whole((tokens, width)), columns(0, width), columns(1, width)]
    specs += [columns(0, 1), columns(1, 1), rows_of(0), rows_of(1)]
    if before is not None:
        args += list(before)
        specs += [whole((tokens, width)), whole((tokens, width))]
    return pl.pallas_call(
        functools.partial(feed_kernel, before is not None),
        grid_spec=pltpu.PrefetchScalarGridSpec(
            num_scalar_prefetch=1,
            grid=(steps,),
            in_specs=specs,
            out_specs=(
                whole((tokens, width)),
                whole((tokens, width)),
                pl.BlockSpec((width, 2 * small), lambda step, which: (0, step)),
                pl.BlockSpec((2 * small, width), lambda step, which: (step, 0)),
                pl.BlockSpec((1, 2 * small), lambda step, which: (0, step)),
            ),
            scratch_shapes=[pltpu.VMEM((width, tokens), BF16)],
        ),
        out_shape=(
            jax.ShapeDtypeStruct((tokens, width), F32),
            jax.ShapeDtypeStruct((tokens, width), F32),
            jax.ShapeDtypeStruct((width, own), BF16),
            jax.ShapeDtypeStruct((own, width), BF16),
            jax.ShapeDtypeStruct((1, own), F32),
        ),
        cost_estimate=pl.CostEstimate(
            flops=12 * tokens * width * own,
            bytes_accessed=2 * (4 * own * width + 8 * tokens * width),
            transcendentals=tokens * own,
        ),
        compiler_params=pltpu.CompilerParams(vmem_limit_bytes=56 << 20),
        name="feed%d" % (before is not None),
    )(which.reshape(1), *args)


def norm_back(values, d_in, scale):
    centered = values - jnp.mean(values, axis=-1, keepdims=True)
    spread = jnp.mean(centered * centered, axis=-1, keepdims=True)
    inverse = lax.rsqrt(spread + EPSILON)
    normed = centered * inverse
    product = d_in * normed
    d_shift = jnp.sum(d_in, axis=0, keepdims=True)
    d_scale = jnp.sum(product, axis=0, keepdims=True)
    scaled = 1.0 + scale
    mean_d = jnp.mean(d_in * scaled, axis=-1, keepdims=True)
    mean_p = jnp.mean(product * scaled, axis=-1, keepdims=True)
    return (d_in * scaled - mean_d - normed * mean_p) * inverse, d_shift, d_scale


def middle_back_kernel(
    d_in_ref,
    middle_ref,
    grad_ref,
    attn_ref,
    feed_ref,
    scale_ref,
    gate_ref,
    feed_gate_ref,
    down_bias_ref,
    rows_ref,
    weight_ref,
    d_middle_ref,
    d_attn_ref,
    layer_ref,
    blocks_ref,
    sums_ref,
):
    frame = pl.program_id(0)
    per_device = pl.num_programs(0) - 1

    @pl.when(frame < per_device)
    def _():
        mine = pl.ds(frame, 1)
        middle = middle_ref[...]
        grads = grad_ref[...].astype(F32)
        back, d_shift, d_scale = norm_back(middle, d_in_ref[...], scale_ref[mine, :])
        d_middle = grads + back
        d_middle_ref[...] = d_middle
        d_attn = (d_middle * gate_ref[mine, :]).astype(BF16)
        d_attn_ref[...] = d_attn
        feed_rows = feed_ref[...] + down_bias_ref[...]
        feed_gate = feed_gate_ref[mine, :]
        layer_ref[...] = (middle + feed_gate * feed_rows).astype(BF16)
        d_feed_out = (feed_gate * grads).astype(BF16).astype(F32)
        sums_ref[frame] = jnp.concatenate(
            [
                jnp.sum(d_middle * attn_ref[...], axis=0, keepdims=True),
                d_shift,
                d_scale,
                jnp.sum(grads * feed_rows, axis=0, keepdims=True),
                jnp.sum(d_attn.astype(F32), axis=0, keepdims=True),
                jnp.sum(d_feed_out, axis=0, keepdims=True),
                jnp.zeros((2, d_shift.shape[1]), F32),
            ],
            axis=0,
        )
        d_mix = dot_over(weight_ref[...], d_attn, 1, 1).astype(BF16)
        for head in range(blocks_ref.shape[0]):
            blocks_ref[head, 0] = d_mix[head * HEAD : (head + 1) * HEAD]

    @pl.when(frame == per_device)
    def _():
        first = sums_ref[0]
        second = sums_ref[1]
        rows = jnp.concatenate(
            [first[:4], second[:4], first[4:6] + second[4:6], rows_ref[...]], axis=0
        ).astype(BF16)
        count = rows.shape[1] // PATCHES
        block = jnp.concatenate(
            [rows[:, nth * PATCHES : (nth + 1) * PATCHES] for nth in range(count)], axis=0
        )
        for head in range(blocks_ref.shape[0]):
            blocks_ref[head, 0] = block


def middle_back(
    per_device, d_in, middle, grads, attn_rows, feed_rows, scale, gate, feed_gate, down_bias, rows, weight
):
    tokens, width = d_in.shape
    heads = width // HEAD
    last = per_device - 1
    per_frame = pl.BlockSpec((PATCHES, width), lambda frame: (jnp.minimum(frame, last), 0))

    def whole(shape):
        return pl.BlockSpec(shape, lambda frame: (0,) * len(shape))

    small = whole((per_device, width))
    return pl.pallas_call(
        middle_back_kernel,
        grid=(per_device + 1,),
        out_shape=(
            jax.ShapeDtypeStruct((tokens, width), F32),
            jax.ShapeDtypeStruct((tokens, width), BF16),
            jax.ShapeDtypeStruct((tokens, width), BF16),
            jax.ShapeDtypeStruct((heads, per_device + 1, HEAD, PATCHES), BF16),
        ),
        in_specs=[per_frame] * 5
        + [small] * 3
        + [whole((1, width)), whole(rows.shape), whole(weight.shape)],
        out_specs=(
            per_frame,
            per_frame,
            per_frame,
            pl.BlockSpec((heads, 1, HEAD, PATCHES), lambda frame: (0, frame, 0, 0)),
        ),
        scratch_shapes=[pltpu.VMEM((per_device, 8, width), F32)],
        cost_estimate=pl.CostEstimate(
            flops=2 * tokens * width * width, bytes_accessed=24 * tokens * width, transcendentals=0
        ),
        compiler_params=pltpu.CompilerParams(vmem_limit_bytes=48 << 20),
        name="middle_back",
    )(
        d_in,
        middle,
        grads,
        attn_rows,
        feed_rows,
        scale,
        gate,
        feed_gate,
        down_bias[None],
        rows,
        weight,
    )


def unproject_kernel(
    per_device, carried, which_ref, in_ref, back_ref, wq_ref, wk_ref, wv_ref, *refs
):
    if carried:
        before_ref, hidden_ref, d_middle_ref, scale_ref, bias_theirs_ref = refs[:5]
        d_weight_ref, grad_ref, rows_ref, d_in_ref, d_bias_ref, turned_ref = refs[5:]
    else:
        d_in_ref, d_weight_ref, d_bias_ref, turned_ref = refs

    @pl.when(pl.program_id(0) == 0)
    def _():
        turned_ref[...] = in_ref[...].astype(F32).T.astype(BF16)
        if carried:
            d_in_ref[...] = before_ref[...]
        else:
            d_in_ref[...] = jnp.zeros_like(d_in_ref)

    group = wq_ref.shape[1] // HEAD

    def token_major(block_of):
        rows = []
        for place in range(per_device):
            block = jnp.concatenate([block_of(head, place) for head in range(group)], axis=0)
            rows.append(block.astype(F32).T.astype(BF16))
        return jnp.concatenate(rows, axis=0)

    sides = jnp.concatenate(
        [
            token_major(lambda head, place: back_ref[head, 2 * per_device + place]),
            token_major(lambda head, place: back_ref[head, place]),
            token_major(lambda head, place: back_ref[head, per_device + place]),
        ],
        axis=1,
    )
    weights = jnp.concatenate([wq_ref[...], wk_ref[...], wv_ref[...]], axis=1)
    d_in_ref[...] += dot_over(sides, weights, 1, 1)
    d_weight = jnp.dot(turned_ref[...], sides, preferred_element_type=F32).astype(BF16)
    d_bias = jnp.sum(sides.astype(F32), axis=0, keepdims=True)
    lanes = group * HEAD
    for kind in range(3):
        d_weight_ref[kind] = d_weight[:, kind * lanes : (kind + 1) * lanes]
        part = d_bias[:, kind * lanes : (kind + 1) * lanes]
        if carried:
            start = pl.multiple_of(pl.program_id(0) * lanes, lanes)
            d_bias_ref[pl.ds(kind, 1), pl.ds(start, lanes)] = part
        else:
            d_bias_ref[kind] = part

    if carried:

        @pl.when(pl.program_id(0) == pl.num_programs(0) - 1)
        def _():
            sums = []
            for place in range(per_device):
                rows = pl.ds(place * PATCHES, PATCHES)
                mine = pl.ds(place, 1)
                back, d_shift, d_scale = norm_back(
                    hidden_ref[rows, :].astype(F32), d_in_ref[rows, :], scale_ref[mine, :]
                )
                grad_ref[rows, :] = (d_middle_ref[rows, :] + back).astype(BF16)
                sums += [d_shift, d_scale]
            for kind in range(3):
                sums.append(
                    jnp.concatenate([d_bias_ref[pl.ds(kind, 1), :], bias_theirs_ref[kind]], axis=1)
                )
            count = 16 - len(sums)
            late = jnp.concatenate(
                sums + [jnp.zeros((count, d_in_ref.shape[1]), F32)], axis=0
            ).astype(BF16)
            for target in range(rows_ref.shape[0]):
                rows_ref[target] = late


def unproject(per_device, targets, which, attn_in, back, weight, before=None, norm_args=()):
    tokens, width = attn_in.shape
    heads = width // HEAD
    group = 2
    lanes = group * HEAD
    groups = heads // group
    steps = groups // 2

    def whole(shape):
        return pl.BlockSpec(shape, lambda step, which: (0,) * len(shape))

    def blocks(array):
        return pl.BlockSpec(
            (group,) + array.shape[1:], lambda step, which: (which[0] * steps + step, 0, 0, 0)
        )

    def part(kind):
        return pl.BlockSpec(
            (width, lanes), lambda step, which: (0, kind * groups + which[0] * steps + step)
        )

    args = [attn_in, back, weight, weight, weight]
    specs = [whole((tokens, width)), blocks(back), part(0), part(1), part(2)]
    weight_shape = (
        jax.ShapeDtypeStruct((3, width, width // 2), BF16),
        jax.ShapeDtypeStruct((3, 1, width // 2), F32),
    )
    weight_specs = (
        pl.BlockSpec((3, width, lanes), lambda step, which: (0, 0, step)),
        pl.BlockSpec((3, 1, lanes), lambda step, which: (0, 0, step)),
    )
    scratch = [pltpu.VMEM((width, tokens), BF16)]
    small = (per_device, width)
    if before is not None:
        args += [before] + list(norm_args)
        specs += [whole((tokens, width))] * 3 + [whole(small), whole((3, 1, width // 2))]
        late = (targets, 16, width)
        outs = weight_shape[:1] + (
            jax.ShapeDtypeStruct((tokens, width), BF16),
            jax.ShapeDtypeStruct(late, BF16),
        )
        out_specs = weight_specs[:1] + (whole((tokens, width)), whole(late))
        scratch = [pltpu.VMEM((tokens, width), F32), pltpu.VMEM((3, width // 2), F32)] + scratch
    else:
        outs = (jax.ShapeDtypeStruct((tokens, width), F32),) + weight_shape
        out_specs = (whole((tokens, width)),) + weight_specs
    return pl.pallas_call(
        functools.partial(unproject_kernel, per_device, before is not None),
        grid_spec=pltpu.PrefetchScalarGridSpec(
            num_scalar_prefetch=1,
            grid=(steps,),
            in_specs=specs,
            out_specs=out_specs,
            scratch_shapes=scratch,
        ),
        out_shape=outs,
        cost_estimate=pl.CostEstimate(
            flops=6 * tokens * width * width,
            bytes_accessed=2 * (3 * width * width + 6 * tokens * width),
            transcendentals=0,
        ),
        compiler_params=pltpu.CompilerParams(vmem_limit_bytes=48 << 20),
        name="unproject%d" % (before is not None),
    )(which.reshape(1), *args)


def columns_of(matrix, start, width, axis=1):
    if isinstance(start, int) and start == 0 and width == matrix.shape[axis]:
        return matrix
    return lax.dynamic_slice_in_dim(matrix, start, width, axis)


def local(
    hidden,
    cotangent,
    levels,
    segments,
    live_frames,
    noise_table,
    mod_weight,
    mod_bias,
    qkv_weight,
    qkv_bias,
    out_weight,
    out_bias,
    up_weight,
    up_bias,
    down_weight,
    down_bias,
):
    seq_index = lax.axis_index("seq")
    seq_count = lax.axis_size("seq")
    tokens = hidden.shape[1]
    width = hidden.shape[2]
    per_device = tokens // PATCHES
    frames = segments.shape[1]
    heads = width // HEAD
    copies = seq_count // heads
    hidden_units = up_weight.shape[1]
    level_count = noise_table.shape[0]
    share = width // seq_count
    clip_ids = segments[0]
    live = live_frames[0]

    pack = lax.axis_index("pack")
    halves = halving_fits()
    frame_ids = jnp.arange(frames, dtype=jnp.int32)
    same_clip = clip_ids[:, None] == clip_ids[None, :]
    clip_starts = jnp.min(jnp.where(same_clip, frame_ids[None, :], frames), axis=1)
    frame_times = (frame_ids - clip_starts).astype(F32)
    own_cos, own_sin = rotary_tables(
        lax.dynamic_slice_in_dim(frame_times, seq_index * per_device, per_device)
    )

    embed = jnp.concatenate(
        [
            lax.dynamic_slice_in_dim(noise_table, levels[0, frame], 1, 0)
            for frame in range(per_device)
        ],
        axis=0,
    )
    cond = jax.nn.silu(embed).astype(BF16)
    modulation = jnp.dot(cond, mod_weight[:, : 2 * width], preferred_element_type=F32)
    attn_shift, attn_scale = jnp.split(modulation + mod_bias[: 2 * width], 2, axis=1)
    attn_in, sent = project(
        per_device, hidden[0], attn_shift, attn_scale, qkv_weight, qkv_bias, own_cos, own_sin
    )

    def to_heads(array):
        if copies > 1:
            array = jnp.concatenate([array] * copies, axis=0)
        return lax.all_to_all(array, "seq", 0, 0, tiled=True)

    def to_tokens(array):
        return lax.all_to_all(array, "seq", 0, 0, tiled=True)[:heads]

    x = to_heads(sent)
    late_modulation = jnp.dot(
        after(cond, attn_in), mod_weight[:, 2 * width :], preferred_element_type=F32
    )
    attn_gate, feed_shift, feed_scale, feed_gate = jnp.split(
        late_modulation + mod_bias[2 * width :], 4, axis=1
    )
    cos_all, sin_all = rotary_tables(after(frame_times, attn_in))
    grad_rows = cotangent[0].astype(F32).reshape(per_device, PATCHES, width)
    d_feed_out = (feed_gate[:, None, :] * grad_rows).reshape(tokens, width).astype(BF16)
    x, d_feed_out, cos_all, sin_all = lax.optimization_barrier((x, d_feed_out, cos_all, sin_all))
    mix, wide, lse, kv = attend(per_device, clip_ids, live, x)
    mix = to_tokens(mix)
    mixes = [mix[:, place].reshape(width, PATCHES) for place in range(per_device)]
    attn_rows = jnp.stack([dot_over(each, out_weight, 0, 0) for each in mixes]) + out_bias
    attn_mix = jnp.concatenate(mixes, axis=1)

    frame_rows = hidden[0].astype(F32).reshape(per_device, PATCHES, width)
    middle = frame_rows + attn_gate[:, None, :] * attn_rows
    feed_in = modulate_norm(middle, feed_shift, feed_scale).reshape(tokens, width).astype(BF16)
    feed_args = (feed_in, d_feed_out, up_weight, up_bias, down_weight)
    theirs = feed(1 - pack if halves else pack * 0 + 1, *feed_args, None)
    mine = feed(pack if halves else pack * 0, *feed_args, theirs[:2])
    small = 128

    def in_order(own, other):
        if halves:
            even, odd = jnp.where(pack == 0, own, other), jnp.where(pack == 0, other, own)
        else:
            even, odd = own, other
        rows = own.shape[0]
        return jnp.stack(
            [even.reshape(rows, -1, small), odd.reshape(rows, -1, small)], axis=2
        ).reshape(rows, -1)

    own_levels = levels[0]
    level_row = jnp.concatenate(
        [
            jnp.broadcast_to(part[frame], (width // (2 * per_device),))
            for frame in range(per_device)
            for part in (lax.div(own_levels, 32), lax.rem(own_levels, 32))
        ]
    ).astype(F32)[None]
    extra_rows = jnp.concatenate(
        [
            in_order(mine[4], theirs[4]).reshape(-1, width),
            level_row,
            jnp.zeros((1, width), F32),
        ],
        axis=0,
    )
    d_middle, d_attn_out, layer_out, blocks = middle_back(
        per_device,
        mine[1],
        middle.reshape(tokens, width),
        cotangent[0],
        attn_rows.reshape(tokens, width),
        mine[0],
        feed_scale,
        attn_gate,
        feed_gate,
        down_bias,
        extra_rows,
        out_weight,
    )
    layer_out = layer_out.reshape(1, tokens, width)
    d_mix = to_heads(blocks)

    def out_term(start, size):
        return dot_over(attn_mix, columns_of(d_attn_out, start, size), 1, 0).astype(BF16)

    sums = ()
    if halves:
        up_sum = RowSum(mine[2], exchange(theirs[2], "pack", 1), (2, 1, 4, 8))
        down_sum = RowSum(mine[3], exchange(theirs[3], "pack", 1), (1, 2, 4, 8))
        out_theirs = exchange(out_term((1 - pack) * (width // 2), width // 2), "pack", 1)
        out_sum = RowSum(out_term(pack * (width // 2), width // 2), out_theirs, (1, 2, 4, 8))
        sums = (down_sum, up_sum)
    def own_share(row):
        piece = row.shape[0] // seq_count
        return lax.dynamic_slice_in_dim(row, seq_index * piece, piece)

    chunks = width // PATCHES
    early_rows = d_mix[:, per_device].reshape(seq_count, chunks, 16, PATCHES)
    early_rows = early_rows.transpose(0, 2, 1, 3).reshape(seq_count, 16, width)
    early_sets = of_packs(early_rows)
    early_sum = functools.reduce(
        jnp.add, [jnp.sum(each.astype(F32), axis=0) for each in early_sets]
    )
    out_bias_grad = own_share(early_sum[8])
    down_bias_grad = own_share(early_sum[9])
    up_bias_grad = own_share(early_sum[10:14].reshape(hidden_units))

    def frames_of(rows, per_frame, kinds):
        return jnp.concatenate(
            [
                jnp.stack(
                    [rows[:, frame * per_frame + kind] for frame in range(per_device)], axis=1
                ).reshape(-1, width)
                for kind in range(kinds)
            ],
            axis=1,
        )

    own_table = lax.dynamic_slice_in_dim(noise_table, seq_index * share, share, 1)
    own_mod = lax.dynamic_slice_in_dim(mod_weight, seq_index * share, share, 0)
    stride = width // (2 * per_device)
    parts = []
    for rows in early_sets:
        coded = rows[:, 14, ::stride].astype(jnp.int32).reshape(-1, 2)
        set_levels = coded[:, 0] * 32 + coded[:, 1]
        picks = (set_levels[:, None] == jnp.arange(level_count, dtype=jnp.int32)[None, :]).astype(F32)
        embeds = jnp.dot(picks, own_table, precision=PRECISE, preferred_element_type=F32)
        set_cond = jax.nn.silu(embeds).astype(BF16)
        d_mod = frames_of(rows, 4, 4)
        parts.append(
            (
                picks,
                embeds,
                set_cond,
                dot_over(d_mod, own_mod[:, 2 * width :], 1, 1),
                dot_over(set_cond, d_mod, 0, 0),
            )
        )
    mod_grad_early = functools.reduce(jnp.add, [each[4] for each in parts])
    mod_sum_early = (early_sum[:4] + early_sum[4:8]).reshape(4 * width)
    early_done = [mod_grad_early, mod_sum_early, out_bias_grad, down_bias_grad, up_bias_grad]
    for part in parts:
        early_done += [part[1], part[3]]

    before = None
    for part in range(per_device):
        sends = [each.stage() for each in sums]
        if halves and part:
            sends.append(out_sum.stage())
        result = attend_back(
            part,
            per_device,
            clip_ids,
            live,
            x,
            kv,
            wide,
            lse,
            after(d_mix, *sends),
            cos_all,
            sin_all,
            before,
        )
        before = result
    sends = [each.stage() for each in sums]
    if halves:
        sends.append(out_sum.stage())
    back = to_tokens(after(result, *sends))
    for each in sums:
        each.hold(back[0, 0, :8])
    back = after(back, *early_done)
    which = (1 - pack, pack) if halves else (pack * 0, pack * 0 + 1)
    d_in_theirs, qkv_theirs, bias_theirs = unproject(
        per_device, seq_count, which[0], attn_in, back, qkv_weight
    )
    qkv_mine, hidden_grad, late = unproject(
        per_device,
        seq_count,
        which[1],
        attn_in,
        back,
        qkv_weight,
        d_in_theirs,
        (hidden[0], d_middle, attn_scale, bias_theirs),
    )
    hidden_grad = hidden_grad.reshape(1, tokens, width)
    late_rows = lax.all_to_all(late, "seq", 0, 0, tiled=True)

    def halves_in_order(own, other):
        if halves:
            return jnp.where(pack == 0, own, other), jnp.where(pack == 0, other, own)
        return other, own

    if halves:
        came = exchange(qkv_theirs, "pack", 1)
        split = width // 4
        qkv_sums = [
            RowSum(qkv_mine[..., :split], came[..., :split], (1, 2, 4, 8)),
            RowSum(qkv_mine[..., split:], came[..., split:], (2, 1, 4, 8)),
        ]
        down_weight_grad = jnp.concatenate(down_sum.finish(), axis=0).astype(F32)
        even, odd = up_sum.finish()
        up_weight_grad = jnp.stack(
            [even.reshape(share, -1, small), odd.reshape(share, -1, small)], axis=2
        ).reshape(share, hidden_units)
        up_weight_grad = up_weight_grad.astype(F32)
        out_weight_grad = jnp.concatenate(out_sum.finish(), axis=1).astype(F32)
        done = [each.finish() for each in qkv_sums]
        qkv_weight_grad = jnp.concatenate(
            [done[0][0], done[1][0], done[0][1], done[1][1]], axis=-1
        )
        qkv_weight_grad = qkv_weight_grad.transpose(1, 0, 2).reshape(share, 3 * width).astype(F32)
    else:
        up_weight_grad = row_sum_direct(in_order(mine[2], theirs[2]))
        pairs = [each[3].reshape(-1, small, width) for each in (mine, theirs)]
        down_weight_grad = row_sum_direct(jnp.stack(pairs, axis=1).reshape(hidden_units, width))
        out_weight_grad = row_sum_direct(out_term(0, width))
        qkv_term = jnp.concatenate(halves_in_order(qkv_mine, qkv_theirs), axis=-1)
        qkv_weight_grad = row_sum_direct(qkv_term.transpose(1, 0, 2).reshape(width, 3 * width))

    late_sets = of_packs(late_rows[:, :8])
    bias_at = 2 * per_device
    bias_sums = [
        jnp.sum(rows[:, bias_at : bias_at + 3].astype(F32), axis=0) for rows in late_sets
    ]
    if halves:
        ones, twos = bias_sums
        half = width // 2
        own_half = ones[:, :half] + twos[:, half:]
        other_half = ones[:, half:] + twos[:, :half]
    else:
        total = functools.reduce(jnp.add, bias_sums)
        own_half, other_half = total[:, : width // 2], total[:, width // 2 :]
    bias_total = jnp.concatenate(halves_in_order(own_half, other_half), axis=1)
    qkv_bias_grad = own_share(bias_total.reshape(3 * width))
    late_mods = [frames_of(rows, 2, 2) for rows in late_sets]
    mod_sum_late = functools.reduce(
        jnp.add, [jnp.sum(each.astype(F32), axis=0) for each in late_mods]
    )
    d_embeds = []
    for part, d_mod in zip(parts, late_mods):
        d_cond = part[3] + dot_over(d_mod, own_mod[:, : 2 * width], 1, 1)
        d_embeds.append(jax.vjp(jax.nn.silu, part[1])[1](d_cond)[0])
    table_grad = lax.dot_general(
        jnp.concatenate([part[0] for part in parts], axis=0),
        jnp.concatenate(d_embeds, axis=0),
        (((0,), (0,)), ((), ())),
        precision=PRECISE,
        preferred_element_type=F32,
    )
    mod_grad_late = functools.reduce(
        jnp.add, [dot_over(part[2], d_mod, 0, 0) for part, d_mod in zip(parts, late_mods)]
    )
    mod_weight_grad = jnp.concatenate([mod_grad_late, mod_grad_early], axis=1)
    mod_bias_grad = own_share(jnp.concatenate([mod_sum_late, mod_sum_early]))
    return (
        layer_out,
        hidden_grad,
        table_grad,
        mod_weight_grad,
        mod_bias_grad,
        qkv_weight_grad,
        qkv_bias_grad,
        out_weight_grad,
        out_bias_grad,
        up_weight_grad,
        up_bias_grad,
        down_weight_grad,
        down_bias_grad,
    )


def solution(mesh):
    in_specs = (
        P("pack", "seq", None),
        P("pack", "seq", None),
        P("pack", "seq"),
        P("pack", None),
        P("pack", None),
    ) + (P(),) * 11
    out_specs = (
        P("pack", "seq", None),
        P("pack", "seq", None),
        P(None, "seq"),
        P("seq", None),
        P("seq"),
        P("seq", None),
        P("seq"),
        P("seq", None),
        P("seq"),
        P("seq", None),
        P("seq"),
        P("seq", None),
        P("seq"),
    )
    return jax.shard_map(local, mesh=mesh, in_specs=in_specs, out_specs=out_specs, check_vma=False)
```

```python
import functools

import jax
import jax.numpy as jnp
from jax import lax
from jax.experimental import pallas as pl
from jax.experimental.pallas import tpu as pltpu
from jax.sharding import PartitionSpec as P

HEAD = 64
PATCHES = 256
SIDE = 16
EPSILON = 1e-06
PRECISE = lax.Precision.HIGHEST
HALF = HEAD // 2
F32 = jnp.float32
BF16 = jnp.bfloat16


def modulate_norm(rows, shift, scale):
    center = jnp.mean(rows, axis=-1, keepdims=True)
    centered = rows - center
    spread = jnp.mean(centered * centered, axis=-1, keepdims=True)
    normed = centered * lax.rsqrt(spread + EPSILON)
    return normed * (1.0 + scale[:, None, :]) + shift[:, None, :]


def gelu_tanh(values):
    return jax.nn.gelu(values, approximate=True)


def dot_over(first, second, first_dim, second_dim):
    return lax.dot_general(
        first, second, (((first_dim,), (second_dim,)), ((), ())), preferred_element_type=F32
    )


def spatial_angles():
    time_pairs = HALF // 4
    space_pairs = (HALF - time_pairs) // 2
    patch = jnp.arange(PATCHES, dtype=jnp.int32)
    row_pos = (patch // SIDE).astype(F32)
    col_pos = (patch % SIDE).astype(F32)
    time_freq = 10000.0 ** (-jnp.arange(time_pairs, dtype=F32) / time_pairs)
    space_freq = 10000.0 ** (-jnp.arange(space_pairs, dtype=F32) / space_pairs)
    space = jnp.concatenate(
        [space_freq[:, None] * row_pos[None, :], space_freq[:, None] * col_pos[None, :]], axis=0
    )
    return time_freq, space


def rotary_tables(time_frames):
    time_freq, space = spatial_angles()
    count = time_frames.shape[0]
    time_angle = time_frames[:, None] * time_freq[None, :]

    def whole(function):
        return jnp.concatenate(
            [
                jnp.broadcast_to(
                    function(time_angle)[:, :, None], (count, time_freq.shape[0], PATCHES)
                ),
                jnp.broadcast_to(function(space)[None], (count,) + space.shape),
            ],
            axis=1,
        )

    return whole(jnp.cos), whole(jnp.sin)


def walk_frames(frames, per_device, segments_ref, live_ref, list_ref, visit):
    def step(source, held):
        for place in range(per_device):
            frame = source * per_device + place
            before = jnp.maximum(frame - 1, 0)
            fresh = (frame == 0) | (segments_ref[frame] != segments_ref[before])
            held = jnp.where(fresh, 0, held)
            list_ref[held] = frame
            visit(source, place, frame, held + 1)
            held = held + jnp.where(live_ref[frame] == 1, 1, 0)
        return held

    lax.fori_loop(0, frames // per_device, step, jnp.int32(0))


def attend_kernel(per_device, segments_ref, live_ref, x_ref, mix_ref, wide_ref, lse_ref, kv_ref, list_ref):
    frames = kv_ref.shape[0]

    def turn(source, carry):
        for place in range(per_device):
            both = jnp.concatenate(
                [x_ref[source, place], x_ref[source, per_device + place]], axis=0
            )
            kv_ref[source * per_device + place] = both.astype(F32).T.astype(BF16)
        return carry

    lax.fori_loop(0, frames // per_device, turn, 0)

    def visit(source, place, frame, count):
        query = x_ref[source, 2 * per_device + place]
        query_side = jnp.concatenate([query, jnp.zeros_like(query)], axis=0)

        def scores_of(other):
            return jnp.dot(kv_ref[other], query_side, preferred_element_type=F32)

        def mixed(other, weights):
            value = x_ref[lax.div(other, per_device), per_device + lax.rem(other, per_device)]
            return jnp.dot(value, weights.astype(BF16), preferred_element_type=F32)

        def join(others, carry):
            scores = [scores_of(other) for other in others]
            tops = [jnp.max(score, axis=0, keepdims=True) for score in scores]
            new_top = functools.reduce(jnp.maximum, tops)
            if carry is not None:
                top, total, accum = carry
                new_top = jnp.maximum(top, new_top)
                shrink = jnp.exp(top - new_top)
                total = total * shrink
                accum = accum * shrink
            for index, score in enumerate(scores):
                weights = jnp.exp(score - new_top)
                added = jnp.sum(weights, axis=0, keepdims=True)
                product = mixed(others[index], weights)
                if carry is None and index == 0:
                    total, accum = added, product
                else:
                    total, accum = total + added, accum + product
            return new_top, total, accum

        others = count - 1
        carry = join([frame], None)
        carry = lax.fori_loop(
            0,
            lax.div(others, 2),
            lambda index, state: join([list_ref[2 * index], list_ref[2 * index + 1]], state),
            carry,
        )
        top, total, accum = lax.fori_loop(
            0,
            lax.rem(others, 2),
            lambda unused, state: join([list_ref[others - 1]], state),
            carry,
        )
        result = accum * (1.0 / total)
        wide_ref[source, place] = result
        mix_ref[source, place] = result.astype(BF16)
        lse_ref[pl.ds(frame, 1), :] = top + jnp.log(total)

    walk_frames(frames, per_device, segments_ref, live_ref, list_ref, visit)


def whole_spec():
    return pl.BlockSpec(memory_space=pltpu.VMEM)


def scalar_spec():
    return pl.BlockSpec(memory_space=pltpu.SMEM)


def attend(per_device, segments, live, x):
    sources = x.shape[0]
    frames = sources * per_device
    pairs = frames * 6
    outs = (
        jax.ShapeDtypeStruct((sources, per_device, HEAD, PATCHES), BF16),
        jax.ShapeDtypeStruct((sources, per_device, HEAD, PATCHES), F32),
        jax.ShapeDtypeStruct((frames, PATCHES), F32),
        jax.ShapeDtypeStruct((frames, PATCHES, 2 * HEAD), BF16),
    )
    return pl.pallas_call(
        functools.partial(attend_kernel, per_device),
        out_shape=outs,
        in_specs=[scalar_spec(), scalar_spec(), whole_spec()],
        out_specs=(whole_spec(),) * len(outs),
        scratch_shapes=[pltpu.SMEM((frames,), jnp.int32)],
        cost_estimate=pl.CostEstimate(
            flops=pairs * 4 * PATCHES * PATCHES * 256,
            bytes_accessed=x.size * 2 * 3,
            transcendentals=pairs * PATCHES * PATCHES,
        ),
        compiler_params=pltpu.CompilerParams(vmem_limit_bytes=40 << 20),
        name="attend",
    )(segments, live, x)


def attend_back_kernel(
    per_device,
    orders,
    segments_ref,
    live_ref,
    x_ref,
    kv_ref,
    wide_ref,
    lse_ref,
    d_mix_ref,
    cos_ref,
    sin_ref,
    *refs
):
    out_ref, dkv_ref, list_ref = refs[orders:]
    frames = kv_ref.shape[0]

    def clear(frame, carry):
        dkv_ref[frame] = jnp.zeros((PATCHES, 2 * HEAD), F32)
        return carry

    lax.fori_loop(0, frames, clear, 0)

    def unturn(frame, values):
        lower = values[:HALF]
        upper = values[HALF:]
        cosine = cos_ref[frame]
        sine = sin_ref[frame]
        return jnp.concatenate([lower * cosine + upper * sine, upper * cosine - lower * sine], axis=0)

    def visit(source, place, frame, count):
        query = x_ref[source, 2 * per_device + place]
        d_mix = d_mix_ref[source, place]
        blank = jnp.zeros_like(query)
        query_side = jnp.concatenate([query, blank], axis=0)
        d_mix_side = jnp.concatenate([blank, d_mix], axis=0)
        both = jnp.concatenate(
            [query_side.astype(F32).T.astype(BF16), d_mix_side.astype(F32).T.astype(BF16)], axis=0
        )
        lse = lse_ref[pl.ds(frame, 1), :]
        delta = jnp.sum(d_mix.astype(F32) * wide_ref[source, place], axis=0, keepdims=True)

        def block(other):
            key_value = kv_ref[other]
            scores = jnp.dot(key_value, query_side, preferred_element_type=F32)
            d_weights = jnp.dot(key_value, d_mix_side, preferred_element_type=F32)
            weights = jnp.exp(scores - lse)
            d_scores = (weights * (d_weights - delta)).astype(BF16)
            sides = jnp.concatenate([d_scores, weights.astype(BF16)], axis=1)
            dkv_ref[other] += jnp.dot(sides, both, preferred_element_type=F32)
            key = x_ref[lax.div(other, per_device), lax.rem(other, per_device)]
            return jnp.dot(key, d_scores, preferred_element_type=F32)

        d_query = lax.fori_loop(
            0,
            lax.div(count, 2),
            lambda index, state: state
            + block(list_ref[2 * index])
            + block(list_ref[2 * index + 1]),
            jnp.zeros((HEAD, PATCHES), F32),
        )
        d_query = lax.fori_loop(
            0,
            lax.rem(count, 2),
            lambda unused, state: state + block(list_ref[count - 1]),
            d_query,
        )
        d_query = unturn(frame, d_query * (HEAD**-0.5)).astype(BF16)
        out_ref[source, 2 * per_device + place] = d_query

    walk_frames(frames, per_device, segments_ref, live_ref, list_ref, visit)

    def finish(source, carry):
        for place in range(per_device):
            frame = source * per_device + place
            both = dkv_ref[frame].T
            out_ref[source, place] = unturn(frame, both[:HEAD]).astype(BF16)
            out_ref[source, per_device + place] = both[HEAD:].astype(BF16)
        return carry

    lax.fori_loop(0, frames // per_device, finish, 0)


def attend_back(per_device, segments, live, x, kv, wide, lse, d_mix, cosine, sine, orders):
    sources = x.shape[0]
    frames = sources * per_device
    pairs = frames * 6
    orders = [each.reshape(-1, each.shape[-1])[:8, :128] for each in orders]
    args = [segments, live, x, kv, wide, lse, d_mix, cosine, sine]
    return pl.pallas_call(
        functools.partial(attend_back_kernel, per_device, len(orders)),
        out_shape=jax.ShapeDtypeStruct(x.shape, BF16),
        in_specs=[scalar_spec(), scalar_spec()]
        + [whole_spec()] * (len(args) - 2)
        + [pl.BlockSpec(memory_space=pl.ANY)] * len(orders),
        out_specs=whole_spec(),
        scratch_shapes=[
            pltpu.VMEM((frames, PATCHES, 2 * HEAD), F32),
            pltpu.SMEM((frames,), jnp.int32),
        ],
        cost_estimate=pl.CostEstimate(
            flops=pairs * 10 * PATCHES * PATCHES * 256,
            bytes_accessed=x.size * 2 * 5,
            transcendentals=pairs * PATCHES * PATCHES,
        ),
        compiler_params=pltpu.CompilerParams(vmem_limit_bytes=60 << 20),
        name="attend_back",
    )(*args, *orders)


def exchange(value, axis, bit):
    count = lax.axis_size(axis)
    return lax.ppermute(value, axis, [(source, source ^ bit) for source in range(count)])


def after(value, *earlier):
    return lax.optimization_barrier((value,) + earlier)[0]


def of_packs(value):
    values = [value]
    bit = lax.axis_size("pack") // 2
    while bit:
        values = values + [exchange(each, "pack", bit) for each in values]
        bit //= 2
    return values


def halving_fits():
    return lax.axis_size("pack") == 2 and lax.axis_size("seq") == 16


class RowSum:
    def __init__(self, mine, came, order):
        self.order = list(order)
        self.index = lax.axis_index("seq")
        rows = mine.shape[-2]
        self.tail = (rows // 16, mine.shape[-1])
        self.lead = mine.shape[:-2]
        shape = self.lead + (2, 2, 2, 2) + self.tail
        self.parts = [mine.reshape(shape), came.reshape(shape)]

    def pick(self, bit, which):
        axis = len(self.lead) + {8: 0, 4: 1, 2: 2, 1: 3}[bit]
        pieces = [lax.dynamic_slice_in_dim(part, which, 1, axis) for part in self.parts]
        return (pieces[0].astype(F32) + pieces[1].astype(F32)).astype(BF16)

    def stage(self):
        bit = self.order.pop(0)
        own_bit = lax.rem(lax.div(self.index, bit), 2)
        send = self.pick(bit, 1 - own_bit)
        came = exchange(send, "seq", bit)
        self.parts = [self.pick(bit, own_bit), came]
        return send

    def finish(self):
        while self.order:
            self.stage()
        own = (self.parts[0].astype(F32) + self.parts[1].astype(F32)).astype(BF16)
        return by_pack(own.reshape(self.lead + self.tail))


def by_pack(own):
    other = exchange(own, "pack", 1)
    first = lax.axis_index("pack") == 0
    return jnp.where(first, own, other), jnp.where(first, other, own)


def scattered(half):
    return by_pack(lax.psum_scatter(half, "seq", scatter_dimension=0, tiled=True))


def row_sum_direct(term):
    part = lax.psum_scatter(term.astype(BF16), "seq", scatter_dimension=0, tiled=True)
    return lax.psum(part, "pack").astype(F32)


def project_kernel(
    per_device,
    hidden_ref,
    shift_ref,
    scale_ref,
    wq_ref,
    wk_ref,
    wv_ref,
    bq_ref,
    bk_ref,
    bv_ref,
    cos_ref,
    sin_ref,
    in_ref,
    x_ref,
):
    @pl.when(pl.program_id(0) == 0)
    def _():
        for place in range(per_device):
            rows = pl.ds(place * PATCHES, PATCHES)
            values = hidden_ref[rows, :].astype(F32)
            centered = values - jnp.mean(values, axis=-1, keepdims=True)
            spread = jnp.mean(centered * centered, axis=-1, keepdims=True)
            normed = centered * lax.rsqrt(spread + EPSILON)
            scale = scale_ref[pl.ds(place, 1), :]
            in_ref[rows, :] = (normed * (1.0 + scale) + shift_ref[pl.ds(place, 1), :]).astype(BF16)

    rows = in_ref[...]
    group = wq_ref.shape[1] // HEAD

    def turned(values, place):
        lower = values[:HALF]
        upper = values[HALF:]
        cosine = cos_ref[place]
        sine = sin_ref[place]
        return jnp.concatenate([lower * cosine - upper * sine, upper * cosine + lower * sine], axis=0)

    for kind, (weight_ref, bias_ref) in enumerate(
        ((wq_ref, bq_ref), (wk_ref, bk_ref), (wv_ref, bv_ref))
    ):
        flat = jnp.dot(rows, weight_ref[...], preferred_element_type=F32) + bias_ref[...]
        for place in range(per_device):
            block = flat[place * PATCHES : (place + 1) * PATCHES].T
            for head in range(group):
                values = block[head * HEAD : (head + 1) * HEAD]
                if kind == 0:
                    values = turned(values, place) * (HEAD**-0.5)
                    x_ref[head, 2 * per_device + place] = values.astype(BF16)
                elif kind == 1:
                    x_ref[head, place] = turned(values, place).astype(BF16)
                else:
                    x_ref[head, per_device + place] = values.astype(BF16)


def project(per_device, hidden, shift, scale, weight, bias, cosine, sine):
    tokens, width = hidden.shape
    heads = width // HEAD
    group = 2
    lanes = group * HEAD
    steps = heads // group
    bias_row = bias[None, :]

    def whole(shape):
        return pl.BlockSpec(shape, lambda step: (0,) * len(shape))

    def part(kind, rows):
        return pl.BlockSpec((rows, lanes), lambda step: (0, kind * steps + step))

    blocks = (heads, 3 * per_device, HEAD, PATCHES)
    return pl.pallas_call(
        functools.partial(project_kernel, per_device),
        grid=(steps,),
        out_shape=(
            jax.ShapeDtypeStruct((tokens, width), BF16),
            jax.ShapeDtypeStruct(blocks, BF16),
        ),
        in_specs=[whole((tokens, width)), whole(shift.shape), whole(scale.shape)]
        + [part(kind, width) for kind in range(3)]
        + [part(kind, 1) for kind in range(3)]
        + [whole(cosine.shape), whole(sine.shape)],
        out_specs=(
            whole((tokens, width)),
            pl.BlockSpec((group,) + blocks[1:], lambda step: (step, 0, 0, 0)),
        ),
        cost_estimate=pl.CostEstimate(
            flops=2 * tokens * width * 3 * width,
            bytes_accessed=2 * (weight.size + 5 * tokens * width),
            transcendentals=0,
        ),
        compiler_params=pltpu.CompilerParams(vmem_limit_bytes=40 << 20),
        name="project",
    )(hidden, shift, scale, weight, weight, weight, bias_row, bias_row, bias_row, cosine, sine)


GELU_SLOPE = 0.7978845608028654
GELU_CUBE = 0.044715


def feed_kernel(
    carried,
    which_ref,
    in_ref,
    d_out_ref,
    up_a_ref,
    up_b_ref,
    bias_a_ref,
    bias_b_ref,
    down_a_ref,
    down_b_ref,
    *refs
):
    if carried:
        out_before_ref, d_in_before_ref = refs[:2]
        refs = refs[2:]
    out_ref, d_in_ref, d_up_ref, d_down_ref, d_bias_ref, turned_ref = refs

    @pl.when(pl.program_id(0) == 0)
    def _():
        turned_ref[...] = in_ref[...].astype(F32).T.astype(BF16)
        if carried:
            out_ref[...] = out_before_ref[...]
            d_in_ref[...] = d_in_before_ref[...]
        else:
            out_ref[...] = jnp.zeros_like(out_ref)
            d_in_ref[...] = jnp.zeros_like(d_in_ref)

    up = jnp.concatenate([up_a_ref[...], up_b_ref[...]], axis=1)
    down = jnp.concatenate([down_a_ref[...], down_b_ref[...]], axis=0)
    bias = jnp.concatenate([bias_a_ref[...], bias_b_ref[...]], axis=1)
    d_out = d_out_ref[...]
    pre = jnp.dot(in_ref[...], up, preferred_element_type=F32) + bias
    d_act = dot_over(d_out, down, 1, 1)
    square = pre * pre
    bend = jnp.tanh(GELU_SLOPE * pre * (1.0 + GELU_CUBE * square))
    half = 0.5 * (1.0 + bend)
    act = (pre * half).astype(BF16)
    slope = half + (0.5 * GELU_SLOPE) * pre * (1.0 - bend * bend) * (
        1.0 + (3.0 * GELU_CUBE) * square
    )
    d_pre = (d_act * slope).astype(BF16)
    out_ref[...] += jnp.dot(act, down, preferred_element_type=F32)
    d_in_ref[...] += dot_over(d_pre, up, 1, 1)
    d_up_ref[...] = jnp.dot(turned_ref[...], d_pre, preferred_element_type=F32).astype(BF16)
    d_down_ref[...] = jnp.dot(
        act.astype(F32).T.astype(BF16), d_out, preferred_element_type=F32
    ).astype(BF16)
    d_bias_ref[...] = jnp.sum(d_pre.astype(F32), axis=0, keepdims=True)


def feed(which, feed_in, d_feed_out, up_weight, up_bias, down_weight, before):
    tokens, width = feed_in.shape
    hidden_units = up_weight.shape[1]
    small = 128
    steps = hidden_units // (4 * small)
    own = hidden_units // 2

    def whole(shape):
        return pl.BlockSpec(shape, lambda step, which: (0,) * len(shape))

    def group(nth):
        return lambda step, which: 2 * (2 * step + nth) + which[0]

    def columns(nth, rows):
        return pl.BlockSpec((rows, small), lambda step, which: (0, group(nth)(step, which)))

    def rows_of(nth):
        return pl.BlockSpec((small, width), lambda step, which: (group(nth)(step, which), 0))

    args = [feed_in, d_feed_out, up_weight, up_weight, up_bias[None], up_bias[None]]
    args += [down_weight, down_weight]
    specs = [whole((tokens, width)), whole((tokens, width)), columns(0, width), columns(1, width)]
    specs += [columns(0, 1), columns(1, 1), rows_of(0), rows_of(1)]
    if before is not None:
        args += list(before)
        specs += [whole((tokens, width)), whole((tokens, width))]
    return pl.pallas_call(
        functools.partial(feed_kernel, before is not None),
        grid_spec=pltpu.PrefetchScalarGridSpec(
            num_scalar_prefetch=1,
            grid=(steps,),
            in_specs=specs,
            out_specs=(
                whole((tokens, width)),
                whole((tokens, width)),
                pl.BlockSpec((width, 2 * small), lambda step, which: (0, step)),
                pl.BlockSpec((2 * small, width), lambda step, which: (step, 0)),
                pl.BlockSpec((1, 2 * small), lambda step, which: (0, step)),
            ),
            scratch_shapes=[pltpu.VMEM((width, tokens), BF16)],
        ),
        out_shape=(
            jax.ShapeDtypeStruct((tokens, width), F32),
            jax.ShapeDtypeStruct((tokens, width), F32),
            jax.ShapeDtypeStruct((width, own), BF16),
            jax.ShapeDtypeStruct((own, width), BF16),
            jax.ShapeDtypeStruct((1, own), F32),
        ),
        cost_estimate=pl.CostEstimate(
            flops=12 * tokens * width * own,
            bytes_accessed=2 * (4 * own * width + 8 * tokens * width),
            transcendentals=tokens * own,
        ),
        compiler_params=pltpu.CompilerParams(vmem_limit_bytes=56 << 20),
        name="feed%d" % (before is not None),
    )(which.reshape(1), *args)


def norm_back(values, d_in, scale):
    centered = values - jnp.mean(values, axis=-1, keepdims=True)
    spread = jnp.mean(centered * centered, axis=-1, keepdims=True)
    inverse = lax.rsqrt(spread + EPSILON)
    normed = centered * inverse
    product = d_in * normed
    d_shift = jnp.sum(d_in, axis=0, keepdims=True)
    d_scale = jnp.sum(product, axis=0, keepdims=True)
    scaled = 1.0 + scale
    mean_d = jnp.mean(d_in * scaled, axis=-1, keepdims=True)
    mean_p = jnp.mean(product * scaled, axis=-1, keepdims=True)
    return (d_in * scaled - mean_d - normed * mean_p) * inverse, d_shift, d_scale


def middle_back_kernel(
    d_in_ref,
    middle_ref,
    grad_ref,
    attn_ref,
    feed_ref,
    scale_ref,
    gate_ref,
    feed_gate_ref,
    down_bias_ref,
    rows_ref,
    weight_ref,
    d_middle_ref,
    d_attn_ref,
    layer_ref,
    blocks_ref,
    sums_ref,
):
    frame = pl.program_id(0)
    per_device = pl.num_programs(0) - 1

    @pl.when(frame < per_device)
    def _():
        mine = pl.ds(frame, 1)
        middle = middle_ref[...]
        grads = grad_ref[...].astype(F32)
        back, d_shift, d_scale = norm_back(middle, d_in_ref[...], scale_ref[mine, :])
        d_middle = grads + back
        d_middle_ref[...] = d_middle
        d_attn = (d_middle * gate_ref[mine, :]).astype(BF16)
        d_attn_ref[...] = d_attn
        feed_rows = feed_ref[...] + down_bias_ref[...]
        feed_gate = feed_gate_ref[mine, :]
        layer_ref[...] = (middle + feed_gate * feed_rows).astype(BF16)
        d_feed_out = (feed_gate * grads).astype(BF16).astype(F32)
        sums_ref[frame] = jnp.concatenate(
            [
                jnp.sum(d_middle * attn_ref[...], axis=0, keepdims=True),
                d_shift,
                d_scale,
                jnp.sum(grads * feed_rows, axis=0, keepdims=True),
                jnp.sum(d_attn.astype(F32), axis=0, keepdims=True),
                jnp.sum(d_feed_out, axis=0, keepdims=True),
                jnp.zeros((2, d_shift.shape[1]), F32),
            ],
            axis=0,
        )
        d_mix = dot_over(weight_ref[...], d_attn, 1, 1).astype(BF16)
        for head in range(blocks_ref.shape[0]):
            blocks_ref[head, 0] = d_mix[head * HEAD : (head + 1) * HEAD]

    @pl.when(frame == per_device)
    def _():
        first = sums_ref[0]
        second = sums_ref[1]
        rows = jnp.concatenate(
            [first[:4], second[:4], first[4:6] + second[4:6], rows_ref[...]], axis=0
        ).astype(BF16)
        count = rows.shape[1] // PATCHES
        block = jnp.concatenate(
            [rows[:, nth * PATCHES : (nth + 1) * PATCHES] for nth in range(count)], axis=0
        )
        for head in range(blocks_ref.shape[0]):
            blocks_ref[head, 0] = block


def middle_back(
    per_device, d_in, middle, grads, attn_rows, feed_rows, scale, gate, feed_gate, down_bias, rows, weight
):
    tokens, width = d_in.shape
    heads = width // HEAD
    last = per_device - 1
    per_frame = pl.BlockSpec((PATCHES, width), lambda frame: (jnp.minimum(frame, last), 0))

    def whole(shape):
        return pl.BlockSpec(shape, lambda frame: (0,) * len(shape))

    small = whole((per_device, width))
    return pl.pallas_call(
        middle_back_kernel,
        grid=(per_device + 1,),
        out_shape=(
            jax.ShapeDtypeStruct((tokens, width), F32),
            jax.ShapeDtypeStruct((tokens, width), BF16),
            jax.ShapeDtypeStruct((tokens, width), BF16),
            jax.ShapeDtypeStruct((heads, per_device + 1, HEAD, PATCHES), BF16),
        ),
        in_specs=[per_frame] * 5
        + [small] * 3
        + [whole((1, width)), whole(rows.shape), whole(weight.shape)],
        out_specs=(
            per_frame,
            per_frame,
            per_frame,
            pl.BlockSpec((heads, 1, HEAD, PATCHES), lambda frame: (0, frame, 0, 0)),
        ),
        scratch_shapes=[pltpu.VMEM((per_device, 8, width), F32)],
        cost_estimate=pl.CostEstimate(
            flops=2 * tokens * width * width, bytes_accessed=24 * tokens * width, transcendentals=0
        ),
        compiler_params=pltpu.CompilerParams(vmem_limit_bytes=48 << 20),
        name="middle_back",
    )(
        d_in,
        middle,
        grads,
        attn_rows,
        feed_rows,
        scale,
        gate,
        feed_gate,
        down_bias[None],
        rows,
        weight,
    )


def unproject_kernel(
    per_device, carried, which_ref, in_ref, back_ref, wq_ref, wk_ref, wv_ref, *refs
):
    if carried:
        before_ref, hidden_ref, d_middle_ref, scale_ref, bias_theirs_ref = refs[:5]
        d_weight_ref, grad_ref, rows_ref, d_in_ref, d_bias_ref, turned_ref = refs[5:]
    else:
        d_in_ref, d_weight_ref, d_bias_ref, turned_ref = refs

    @pl.when(pl.program_id(0) == 0)
    def _():
        turned_ref[...] = in_ref[...].astype(F32).T.astype(BF16)
        if carried:
            d_in_ref[...] = before_ref[...]
        else:
            d_in_ref[...] = jnp.zeros_like(d_in_ref)

    group = wq_ref.shape[1] // HEAD

    def token_major(block_of):
        rows = []
        for place in range(per_device):
            block = jnp.concatenate([block_of(head, place) for head in range(group)], axis=0)
            rows.append(block.astype(F32).T.astype(BF16))
        return jnp.concatenate(rows, axis=0)

    sides = jnp.concatenate(
        [
            token_major(lambda head, place: back_ref[head, 2 * per_device + place]),
            token_major(lambda head, place: back_ref[head, place]),
            token_major(lambda head, place: back_ref[head, per_device + place]),
        ],
        axis=1,
    )
    weights = jnp.concatenate([wq_ref[...], wk_ref[...], wv_ref[...]], axis=1)
    d_in_ref[...] += dot_over(sides, weights, 1, 1)
    d_weight = jnp.dot(turned_ref[...], sides, preferred_element_type=F32).astype(BF16)
    d_bias = jnp.sum(sides.astype(F32), axis=0, keepdims=True)
    lanes = group * HEAD
    for kind in range(3):
        d_weight_ref[kind] = d_weight[:, kind * lanes : (kind + 1) * lanes]
        part = d_bias[:, kind * lanes : (kind + 1) * lanes]
        if carried:
            start = pl.multiple_of(pl.program_id(0) * lanes, lanes)
            d_bias_ref[pl.ds(kind, 1), pl.ds(start, lanes)] = part
        else:
            d_bias_ref[kind] = part

    if carried:

        @pl.when(pl.program_id(0) == pl.num_programs(0) - 1)
        def _():
            sums = []
            for place in range(per_device):
                rows = pl.ds(place * PATCHES, PATCHES)
                mine = pl.ds(place, 1)
                back, d_shift, d_scale = norm_back(
                    hidden_ref[rows, :].astype(F32), d_in_ref[rows, :], scale_ref[mine, :]
                )
                grad_ref[rows, :] = (d_middle_ref[rows, :] + back).astype(BF16)
                sums += [d_shift, d_scale]
            for kind in range(3):
                sums.append(
                    jnp.concatenate([d_bias_ref[pl.ds(kind, 1), :], bias_theirs_ref[kind]], axis=1)
                )
            count = 16 - len(sums)
            late = jnp.concatenate(
                sums + [jnp.zeros((count, d_in_ref.shape[1]), F32)], axis=0
            ).astype(BF16)
            for target in range(rows_ref.shape[0]):
                rows_ref[target] = late


def unproject(per_device, targets, which, attn_in, back, weight, before=None, norm_args=()):
    tokens, width = attn_in.shape
    heads = width // HEAD
    group = 2
    lanes = group * HEAD
    groups = heads // group
    steps = groups // 2

    def whole(shape):
        return pl.BlockSpec(shape, lambda step, which: (0,) * len(shape))

    def blocks(array):
        return pl.BlockSpec(
            (group,) + array.shape[1:], lambda step, which: (which[0] * steps + step, 0, 0, 0)
        )

    def part(kind):
        return pl.BlockSpec(
            (width, lanes), lambda step, which: (0, kind * groups + which[0] * steps + step)
        )

    args = [attn_in, back, weight, weight, weight]
    specs = [whole((tokens, width)), blocks(back), part(0), part(1), part(2)]
    weight_shape = (
        jax.ShapeDtypeStruct((3, width, width // 2), BF16),
        jax.ShapeDtypeStruct((3, 1, width // 2), F32),
    )
    weight_specs = (
        pl.BlockSpec((3, width, lanes), lambda step, which: (0, 0, step)),
        pl.BlockSpec((3, 1, lanes), lambda step, which: (0, 0, step)),
    )
    scratch = [pltpu.VMEM((width, tokens), BF16)]
    small = (per_device, width)
    if before is not None:
        args += [before] + list(norm_args)
        specs += [whole((tokens, width))] * 3 + [whole(small), whole((3, 1, width // 2))]
        late = (targets, 16, width)
        outs = weight_shape[:1] + (
            jax.ShapeDtypeStruct((tokens, width), BF16),
            jax.ShapeDtypeStruct(late, BF16),
        )
        out_specs = weight_specs[:1] + (whole((tokens, width)), whole(late))
        scratch = [pltpu.VMEM((tokens, width), F32), pltpu.VMEM((3, width // 2), F32)] + scratch
    else:
        outs = (jax.ShapeDtypeStruct((tokens, width), F32),) + weight_shape
        out_specs = (whole((tokens, width)),) + weight_specs
    return pl.pallas_call(
        functools.partial(unproject_kernel, per_device, before is not None),
        grid_spec=pltpu.PrefetchScalarGridSpec(
            num_scalar_prefetch=1,
            grid=(steps,),
            in_specs=specs,
            out_specs=out_specs,
            scratch_shapes=scratch,
        ),
        out_shape=outs,
        cost_estimate=pl.CostEstimate(
            flops=6 * tokens * width * width,
            bytes_accessed=2 * (3 * width * width + 6 * tokens * width),
            transcendentals=0,
        ),
        compiler_params=pltpu.CompilerParams(vmem_limit_bytes=48 << 20),
        name="unproject%d" % (before is not None),
    )(which.reshape(1), *args)


def columns_of(matrix, start, width, axis=1):
    if isinstance(start, int) and start == 0 and width == matrix.shape[axis]:
        return matrix
    return lax.dynamic_slice_in_dim(matrix, start, width, axis)


def local(
    hidden,
    cotangent,
    levels,
    segments,
    live_frames,
    noise_table,
    mod_weight,
    mod_bias,
    qkv_weight,
    qkv_bias,
    out_weight,
    out_bias,
    up_weight,
    up_bias,
    down_weight,
    down_bias,
):
    seq_index = lax.axis_index("seq")
    seq_count = lax.axis_size("seq")
    tokens = hidden.shape[1]
    width = hidden.shape[2]
    per_device = tokens // PATCHES
    frames = segments.shape[1]
    heads = width // HEAD
    copies = seq_count // heads
    hidden_units = up_weight.shape[1]
    level_count = noise_table.shape[0]
    share = width // seq_count
    clip_ids = segments[0]
    live = live_frames[0]

    pack = lax.axis_index("pack")
    halves = halving_fits()
    frame_ids = jnp.arange(frames, dtype=jnp.int32)
    same_clip = clip_ids[:, None] == clip_ids[None, :]
    clip_starts = jnp.min(jnp.where(same_clip, frame_ids[None, :], frames), axis=1)
    frame_times = (frame_ids - clip_starts).astype(F32)
    own_cos, own_sin = rotary_tables(
        lax.dynamic_slice_in_dim(frame_times, seq_index * per_device, per_device)
    )

    embed = jnp.concatenate(
        [
            lax.dynamic_slice_in_dim(noise_table, levels[0, frame], 1, 0)
            for frame in range(per_device)
        ],
        axis=0,
    )
    cond = jax.nn.silu(embed).astype(BF16)
    modulation = jnp.dot(cond, mod_weight[:, : 2 * width], preferred_element_type=F32)
    attn_shift, attn_scale = jnp.split(modulation + mod_bias[: 2 * width], 2, axis=1)
    attn_in, sent = project(
        per_device, hidden[0], attn_shift, attn_scale, qkv_weight, qkv_bias, own_cos, own_sin
    )

    def to_heads(array):
        if copies > 1:
            array = jnp.concatenate([array] * copies, axis=0)
        return lax.all_to_all(array, "seq", 0, 0, tiled=True)

    def to_tokens(array):
        return lax.all_to_all(array, "seq", 0, 0, tiled=True)[:heads]

    x = to_heads(sent)
    late_modulation = jnp.dot(
        after(cond, attn_in), mod_weight[:, 2 * width :], preferred_element_type=F32
    )
    attn_gate, feed_shift, feed_scale, feed_gate = jnp.split(
        late_modulation + mod_bias[2 * width :], 4, axis=1
    )
    cos_all, sin_all = rotary_tables(after(frame_times, attn_in))
    grad_rows = cotangent[0].astype(F32).reshape(per_device, PATCHES, width)
    d_feed_out = (feed_gate[:, None, :] * grad_rows).reshape(tokens, width).astype(BF16)
    x, d_feed_out, cos_all, sin_all = lax.optimization_barrier((x, d_feed_out, cos_all, sin_all))
    mix, wide, lse, kv = attend(per_device, clip_ids, live, x)
    mix = to_tokens(mix)
    mixes = [mix[:, place].reshape(width, PATCHES) for place in range(per_device)]
    attn_rows = jnp.stack([dot_over(each, out_weight, 0, 0) for each in mixes]) + out_bias
    attn_mix = jnp.concatenate(mixes, axis=1)

    frame_rows = hidden[0].astype(F32).reshape(per_device, PATCHES, width)
    middle = frame_rows + attn_gate[:, None, :] * attn_rows
    feed_in = modulate_norm(middle, feed_shift, feed_scale).reshape(tokens, width).astype(BF16)
    feed_args = (feed_in, d_feed_out, up_weight, up_bias, down_weight)
    theirs = feed(1 - pack if halves else pack * 0 + 1, *feed_args, None)
    mine = feed(pack if halves else pack * 0, *feed_args, theirs[:2])
    small = 128

    def in_order(own, other):
        if halves:
            even, odd = jnp.where(pack == 0, own, other), jnp.where(pack == 0, other, own)
        else:
            even, odd = own, other
        rows = own.shape[0]
        return jnp.stack(
            [even.reshape(rows, -1, small), odd.reshape(rows, -1, small)], axis=2
        ).reshape(rows, -1)

    own_levels = levels[0]
    level_row = jnp.concatenate(
        [
            jnp.broadcast_to(part[frame], (width // (2 * per_device),))
            for frame in range(per_device)
            for part in (lax.div(own_levels, 32), lax.rem(own_levels, 32))
        ]
    ).astype(F32)[None]
    extra_rows = jnp.concatenate(
        [
            in_order(mine[4], theirs[4]).reshape(-1, width),
            level_row,
            jnp.zeros((1, width), F32),
        ],
        axis=0,
    )
    d_middle, d_attn_out, layer_out, blocks = middle_back(
        per_device,
        mine[1],
        middle.reshape(tokens, width),
        cotangent[0],
        attn_rows.reshape(tokens, width),
        mine[0],
        feed_scale,
        attn_gate,
        feed_gate,
        down_bias,
        extra_rows,
        out_weight,
    )
    layer_out = layer_out.reshape(1, tokens, width)
    d_mix = to_heads(blocks)

    def out_term(start, size):
        return dot_over(attn_mix, columns_of(d_attn_out, start, size), 1, 0).astype(BF16)

    sums = []
    if halves:
        half = width // 2
        out_theirs = exchange(out_term((1 - pack) * half, half), "pack", 1)
        sums = [
            mine[3] + exchange(theirs[3], "pack", 1),
            mine[2] + exchange(theirs[2], "pack", 1),
            out_term(pack * half, half) + out_theirs,
        ]

    def own_share(row):
        piece = row.shape[0] // seq_count
        return lax.dynamic_slice_in_dim(row, seq_index * piece, piece)

    chunks = width // PATCHES
    early_rows = d_mix[:, per_device].reshape(seq_count, chunks, 16, PATCHES)
    early_rows = early_rows.transpose(0, 2, 1, 3).reshape(seq_count, 16, width)
    early_sets = of_packs(early_rows)
    early_sum = functools.reduce(
        jnp.add, [jnp.sum(each.astype(F32), axis=0) for each in early_sets]
    )
    out_bias_grad = own_share(early_sum[8])
    down_bias_grad = own_share(early_sum[9])
    up_bias_grad = own_share(early_sum[10:14].reshape(hidden_units))

    def frames_of(rows, per_frame, kinds):
        return jnp.concatenate(
            [
                jnp.stack(
                    [rows[:, frame * per_frame + kind] for frame in range(per_device)], axis=1
                ).reshape(-1, width)
                for kind in range(kinds)
            ],
            axis=1,
        )

    own_table = lax.dynamic_slice_in_dim(noise_table, seq_index * share, share, 1)
    own_mod = lax.dynamic_slice_in_dim(mod_weight, seq_index * share, share, 0)
    stride = width // (2 * per_device)
    parts = []
    for rows in early_sets:
        coded = rows[:, 14, ::stride].astype(jnp.int32).reshape(-1, 2)
        set_levels = coded[:, 0] * 32 + coded[:, 1]
        picks = (set_levels[:, None] == jnp.arange(level_count, dtype=jnp.int32)[None, :]).astype(F32)
        embeds = jnp.dot(picks, own_table, precision=PRECISE, preferred_element_type=F32)
        set_cond = jax.nn.silu(embeds).astype(BF16)
        d_mod = frames_of(rows, 4, 4)
        parts.append(
            (
                picks,
                embeds,
                set_cond,
                dot_over(d_mod, own_mod[:, 2 * width :], 1, 1),
                dot_over(set_cond, d_mod, 0, 0),
            )
        )
    mod_grad_early = functools.reduce(jnp.add, [each[4] for each in parts])
    mod_sum_early = (early_sum[:4] + early_sum[4:8]).reshape(4 * width)
    early_done = [mod_grad_early, mod_sum_early, out_bias_grad, down_bias_grad, up_bias_grad]
    for part in parts:
        early_done += [part[1], part[3]]

    result = attend_back(
        per_device, clip_ids, live, x, kv, wide, lse, d_mix, cos_all, sin_all, sums
    )
    back = to_tokens(result)
    back = after(back, *early_done)
    which = (1 - pack, pack) if halves else (pack * 0, pack * 0 + 1)
    d_in_theirs, qkv_theirs, bias_theirs = unproject(
        per_device, seq_count, which[0], attn_in, back, qkv_weight
    )
    qkv_mine, hidden_grad, late = unproject(
        per_device,
        seq_count,
        which[1],
        attn_in,
        back,
        qkv_weight,
        d_in_theirs,
        (hidden[0], d_middle, attn_scale, bias_theirs),
    )
    hidden_grad = hidden_grad.reshape(1, tokens, width)
    late_rows = lax.all_to_all(late, "seq", 0, 0, tiled=True)

    def halves_in_order(own, other):
        if halves:
            return jnp.where(pack == 0, own, other), jnp.where(pack == 0, other, own)
        return other, own

    if halves:
        came = exchange(qkv_theirs, "pack", 1)
        split = width // 4
        qkv_sums = [
            RowSum(qkv_mine[..., :split], came[..., :split], (1, 2, 4, 8)),
            RowSum(qkv_mine[..., split:], came[..., split:], (2, 1, 4, 8)),
        ]
        down_weight_grad = jnp.concatenate(scattered(sums[0]), axis=0).astype(F32)
        even, odd = scattered(sums[1])
        up_weight_grad = jnp.stack(
            [even.reshape(share, -1, small), odd.reshape(share, -1, small)], axis=2
        ).reshape(share, hidden_units)
        up_weight_grad = up_weight_grad.astype(F32)
        out_weight_grad = jnp.concatenate(scattered(sums[2]), axis=1).astype(F32)
        done = [each.finish() for each in qkv_sums]
        qkv_weight_grad = jnp.concatenate(
            [done[0][0], done[1][0], done[0][1], done[1][1]], axis=-1
        )
        qkv_weight_grad = qkv_weight_grad.transpose(1, 0, 2).reshape(share, 3 * width).astype(F32)
    else:
        up_weight_grad = row_sum_direct(in_order(mine[2], theirs[2]))
        pairs = [each[3].reshape(-1, small, width) for each in (mine, theirs)]
        down_weight_grad = row_sum_direct(jnp.stack(pairs, axis=1).reshape(hidden_units, width))
        out_weight_grad = row_sum_direct(out_term(0, width))
        qkv_term = jnp.concatenate(halves_in_order(qkv_mine, qkv_theirs), axis=-1)
        qkv_weight_grad = row_sum_direct(qkv_term.transpose(1, 0, 2).reshape(width, 3 * width))

    late_sets = of_packs(late_rows[:, :8])
    bias_at = 2 * per_device
    bias_sums = [
        jnp.sum(rows[:, bias_at : bias_at + 3].astype(F32), axis=0) for rows in late_sets
    ]
    if halves:
        ones, twos = bias_sums
        half = width // 2
        own_half = ones[:, :half] + twos[:, half:]
        other_half = ones[:, half:] + twos[:, :half]
    else:
        total = functools.reduce(jnp.add, bias_sums)
        own_half, other_half = total[:, : width // 2], total[:, width // 2 :]
    bias_total = jnp.concatenate(halves_in_order(own_half, other_half), axis=1)
    qkv_bias_grad = own_share(bias_total.reshape(3 * width))
    late_mods = [frames_of(rows, 2, 2) for rows in late_sets]
    mod_sum_late = functools.reduce(
        jnp.add, [jnp.sum(each.astype(F32), axis=0) for each in late_mods]
    )
    d_embeds = []
    for part, d_mod in zip(parts, late_mods):
        d_cond = part[3] + dot_over(d_mod, own_mod[:, : 2 * width], 1, 1)
        d_embeds.append(jax.vjp(jax.nn.silu, part[1])[1](d_cond)[0])
    table_grad = lax.dot_general(
        jnp.concatenate([part[0] for part in parts], axis=0),
        jnp.concatenate(d_embeds, axis=0),
        (((0,), (0,)), ((), ())),
        precision=PRECISE,
        preferred_element_type=F32,
    )
    mod_grad_late = functools.reduce(
        jnp.add, [dot_over(part[2], d_mod, 0, 0) for part, d_mod in zip(parts, late_mods)]
    )
    mod_weight_grad = jnp.concatenate([mod_grad_late, mod_grad_early], axis=1)
    mod_bias_grad = own_share(jnp.concatenate([mod_sum_late, mod_sum_early]))
    return (
        layer_out,
        hidden_grad,
        table_grad,
        mod_weight_grad,
        mod_bias_grad,
        qkv_weight_grad,
        qkv_bias_grad,
        out_weight_grad,
        out_bias_grad,
        up_weight_grad,
        up_bias_grad,
        down_weight_grad,
        down_bias_grad,
    )


def solution(mesh):
    in_specs = (
        P("pack", "seq", None),
        P("pack", "seq", None),
        P("pack", "seq"),
        P("pack", None),
        P("pack", None),
    ) + (P(),) * 11
    out_specs = (
        P("pack", "seq", None),
        P("pack", "seq", None),
        P(None, "seq"),
        P("seq", None),
        P("seq"),
        P("seq", None),
        P("seq"),
        P("seq", None),
        P("seq"),
        P("seq", None),
        P("seq"),
        P("seq", None),
        P("seq"),
    )
    return jax.shard_map(local, mesh=mesh, in_specs=in_specs, out_specs=out_specs, check_vma=False)
```

```python
import functools

import jax
import jax.numpy as jnp
from jax import lax
from jax.experimental import pallas as pl
from jax.experimental.pallas import tpu as pltpu
from jax.sharding import PartitionSpec as P

HEAD = 64
PATCHES = 256
SIDE = 16
EPSILON = 1e-06
PRECISE = lax.Precision.HIGHEST
HALF = HEAD // 2
F32 = jnp.float32
BF16 = jnp.bfloat16


def modulate_norm(rows, shift, scale):
    center = jnp.mean(rows, axis=-1, keepdims=True)
    centered = rows - center
    spread = jnp.mean(centered * centered, axis=-1, keepdims=True)
    normed = centered * lax.rsqrt(spread + EPSILON)
    return normed * (1.0 + scale[:, None, :]) + shift[:, None, :]


def gelu_tanh(values):
    return jax.nn.gelu(values, approximate=True)


def dot_over(first, second, first_dim, second_dim):
    return lax.dot_general(
        first, second, (((first_dim,), (second_dim,)), ((), ())), preferred_element_type=F32
    )


def spatial_angles():
    time_pairs = HALF // 4
    space_pairs = (HALF - time_pairs) // 2
    patch = jnp.arange(PATCHES, dtype=jnp.int32)
    row_pos = (patch // SIDE).astype(F32)
    col_pos = (patch % SIDE).astype(F32)
    time_freq = 10000.0 ** (-jnp.arange(time_pairs, dtype=F32) / time_pairs)
    space_freq = 10000.0 ** (-jnp.arange(space_pairs, dtype=F32) / space_pairs)
    space = jnp.concatenate(
        [space_freq[:, None] * row_pos[None, :], space_freq[:, None] * col_pos[None, :]], axis=0
    )
    return time_freq, space


def rotary_tables(time_frames):
    time_freq, space = spatial_angles()
    count = time_frames.shape[0]
    time_angle = time_frames[:, None] * time_freq[None, :]

    def whole(function):
        return jnp.concatenate(
            [
                jnp.broadcast_to(
                    function(time_angle)[:, :, None], (count, time_freq.shape[0], PATCHES)
                ),
                jnp.broadcast_to(function(space)[None], (count,) + space.shape),
            ],
            axis=1,
        )

    return whole(jnp.cos), whole(jnp.sin)


def walk_frames(frames, per_device, parts, segments_ref, live_ref, list_ref, visit):
    def step(source, held):
        for place in range(per_device):
            frame = source * per_device + place
            before = jnp.maximum(frame - 1, 0)
            fresh = (frame == 0) | (segments_ref[frame] != segments_ref[before])
            held = jnp.where(fresh, 0, held)
            list_ref[held] = frame
            if place in parts:
                visit(source, place, frame, held + 1)
            held = held + jnp.where(live_ref[frame] == 1, 1, 0)
        return held

    lax.fori_loop(0, frames // per_device, step, jnp.int32(0))


def attend_kernel(per_device, segments_ref, live_ref, x_ref, mix_ref, wide_ref, lse_ref, kv_ref, list_ref):
    frames = kv_ref.shape[0]

    def turn(source, carry):
        for place in range(per_device):
            both = jnp.concatenate(
                [x_ref[source, place], x_ref[source, per_device + place]], axis=0
            )
            kv_ref[source * per_device + place] = both.astype(F32).T.astype(BF16)
        return carry

    lax.fori_loop(0, frames // per_device, turn, 0)

    def visit(source, place, frame, count):
        query = x_ref[source, 2 * per_device + place]
        query_side = jnp.concatenate([query, jnp.zeros_like(query)], axis=0)

        def scores_of(other):
            return jnp.dot(kv_ref[other], query_side, preferred_element_type=F32)

        def mixed(other, weights):
            value = x_ref[lax.div(other, per_device), per_device + lax.rem(other, per_device)]
            return jnp.dot(value, weights.astype(BF16), preferred_element_type=F32)

        def join(others, carry):
            scores = [scores_of(other) for other in others]
            tops = [jnp.max(score, axis=0, keepdims=True) for score in scores]
            new_top = functools.reduce(jnp.maximum, tops)
            if carry is not None:
                top, total, accum = carry
                new_top = jnp.maximum(top, new_top)
                shrink = jnp.exp(top - new_top)
                total = total * shrink
                accum = accum * shrink
            for index, score in enumerate(scores):
                weights = jnp.exp(score - new_top)
                added = jnp.sum(weights, axis=0, keepdims=True)
                product = mixed(others[index], weights)
                if carry is None and index == 0:
                    total, accum = added, product
                else:
                    total, accum = total + added, accum + product
            return new_top, total, accum

        others = count - 1
        carry = join([frame], None)
        carry = lax.fori_loop(
            0,
            lax.div(others, 2),
            lambda index, state: join([list_ref[2 * index], list_ref[2 * index + 1]], state),
            carry,
        )
        top, total, accum = lax.fori_loop(
            0,
            lax.rem(others, 2),
            lambda unused, state: join([list_ref[others - 1]], state),
            carry,
        )
        result = accum * (1.0 / total)
        wide_ref[source, place] = result
        mix_ref[source, place] = result.astype(BF16)
        lse_ref[pl.ds(frame, 1), :] = top + jnp.log(total)

    walk_frames(frames, per_device, range(per_device), segments_ref, live_ref, list_ref, visit)


def corners(values):
    return [each.reshape(-1, each.shape[-1])[:1, :128] for each in values]


def unread_spec():
    return pl.BlockSpec(memory_space=pl.ANY)


def whole_spec():
    return pl.BlockSpec(memory_space=pltpu.VMEM)


def scalar_spec():
    return pl.BlockSpec(memory_space=pltpu.SMEM)


def attend(per_device, segments, live, x):
    sources = x.shape[0]
    frames = sources * per_device
    pairs = frames * 6
    outs = (
        jax.ShapeDtypeStruct((sources, per_device, HEAD, PATCHES), BF16),
        jax.ShapeDtypeStruct((sources, per_device, HEAD, PATCHES), F32),
        jax.ShapeDtypeStruct((frames, PATCHES), F32),
        jax.ShapeDtypeStruct((frames, PATCHES, 2 * HEAD), BF16),
    )
    return pl.pallas_call(
        functools.partial(attend_kernel, per_device),
        out_shape=outs,
        in_specs=[scalar_spec(), scalar_spec(), whole_spec()],
        out_specs=(whole_spec(),) * len(outs),
        scratch_shapes=[pltpu.SMEM((frames,), jnp.int32)],
        cost_estimate=pl.CostEstimate(
            flops=pairs * 4 * PATCHES * PATCHES * 256,
            bytes_accessed=x.size * 2 * 3,
            transcendentals=pairs * PATCHES * PATCHES,
        ),
        compiler_params=pltpu.CompilerParams(vmem_limit_bytes=40 << 20),
        name="attend",
    )(segments, live, x)


def attend_back_kernel(
    per_device,
    part,
    last,
    segments_ref,
    live_ref,
    x_ref,
    kv_ref,
    wide_ref,
    lse_ref,
    d_mix_ref,
    cos_ref,
    sin_ref,
    *refs
):
    if last:
        before_ref, d_query_ref = refs[:2]
    out_ref, dkv_ref, list_ref = refs[-3:]
    frames = kv_ref.shape[0]

    def clear(frame, carry):
        dkv_ref[frame] = jnp.zeros((PATCHES, 2 * HEAD), F32)
        return carry

    lax.fori_loop(0, frames, clear, 0)

    def unturn(frame, values):
        lower = values[:HALF]
        upper = values[HALF:]
        cosine = cos_ref[frame]
        sine = sin_ref[frame]
        return jnp.concatenate([lower * cosine + upper * sine, upper * cosine - lower * sine], axis=0)

    def visit(source, place, frame, count):
        query = x_ref[source, 2 * per_device + place]
        d_mix = d_mix_ref[source, place]
        blank = jnp.zeros_like(query)
        query_side = jnp.concatenate([query, blank], axis=0)
        d_mix_side = jnp.concatenate([blank, d_mix], axis=0)
        both = jnp.concatenate(
            [query_side.astype(F32).T.astype(BF16), d_mix_side.astype(F32).T.astype(BF16)], axis=0
        )
        lse = lse_ref[pl.ds(frame, 1), :]
        delta = jnp.sum(d_mix.astype(F32) * wide_ref[source, place], axis=0, keepdims=True)

        def block(other):
            key_value = kv_ref[other]
            scores = jnp.dot(key_value, query_side, preferred_element_type=F32)
            d_weights = jnp.dot(key_value, d_mix_side, preferred_element_type=F32)
            weights = jnp.exp(scores - lse)
            d_scores = (weights * (d_weights - delta)).astype(BF16)
            sides = jnp.concatenate([d_scores, weights.astype(BF16)], axis=1)
            dkv_ref[other] += jnp.dot(sides, both, preferred_element_type=F32)
            key = x_ref[lax.div(other, per_device), lax.rem(other, per_device)]
            return jnp.dot(key, d_scores, preferred_element_type=F32)

        d_query = lax.fori_loop(
            0,
            lax.div(count, 2),
            lambda index, state: state
            + block(list_ref[2 * index])
            + block(list_ref[2 * index + 1]),
            jnp.zeros((HEAD, PATCHES), F32),
        )
        d_query = lax.fori_loop(
            0,
            lax.rem(count, 2),
            lambda unused, state: state + block(list_ref[count - 1]),
            d_query,
        )
        d_query = unturn(frame, d_query * (HEAD**-0.5)).astype(BF16)
        if last:
            out_ref[source, 2 * per_device + part] = d_query
        else:
            out_ref[source] = d_query

    walk_frames(frames, per_device, (part,), segments_ref, live_ref, list_ref, visit)

    def finish(source, carry):
        for place in range(per_device):
            frame = source * per_device + place
            both = (dkv_ref[frame] + before_ref[frame]).T
            out_ref[source, place] = unturn(frame, both[:HEAD]).astype(BF16)
            out_ref[source, per_device + place] = both[HEAD:].astype(BF16)
        for place in range(part):
            out_ref[source, 2 * per_device + place] = d_query_ref[source]
        return carry

    if last:
        lax.fori_loop(0, frames // per_device, finish, 0)


def attend_back(
    part, per_device, segments, live, x, kv, wide, lse, d_mix, cosine, sine, before, orders
):
    sources = x.shape[0]
    frames = sources * per_device
    pairs = sources * 6
    last = part == per_device - 1
    args = [segments, live, x, kv, wide, lse, d_mix, cosine, sine]
    dkv = (frames, PATCHES, 2 * HEAD)
    lists = pltpu.SMEM((frames,), jnp.int32)
    if last:
        args += [before[1], before[0]]
        outs = jax.ShapeDtypeStruct(x.shape, BF16)
        out_specs = whole_spec()
        scratch = [pltpu.VMEM(dkv, F32), lists]
    else:
        outs = (
            jax.ShapeDtypeStruct((sources, HEAD, PATCHES), BF16),
            jax.ShapeDtypeStruct(dkv, F32),
        )
        out_specs = (whole_spec(), whole_spec())
        scratch = [lists]
    specs = [scalar_spec(), scalar_spec()] + [whole_spec()] * (len(args) - 2)
    orders = corners(orders)
    return pl.pallas_call(
        functools.partial(attend_back_kernel, per_device, part, last),
        out_shape=outs,
        in_specs=specs + [unread_spec()] * len(orders),
        out_specs=out_specs,
        scratch_shapes=scratch,
        cost_estimate=pl.CostEstimate(
            flops=pairs * 10 * PATCHES * PATCHES * 256,
            bytes_accessed=x.size * 2 * 5,
            transcendentals=pairs * PATCHES * PATCHES,
        ),
        compiler_params=pltpu.CompilerParams(vmem_limit_bytes=60 << 20),
        name="attend_back%d" % part,
    )(*args, *orders)


def exchange(value, axis, bit):
    count = lax.axis_size(axis)
    return lax.ppermute(value, axis, [(source, source ^ bit) for source in range(count)])


def after(value, *earlier):
    return lax.optimization_barrier((value,) + earlier)[0]


def of_packs(value):
    values = [value]
    bit = lax.axis_size("pack") // 2
    while bit:
        values = values + [exchange(each, "pack", bit) for each in values]
        bit //= 2
    return values


def halving_fits():
    return lax.axis_size("pack") == 2 and lax.axis_size("seq") == 16


class RowSum:
    def __init__(self, mine, came, order):
        self.order = list(order)
        self.index = lax.axis_index("seq")
        rows = mine.shape[-2]
        self.tail = (rows // 16, mine.shape[-1])
        self.lead = mine.shape[:-2]
        shape = self.lead + (2, 2, 2, 2) + self.tail
        self.parts = [mine.reshape(shape), came.reshape(shape)]

    def pick(self, bit, which):
        axis = len(self.lead) + {8: 0, 4: 1, 2: 2, 1: 3}[bit]
        pieces = [lax.dynamic_slice_in_dim(part, which, 1, axis) for part in self.parts]
        return (pieces[0].astype(F32) + pieces[1].astype(F32)).astype(BF16)

    def stage(self):
        bit = self.order.pop(0)
        own_bit = lax.rem(lax.div(self.index, bit), 2)
        send = self.pick(bit, 1 - own_bit)
        came = exchange(send, "seq", bit)
        self.parts = [self.pick(bit, own_bit), came]
        return send

    def tie(self, value):
        value, *self.parts = lax.optimization_barrier((value, *self.parts))
        return value

    def finish(self):
        while self.order:
            self.stage()
        own = (self.parts[0].astype(F32) + self.parts[1].astype(F32)).astype(BF16)
        own = own.reshape(self.lead + self.tail)
        return own, exchange(own, "pack", 1)


def settle_kernel(pack_ref, *refs):
    ups, downs, outs, firsts, seconds = [refs[2 * nth : 2 * nth + 2] for nth in range(5)]
    up_ref, down_ref, out_ref, qkv_ref = refs[10:]
    own_first = pack_ref[0] == 0
    small = 128

    def of_pack(pack, pair, *index):
        one, two = pair[0][index].astype(F32), pair[1][index].astype(F32)
        return jnp.where(own_first, one, two) if pack == 0 else jnp.where(own_first, two, one)

    every = slice(None)
    for pack in range(2):
        for group in range(ups[0].shape[1] // small):
            at = (2 * group + pack) * small
            columns = slice(group * small, (group + 1) * small)
            up_ref[:, at : at + small] = of_pack(pack, ups, every, columns)
        rows = downs[0].shape[0]
        down_ref[pack * rows : (pack + 1) * rows, :] = of_pack(pack, downs, every, every)
        columns = outs[0].shape[1]
        out_ref[:, pack * columns : (pack + 1) * columns] = of_pack(pack, outs, every, every)
        for kind in range(3):
            for nth, pair in enumerate((firsts, seconds)):
                columns = pair[0].shape[2]
                at = (4 * kind + 2 * pack + nth) * columns
                qkv_ref[:, at : at + columns] = of_pack(pack, pair, kind, every, every)


def settle(pack, *pairs):
    up, down, out, qkv = pairs[0][0], pairs[1][0], pairs[2][0], pairs[3][0]
    shapes = (
        (up.shape[0], 2 * up.shape[1]),
        (2 * down.shape[0], down.shape[1]),
        (out.shape[0], 2 * out.shape[1]),
        (qkv.shape[1], 12 * qkv.shape[2]),
    )
    args = [each for pair in pairs for each in pair]
    return pl.pallas_call(
        settle_kernel,
        out_shape=tuple(jax.ShapeDtypeStruct(shape, F32) for shape in shapes),
        in_specs=[scalar_spec()] + [whole_spec()] * len(args),
        out_specs=(whole_spec(),) * 4,
        compiler_params=pltpu.CompilerParams(vmem_limit_bytes=32 << 20),
        name="settle",
    )(pack.reshape(1), *args)


def row_sum_direct(term):
    part = lax.psum_scatter(term.astype(BF16), "seq", scatter_dimension=0, tiled=True)
    return lax.psum(part, "pack").astype(F32)


def project_kernel(
    per_device,
    hidden_ref,
    shift_ref,
    scale_ref,
    wq_ref,
    wk_ref,
    wv_ref,
    bq_ref,
    bk_ref,
    bv_ref,
    cos_ref,
    sin_ref,
    in_ref,
    x_ref,
):
    @pl.when(pl.program_id(0) == 0)
    def _():
        for place in range(per_device):
            rows = pl.ds(place * PATCHES, PATCHES)
            values = hidden_ref[rows, :].astype(F32)
            centered = values - jnp.mean(values, axis=-1, keepdims=True)
            spread = jnp.mean(centered * centered, axis=-1, keepdims=True)
            normed = centered * lax.rsqrt(spread + EPSILON)
            scale = scale_ref[pl.ds(place, 1), :]
            in_ref[rows, :] = (normed * (1.0 + scale) + shift_ref[pl.ds(place, 1), :]).astype(BF16)

    rows = in_ref[...]
    group = wq_ref.shape[1] // HEAD

    def turned(values, place):
        lower = values[:HALF]
        upper = values[HALF:]
        cosine = cos_ref[place]
        sine = sin_ref[place]
        return jnp.concatenate([lower * cosine - upper * sine, upper * cosine + lower * sine], axis=0)

    for kind, (weight_ref, bias_ref) in enumerate(
        ((wq_ref, bq_ref), (wk_ref, bk_ref), (wv_ref, bv_ref))
    ):
        flat = jnp.dot(rows, weight_ref[...], preferred_element_type=F32) + bias_ref[...]
        for place in range(per_device):
            block = flat[place * PATCHES : (place + 1) * PATCHES].T
            for head in range(group):
                values = block[head * HEAD : (head + 1) * HEAD]
                if kind == 0:
                    values = turned(values, place) * (HEAD**-0.5)
                    x_ref[head, 2 * per_device + place] = values.astype(BF16)
                elif kind == 1:
                    x_ref[head, place] = turned(values, place).astype(BF16)
                else:
                    x_ref[head, per_device + place] = values.astype(BF16)


def project(per_device, hidden, shift, scale, weight, bias, cosine, sine):
    tokens, width = hidden.shape
    heads = width // HEAD
    group = 2
    lanes = group * HEAD
    steps = heads // group
    bias_row = bias[None, :]

    def whole(shape):
        return pl.BlockSpec(shape, lambda step: (0,) * len(shape))

    def part(kind, rows):
        return pl.BlockSpec((rows, lanes), lambda step: (0, kind * steps + step))

    blocks = (heads, 3 * per_device, HEAD, PATCHES)
    return pl.pallas_call(
        functools.partial(project_kernel, per_device),
        grid=(steps,),
        out_shape=(
            jax.ShapeDtypeStruct((tokens, width), BF16),
            jax.ShapeDtypeStruct(blocks, BF16),
        ),
        in_specs=[whole((tokens, width)), whole(shift.shape), whole(scale.shape)]
        + [part(kind, width) for kind in range(3)]
        + [part(kind, 1) for kind in range(3)]
        + [whole(cosine.shape), whole(sine.shape)],
        out_specs=(
            whole((tokens, width)),
            pl.BlockSpec((group,) + blocks[1:], lambda step: (step, 0, 0, 0)),
        ),
        cost_estimate=pl.CostEstimate(
            flops=2 * tokens * width * 3 * width,
            bytes_accessed=2 * (weight.size + 5 * tokens * width),
            transcendentals=0,
        ),
        compiler_params=pltpu.CompilerParams(vmem_limit_bytes=40 << 20),
        name="project",
    )(hidden, shift, scale, weight, weight, weight, bias_row, bias_row, bias_row, cosine, sine)


GELU_SLOPE = 0.7978845608028654
GELU_CUBE = 0.044715


def feed_kernel(
    carried,
    which_ref,
    in_ref,
    d_out_ref,
    up_a_ref,
    up_b_ref,
    bias_a_ref,
    bias_b_ref,
    down_a_ref,
    down_b_ref,
    *refs
):
    if carried:
        out_before_ref, d_in_before_ref = refs[:2]
        refs = refs[2:]
    out_ref, d_in_ref, d_up_ref, d_down_ref, d_bias_ref, turned_ref = refs

    @pl.when(pl.program_id(0) == 0)
    def _():
        turned_ref[...] = in_ref[...].astype(F32).T.astype(BF16)
        if carried:
            out_ref[...] = out_before_ref[...]
            d_in_ref[...] = d_in_before_ref[...]
        else:
            out_ref[...] = jnp.zeros_like(out_ref)
            d_in_ref[...] = jnp.zeros_like(d_in_ref)

    up = jnp.concatenate([up_a_ref[...], up_b_ref[...]], axis=1)
    down = jnp.concatenate([down_a_ref[...], down_b_ref[...]], axis=0)
    bias = jnp.concatenate([bias_a_ref[...], bias_b_ref[...]], axis=1)
    d_out = d_out_ref[...]
    pre = jnp.dot(in_ref[...], up, preferred_element_type=F32) + bias
    d_act = dot_over(d_out, down, 1, 1)
    square = pre * pre
    bend = jnp.tanh(GELU_SLOPE * pre * (1.0 + GELU_CUBE * square))
    half = 0.5 * (1.0 + bend)
    act = (pre * half).astype(BF16)
    slope = half + (0.5 * GELU_SLOPE) * pre * (1.0 - bend * bend) * (
        1.0 + (3.0 * GELU_CUBE) * square
    )
    d_pre = (d_act * slope).astype(BF16)
    out_ref[...] += jnp.dot(act, down, preferred_element_type=F32)
    d_in_ref[...] += dot_over(d_pre, up, 1, 1)
    d_up_ref[...] = jnp.dot(turned_ref[...], d_pre, preferred_element_type=F32).astype(BF16)
    d_down_ref[...] = jnp.dot(
        act.astype(F32).T.astype(BF16), d_out, preferred_element_type=F32
    ).astype(BF16)
    d_bias_ref[...] = jnp.sum(d_pre.astype(F32), axis=0, keepdims=True)


def feed(which, feed_in, d_feed_out, up_weight, up_bias, down_weight, before):
    tokens, width = feed_in.shape
    hidden_units = up_weight.shape[1]
    small = 128
    steps = hidden_units // (4 * small)
    own = hidden_units // 2

    def whole(shape):
        return pl.BlockSpec(shape, lambda step, which: (0,) * len(shape))

    def group(nth):
        return lambda step, which: 2 * (2 * step + nth) + which[0]

    def columns(nth, rows):
        return pl.BlockSpec((rows, small), lambda step, which: (0, group(nth)(step, which)))

    def rows_of(nth):
        return pl.BlockSpec((small, width), lambda step, which: (group(nth)(step, which), 0))

    args = [feed_in, d_feed_out, up_weight, up_weight, up_bias[None], up_bias[None]]
    args += [down_weight, down_weight]
    specs = [whole((tokens, width)), whole((tokens, width)), columns(0, width), columns(1, width)]
    specs += [columns(0, 1), columns(1, 1), rows_of(0), rows_of(1)]
    if before is not None:
        args += list(before)
        specs += [whole((tokens, width)), whole((tokens, width))]
    return pl.pallas_call(
        functools.partial(feed_kernel, before is not None),
        grid_spec=pltpu.PrefetchScalarGridSpec(
            num_scalar_prefetch=1,
            grid=(steps,),
            in_specs=specs,
            out_specs=(
                whole((tokens, width)),
                whole((tokens, width)),
                pl.BlockSpec((width, 2 * small), lambda step, which: (0, step)),
                pl.BlockSpec((2 * small, width), lambda step, which: (step, 0)),
                pl.BlockSpec((1, 2 * small), lambda step, which: (0, step)),
            ),
            scratch_shapes=[pltpu.VMEM((width, tokens), BF16)],
        ),
        out_shape=(
            jax.ShapeDtypeStruct((tokens, width), F32),
            jax.ShapeDtypeStruct((tokens, width), F32),
            jax.ShapeDtypeStruct((width, own), BF16),
            jax.ShapeDtypeStruct((own, width), BF16),
            jax.ShapeDtypeStruct((1, own), F32),
        ),
        cost_estimate=pl.CostEstimate(
            flops=12 * tokens * width * own,
            bytes_accessed=2 * (4 * own * width + 8 * tokens * width),
            transcendentals=tokens * own,
        ),
        compiler_params=pltpu.CompilerParams(vmem_limit_bytes=56 << 20),
        name="feed%d" % (before is not None),
    )(which.reshape(1), *args)


def norm_back(values, d_in, scale):
    centered = values - jnp.mean(values, axis=-1, keepdims=True)
    spread = jnp.mean(centered * centered, axis=-1, keepdims=True)
    inverse = lax.rsqrt(spread + EPSILON)
    normed = centered * inverse
    product = d_in * normed
    d_shift = jnp.sum(d_in, axis=0, keepdims=True)
    d_scale = jnp.sum(product, axis=0, keepdims=True)
    scaled = 1.0 + scale
    mean_d = jnp.mean(d_in * scaled, axis=-1, keepdims=True)
    mean_p = jnp.mean(product * scaled, axis=-1, keepdims=True)
    return (d_in * scaled - mean_d - normed * mean_p) * inverse, d_shift, d_scale


def middle_back_kernel(
    d_in_ref,
    middle_ref,
    grad_ref,
    attn_ref,
    feed_ref,
    scale_ref,
    gate_ref,
    feed_gate_ref,
    down_bias_ref,
    rows_ref,
    weight_ref,
    d_middle_ref,
    d_attn_ref,
    layer_ref,
    blocks_ref,
    sums_ref,
):
    frame = pl.program_id(0)
    per_device = pl.num_programs(0) - 1

    @pl.when(frame < per_device)
    def _():
        mine = pl.ds(frame, 1)
        middle = middle_ref[...]
        grads = grad_ref[...].astype(F32)
        back, d_shift, d_scale = norm_back(middle, d_in_ref[...], scale_ref[mine, :])
        d_middle = grads + back
        d_middle_ref[...] = d_middle
        d_attn = (d_middle * gate_ref[mine, :]).astype(BF16)
        d_attn_ref[...] = d_attn
        feed_rows = feed_ref[...] + down_bias_ref[...]
        feed_gate = feed_gate_ref[mine, :]
        layer_ref[...] = (middle + feed_gate * feed_rows).astype(BF16)
        d_feed_out = (feed_gate * grads).astype(BF16).astype(F32)
        sums_ref[frame] = jnp.concatenate(
            [
                jnp.sum(d_middle * attn_ref[...], axis=0, keepdims=True),
                d_shift,
                d_scale,
                jnp.sum(grads * feed_rows, axis=0, keepdims=True),
                jnp.sum(d_attn.astype(F32), axis=0, keepdims=True),
                jnp.sum(d_feed_out, axis=0, keepdims=True),
                jnp.zeros((2, d_shift.shape[1]), F32),
            ],
            axis=0,
        )
        d_mix = dot_over(weight_ref[...], d_attn, 1, 1).astype(BF16)
        for head in range(blocks_ref.shape[0]):
            blocks_ref[head, 0] = d_mix[head * HEAD : (head + 1) * HEAD]

    @pl.when(frame == per_device)
    def _():
        first = sums_ref[0]
        second = sums_ref[1]
        rows = jnp.concatenate(
            [first[:4], second[:4], first[4:6] + second[4:6], rows_ref[...]], axis=0
        ).astype(BF16)
        count = rows.shape[1] // PATCHES
        block = jnp.concatenate(
            [rows[:, nth * PATCHES : (nth + 1) * PATCHES] for nth in range(count)], axis=0
        )
        for head in range(blocks_ref.shape[0]):
            blocks_ref[head, 0] = block


def middle_back(
    per_device, d_in, middle, grads, attn_rows, feed_rows, scale, gate, feed_gate, down_bias, rows, weight
):
    tokens, width = d_in.shape
    heads = width // HEAD
    last = per_device - 1
    per_frame = pl.BlockSpec((PATCHES, width), lambda frame: (jnp.minimum(frame, last), 0))

    def whole(shape):
        return pl.BlockSpec(shape, lambda frame: (0,) * len(shape))

    small = whole((per_device, width))
    return pl.pallas_call(
        middle_back_kernel,
        grid=(per_device + 1,),
        out_shape=(
            jax.ShapeDtypeStruct((tokens, width), F32),
            jax.ShapeDtypeStruct((tokens, width), BF16),
            jax.ShapeDtypeStruct((tokens, width), BF16),
            jax.ShapeDtypeStruct((heads, per_device + 1, HEAD, PATCHES), BF16),
        ),
        in_specs=[per_frame] * 5
        + [small] * 3
        + [whole((1, width)), whole(rows.shape), whole(weight.shape)],
        out_specs=(
            per_frame,
            per_frame,
            per_frame,
            pl.BlockSpec((heads, 1, HEAD, PATCHES), lambda frame: (0, frame, 0, 0)),
        ),
        scratch_shapes=[pltpu.VMEM((per_device, 8, width), F32)],
        cost_estimate=pl.CostEstimate(
            flops=2 * tokens * width * width, bytes_accessed=24 * tokens * width, transcendentals=0
        ),
        compiler_params=pltpu.CompilerParams(vmem_limit_bytes=48 << 20),
        name="middle_back",
    )(
        d_in,
        middle,
        grads,
        attn_rows,
        feed_rows,
        scale,
        gate,
        feed_gate,
        down_bias[None],
        rows,
        weight,
    )


def unproject_kernel(
    per_device, carried, which_ref, in_ref, back_ref, wq_ref, wk_ref, wv_ref, *refs
):
    if not carried:
        refs = refs[-4:]
    if carried:
        before_ref, hidden_ref, d_middle_ref, scale_ref, bias_theirs_ref = refs[:5]
        d_weight_ref, grad_ref, rows_ref, d_in_ref, d_bias_ref, turned_ref = refs[5:]
    else:
        d_in_ref, d_weight_ref, d_bias_ref, turned_ref = refs

    @pl.when(pl.program_id(0) == 0)
    def _():
        turned_ref[...] = in_ref[...].astype(F32).T.astype(BF16)
        if carried:
            d_in_ref[...] = before_ref[...]
        else:
            d_in_ref[...] = jnp.zeros_like(d_in_ref)

    group = wq_ref.shape[1] // HEAD

    def token_major(block_of):
        rows = []
        for place in range(per_device):
            block = jnp.concatenate([block_of(head, place) for head in range(group)], axis=0)
            rows.append(block.astype(F32).T.astype(BF16))
        return jnp.concatenate(rows, axis=0)

    sides = jnp.concatenate(
        [
            token_major(lambda head, place: back_ref[head, 2 * per_device + place]),
            token_major(lambda head, place: back_ref[head, place]),
            token_major(lambda head, place: back_ref[head, per_device + place]),
        ],
        axis=1,
    )
    weights = jnp.concatenate([wq_ref[...], wk_ref[...], wv_ref[...]], axis=1)
    d_in_ref[...] += dot_over(sides, weights, 1, 1)
    d_weight = jnp.dot(turned_ref[...], sides, preferred_element_type=F32).astype(BF16)
    d_bias = jnp.sum(sides.astype(F32), axis=0, keepdims=True)
    lanes = group * HEAD
    for kind in range(3):
        d_weight_ref[kind] = d_weight[:, kind * lanes : (kind + 1) * lanes]
        part = d_bias[:, kind * lanes : (kind + 1) * lanes]
        if carried:
            start = pl.multiple_of(pl.program_id(0) * lanes, lanes)
            d_bias_ref[pl.ds(kind, 1), pl.ds(start, lanes)] = part
        else:
            d_bias_ref[kind] = part

    if carried:

        @pl.when(pl.program_id(0) == pl.num_programs(0) - 1)
        def _():
            sums = []
            for place in range(per_device):
                rows = pl.ds(place * PATCHES, PATCHES)
                mine = pl.ds(place, 1)
                back, d_shift, d_scale = norm_back(
                    hidden_ref[rows, :].astype(F32), d_in_ref[rows, :], scale_ref[mine, :]
                )
                grad_ref[rows, :] = (d_middle_ref[rows, :] + back).astype(BF16)
                sums += [d_shift, d_scale]
            for kind in range(3):
                sums.append(
                    jnp.concatenate([d_bias_ref[pl.ds(kind, 1), :], bias_theirs_ref[kind]], axis=1)
                )
            count = 16 - len(sums)
            late = jnp.concatenate(
                sums + [jnp.zeros((count, d_in_ref.shape[1]), F32)], axis=0
            ).astype(BF16)
            for target in range(rows_ref.shape[0]):
                rows_ref[target] = late


def unproject(per_device, targets, which, attn_in, back, weight, orders, before=None, norm_args=()):
    tokens, width = attn_in.shape
    heads = width // HEAD
    group = 2
    lanes = group * HEAD
    groups = heads // group
    steps = groups // 2

    def whole(shape):
        return pl.BlockSpec(shape, lambda step, which: (0,) * len(shape))

    def blocks(array):
        return pl.BlockSpec(
            (group,) + array.shape[1:], lambda step, which: (which[0] * steps + step, 0, 0, 0)
        )

    def part(kind):
        return pl.BlockSpec(
            (width, lanes), lambda step, which: (0, kind * groups + which[0] * steps + step)
        )

    args = [attn_in, back, weight, weight, weight]
    specs = [whole((tokens, width)), blocks(back), part(0), part(1), part(2)]
    weight_shape = (
        jax.ShapeDtypeStruct((3, width, width // 2), BF16),
        jax.ShapeDtypeStruct((3, 1, width // 2), F32),
    )
    weight_specs = (
        pl.BlockSpec((3, width, lanes), lambda step, which: (0, 0, step)),
        pl.BlockSpec((3, 1, lanes), lambda step, which: (0, 0, step)),
    )
    scratch = [pltpu.VMEM((width, tokens), BF16)]
    small = (per_device, width)
    if before is not None:
        args += [before] + list(norm_args)
        specs += [whole((tokens, width))] * 3 + [whole(small), whole((3, 1, width // 2))]
        late = (targets, 16, width)
        outs = weight_shape[:1] + (
            jax.ShapeDtypeStruct((tokens, width), BF16),
            jax.ShapeDtypeStruct(late, BF16),
        )
        out_specs = weight_specs[:1] + (whole((tokens, width)), whole(late))
        scratch = [pltpu.VMEM((tokens, width), F32), pltpu.VMEM((3, width // 2), F32)] + scratch
    else:
        outs = (jax.ShapeDtypeStruct((tokens, width), F32),) + weight_shape
        out_specs = (whole((tokens, width)),) + weight_specs
        orders = corners(orders)
        args += orders
        specs += [unread_spec()] * len(orders)
    return pl.pallas_call(
        functools.partial(unproject_kernel, per_device, before is not None),
        grid_spec=pltpu.PrefetchScalarGridSpec(
            num_scalar_prefetch=1,
            grid=(steps,),
            in_specs=specs,
            out_specs=out_specs,
            scratch_shapes=scratch,
        ),
        out_shape=outs,
        cost_estimate=pl.CostEstimate(
            flops=6 * tokens * width * width,
            bytes_accessed=2 * (3 * width * width + 6 * tokens * width),
            transcendentals=0,
        ),
        compiler_params=pltpu.CompilerParams(vmem_limit_bytes=48 << 20),
        name="unproject%d" % (before is not None),
    )(which.reshape(1), *args)


def columns_of(matrix, start, width, axis=1):
    if isinstance(start, int) and start == 0 and width == matrix.shape[axis]:
        return matrix
    return lax.dynamic_slice_in_dim(matrix, start, width, axis)


def local(
    hidden,
    cotangent,
    levels,
    segments,
    live_frames,
    noise_table,
    mod_weight,
    mod_bias,
    qkv_weight,
    qkv_bias,
    out_weight,
    out_bias,
    up_weight,
    up_bias,
    down_weight,
    down_bias,
):
    seq_index = lax.axis_index("seq")
    seq_count = lax.axis_size("seq")
    tokens = hidden.shape[1]
    width = hidden.shape[2]
    per_device = tokens // PATCHES
    frames = segments.shape[1]
    heads = width // HEAD
    copies = seq_count // heads
    hidden_units = up_weight.shape[1]
    level_count = noise_table.shape[0]
    share = width // seq_count
    clip_ids = segments[0]
    live = live_frames[0]

    pack = lax.axis_index("pack")
    halves = halving_fits()
    frame_ids = jnp.arange(frames, dtype=jnp.int32)
    same_clip = clip_ids[:, None] == clip_ids[None, :]
    clip_starts = jnp.min(jnp.where(same_clip, frame_ids[None, :], frames), axis=1)
    frame_times = (frame_ids - clip_starts).astype(F32)
    own_cos, own_sin = rotary_tables(
        lax.dynamic_slice_in_dim(frame_times, seq_index * per_device, per_device)
    )

    embed = jnp.concatenate(
        [
            lax.dynamic_slice_in_dim(noise_table, levels[0, frame], 1, 0)
            for frame in range(per_device)
        ],
        axis=0,
    )
    cond = jax.nn.silu(embed).astype(BF16)
    modulation = jnp.dot(cond, mod_weight[:, : 2 * width], preferred_element_type=F32)
    attn_shift, attn_scale = jnp.split(modulation + mod_bias[: 2 * width], 2, axis=1)
    attn_in, sent = project(
        per_device, hidden[0], attn_shift, attn_scale, qkv_weight, qkv_bias, own_cos, own_sin
    )

    def to_heads(array):
        if copies > 1:
            array = jnp.concatenate([array] * copies, axis=0)
        return lax.all_to_all(array, "seq", 0, 0, tiled=True)

    def to_tokens(array):
        return lax.all_to_all(array, "seq", 0, 0, tiled=True)[:heads]

    x = to_heads(sent)
    late_modulation = jnp.dot(
        after(cond, attn_in), mod_weight[:, 2 * width :], preferred_element_type=F32
    )
    attn_gate, feed_shift, feed_scale, feed_gate = jnp.split(
        late_modulation + mod_bias[2 * width :], 4, axis=1
    )
    cos_all, sin_all = rotary_tables(after(frame_times, attn_in))
    grad_rows = cotangent[0].astype(F32).reshape(per_device, PATCHES, width)
    d_feed_out = (feed_gate[:, None, :] * grad_rows).reshape(tokens, width).astype(BF16)
    x, d_feed_out, cos_all, sin_all = lax.optimization_barrier((x, d_feed_out, cos_all, sin_all))
    mix, wide, lse, kv = attend(per_device, clip_ids, live, x)
    mix = to_tokens(mix)
    mixes = [mix[:, place].reshape(width, PATCHES) for place in range(per_device)]
    attn_rows = jnp.stack([dot_over(each, out_weight, 0, 0) for each in mixes]) + out_bias
    attn_mix = jnp.concatenate(mixes, axis=1)

    frame_rows = hidden[0].astype(F32).reshape(per_device, PATCHES, width)
    middle = frame_rows + attn_gate[:, None, :] * attn_rows
    feed_in = modulate_norm(middle, feed_shift, feed_scale).reshape(tokens, width).astype(BF16)
    feed_args = (feed_in, d_feed_out, up_weight, up_bias, down_weight)
    theirs = feed(1 - pack if halves else pack * 0 + 1, *feed_args, None)
    mine = feed(pack if halves else pack * 0, *feed_args, theirs[:2])
    small = 128

    def in_order(own, other):
        if halves:
            even, odd = jnp.where(pack == 0, own, other), jnp.where(pack == 0, other, own)
        else:
            even, odd = own, other
        rows = own.shape[0]
        return jnp.stack(
            [even.reshape(rows, -1, small), odd.reshape(rows, -1, small)], axis=2
        ).reshape(rows, -1)

    own_levels = levels[0]
    level_row = jnp.concatenate(
        [
            jnp.broadcast_to(part[frame], (width // (2 * per_device),))
            for frame in range(per_device)
            for part in (lax.div(own_levels, 32), lax.rem(own_levels, 32))
        ]
    ).astype(F32)[None]
    extra_rows = jnp.concatenate(
        [
            in_order(mine[4], theirs[4]).reshape(-1, width),
            level_row,
            jnp.zeros((1, width), F32),
        ],
        axis=0,
    )
    d_middle, d_attn_out, layer_out, blocks = middle_back(
        per_device,
        mine[1],
        middle.reshape(tokens, width),
        cotangent[0],
        attn_rows.reshape(tokens, width),
        mine[0],
        feed_scale,
        attn_gate,
        feed_gate,
        down_bias,
        extra_rows,
        out_weight,
    )
    layer_out = layer_out.reshape(1, tokens, width)
    d_mix = to_heads(blocks)

    def out_term(start, size):
        return dot_over(attn_mix, columns_of(d_attn_out, start, size), 1, 0).astype(BF16)

    sums = ()
    if halves:
        up_sum = RowSum(mine[2], exchange(theirs[2], "pack", 1), (2, 1, 4, 8))
        down_sum = RowSum(mine[3], exchange(theirs[3], "pack", 1), (1, 2, 4, 8))
        out_theirs = exchange(out_term((1 - pack) * (width // 2), width // 2), "pack", 1)
        out_sum = RowSum(out_term(pack * (width // 2), width // 2), out_theirs, (1, 2, 4, 8))
        sums = (down_sum, up_sum)
    def own_share(row):
        piece = row.shape[0] // seq_count
        return lax.dynamic_slice_in_dim(row, seq_index * piece, piece)

    chunks = width // PATCHES
    early_rows = d_mix[:, per_device].reshape(seq_count, chunks, 16, PATCHES)
    early_rows = early_rows.transpose(0, 2, 1, 3).reshape(seq_count, 16, width)
    early_sets = of_packs(early_rows)
    early_sum = functools.reduce(
        jnp.add, [jnp.sum(each.astype(F32), axis=0) for each in early_sets]
    )
    out_bias_grad = own_share(early_sum[8])
    down_bias_grad = own_share(early_sum[9])
    up_bias_grad = own_share(early_sum[10:14].reshape(hidden_units))

    def frames_of(rows, per_frame, kinds):
        return jnp.concatenate(
            [
                jnp.stack(
                    [rows[:, frame * per_frame + kind] for frame in range(per_device)], axis=1
                ).reshape(-1, width)
                for kind in range(kinds)
            ],
            axis=1,
        )

    own_table = lax.dynamic_slice_in_dim(noise_table, seq_index * share, share, 1)
    own_mod = lax.dynamic_slice_in_dim(mod_weight, seq_index * share, share, 0)
    stride = width // (2 * per_device)
    parts = []
    for rows in early_sets:
        coded = rows[:, 14, ::stride].astype(jnp.int32).reshape(-1, 2)
        set_levels = coded[:, 0] * 32 + coded[:, 1]
        picks = (set_levels[:, None] == jnp.arange(level_count, dtype=jnp.int32)[None, :]).astype(F32)
        embeds = jnp.dot(picks, own_table, precision=PRECISE, preferred_element_type=F32)
        set_cond = jax.nn.silu(embeds).astype(BF16)
        d_mod = frames_of(rows, 4, 4)
        parts.append(
            (
                picks,
                embeds,
                set_cond,
                dot_over(d_mod, own_mod[:, 2 * width :], 1, 1),
                dot_over(set_cond, d_mod, 0, 0),
            )
        )
    mod_grad_early = functools.reduce(jnp.add, [each[4] for each in parts])
    mod_sum_early = (early_sum[:4] + early_sum[4:8]).reshape(4 * width)
    before = None
    for part in range(per_device):
        orders = [each.stage() for each in sums]
        if halves and part:
            before = (out_sum.tie(before[0]), before[1])
            orders.append(out_sum.stage())
        before = attend_back(
            part,
            per_device,
            clip_ids,
            live,
            x,
            kv,
            wide,
            lse,
            d_mix,
            cos_all,
            sin_all,
            before,
            orders,
        )
    back = to_tokens(before)
    orders = [each.stage() for each in sums]
    if halves:
        orders.append(out_sum.stage())
        orders.append(out_sum.stage())
    orders += [mod_grad_early] + [part[3] for part in parts]
    which = (1 - pack, pack) if halves else (pack * 0, pack * 0 + 1)
    d_in_theirs, qkv_theirs, bias_theirs = unproject(
        per_device, seq_count, which[0], attn_in, back, qkv_weight, orders
    )
    qkv_mine, hidden_grad, late = unproject(
        per_device,
        seq_count,
        which[1],
        attn_in,
        back,
        qkv_weight,
        (),
        d_in_theirs,
        (hidden[0], d_middle, attn_scale, bias_theirs),
    )
    hidden_grad = hidden_grad.reshape(1, tokens, width)
    if halves:
        for each in (up_sum, down_sum, out_sum):
            late = each.tie(late)
    late_rows = lax.all_to_all(late, "seq", 0, 0, tiled=True)

    def halves_in_order(own, other):
        if halves:
            return jnp.where(pack == 0, own, other), jnp.where(pack == 0, other, own)
        return other, own

    if halves:
        came = exchange(qkv_theirs, "pack", 1)
        split = width // 4
        qkv_sums = [
            RowSum(qkv_mine[..., :split], came[..., :split], (1, 2, 4, 8)),
            RowSum(qkv_mine[..., split:], came[..., split:], (2, 1, 4, 8)),
        ]
        up_weight_grad, down_weight_grad, out_weight_grad, qkv_weight_grad = settle(
            pack, *[each.finish() for each in (up_sum, down_sum, out_sum, *qkv_sums)]
        )
    else:
        up_weight_grad = row_sum_direct(in_order(mine[2], theirs[2]))
        pairs = [each[3].reshape(-1, small, width) for each in (mine, theirs)]
        down_weight_grad = row_sum_direct(jnp.stack(pairs, axis=1).reshape(hidden_units, width))
        out_weight_grad = row_sum_direct(out_term(0, width))
        qkv_term = jnp.concatenate(halves_in_order(qkv_mine, qkv_theirs), axis=-1)
        qkv_weight_grad = row_sum_direct(qkv_term.transpose(1, 0, 2).reshape(width, 3 * width))

    late_sets = of_packs(late_rows[:, :8])
    bias_at = 2 * per_device
    bias_sums = [
        jnp.sum(rows[:, bias_at : bias_at + 3].astype(F32), axis=0) for rows in late_sets
    ]
    if halves:
        ones, twos = bias_sums
        half = width // 2
        own_half = ones[:, :half] + twos[:, half:]
        other_half = ones[:, half:] + twos[:, :half]
    else:
        total = functools.reduce(jnp.add, bias_sums)
        own_half, other_half = total[:, : width // 2], total[:, width // 2 :]
    bias_total = jnp.concatenate(halves_in_order(own_half, other_half), axis=1)
    qkv_bias_grad = own_share(bias_total.reshape(3 * width))
    late_mods = [frames_of(rows, 2, 2) for rows in late_sets]
    mod_sum_late = functools.reduce(
        jnp.add, [jnp.sum(each.astype(F32), axis=0) for each in late_mods]
    )
    d_embeds = []
    for part, d_mod in zip(parts, late_mods):
        d_cond = part[3] + dot_over(d_mod, own_mod[:, : 2 * width], 1, 1)
        d_embeds.append(jax.vjp(jax.nn.silu, part[1])[1](d_cond)[0])
    table_grad = lax.dot_general(
        jnp.concatenate([part[0] for part in parts], axis=0),
        jnp.concatenate(d_embeds, axis=0),
        (((0,), (0,)), ((), ())),
        precision=PRECISE,
        preferred_element_type=F32,
    )
    mod_grad_late = functools.reduce(
        jnp.add, [dot_over(part[2], d_mod, 0, 0) for part, d_mod in zip(parts, late_mods)]
    )
    mod_weight_grad = jnp.concatenate([mod_grad_late, mod_grad_early], axis=1)
    mod_bias_grad = own_share(jnp.concatenate([mod_sum_late, mod_sum_early]))
    return (
        layer_out,
        hidden_grad,
        table_grad,
        mod_weight_grad,
        mod_bias_grad,
        qkv_weight_grad,
        qkv_bias_grad,
        out_weight_grad,
        out_bias_grad,
        up_weight_grad,
        up_bias_grad,
        down_weight_grad,
        down_bias_grad,
    )


def solution(mesh):
    in_specs = (
        P("pack", "seq", None),
        P("pack", "seq", None),
        P("pack", "seq"),
        P("pack", None),
        P("pack", None),
    ) + (P(),) * 11
    out_specs = (
        P("pack", "seq", None),
        P("pack", "seq", None),
        P(None, "seq"),
        P("seq", None),
        P("seq"),
        P("seq", None),
        P("seq"),
        P("seq", None),
        P("seq"),
        P("seq", None),
        P("seq"),
        P("seq", None),
        P("seq"),
    )
    return jax.shard_map(local, mesh=mesh, in_specs=in_specs, out_specs=out_specs, check_vma=False)
```

```python
import functools

import jax
import jax.numpy as jnp
from jax import lax
from jax.experimental import pallas as pl
from jax.experimental.pallas import tpu as pltpu
from jax.sharding import PartitionSpec as P

HEAD = 64
PATCHES = 256
SIDE = 16
EPSILON = 1e-06
PRECISE = lax.Precision.HIGHEST
HALF = HEAD // 2
F32 = jnp.float32
BF16 = jnp.bfloat16


def modulate_norm(rows, shift, scale):
    center = jnp.mean(rows, axis=-1, keepdims=True)
    centered = rows - center
    spread = jnp.mean(centered * centered, axis=-1, keepdims=True)
    normed = centered * lax.rsqrt(spread + EPSILON)
    return normed * (1.0 + scale[:, None, :]) + shift[:, None, :]


def gelu_tanh(values):
    return jax.nn.gelu(values, approximate=True)


def dot_over(first, second, first_dim, second_dim):
    return lax.dot_general(
        first, second, (((first_dim,), (second_dim,)), ((), ())), preferred_element_type=F32
    )


def spatial_angles():
    time_pairs = HALF // 4
    space_pairs = (HALF - time_pairs) // 2
    patch = jnp.arange(PATCHES, dtype=jnp.int32)
    row_pos = (patch // SIDE).astype(F32)
    col_pos = (patch % SIDE).astype(F32)
    time_freq = 10000.0 ** (-jnp.arange(time_pairs, dtype=F32) / time_pairs)
    space_freq = 10000.0 ** (-jnp.arange(space_pairs, dtype=F32) / space_pairs)
    space = jnp.concatenate(
        [space_freq[:, None] * row_pos[None, :], space_freq[:, None] * col_pos[None, :]], axis=0
    )
    return time_freq, space


def rotary_tables(time_frames):
    time_freq, space = spatial_angles()
    count = time_frames.shape[0]
    time_angle = time_frames[:, None] * time_freq[None, :]

    def whole(function):
        return jnp.concatenate(
            [
                jnp.broadcast_to(
                    function(time_angle)[:, :, None], (count, time_freq.shape[0], PATCHES)
                ),
                jnp.broadcast_to(function(space)[None], (count,) + space.shape),
            ],
            axis=1,
        )

    return whole(jnp.cos), whole(jnp.sin)


def walk_frames(frames, per_device, parts, segments_ref, live_ref, list_ref, visit):
    def step(source, held):
        for place in range(per_device):
            frame = source * per_device + place
            before = jnp.maximum(frame - 1, 0)
            fresh = (frame == 0) | (segments_ref[frame] != segments_ref[before])
            held = jnp.where(fresh, 0, held)
            list_ref[held] = frame
            if place in parts:
                visit(source, place, frame, held + 1)
            held = held + jnp.where(live_ref[frame] == 1, 1, 0)
        return held

    lax.fori_loop(0, frames // per_device, step, jnp.int32(0))


def attend_kernel(per_device, segments_ref, live_ref, x_ref, mix_ref, wide_ref, lse_ref, kv_ref, list_ref):
    frames = kv_ref.shape[0]

    def turn(source, carry):
        for place in range(per_device):
            both = jnp.concatenate(
                [x_ref[source, place], x_ref[source, per_device + place]], axis=0
            )
            kv_ref[source * per_device + place] = both.astype(F32).T.astype(BF16)
        return carry

    lax.fori_loop(0, frames // per_device, turn, 0)

    def visit(source, place, frame, count):
        query = x_ref[source, 2 * per_device + place]
        query_side = jnp.concatenate([query, jnp.zeros_like(query)], axis=0)

        def scores_of(other):
            return jnp.dot(kv_ref[other], query_side, preferred_element_type=F32)

        def mixed(other, weights):
            value = x_ref[lax.div(other, per_device), per_device + lax.rem(other, per_device)]
            return jnp.dot(value, weights.astype(BF16), preferred_element_type=F32)

        def join(others, carry):
            scores = [scores_of(other) for other in others]
            tops = [jnp.max(score, axis=0, keepdims=True) for score in scores]
            new_top = functools.reduce(jnp.maximum, tops)
            if carry is not None:
                top, total, accum = carry
                new_top = jnp.maximum(top, new_top)
                shrink = jnp.exp(top - new_top)
                total = total * shrink
                accum = accum * shrink
            for index, score in enumerate(scores):
                weights = jnp.exp(score - new_top)
                added = jnp.sum(weights, axis=0, keepdims=True)
                product = mixed(others[index], weights)
                if carry is None and index == 0:
                    total, accum = added, product
                else:
                    total, accum = total + added, accum + product
            return new_top, total, accum

        others = count - 1
        carry = join([frame], None)
        carry = lax.fori_loop(
            0,
            lax.div(others, 2),
            lambda index, state: join([list_ref[2 * index], list_ref[2 * index + 1]], state),
            carry,
        )
        top, total, accum = lax.fori_loop(
            0,
            lax.rem(others, 2),
            lambda unused, state: join([list_ref[others - 1]], state),
            carry,
        )
        result = accum * (1.0 / total)
        wide_ref[source, place] = result
        mix_ref[source, place] = result.astype(BF16)
        lse_ref[pl.ds(frame, 1), :] = top + jnp.log(total)

    walk_frames(frames, per_device, range(per_device), segments_ref, live_ref, list_ref, visit)


def corners(values):
    return [each.reshape(-1, each.shape[-1])[:1, :128] for each in values]


def unread_spec():
    return pl.BlockSpec(memory_space=pl.ANY)


def whole_spec():
    return pl.BlockSpec(memory_space=pltpu.VMEM)


def scalar_spec():
    return pl.BlockSpec(memory_space=pltpu.SMEM)


def attend(per_device, segments, live, x):
    sources = x.shape[0]
    frames = sources * per_device
    pairs = frames * 6
    outs = (
        jax.ShapeDtypeStruct((sources, per_device, HEAD, PATCHES), BF16),
        jax.ShapeDtypeStruct((sources, per_device, HEAD, PATCHES), F32),
        jax.ShapeDtypeStruct((frames, PATCHES), F32),
        jax.ShapeDtypeStruct((frames, PATCHES, 2 * HEAD), BF16),
    )
    return pl.pallas_call(
        functools.partial(attend_kernel, per_device),
        out_shape=outs,
        in_specs=[scalar_spec(), scalar_spec(), whole_spec()],
        out_specs=(whole_spec(),) * len(outs),
        scratch_shapes=[pltpu.SMEM((frames,), jnp.int32)],
        cost_estimate=pl.CostEstimate(
            flops=pairs * 4 * PATCHES * PATCHES * 256,
            bytes_accessed=x.size * 2 * 3,
            transcendentals=pairs * PATCHES * PATCHES,
        ),
        compiler_params=pltpu.CompilerParams(vmem_limit_bytes=40 << 20),
        name="attend",
    )(segments, live, x)


def attend_back_kernel(
    per_device,
    part,
    last,
    segments_ref,
    live_ref,
    x_ref,
    kv_ref,
    wide_ref,
    lse_ref,
    d_mix_ref,
    cos_ref,
    sin_ref,
    *refs
):
    if last:
        before_ref, d_query_ref = refs[:2]
    out_ref, dkv_ref, list_ref = refs[-3:]
    frames = kv_ref.shape[0]

    def clear(frame, carry):
        dkv_ref[frame] = jnp.zeros((PATCHES, 2 * HEAD), F32)
        return carry

    lax.fori_loop(0, frames, clear, 0)

    def unturn(frame, values):
        lower = values[:HALF]
        upper = values[HALF:]
        cosine = cos_ref[frame]
        sine = sin_ref[frame]
        return jnp.concatenate([lower * cosine + upper * sine, upper * cosine - lower * sine], axis=0)

    def visit(source, place, frame, count):
        query = x_ref[source, 2 * per_device + place]
        d_mix = d_mix_ref[source, place]
        blank = jnp.zeros_like(query)
        query_side = jnp.concatenate([query, blank], axis=0)
        d_mix_side = jnp.concatenate([blank, d_mix], axis=0)
        both = jnp.concatenate(
            [query_side.astype(F32).T.astype(BF16), d_mix_side.astype(F32).T.astype(BF16)], axis=0
        )
        lse = lse_ref[pl.ds(frame, 1), :]
        delta = jnp.sum(d_mix.astype(F32) * wide_ref[source, place], axis=0, keepdims=True)

        def block(other):
            key_value = kv_ref[other]
            scores = jnp.dot(key_value, query_side, preferred_element_type=F32)
            d_weights = jnp.dot(key_value, d_mix_side, preferred_element_type=F32)
            weights = jnp.exp(scores - lse)
            d_scores = (weights * (d_weights - delta)).astype(BF16)
            sides = jnp.concatenate([d_scores, weights.astype(BF16)], axis=1)
            dkv_ref[other] += jnp.dot(sides, both, preferred_element_type=F32)
            key = x_ref[lax.div(other, per_device), lax.rem(other, per_device)]
            return jnp.dot(key, d_scores, preferred_element_type=F32)

        d_query = lax.fori_loop(
            0,
            lax.div(count, 2),
            lambda index, state: state
            + block(list_ref[2 * index])
            + block(list_ref[2 * index + 1]),
            jnp.zeros((HEAD, PATCHES), F32),
        )
        d_query = lax.fori_loop(
            0,
            lax.rem(count, 2),
            lambda unused, state: state + block(list_ref[count - 1]),
            d_query,
        )
        d_query = unturn(frame, d_query * (HEAD**-0.5)).astype(BF16)
        if last:
            out_ref[source, 2 * per_device + part] = d_query
        else:
            out_ref[source] = d_query

    walk_frames(frames, per_device, (part,), segments_ref, live_ref, list_ref, visit)

    def finish(source, carry):
        for place in range(per_device):
            frame = source * per_device + place
            both = (dkv_ref[frame] + before_ref[frame]).T
            out_ref[source, place] = unturn(frame, both[:HEAD]).astype(BF16)
            out_ref[source, per_device + place] = both[HEAD:].astype(BF16)
        for place in range(part):
            out_ref[source, 2 * per_device + place] = d_query_ref[source]
        return carry

    if last:
        lax.fori_loop(0, frames // per_device, finish, 0)


def attend_back(
    part, per_device, segments, live, x, kv, wide, lse, d_mix, cosine, sine, before, orders
):
    sources = x.shape[0]
    frames = sources * per_device
    pairs = sources * 6
    last = part == per_device - 1
    args = [segments, live, x, kv, wide, lse, d_mix, cosine, sine]
    dkv = (frames, PATCHES, 2 * HEAD)
    lists = pltpu.SMEM((frames,), jnp.int32)
    if last:
        args += [before[1], before[0]]
        outs = jax.ShapeDtypeStruct(x.shape, BF16)
        out_specs = whole_spec()
        scratch = [pltpu.VMEM(dkv, F32), lists]
    else:
        outs = (
            jax.ShapeDtypeStruct((sources, HEAD, PATCHES), BF16),
            jax.ShapeDtypeStruct(dkv, F32),
        )
        out_specs = (whole_spec(), whole_spec())
        scratch = [lists]
    specs = [scalar_spec(), scalar_spec()] + [whole_spec()] * (len(args) - 2)
    orders = corners(orders)
    return pl.pallas_call(
        functools.partial(attend_back_kernel, per_device, part, last),
        out_shape=outs,
        in_specs=specs + [unread_spec()] * len(orders),
        out_specs=out_specs,
        scratch_shapes=scratch,
        cost_estimate=pl.CostEstimate(
            flops=pairs * 10 * PATCHES * PATCHES * 256,
            bytes_accessed=x.size * 2 * 5,
            transcendentals=pairs * PATCHES * PATCHES,
        ),
        compiler_params=pltpu.CompilerParams(vmem_limit_bytes=60 << 20),
        name="attend_back%d" % part,
    )(*args, *orders)


def exchange(value, axis, bit):
    count = lax.axis_size(axis)
    return lax.ppermute(value, axis, [(source, source ^ bit) for source in range(count)])


def after(value, *earlier):
    return lax.optimization_barrier((value,) + earlier)[0]


def of_packs(value):
    values = [value]
    bit = lax.axis_size("pack") // 2
    while bit:
        values = values + [exchange(each, "pack", bit) for each in values]
        bit //= 2
    return values


def halving_fits():
    return lax.axis_size("pack") == 2 and lax.axis_size("seq") == 16


class RowSum:
    def __init__(self, mine, came, order):
        self.order = list(order)
        self.index = lax.axis_index("seq")
        rows = mine.shape[-2]
        self.tail = (rows // 16, mine.shape[-1])
        self.lead = mine.shape[:-2]
        shape = self.lead + (2, 2, 2, 2) + self.tail
        self.parts = [mine.reshape(shape), came.reshape(shape)]

    def pick(self, bit, which):
        axis = len(self.lead) + {8: 0, 4: 1, 2: 2, 1: 3}[bit]
        pieces = [lax.dynamic_slice_in_dim(part, which, 1, axis) for part in self.parts]
        return (pieces[0].astype(F32) + pieces[1].astype(F32)).astype(BF16)

    def stage(self, later=()):
        bit = self.order.pop(0)
        own_bit = lax.rem(lax.div(self.index, bit), 2)
        send = self.pick(bit, 1 - own_bit)
        for each in later:
            send = each.tie(send)
        came = exchange(send, "seq", bit)
        self.parts = [self.pick(bit, own_bit), came]
        return send

    def tie(self, value):
        value, *self.parts = lax.optimization_barrier((value, *self.parts))
        return value

    def finish(self):
        while self.order:
            self.stage()
        own = (self.parts[0].astype(F32) + self.parts[1].astype(F32)).astype(BF16)
        own = own.reshape(self.lead + self.tail)
        return own, exchange(own, "pack", 1)


def settle_kernel(pack_ref, *refs):
    ups, downs, outs, firsts, seconds = [refs[2 * nth : 2 * nth + 2] for nth in range(5)]
    up_ref, down_ref, out_ref, qkv_ref = refs[10:]
    own_first = pack_ref[0] == 0
    small = 128

    def of_pack(pack, pair, *index):
        one, two = pair[0][index].astype(F32), pair[1][index].astype(F32)
        return jnp.where(own_first, one, two) if pack == 0 else jnp.where(own_first, two, one)

    every = slice(None)
    for pack in range(2):
        for group in range(ups[0].shape[1] // small):
            at = (2 * group + pack) * small
            columns = slice(group * small, (group + 1) * small)
            up_ref[:, at : at + small] = of_pack(pack, ups, every, columns)
        rows = downs[0].shape[0]
        down_ref[pack * rows : (pack + 1) * rows, :] = of_pack(pack, downs, every, every)
        columns = outs[0].shape[1]
        out_ref[:, pack * columns : (pack + 1) * columns] = of_pack(pack, outs, every, every)
        for kind in range(3):
            for nth, pair in enumerate((firsts, seconds)):
                columns = pair[0].shape[2]
                at = (4 * kind + 2 * pack + nth) * columns
                qkv_ref[:, at : at + columns] = of_pack(pack, pair, kind, every, every)


def settle(pack, *pairs):
    up, down, out, qkv = pairs[0][0], pairs[1][0], pairs[2][0], pairs[3][0]
    shapes = (
        (up.shape[0], 2 * up.shape[1]),
        (2 * down.shape[0], down.shape[1]),
        (out.shape[0], 2 * out.shape[1]),
        (qkv.shape[1], 12 * qkv.shape[2]),
    )
    args = [each for pair in pairs for each in pair]
    return pl.pallas_call(
        settle_kernel,
        out_shape=tuple(jax.ShapeDtypeStruct(shape, F32) for shape in shapes),
        in_specs=[scalar_spec()] + [whole_spec()] * len(args),
        out_specs=(whole_spec(),) * 4,
        compiler_params=pltpu.CompilerParams(vmem_limit_bytes=32 << 20),
        name="settle",
    )(pack.reshape(1), *args)


def row_sum_direct(term):
    part = lax.psum_scatter(term.astype(BF16), "seq", scatter_dimension=0, tiled=True)
    return lax.psum(part, "pack").astype(F32)


def project_kernel(
    per_device,
    hidden_ref,
    shift_ref,
    scale_ref,
    wq_ref,
    wk_ref,
    wv_ref,
    bq_ref,
    bk_ref,
    bv_ref,
    cos_ref,
    sin_ref,
    in_ref,
    x_ref,
):
    @pl.when(pl.program_id(0) == 0)
    def _():
        for place in range(per_device):
            rows = pl.ds(place * PATCHES, PATCHES)
            values = hidden_ref[rows, :].astype(F32)
            centered = values - jnp.mean(values, axis=-1, keepdims=True)
            spread = jnp.mean(centered * centered, axis=-1, keepdims=True)
            normed = centered * lax.rsqrt(spread + EPSILON)
            scale = scale_ref[pl.ds(place, 1), :]
            in_ref[rows, :] = (normed * (1.0 + scale) + shift_ref[pl.ds(place, 1), :]).astype(BF16)

    rows = in_ref[...]
    group = wq_ref.shape[1] // HEAD

    def turned(values, place):
        lower = values[:HALF]
        upper = values[HALF:]
        cosine = cos_ref[place]
        sine = sin_ref[place]
        return jnp.concatenate([lower * cosine - upper * sine, upper * cosine + lower * sine], axis=0)

    for kind, (weight_ref, bias_ref) in enumerate(
        ((wq_ref, bq_ref), (wk_ref, bk_ref), (wv_ref, bv_ref))
    ):
        flat = jnp.dot(rows, weight_ref[...], preferred_element_type=F32) + bias_ref[...]
        for place in range(per_device):
            block = flat[place * PATCHES : (place + 1) * PATCHES].T
            for head in range(group):
                values = block[head * HEAD : (head + 1) * HEAD]
                if kind == 0:
                    values = turned(values, place) * (HEAD**-0.5)
                    x_ref[head, 2 * per_device + place] = values.astype(BF16)
                elif kind == 1:
                    x_ref[head, place] = turned(values, place).astype(BF16)
                else:
                    x_ref[head, per_device + place] = values.astype(BF16)


def project(per_device, hidden, shift, scale, weight, bias, cosine, sine):
    tokens, width = hidden.shape
    heads = width // HEAD
    group = 2
    lanes = group * HEAD
    steps = heads // group
    bias_row = bias[None, :]

    def whole(shape):
        return pl.BlockSpec(shape, lambda step: (0,) * len(shape))

    def part(kind, rows):
        return pl.BlockSpec((rows, lanes), lambda step: (0, kind * steps + step))

    blocks = (heads, 3 * per_device, HEAD, PATCHES)
    return pl.pallas_call(
        functools.partial(project_kernel, per_device),
        grid=(steps,),
        out_shape=(
            jax.ShapeDtypeStruct((tokens, width), BF16),
            jax.ShapeDtypeStruct(blocks, BF16),
        ),
        in_specs=[whole((tokens, width)), whole(shift.shape), whole(scale.shape)]
        + [part(kind, width) for kind in range(3)]
        + [part(kind, 1) for kind in range(3)]
        + [whole(cosine.shape), whole(sine.shape)],
        out_specs=(
            whole((tokens, width)),
            pl.BlockSpec((group,) + blocks[1:], lambda step: (step, 0, 0, 0)),
        ),
        cost_estimate=pl.CostEstimate(
            flops=2 * tokens * width * 3 * width,
            bytes_accessed=2 * (weight.size + 5 * tokens * width),
            transcendentals=0,
        ),
        compiler_params=pltpu.CompilerParams(vmem_limit_bytes=40 << 20),
        name="project",
    )(hidden, shift, scale, weight, weight, weight, bias_row, bias_row, bias_row, cosine, sine)


GELU_SLOPE = 0.7978845608028654
GELU_CUBE = 0.044715


def feed_kernel(
    carried,
    which_ref,
    in_ref,
    d_out_ref,
    up_a_ref,
    up_b_ref,
    bias_a_ref,
    bias_b_ref,
    down_a_ref,
    down_b_ref,
    *refs
):
    if carried:
        out_before_ref, d_in_before_ref = refs[:2]
        refs = refs[2:]
    out_ref, d_in_ref, d_up_ref, d_down_ref, d_bias_ref, turned_ref = refs

    @pl.when(pl.program_id(0) == 0)
    def _():
        turned_ref[...] = in_ref[...].astype(F32).T.astype(BF16)
        if carried:
            out_ref[...] = out_before_ref[...]
            d_in_ref[...] = d_in_before_ref[...]
        else:
            out_ref[...] = jnp.zeros_like(out_ref)
            d_in_ref[...] = jnp.zeros_like(d_in_ref)

    up = jnp.concatenate([up_a_ref[...], up_b_ref[...]], axis=1)
    down = jnp.concatenate([down_a_ref[...], down_b_ref[...]], axis=0)
    bias = jnp.concatenate([bias_a_ref[...], bias_b_ref[...]], axis=1)
    d_out = d_out_ref[...]
    pre = jnp.dot(in_ref[...], up, preferred_element_type=F32) + bias
    d_act = dot_over(d_out, down, 1, 1)
    square = pre * pre
    bend = jnp.tanh(GELU_SLOPE * pre * (1.0 + GELU_CUBE * square))
    half = 0.5 * (1.0 + bend)
    act = (pre * half).astype(BF16)
    slope = half + (0.5 * GELU_SLOPE) * pre * (1.0 - bend * bend) * (
        1.0 + (3.0 * GELU_CUBE) * square
    )
    d_pre = (d_act * slope).astype(BF16)
    out_ref[...] += jnp.dot(act, down, preferred_element_type=F32)
    d_in_ref[...] += dot_over(d_pre, up, 1, 1)
    d_up_ref[...] = jnp.dot(turned_ref[...], d_pre, preferred_element_type=F32).astype(BF16)
    d_down_ref[...] = jnp.dot(
        act.astype(F32).T.astype(BF16), d_out, preferred_element_type=F32
    ).astype(BF16)
    d_bias_ref[...] = jnp.sum(d_pre.astype(F32), axis=0, keepdims=True)


def feed(which, feed_in, d_feed_out, up_weight, up_bias, down_weight, before):
    tokens, width = feed_in.shape
    hidden_units = up_weight.shape[1]
    small = 128
    steps = hidden_units // (4 * small)
    own = hidden_units // 2

    def whole(shape):
        return pl.BlockSpec(shape, lambda step, which: (0,) * len(shape))

    def group(nth):
        return lambda step, which: 2 * (2 * step + nth) + which[0]

    def columns(nth, rows):
        return pl.BlockSpec((rows, small), lambda step, which: (0, group(nth)(step, which)))

    def rows_of(nth):
        return pl.BlockSpec((small, width), lambda step, which: (group(nth)(step, which), 0))

    args = [feed_in, d_feed_out, up_weight, up_weight, up_bias[None], up_bias[None]]
    args += [down_weight, down_weight]
    specs = [whole((tokens, width)), whole((tokens, width)), columns(0, width), columns(1, width)]
    specs += [columns(0, 1), columns(1, 1), rows_of(0), rows_of(1)]
    if before is not None:
        args += list(before)
        specs += [whole((tokens, width)), whole((tokens, width))]
    return pl.pallas_call(
        functools.partial(feed_kernel, before is not None),
        grid_spec=pltpu.PrefetchScalarGridSpec(
            num_scalar_prefetch=1,
            grid=(steps,),
            in_specs=specs,
            out_specs=(
                whole((tokens, width)),
                whole((tokens, width)),
                pl.BlockSpec((width, 2 * small), lambda step, which: (0, step)),
                pl.BlockSpec((2 * small, width), lambda step, which: (step, 0)),
                pl.BlockSpec((1, 2 * small), lambda step, which: (0, step)),
            ),
            scratch_shapes=[pltpu.VMEM((width, tokens), BF16)],
        ),
        out_shape=(
            jax.ShapeDtypeStruct((tokens, width), F32),
            jax.ShapeDtypeStruct((tokens, width), F32),
            jax.ShapeDtypeStruct((width, own), BF16),
            jax.ShapeDtypeStruct((own, width), BF16),
            jax.ShapeDtypeStruct((1, own), F32),
        ),
        cost_estimate=pl.CostEstimate(
            flops=12 * tokens * width * own,
            bytes_accessed=2 * (4 * own * width + 8 * tokens * width),
            transcendentals=tokens * own,
        ),
        compiler_params=pltpu.CompilerParams(vmem_limit_bytes=56 << 20),
        name="feed%d" % (before is not None),
    )(which.reshape(1), *args)


def norm_back(values, d_in, scale):
    centered = values - jnp.mean(values, axis=-1, keepdims=True)
    spread = jnp.mean(centered * centered, axis=-1, keepdims=True)
    inverse = lax.rsqrt(spread + EPSILON)
    normed = centered * inverse
    product = d_in * normed
    d_shift = jnp.sum(d_in, axis=0, keepdims=True)
    d_scale = jnp.sum(product, axis=0, keepdims=True)
    scaled = 1.0 + scale
    mean_d = jnp.mean(d_in * scaled, axis=-1, keepdims=True)
    mean_p = jnp.mean(product * scaled, axis=-1, keepdims=True)
    return (d_in * scaled - mean_d - normed * mean_p) * inverse, d_shift, d_scale


def middle_back_kernel(
    d_in_ref,
    middle_ref,
    grad_ref,
    attn_ref,
    feed_ref,
    scale_ref,
    gate_ref,
    feed_gate_ref,
    down_bias_ref,
    rows_ref,
    weight_ref,
    d_middle_ref,
    d_attn_ref,
    layer_ref,
    blocks_ref,
    sums_ref,
):
    frame = pl.program_id(0)
    per_device = pl.num_programs(0) - 1

    @pl.when(frame < per_device)
    def _():
        mine = pl.ds(frame, 1)
        middle = middle_ref[...]
        grads = grad_ref[...].astype(F32)
        back, d_shift, d_scale = norm_back(middle, d_in_ref[...], scale_ref[mine, :])
        d_middle = grads + back
        d_middle_ref[...] = d_middle
        d_attn = (d_middle * gate_ref[mine, :]).astype(BF16)
        d_attn_ref[...] = d_attn
        feed_rows = feed_ref[...] + down_bias_ref[...]
        feed_gate = feed_gate_ref[mine, :]
        layer_ref[...] = (middle + feed_gate * feed_rows).astype(BF16)
        d_feed_out = (feed_gate * grads).astype(BF16).astype(F32)
        sums_ref[frame] = jnp.concatenate(
            [
                jnp.sum(d_middle * attn_ref[...], axis=0, keepdims=True),
                d_shift,
                d_scale,
                jnp.sum(grads * feed_rows, axis=0, keepdims=True),
                jnp.sum(d_attn.astype(F32), axis=0, keepdims=True),
                jnp.sum(d_feed_out, axis=0, keepdims=True),
                jnp.zeros((2, d_shift.shape[1]), F32),
            ],
            axis=0,
        )
        d_mix = dot_over(weight_ref[...], d_attn, 1, 1).astype(BF16)
        for head in range(blocks_ref.shape[0]):
            blocks_ref[head, 0] = d_mix[head * HEAD : (head + 1) * HEAD]

    @pl.when(frame == per_device)
    def _():
        first = sums_ref[0]
        second = sums_ref[1]
        rows = jnp.concatenate(
            [first[:4], second[:4], first[4:6] + second[4:6], rows_ref[...]], axis=0
        ).astype(BF16)
        count = rows.shape[1] // PATCHES
        block = jnp.concatenate(
            [rows[:, nth * PATCHES : (nth + 1) * PATCHES] for nth in range(count)], axis=0
        )
        for head in range(blocks_ref.shape[0]):
            blocks_ref[head, 0] = block


def middle_back(
    per_device, d_in, middle, grads, attn_rows, feed_rows, scale, gate, feed_gate, down_bias, rows, weight
):
    tokens, width = d_in.shape
    heads = width // HEAD
    last = per_device - 1
    per_frame = pl.BlockSpec((PATCHES, width), lambda frame: (jnp.minimum(frame, last), 0))

    def whole(shape):
        return pl.BlockSpec(shape, lambda frame: (0,) * len(shape))

    small = whole((per_device, width))
    return pl.pallas_call(
        middle_back_kernel,
        grid=(per_device + 1,),
        out_shape=(
            jax.ShapeDtypeStruct((tokens, width), F32),
            jax.ShapeDtypeStruct((tokens, width), BF16),
            jax.ShapeDtypeStruct((tokens, width), BF16),
            jax.ShapeDtypeStruct((heads, per_device + 1, HEAD, PATCHES), BF16),
        ),
        in_specs=[per_frame] * 5
        + [small] * 3
        + [whole((1, width)), whole(rows.shape), whole(weight.shape)],
        out_specs=(
            per_frame,
            per_frame,
            per_frame,
            pl.BlockSpec((heads, 1, HEAD, PATCHES), lambda frame: (0, frame, 0, 0)),
        ),
        scratch_shapes=[pltpu.VMEM((per_device, 8, width), F32)],
        cost_estimate=pl.CostEstimate(
            flops=2 * tokens * width * width, bytes_accessed=24 * tokens * width, transcendentals=0
        ),
        compiler_params=pltpu.CompilerParams(vmem_limit_bytes=48 << 20),
        name="middle_back",
    )(
        d_in,
        middle,
        grads,
        attn_rows,
        feed_rows,
        scale,
        gate,
        feed_gate,
        down_bias[None],
        rows,
        weight,
    )


def unproject_kernel(
    per_device, carried, which_ref, in_ref, back_ref, wq_ref, wk_ref, wv_ref, *refs
):
    if not carried:
        refs = refs[-4:]
    if carried:
        before_ref, hidden_ref, d_middle_ref, scale_ref, bias_theirs_ref = refs[:5]
        d_weight_ref, grad_ref, rows_ref, d_in_ref, d_bias_ref, turned_ref = refs[5:]
    else:
        d_in_ref, d_weight_ref, d_bias_ref, turned_ref = refs

    @pl.when(pl.program_id(0) == 0)
    def _():
        turned_ref[...] = in_ref[...].astype(F32).T.astype(BF16)
        if carried:
            d_in_ref[...] = before_ref[...]
        else:
            d_in_ref[...] = jnp.zeros_like(d_in_ref)

    group = wq_ref.shape[1] // HEAD

    def token_major(block_of):
        rows = []
        for place in range(per_device):
            block = jnp.concatenate([block_of(head, place) for head in range(group)], axis=0)
            rows.append(block.astype(F32).T.astype(BF16))
        return jnp.concatenate(rows, axis=0)

    sides = jnp.concatenate(
        [
            token_major(lambda head, place: back_ref[head, 2 * per_device + place]),
            token_major(lambda head, place: back_ref[head, place]),
            token_major(lambda head, place: back_ref[head, per_device + place]),
        ],
        axis=1,
    )
    weights = jnp.concatenate([wq_ref[...], wk_ref[...], wv_ref[...]], axis=1)
    d_in_ref[...] += dot_over(sides, weights, 1, 1)
    d_weight = jnp.dot(turned_ref[...], sides, preferred_element_type=F32).astype(BF16)
    d_bias = jnp.sum(sides.astype(F32), axis=0, keepdims=True)
    lanes = group * HEAD
    for kind in range(3):
        d_weight_ref[kind] = d_weight[:, kind * lanes : (kind + 1) * lanes]
        part = d_bias[:, kind * lanes : (kind + 1) * lanes]
        if carried:
            start = pl.multiple_of(pl.program_id(0) * lanes, lanes)
            d_bias_ref[pl.ds(kind, 1), pl.ds(start, lanes)] = part
        else:
            d_bias_ref[kind] = part

    if carried:

        @pl.when(pl.program_id(0) == pl.num_programs(0) - 1)
        def _():
            sums = []
            for place in range(per_device):
                rows = pl.ds(place * PATCHES, PATCHES)
                mine = pl.ds(place, 1)
                back, d_shift, d_scale = norm_back(
                    hidden_ref[rows, :].astype(F32), d_in_ref[rows, :], scale_ref[mine, :]
                )
                grad_ref[rows, :] = (d_middle_ref[rows, :] + back).astype(BF16)
                sums += [d_shift, d_scale]
            for kind in range(3):
                sums.append(
                    jnp.concatenate([d_bias_ref[pl.ds(kind, 1), :], bias_theirs_ref[kind]], axis=1)
                )
            count = 16 - len(sums)
            late = jnp.concatenate(
                sums + [jnp.zeros((count, d_in_ref.shape[1]), F32)], axis=0
            ).astype(BF16)
            for target in range(rows_ref.shape[0]):
                rows_ref[target] = late


def unproject(per_device, targets, which, attn_in, back, weight, orders, before=None, norm_args=()):
    tokens, width = attn_in.shape
    heads = width // HEAD
    group = 2
    lanes = group * HEAD
    groups = heads // group
    steps = groups // 2

    def whole(shape):
        return pl.BlockSpec(shape, lambda step, which: (0,) * len(shape))

    def blocks(array):
        return pl.BlockSpec(
            (group,) + array.shape[1:], lambda step, which: (which[0] * steps + step, 0, 0, 0)
        )

    def part(kind):
        return pl.BlockSpec(
            (width, lanes), lambda step, which: (0, kind * groups + which[0] * steps + step)
        )

    args = [attn_in, back, weight, weight, weight]
    specs = [whole((tokens, width)), blocks(back), part(0), part(1), part(2)]
    weight_shape = (
        jax.ShapeDtypeStruct((3, width, width // 2), BF16),
        jax.ShapeDtypeStruct((3, 1, width // 2), F32),
    )
    weight_specs = (
        pl.BlockSpec((3, width, lanes), lambda step, which: (0, 0, step)),
        pl.BlockSpec((3, 1, lanes), lambda step, which: (0, 0, step)),
    )
    scratch = [pltpu.VMEM((width, tokens), BF16)]
    small = (per_device, width)
    if before is not None:
        args += [before] + list(norm_args)
        specs += [whole((tokens, width))] * 3 + [whole(small), whole((3, 1, width // 2))]
        late = (targets, 16, width)
        outs = weight_shape[:1] + (
            jax.ShapeDtypeStruct((tokens, width), BF16),
            jax.ShapeDtypeStruct(late, BF16),
        )
        out_specs = weight_specs[:1] + (whole((tokens, width)), whole(late))
        scratch = [pltpu.VMEM((tokens, width), F32), pltpu.VMEM((3, width // 2), F32)] + scratch
    else:
        outs = (jax.ShapeDtypeStruct((tokens, width), F32),) + weight_shape
        out_specs = (whole((tokens, width)),) + weight_specs
        orders = corners(orders)
        args += orders
        specs += [unread_spec()] * len(orders)
    return pl.pallas_call(
        functools.partial(unproject_kernel, per_device, before is not None),
        grid_spec=pltpu.PrefetchScalarGridSpec(
            num_scalar_prefetch=1,
            grid=(steps,),
            in_specs=specs,
            out_specs=out_specs,
            scratch_shapes=scratch,
        ),
        out_shape=outs,
        cost_estimate=pl.CostEstimate(
            flops=6 * tokens * width * width,
            bytes_accessed=2 * (3 * width * width + 6 * tokens * width),
            transcendentals=0,
        ),
        compiler_params=pltpu.CompilerParams(vmem_limit_bytes=48 << 20),
        name="unproject%d" % (before is not None),
    )(which.reshape(1), *args)


def columns_of(matrix, start, width, axis=1):
    if isinstance(start, int) and start == 0 and width == matrix.shape[axis]:
        return matrix
    return lax.dynamic_slice_in_dim(matrix, start, width, axis)


def local(
    hidden,
    cotangent,
    levels,
    segments,
    live_frames,
    noise_table,
    mod_weight,
    mod_bias,
    qkv_weight,
    qkv_bias,
    out_weight,
    out_bias,
    up_weight,
    up_bias,
    down_weight,
    down_bias,
):
    seq_index = lax.axis_index("seq")
    seq_count = lax.axis_size("seq")
    tokens = hidden.shape[1]
    width = hidden.shape[2]
    per_device = tokens // PATCHES
    frames = segments.shape[1]
    heads = width // HEAD
    copies = seq_count // heads
    hidden_units = up_weight.shape[1]
    level_count = noise_table.shape[0]
    share = width // seq_count
    clip_ids = segments[0]
    live = live_frames[0]

    pack = lax.axis_index("pack")
    halves = halving_fits()
    frame_ids = jnp.arange(frames, dtype=jnp.int32)
    same_clip = clip_ids[:, None] == clip_ids[None, :]
    clip_starts = jnp.min(jnp.where(same_clip, frame_ids[None, :], frames), axis=1)
    frame_times = (frame_ids - clip_starts).astype(F32)
    own_cos, own_sin = rotary_tables(
        lax.dynamic_slice_in_dim(frame_times, seq_index * per_device, per_device)
    )

    embed = jnp.concatenate(
        [
            lax.dynamic_slice_in_dim(noise_table, levels[0, frame], 1, 0)
            for frame in range(per_device)
        ],
        axis=0,
    )
    cond = jax.nn.silu(embed).astype(BF16)
    modulation = jnp.dot(cond, mod_weight[:, : 2 * width], preferred_element_type=F32)
    attn_shift, attn_scale = jnp.split(modulation + mod_bias[: 2 * width], 2, axis=1)
    attn_in, sent = project(
        per_device, hidden[0], attn_shift, attn_scale, qkv_weight, qkv_bias, own_cos, own_sin
    )

    def to_heads(array):
        if copies > 1:
            array = jnp.concatenate([array] * copies, axis=0)
        return lax.all_to_all(array, "seq", 0, 0, tiled=True)

    def to_tokens(array):
        return lax.all_to_all(array, "seq", 0, 0, tiled=True)[:heads]

    x = to_heads(sent)
    late_modulation = jnp.dot(
        after(cond, attn_in), mod_weight[:, 2 * width :], preferred_element_type=F32
    )
    attn_gate, feed_shift, feed_scale, feed_gate = jnp.split(
        late_modulation + mod_bias[2 * width :], 4, axis=1
    )
    cos_all, sin_all = rotary_tables(after(frame_times, attn_in))
    grad_rows = cotangent[0].astype(F32).reshape(per_device, PATCHES, width)
    d_feed_out = (feed_gate[:, None, :] * grad_rows).reshape(tokens, width).astype(BF16)
    x, d_feed_out, cos_all, sin_all = lax.optimization_barrier((x, d_feed_out, cos_all, sin_all))
    mix, wide, lse, kv = attend(per_device, clip_ids, live, x)
    mix = to_tokens(mix)
    mixes = [mix[:, place].reshape(width, PATCHES) for place in range(per_device)]
    attn_rows = jnp.stack([dot_over(each, out_weight, 0, 0) for each in mixes]) + out_bias
    attn_mix = jnp.concatenate(mixes, axis=1)

    frame_rows = hidden[0].astype(F32).reshape(per_device, PATCHES, width)
    middle = frame_rows + attn_gate[:, None, :] * attn_rows
    feed_in = modulate_norm(middle, feed_shift, feed_scale).reshape(tokens, width).astype(BF16)
    feed_args = (feed_in, d_feed_out, up_weight, up_bias, down_weight)
    theirs = feed(1 - pack if halves else pack * 0 + 1, *feed_args, None)
    mine = feed(pack if halves else pack * 0, *feed_args, theirs[:2])
    small = 128

    def in_order(own, other):
        if halves:
            even, odd = jnp.where(pack == 0, own, other), jnp.where(pack == 0, other, own)
        else:
            even, odd = own, other
        rows = own.shape[0]
        return jnp.stack(
            [even.reshape(rows, -1, small), odd.reshape(rows, -1, small)], axis=2
        ).reshape(rows, -1)

    own_levels = levels[0]
    level_row = jnp.concatenate(
        [
            jnp.broadcast_to(part[frame], (width // (2 * per_device),))
            for frame in range(per_device)
            for part in (lax.div(own_levels, 32), lax.rem(own_levels, 32))
        ]
    ).astype(F32)[None]
    extra_rows = jnp.concatenate(
        [
            in_order(mine[4], theirs[4]).reshape(-1, width),
            level_row,
            jnp.zeros((1, width), F32),
        ],
        axis=0,
    )
    d_middle, d_attn_out, layer_out, blocks = middle_back(
        per_device,
        mine[1],
        middle.reshape(tokens, width),
        cotangent[0],
        attn_rows.reshape(tokens, width),
        mine[0],
        feed_scale,
        attn_gate,
        feed_gate,
        down_bias,
        extra_rows,
        out_weight,
    )
    layer_out = layer_out.reshape(1, tokens, width)
    d_mix = to_heads(blocks)

    def out_term(start, size):
        return dot_over(attn_mix, columns_of(d_attn_out, start, size), 1, 0).astype(BF16)

    sums = ()
    if halves:
        up_sum = RowSum(mine[2], exchange(theirs[2], "pack", 1), (2, 1, 4, 8))
        down_sum = RowSum(mine[3], exchange(theirs[3], "pack", 1), (1, 2, 4, 8))
        out_theirs = exchange(out_term((1 - pack) * (width // 2), width // 2), "pack", 1)
        out_sum = RowSum(out_term(pack * (width // 2), width // 2), out_theirs, (1, 2, 4, 8))
        sums = (down_sum, up_sum)
    def own_share(row):
        piece = row.shape[0] // seq_count
        return lax.dynamic_slice_in_dim(row, seq_index * piece, piece)

    chunks = width // PATCHES
    early_rows = d_mix[:, per_device].reshape(seq_count, chunks, 16, PATCHES)
    early_rows = early_rows.transpose(0, 2, 1, 3).reshape(seq_count, 16, width)
    early_sets = of_packs(early_rows)
    early_sum = functools.reduce(
        jnp.add, [jnp.sum(each.astype(F32), axis=0) for each in early_sets]
    )
    out_bias_grad = own_share(early_sum[8])
    down_bias_grad = own_share(early_sum[9])
    up_bias_grad = own_share(early_sum[10:14].reshape(hidden_units))

    def frames_of(rows, per_frame, kinds):
        return jnp.concatenate(
            [
                jnp.stack(
                    [rows[:, frame * per_frame + kind] for frame in range(per_device)], axis=1
                ).reshape(-1, width)
                for kind in range(kinds)
            ],
            axis=1,
        )

    own_table = lax.dynamic_slice_in_dim(noise_table, seq_index * share, share, 1)
    own_mod = lax.dynamic_slice_in_dim(mod_weight, seq_index * share, share, 0)
    stride = width // (2 * per_device)
    parts = []
    for rows in early_sets:
        coded = rows[:, 14, ::stride].astype(jnp.int32).reshape(-1, 2)
        set_levels = coded[:, 0] * 32 + coded[:, 1]
        picks = (set_levels[:, None] == jnp.arange(level_count, dtype=jnp.int32)[None, :]).astype(F32)
        embeds = jnp.dot(picks, own_table, precision=PRECISE, preferred_element_type=F32)
        set_cond = jax.nn.silu(embeds).astype(BF16)
        d_mod = frames_of(rows, 4, 4)
        parts.append(
            (
                picks,
                embeds,
                set_cond,
                dot_over(d_mod, own_mod[:, 2 * width :], 1, 1),
                dot_over(set_cond, d_mod, 0, 0),
            )
        )
    mod_grad_early = functools.reduce(jnp.add, [each[4] for each in parts])
    mod_sum_early = (early_sum[:4] + early_sum[4:8]).reshape(4 * width)
    before = None
    for part in range(per_device):
        orders = [each.stage() for each in sums]
        if halves and part:
            before = (out_sum.tie(before[0]), before[1])
            orders.append(out_sum.stage())
        before = attend_back(
            part,
            per_device,
            clip_ids,
            live,
            x,
            kv,
            wide,
            lse,
            d_mix,
            cos_all,
            sin_all,
            before,
            orders,
        )
    back = to_tokens(before)
    orders = [each.stage() for each in sums]
    if halves:
        orders.append(out_sum.stage())
        orders.append(out_sum.stage())
    orders += [mod_grad_early] + [part[3] for part in parts]
    which = (1 - pack, pack) if halves else (pack * 0, pack * 0 + 1)
    d_in_theirs, qkv_theirs, bias_theirs = unproject(
        per_device, seq_count, which[0], attn_in, back, qkv_weight, orders
    )
    qkv_mine, hidden_grad, late = unproject(
        per_device,
        seq_count,
        which[1],
        attn_in,
        back,
        qkv_weight,
        (),
        d_in_theirs,
        (hidden[0], d_middle, attn_scale, bias_theirs),
    )
    hidden_grad = hidden_grad.reshape(1, tokens, width)
    late_rows = lax.all_to_all(late, "seq", 0, 0, tiled=True)

    def halves_in_order(own, other):
        if halves:
            return jnp.where(pack == 0, own, other), jnp.where(pack == 0, other, own)
        return other, own

    if halves:
        came = exchange(qkv_theirs, "pack", 1)
        split = width // 4
        qkv_sums = [
            RowSum(qkv_mine[..., :split], came[..., :split], (1, 2, 4, 8)),
            RowSum(qkv_mine[..., split:], came[..., split:], (2, 1, 4, 8)),
        ]
        for each in qkv_sums:
            each.stage((up_sum, down_sum, out_sum))
        up_weight_grad, down_weight_grad, out_weight_grad, qkv_weight_grad = settle(
            pack, *[each.finish() for each in (up_sum, down_sum, out_sum, *qkv_sums)]
        )
    else:
        up_weight_grad = row_sum_direct(in_order(mine[2], theirs[2]))
        pairs = [each[3].reshape(-1, small, width) for each in (mine, theirs)]
        down_weight_grad = row_sum_direct(jnp.stack(pairs, axis=1).reshape(hidden_units, width))
        out_weight_grad = row_sum_direct(out_term(0, width))
        qkv_term = jnp.concatenate(halves_in_order(qkv_mine, qkv_theirs), axis=-1)
        qkv_weight_grad = row_sum_direct(qkv_term.transpose(1, 0, 2).reshape(width, 3 * width))

    late_sets = of_packs(late_rows[:, :8])
    bias_at = 2 * per_device
    bias_sums = [
        jnp.sum(rows[:, bias_at : bias_at + 3].astype(F32), axis=0) for rows in late_sets
    ]
    if halves:
        ones, twos = bias_sums
        half = width // 2
        own_half = ones[:, :half] + twos[:, half:]
        other_half = ones[:, half:] + twos[:, :half]
    else:
        total = functools.reduce(jnp.add, bias_sums)
        own_half, other_half = total[:, : width // 2], total[:, width // 2 :]
    bias_total = jnp.concatenate(halves_in_order(own_half, other_half), axis=1)
    qkv_bias_grad = own_share(bias_total.reshape(3 * width))
    late_mods = [frames_of(rows, 2, 2) for rows in late_sets]
    mod_sum_late = functools.reduce(
        jnp.add, [jnp.sum(each.astype(F32), axis=0) for each in late_mods]
    )
    d_embeds = []
    for part, d_mod in zip(parts, late_mods):
        d_cond = part[3] + dot_over(d_mod, own_mod[:, : 2 * width], 1, 1)
        d_embeds.append(jax.vjp(jax.nn.silu, part[1])[1](d_cond)[0])
    table_grad = lax.dot_general(
        jnp.concatenate([part[0] for part in parts], axis=0),
        jnp.concatenate(d_embeds, axis=0),
        (((0,), (0,)), ((), ())),
        precision=PRECISE,
        preferred_element_type=F32,
    )
    mod_grad_late = functools.reduce(
        jnp.add, [dot_over(part[2], d_mod, 0, 0) for part, d_mod in zip(parts, late_mods)]
    )
    mod_weight_grad = jnp.concatenate([mod_grad_late, mod_grad_early], axis=1)
    mod_bias_grad = own_share(jnp.concatenate([mod_sum_late, mod_sum_early]))
    return (
        layer_out,
        hidden_grad,
        table_grad,
        mod_weight_grad,
        mod_bias_grad,
        qkv_weight_grad,
        qkv_bias_grad,
        out_weight_grad,
        out_bias_grad,
        up_weight_grad,
        up_bias_grad,
        down_weight_grad,
        down_bias_grad,
    )


def solution(mesh):
    in_specs = (
        P("pack", "seq", None),
        P("pack", "seq", None),
        P("pack", "seq"),
        P("pack", None),
        P("pack", None),
    ) + (P(),) * 11
    out_specs = (
        P("pack", "seq", None),
        P("pack", "seq", None),
        P(None, "seq"),
        P("seq", None),
        P("seq"),
        P("seq", None),
        P("seq"),
        P("seq", None),
        P("seq"),
        P("seq", None),
        P("seq"),
        P("seq", None),
        P("seq"),
    )
    return jax.shard_map(local, mesh=mesh, in_specs=in_specs, out_specs=out_specs, check_vma=False)
```

```python
import functools

import jax
import jax.numpy as jnp
from jax import lax
from jax.experimental import pallas as pl
from jax.experimental.pallas import tpu as pltpu
from jax.sharding import PartitionSpec as P

HEAD = 64
PATCHES = 256
SIDE = 16
EPSILON = 1e-06
PRECISE = lax.Precision.HIGHEST
HALF = HEAD // 2
F32 = jnp.float32
BF16 = jnp.bfloat16


def modulate_norm(rows, shift, scale):
    center = jnp.mean(rows, axis=-1, keepdims=True)
    centered = rows - center
    spread = jnp.mean(centered * centered, axis=-1, keepdims=True)
    normed = centered * lax.rsqrt(spread + EPSILON)
    return normed * (1.0 + scale[:, None, :]) + shift[:, None, :]


def gelu_tanh(values):
    return jax.nn.gelu(values, approximate=True)


def dot_over(first, second, first_dim, second_dim):
    return lax.dot_general(
        first, second, (((first_dim,), (second_dim,)), ((), ())), preferred_element_type=F32
    )


def spatial_angles():
    time_pairs = HALF // 4
    space_pairs = (HALF - time_pairs) // 2
    patch = jnp.arange(PATCHES, dtype=jnp.int32)
    row_pos = (patch // SIDE).astype(F32)
    col_pos = (patch % SIDE).astype(F32)
    time_freq = 10000.0 ** (-jnp.arange(time_pairs, dtype=F32) / time_pairs)
    space_freq = 10000.0 ** (-jnp.arange(space_pairs, dtype=F32) / space_pairs)
    space = jnp.concatenate(
        [space_freq[:, None] * row_pos[None, :], space_freq[:, None] * col_pos[None, :]], axis=0
    )
    return time_freq, space


def rotary_tables(time_frames):
    time_freq, space = spatial_angles()
    count = time_frames.shape[0]
    time_angle = time_frames[:, None] * time_freq[None, :]

    def whole(function):
        return jnp.concatenate(
            [
                jnp.broadcast_to(
                    function(time_angle)[:, :, None], (count, time_freq.shape[0], PATCHES)
                ),
                jnp.broadcast_to(function(space)[None], (count,) + space.shape),
            ],
            axis=1,
        )

    return whole(jnp.cos), whole(jnp.sin)


def walk_frames(frames, per_device, segments_ref, live_ref, list_ref, visit):
    def step(source, held):
        for place in range(per_device):
            frame = source * per_device + place
            before = jnp.maximum(frame - 1, 0)
            fresh = (frame == 0) | (segments_ref[frame] != segments_ref[before])
            held = jnp.where(fresh, 0, held)
            list_ref[held] = frame
            visit(source, place, frame, held + 1)
            held = held + jnp.where(live_ref[frame] == 1, 1, 0)
        return held

    lax.fori_loop(0, frames // per_device, step, jnp.int32(0))


def attend_kernel(per_device, segments_ref, live_ref, x_ref, mix_ref, wide_ref, lse_ref, kv_ref, list_ref):
    frames = kv_ref.shape[0]

    def turn(source, carry):
        for place in range(per_device):
            both = jnp.concatenate(
                [x_ref[source, place], x_ref[source, per_device + place]], axis=0
            )
            kv_ref[source * per_device + place] = both.T
        return carry

    lax.fori_loop(0, frames // per_device, turn, 0)

    def visit(source, place, frame, count):
        query = x_ref[source, 2 * per_device + place]
        query_side = jnp.concatenate([query, jnp.zeros_like(query)], axis=0)

        def scores_of(other):
            return jnp.dot(kv_ref[other], query_side, preferred_element_type=F32)

        def mixed(other, weights):
            value = x_ref[lax.div(other, per_device), per_device + lax.rem(other, per_device)]
            return jnp.dot(value, weights.astype(BF16), preferred_element_type=F32)

        def join(others, carry):
            scores = [scores_of(other) for other in others]
            tops = [jnp.max(score, axis=0, keepdims=True) for score in scores]
            new_top = functools.reduce(jnp.maximum, tops)
            if carry is not None:
                top, total, accum = carry
                new_top = jnp.maximum(top, new_top)
                shrink = jnp.exp(top - new_top)
                total = total * shrink
                accum = accum * shrink
            for index, score in enumerate(scores):
                weights = jnp.exp(score - new_top)
                added = jnp.sum(weights, axis=0, keepdims=True)
                product = mixed(others[index], weights)
                if carry is None and index == 0:
                    total, accum = added, product
                else:
                    total, accum = total + added, accum + product
            return new_top, total, accum

        others = count - 1
        carry = join([frame], None)
        carry = lax.fori_loop(
            0,
            lax.div(others, 4),
            lambda index, state: join([list_ref[4 * index + nth] for nth in range(4)], state),
            carry,
        )
        carry = lax.fori_loop(
            lax.div(others, 4) * 2,
            lax.div(others, 2),
            lambda index, state: join([list_ref[2 * index], list_ref[2 * index + 1]], state),
            carry,
        )
        top, total, accum = lax.fori_loop(
            0,
            lax.rem(others, 2),
            lambda unused, state: join([list_ref[others - 1]], state),
            carry,
        )
        result = accum * (1.0 / total)
        wide_ref[source, place] = result
        mix_ref[source, place] = result.astype(BF16)
        lse_ref[pl.ds(frame, 1), :] = top + jnp.log(total)

    walk_frames(frames, per_device, segments_ref, live_ref, list_ref, visit)


def corners(values):
    return [each.reshape(-1, each.shape[-1])[:1, :128] for each in values]


def unread_spec():
    return pl.BlockSpec(memory_space=pl.ANY)


def whole_spec():
    return pl.BlockSpec(memory_space=pltpu.VMEM)


def scalar_spec():
    return pl.BlockSpec(memory_space=pltpu.SMEM)


def attend(per_device, segments, live, x):
    sources = x.shape[0]
    frames = sources * per_device
    pairs = frames * 6
    outs = (
        jax.ShapeDtypeStruct((sources, per_device, HEAD, PATCHES), BF16),
        jax.ShapeDtypeStruct((sources, per_device, HEAD, PATCHES), F32),
        jax.ShapeDtypeStruct((frames, PATCHES), F32),
        jax.ShapeDtypeStruct((frames, PATCHES, 2 * HEAD), BF16),
    )
    return pl.pallas_call(
        functools.partial(attend_kernel, per_device),
        out_shape=outs,
        in_specs=[scalar_spec(), scalar_spec(), whole_spec()],
        out_specs=(whole_spec(),) * len(outs),
        scratch_shapes=[pltpu.SMEM((frames,), jnp.int32)],
        cost_estimate=pl.CostEstimate(
            flops=pairs * 4 * PATCHES * PATCHES * 256,
            bytes_accessed=x.size * 2 * 3,
            transcendentals=pairs * PATCHES * PATCHES,
        ),
        compiler_params=pltpu.CompilerParams(vmem_limit_bytes=40 << 20),
        name="attend",
    )(segments, live, x)


def attend_back_kernel(
    per_device,
    segments_ref,
    live_ref,
    x_ref,
    kv_ref,
    wide_ref,
    lse_ref,
    d_mix_ref,
    cos_ref,
    sin_ref,
    *refs
):
    out_ref, dkv_ref, list_ref = refs[-3:]
    frames = kv_ref.shape[0]

    def unturn(frame, values):
        lower = values[:HALF]
        upper = values[HALF:]
        cosine = cos_ref[frame]
        sine = sin_ref[frame]
        return jnp.concatenate([lower * cosine + upper * sine, upper * cosine - lower * sine], axis=0)

    def visit(source, place, frame, count):
        query = x_ref[source, 2 * per_device + place]
        d_mix = d_mix_ref[source, place]
        blank = jnp.zeros_like(query)
        query_side = jnp.concatenate([query, blank], axis=0)
        d_mix_side = jnp.concatenate([blank, d_mix], axis=0)
        turned = jnp.concatenate([query, d_mix], axis=0).T
        first = lax.broadcasted_iota(jnp.int32, turned.shape, 1) < HEAD
        nothing = jnp.zeros_like(turned)
        both = jnp.concatenate(
            [jnp.where(first, turned, nothing), jnp.where(first, nothing, turned)], axis=0
        )
        lse = lse_ref[pl.ds(frame, 1), :]
        delta = jnp.sum(d_mix.astype(F32) * wide_ref[source, place], axis=0, keepdims=True)

        def block(other, own=False):
            key_value = kv_ref[other]
            scores = jnp.dot(key_value, query_side, preferred_element_type=F32)
            d_weights = jnp.dot(key_value, d_mix_side, preferred_element_type=F32)
            weights = jnp.exp(scores - lse)
            d_scores = (weights * (d_weights - delta)).astype(BF16)
            sides = jnp.concatenate([d_scores, weights.astype(BF16)], axis=1)
            d_both = jnp.dot(sides, both, preferred_element_type=F32)
            if own:
                dkv_ref[other] = d_both
            else:
                dkv_ref[other] += d_both
            key = x_ref[lax.div(other, per_device), lax.rem(other, per_device)]
            return jnp.dot(key, d_scores, preferred_element_type=F32)

        others = count - 1
        d_query = block(frame, True)
        d_query = lax.fori_loop(
            0,
            lax.div(others, 2),
            lambda index, state: state
            + block(list_ref[2 * index])
            + block(list_ref[2 * index + 1]),
            d_query,
        )
        d_query = lax.fori_loop(
            0,
            lax.rem(others, 2),
            lambda unused, state: state + block(list_ref[others - 1]),
            d_query,
        )
        d_query = unturn(frame, d_query * (HEAD**-0.5)).astype(BF16)
        out_ref[source, 2 * per_device + place] = d_query

    walk_frames(frames, per_device, segments_ref, live_ref, list_ref, visit)

    def finish(source, carry):
        for place in range(per_device):
            frame = source * per_device + place
            both = dkv_ref[frame].T
            out_ref[source, place] = unturn(frame, both[:HEAD]).astype(BF16)
            out_ref[source, per_device + place] = both[HEAD:].astype(BF16)
        return carry

    lax.fori_loop(0, frames // per_device, finish, 0)


def attend_back(per_device, segments, live, x, kv, wide, lse, d_mix, cosine, sine, orders):
    sources = x.shape[0]
    frames = sources * per_device
    pairs = frames * 6
    args = [segments, live, x, kv, wide, lse, d_mix, cosine, sine]
    specs = [scalar_spec(), scalar_spec()] + [whole_spec()] * (len(args) - 2)
    orders = corners(orders)
    return pl.pallas_call(
        functools.partial(attend_back_kernel, per_device),
        out_shape=jax.ShapeDtypeStruct(x.shape, BF16),
        in_specs=specs + [unread_spec()] * len(orders),
        out_specs=whole_spec(),
        scratch_shapes=[
            pltpu.VMEM((frames, PATCHES, 2 * HEAD), F32),
            pltpu.SMEM((frames,), jnp.int32),
        ],
        cost_estimate=pl.CostEstimate(
            flops=pairs * 10 * PATCHES * PATCHES * 256,
            bytes_accessed=x.size * 2 * 5,
            transcendentals=pairs * PATCHES * PATCHES,
        ),
        compiler_params=pltpu.CompilerParams(vmem_limit_bytes=60 << 20),
        name="attend_back",
    )(*args, *orders)


def exchange(value, axis, bit):
    count = lax.axis_size(axis)
    return lax.ppermute(value, axis, [(source, source ^ bit) for source in range(count)])


def after(value, *earlier):
    return lax.optimization_barrier((value,) + earlier)[0]


def of_packs(value):
    values = [value]
    bit = lax.axis_size("pack") // 2
    while bit:
        values = values + [exchange(each, "pack", bit) for each in values]
        bit //= 2
    return values


def halving_fits():
    return lax.axis_size("pack") == 2 and lax.axis_size("seq") == 16


class RowSum:
    def __init__(self, mine, came, order):
        self.order = list(order)
        self.index = lax.axis_index("seq")
        rows = mine.shape[-2]
        self.tail = (rows // 16, mine.shape[-1])
        self.lead = mine.shape[:-2]
        shape = self.lead + (2, 2, 2, 2) + self.tail
        self.parts = [mine.reshape(shape), came.reshape(shape)]

    def pick(self, bit, which):
        axis = len(self.lead) + {8: 0, 4: 1, 2: 2, 1: 3}[bit]
        pieces = [lax.dynamic_slice_in_dim(part, which, 1, axis) for part in self.parts]
        return (pieces[0].astype(F32) + pieces[1].astype(F32)).astype(BF16)

    def stage(self, later=()):
        bit = self.order.pop(0)
        own_bit = lax.rem(lax.div(self.index, bit), 2)
        send = self.pick(bit, 1 - own_bit)
        for each in later:
            send = each.tie(send)
        came = exchange(send, "seq", bit)
        self.parts = [self.pick(bit, own_bit), came]
        return send

    def tie(self, value):
        value, *self.parts = lax.optimization_barrier((value, *self.parts))
        return value

    def finish(self):
        while self.order:
            self.stage()
        own = (self.parts[0].astype(F32) + self.parts[1].astype(F32)).astype(BF16)
        own = own.reshape(self.lead + self.tail)
        return own, exchange(own, "pack", 1)


def settle_kernel(pack_ref, *refs):
    ups, downs, outs, firsts, seconds = [refs[2 * nth : 2 * nth + 2] for nth in range(5)]
    up_ref, down_ref, out_ref, qkv_ref = refs[10:]
    own_first = pack_ref[0] == 0
    small = 128

    def of_pack(pack, pair, *index):
        one, two = pair[0][index].astype(F32), pair[1][index].astype(F32)
        return jnp.where(own_first, one, two) if pack == 0 else jnp.where(own_first, two, one)

    every = slice(None)
    for pack in range(2):
        for group in range(ups[0].shape[1] // small):
            at = (2 * group + pack) * small
            columns = slice(group * small, (group + 1) * small)
            up_ref[:, at : at + small] = of_pack(pack, ups, every, columns)
        rows = downs[0].shape[0]
        down_ref[pack * rows : (pack + 1) * rows, :] = of_pack(pack, downs, every, every)
        columns = outs[0].shape[1]
        out_ref[:, pack * columns : (pack + 1) * columns] = of_pack(pack, outs, every, every)
        for kind in range(3):
            for nth, pair in enumerate((firsts, seconds)):
                columns = pair[0].shape[2]
                at = (4 * kind + 2 * pack + nth) * columns
                qkv_ref[:, at : at + columns] = of_pack(pack, pair, kind, every, every)


def settle(pack, *pairs):
    up, down, out, qkv = pairs[0][0], pairs[1][0], pairs[2][0], pairs[3][0]
    shapes = (
        (up.shape[0], 2 * up.shape[1]),
        (2 * down.shape[0], down.shape[1]),
        (out.shape[0], 2 * out.shape[1]),
        (qkv.shape[1], 12 * qkv.shape[2]),
    )
    args = [each for pair in pairs for each in pair]
    return pl.pallas_call(
        settle_kernel,
        out_shape=tuple(jax.ShapeDtypeStruct(shape, F32) for shape in shapes),
        in_specs=[scalar_spec()] + [whole_spec()] * len(args),
        out_specs=(whole_spec(),) * 4,
        compiler_params=pltpu.CompilerParams(vmem_limit_bytes=32 << 20),
        name="settle",
    )(pack.reshape(1), *args)


def row_sum_direct(term):
    part = lax.psum_scatter(term.astype(BF16), "seq", scatter_dimension=0, tiled=True)
    return lax.psum(part, "pack").astype(F32)


def project_kernel(
    per_device,
    hidden_ref,
    shift_ref,
    scale_ref,
    wq_ref,
    wk_ref,
    wv_ref,
    bq_ref,
    bk_ref,
    bv_ref,
    cos_ref,
    sin_ref,
    in_ref,
    x_ref,
):
    @pl.when(pl.program_id(0) == 0)
    def _():
        for place in range(per_device):
            rows = pl.ds(place * PATCHES, PATCHES)
            values = hidden_ref[rows, :].astype(F32)
            centered = values - jnp.mean(values, axis=-1, keepdims=True)
            spread = jnp.mean(centered * centered, axis=-1, keepdims=True)
            normed = centered * lax.rsqrt(spread + EPSILON)
            scale = scale_ref[pl.ds(place, 1), :]
            in_ref[rows, :] = (normed * (1.0 + scale) + shift_ref[pl.ds(place, 1), :]).astype(BF16)

    rows = in_ref[...]
    group = wq_ref.shape[1] // HEAD

    def turned(values, place):
        lower = values[:HALF]
        upper = values[HALF:]
        cosine = cos_ref[place]
        sine = sin_ref[place]
        return jnp.concatenate([lower * cosine - upper * sine, upper * cosine + lower * sine], axis=0)

    for kind, (weight_ref, bias_ref) in enumerate(
        ((wq_ref, bq_ref), (wk_ref, bk_ref), (wv_ref, bv_ref))
    ):
        flat = jnp.dot(rows, weight_ref[...], preferred_element_type=F32) + bias_ref[...]
        for place in range(per_device):
            block = flat[place * PATCHES : (place + 1) * PATCHES].T
            for head in range(group):
                values = block[head * HEAD : (head + 1) * HEAD]
                if kind == 0:
                    values = turned(values, place) * (HEAD**-0.5)
                    x_ref[head, 2 * per_device + place] = values.astype(BF16)
                elif kind == 1:
                    x_ref[head, place] = turned(values, place).astype(BF16)
                else:
                    x_ref[head, per_device + place] = values.astype(BF16)


def project(per_device, hidden, shift, scale, weight, bias, cosine, sine):
    tokens, width = hidden.shape
    heads = width // HEAD
    group = 2
    lanes = group * HEAD
    steps = heads // group
    bias_row = bias[None, :]

    def whole(shape):
        return pl.BlockSpec(shape, lambda step: (0,) * len(shape))

    def part(kind, rows):
        return pl.BlockSpec((rows, lanes), lambda step: (0, kind * steps + step))

    blocks = (heads, 3 * per_device, HEAD, PATCHES)
    return pl.pallas_call(
        functools.partial(project_kernel, per_device),
        grid=(steps,),
        out_shape=(
            jax.ShapeDtypeStruct((tokens, width), BF16),
            jax.ShapeDtypeStruct(blocks, BF16),
        ),
        in_specs=[whole((tokens, width)), whole(shift.shape), whole(scale.shape)]
        + [part(kind, width) for kind in range(3)]
        + [part(kind, 1) for kind in range(3)]
        + [whole(cosine.shape), whole(sine.shape)],
        out_specs=(
            whole((tokens, width)),
            pl.BlockSpec((group,) + blocks[1:], lambda step: (step, 0, 0, 0)),
        ),
        cost_estimate=pl.CostEstimate(
            flops=2 * tokens * width * 3 * width,
            bytes_accessed=2 * (weight.size + 5 * tokens * width),
            transcendentals=0,
        ),
        compiler_params=pltpu.CompilerParams(vmem_limit_bytes=40 << 20),
        name="project",
    )(hidden, shift, scale, weight, weight, weight, bias_row, bias_row, bias_row, cosine, sine)


GELU_SLOPE = 0.7978845608028654
GELU_CUBE = 0.044715


def feed_kernel(
    carried,
    which_ref,
    in_ref,
    d_out_ref,
    up_a_ref,
    up_b_ref,
    bias_a_ref,
    bias_b_ref,
    down_a_ref,
    down_b_ref,
    *refs
):
    if carried:
        out_before_ref, d_in_before_ref = refs[:2]
        refs = refs[2:]
    out_ref, d_in_ref, d_up_ref, d_down_ref, d_bias_ref, turned_ref = refs

    @pl.when(pl.program_id(0) == 0)
    def _():
        turned_ref[...] = in_ref[...].astype(F32).T.astype(BF16)
        if carried:
            out_ref[...] = out_before_ref[...]
            d_in_ref[...] = d_in_before_ref[...]
        else:
            out_ref[...] = jnp.zeros_like(out_ref)
            d_in_ref[...] = jnp.zeros_like(d_in_ref)

    up = jnp.concatenate([up_a_ref[...], up_b_ref[...]], axis=1)
    down = jnp.concatenate([down_a_ref[...], down_b_ref[...]], axis=0)
    bias = jnp.concatenate([bias_a_ref[...], bias_b_ref[...]], axis=1)
    d_out = d_out_ref[...]
    pre = jnp.dot(in_ref[...], up, preferred_element_type=F32) + bias
    d_act = dot_over(d_out, down, 1, 1)
    square = pre * pre
    bend = jnp.tanh(GELU_SLOPE * pre * (1.0 + GELU_CUBE * square))
    half = 0.5 * (1.0 + bend)
    act = (pre * half).astype(BF16)
    slope = half + (0.5 * GELU_SLOPE) * pre * (1.0 - bend * bend) * (
        1.0 + (3.0 * GELU_CUBE) * square
    )
    d_pre = (d_act * slope).astype(BF16)
    out_ref[...] += jnp.dot(act, down, preferred_element_type=F32)
    d_in_ref[...] += dot_over(d_pre, up, 1, 1)
    d_up_ref[...] = jnp.dot(turned_ref[...], d_pre, preferred_element_type=F32).astype(BF16)
    d_down_ref[...] = jnp.dot(
        act.astype(F32).T.astype(BF16), d_out, preferred_element_type=F32
    ).astype(BF16)
    d_bias_ref[...] = jnp.sum(d_pre.astype(F32), axis=0, keepdims=True)


def feed(which, feed_in, d_feed_out, up_weight, up_bias, down_weight, before):
    tokens, width = feed_in.shape
    hidden_units = up_weight.shape[1]
    small = 128
    steps = hidden_units // (4 * small)
    own = hidden_units // 2

    def whole(shape):
        return pl.BlockSpec(shape, lambda step, which: (0,) * len(shape))

    def group(nth):
        return lambda step, which: 2 * (2 * step + nth) + which[0]

    def columns(nth, rows):
        return pl.BlockSpec((rows, small), lambda step, which: (0, group(nth)(step, which)))

    def rows_of(nth):
        return pl.BlockSpec((small, width), lambda step, which: (group(nth)(step, which), 0))

    args = [feed_in, d_feed_out, up_weight, up_weight, up_bias[None], up_bias[None]]
    args += [down_weight, down_weight]
    specs = [whole((tokens, width)), whole((tokens, width)), columns(0, width), columns(1, width)]
    specs += [columns(0, 1), columns(1, 1), rows_of(0), rows_of(1)]
    if before is not None:
        args += list(before)
        specs += [whole((tokens, width)), whole((tokens, width))]
    return pl.pallas_call(
        functools.partial(feed_kernel, before is not None),
        grid_spec=pltpu.PrefetchScalarGridSpec(
            num_scalar_prefetch=1,
            grid=(steps,),
            in_specs=specs,
            out_specs=(
                whole((tokens, width)),
                whole((tokens, width)),
                pl.BlockSpec((width, 2 * small), lambda step, which: (0, step)),
                pl.BlockSpec((2 * small, width), lambda step, which: (step, 0)),
                pl.BlockSpec((1, 2 * small), lambda step, which: (0, step)),
            ),
            scratch_shapes=[pltpu.VMEM((width, tokens), BF16)],
        ),
        out_shape=(
            jax.ShapeDtypeStruct((tokens, width), F32),
            jax.ShapeDtypeStruct((tokens, width), F32),
            jax.ShapeDtypeStruct((width, own), BF16),
            jax.ShapeDtypeStruct((own, width), BF16),
            jax.ShapeDtypeStruct((1, own), F32),
        ),
        cost_estimate=pl.CostEstimate(
            flops=12 * tokens * width * own,
            bytes_accessed=2 * (4 * own * width + 8 * tokens * width),
            transcendentals=tokens * own,
        ),
        compiler_params=pltpu.CompilerParams(vmem_limit_bytes=56 << 20),
        name="feed%d" % (before is not None),
    )(which.reshape(1), *args)


def norm_back(values, d_in, scale):
    centered = values - jnp.mean(values, axis=-1, keepdims=True)
    spread = jnp.mean(centered * centered, axis=-1, keepdims=True)
    inverse = lax.rsqrt(spread + EPSILON)
    normed = centered * inverse
    product = d_in * normed
    d_shift = jnp.sum(d_in, axis=0, keepdims=True)
    d_scale = jnp.sum(product, axis=0, keepdims=True)
    scaled = 1.0 + scale
    mean_d = jnp.mean(d_in * scaled, axis=-1, keepdims=True)
    mean_p = jnp.mean(product * scaled, axis=-1, keepdims=True)
    return (d_in * scaled - mean_d - normed * mean_p) * inverse, d_shift, d_scale


def middle_back_kernel(
    d_in_ref,
    middle_ref,
    grad_ref,
    attn_ref,
    feed_ref,
    scale_ref,
    gate_ref,
    feed_gate_ref,
    down_bias_ref,
    rows_ref,
    weight_ref,
    d_middle_ref,
    d_attn_ref,
    layer_ref,
    blocks_ref,
    sums_ref,
):
    frame = pl.program_id(0)
    per_device = pl.num_programs(0) - 1

    @pl.when(frame < per_device)
    def _():
        mine = pl.ds(frame, 1)
        middle = middle_ref[...]
        grads = grad_ref[...].astype(F32)
        back, d_shift, d_scale = norm_back(middle, d_in_ref[...], scale_ref[mine, :])
        d_middle = grads + back
        d_middle_ref[...] = d_middle
        d_attn = (d_middle * gate_ref[mine, :]).astype(BF16)
        d_attn_ref[...] = d_attn
        feed_rows = feed_ref[...] + down_bias_ref[...]
        feed_gate = feed_gate_ref[mine, :]
        layer_ref[...] = (middle + feed_gate * feed_rows).astype(BF16)
        d_feed_out = (feed_gate * grads).astype(BF16).astype(F32)
        sums_ref[frame] = jnp.concatenate(
            [
                jnp.sum(d_middle * attn_ref[...], axis=0, keepdims=True),
                d_shift,
                d_scale,
                jnp.sum(grads * feed_rows, axis=0, keepdims=True),
                jnp.sum(d_attn.astype(F32), axis=0, keepdims=True),
                jnp.sum(d_feed_out, axis=0, keepdims=True),
                jnp.zeros((2, d_shift.shape[1]), F32),
            ],
            axis=0,
        )
        d_mix = dot_over(weight_ref[...], d_attn, 1, 1).astype(BF16)
        for head in range(blocks_ref.shape[0]):
            blocks_ref[head, 0] = d_mix[head * HEAD : (head + 1) * HEAD]

    @pl.when(frame == per_device)
    def _():
        first = sums_ref[0]
        second = sums_ref[1]
        rows = jnp.concatenate(
            [first[:4], second[:4], first[4:6] + second[4:6], rows_ref[...]], axis=0
        ).astype(BF16)
        count = rows.shape[1] // PATCHES
        block = jnp.concatenate(
            [rows[:, nth * PATCHES : (nth + 1) * PATCHES] for nth in range(count)], axis=0
        )
        for head in range(blocks_ref.shape[0]):
            blocks_ref[head, 0] = block


def middle_back(
    per_device, d_in, middle, grads, attn_rows, feed_rows, scale, gate, feed_gate, down_bias, rows, weight
):
    tokens, width = d_in.shape
    heads = width // HEAD
    last = per_device - 1
    per_frame = pl.BlockSpec((PATCHES, width), lambda frame: (jnp.minimum(frame, last), 0))

    def whole(shape):
        return pl.BlockSpec(shape, lambda frame: (0,) * len(shape))

    small = whole((per_device, width))
    return pl.pallas_call(
        middle_back_kernel,
        grid=(per_device + 1,),
        out_shape=(
            jax.ShapeDtypeStruct((tokens, width), F32),
            jax.ShapeDtypeStruct((tokens, width), BF16),
            jax.ShapeDtypeStruct((tokens, width), BF16),
            jax.ShapeDtypeStruct((heads, per_device + 1, HEAD, PATCHES), BF16),
        ),
        in_specs=[per_frame] * 5
        + [small] * 3
        + [whole((1, width)), whole(rows.shape), whole(weight.shape)],
        out_specs=(
            per_frame,
            per_frame,
            per_frame,
            pl.BlockSpec((heads, 1, HEAD, PATCHES), lambda frame: (0, frame, 0, 0)),
        ),
        scratch_shapes=[pltpu.VMEM((per_device, 8, width), F32)],
        cost_estimate=pl.CostEstimate(
            flops=2 * tokens * width * width, bytes_accessed=24 * tokens * width, transcendentals=0
        ),
        compiler_params=pltpu.CompilerParams(vmem_limit_bytes=48 << 20),
        name="middle_back",
    )(
        d_in,
        middle,
        grads,
        attn_rows,
        feed_rows,
        scale,
        gate,
        feed_gate,
        down_bias[None],
        rows,
        weight,
    )


def unproject_kernel(
    per_device, carried, which_ref, in_ref, back_ref, wq_ref, wk_ref, wv_ref, *refs
):
    if not carried:
        refs = refs[-4:]
    if carried:
        before_ref, hidden_ref, d_middle_ref, scale_ref, bias_theirs_ref = refs[:5]
        d_weight_ref, grad_ref, rows_ref, d_in_ref, d_bias_ref, turned_ref = refs[5:]
    else:
        d_in_ref, d_weight_ref, d_bias_ref, turned_ref = refs

    @pl.when(pl.program_id(0) == 0)
    def _():
        turned_ref[...] = in_ref[...].astype(F32).T.astype(BF16)
        if carried:
            d_in_ref[...] = before_ref[...]
        else:
            d_in_ref[...] = jnp.zeros_like(d_in_ref)

    group = wq_ref.shape[1] // HEAD

    def token_major(block_of):
        rows = []
        for place in range(per_device):
            block = jnp.concatenate([block_of(head, place) for head in range(group)], axis=0)
            rows.append(block.astype(F32).T.astype(BF16))
        return jnp.concatenate(rows, axis=0)

    sides = jnp.concatenate(
        [
            token_major(lambda head, place: back_ref[head, 2 * per_device + place]),
            token_major(lambda head, place: back_ref[head, place]),
            token_major(lambda head, place: back_ref[head, per_device + place]),
        ],
        axis=1,
    )
    weights = jnp.concatenate([wq_ref[...], wk_ref[...], wv_ref[...]], axis=1)
    d_in_ref[...] += dot_over(sides, weights, 1, 1)
    d_weight = jnp.dot(turned_ref[...], sides, preferred_element_type=F32).astype(BF16)
    d_bias = jnp.sum(sides.astype(F32), axis=0, keepdims=True)
    lanes = group * HEAD
    for kind in range(3):
        d_weight_ref[kind] = d_weight[:, kind * lanes : (kind + 1) * lanes]
        part = d_bias[:, kind * lanes : (kind + 1) * lanes]
        if carried:
            start = pl.multiple_of(pl.program_id(0) * lanes, lanes)
            d_bias_ref[pl.ds(kind, 1), pl.ds(start, lanes)] = part
        else:
            d_bias_ref[kind] = part

    if carried:

        @pl.when(pl.program_id(0) == pl.num_programs(0) - 1)
        def _():
            sums = []
            for place in range(per_device):
                rows = pl.ds(place * PATCHES, PATCHES)
                mine = pl.ds(place, 1)
                back, d_shift, d_scale = norm_back(
                    hidden_ref[rows, :].astype(F32), d_in_ref[rows, :], scale_ref[mine, :]
                )
                grad_ref[rows, :] = (d_middle_ref[rows, :] + back).astype(BF16)
                sums += [d_shift, d_scale]
            for kind in range(3):
                sums.append(
                    jnp.concatenate([d_bias_ref[pl.ds(kind, 1), :], bias_theirs_ref[kind]], axis=1)
                )
            count = 16 - len(sums)
            late = jnp.concatenate(
                sums + [jnp.zeros((count, d_in_ref.shape[1]), F32)], axis=0
            ).astype(BF16)
            for target in range(rows_ref.shape[0]):
                rows_ref[target] = late


def unproject(per_device, targets, which, attn_in, back, weight, orders, before=None, norm_args=()):
    tokens, width = attn_in.shape
    heads = width // HEAD
    group = 2
    lanes = group * HEAD
    groups = heads // group
    steps = groups // 2

    def whole(shape):
        return pl.BlockSpec(shape, lambda step, which: (0,) * len(shape))

    def blocks(array):
        return pl.BlockSpec(
            (group,) + array.shape[1:], lambda step, which: (which[0] * steps + step, 0, 0, 0)
        )

    def part(kind):
        return pl.BlockSpec(
            (width, lanes), lambda step, which: (0, kind * groups + which[0] * steps + step)
        )

    args = [attn_in, back, weight, weight, weight]
    specs = [whole((tokens, width)), blocks(back), part(0), part(1), part(2)]
    weight_shape = (
        jax.ShapeDtypeStruct((3, width, width // 2), BF16),
        jax.ShapeDtypeStruct((3, 1, width // 2), F32),
    )
    weight_specs = (
        pl.BlockSpec((3, width, lanes), lambda step, which: (0, 0, step)),
        pl.BlockSpec((3, 1, lanes), lambda step, which: (0, 0, step)),
    )
    scratch = [pltpu.VMEM((width, tokens), BF16)]
    small = (per_device, width)
    if before is not None:
        args += [before] + list(norm_args)
        specs += [whole((tokens, width))] * 3 + [whole(small), whole((3, 1, width // 2))]
        late = (targets, 16, width)
        outs = weight_shape[:1] + (
            jax.ShapeDtypeStruct((tokens, width), BF16),
            jax.ShapeDtypeStruct(late, BF16),
        )
        out_specs = weight_specs[:1] + (whole((tokens, width)), whole(late))
        scratch = [pltpu.VMEM((tokens, width), F32), pltpu.VMEM((3, width // 2), F32)] + scratch
    else:
        outs = (jax.ShapeDtypeStruct((tokens, width), F32),) + weight_shape
        out_specs = (whole((tokens, width)),) + weight_specs
        orders = corners(orders)
        args += orders
        specs += [unread_spec()] * len(orders)
    return pl.pallas_call(
        functools.partial(unproject_kernel, per_device, before is not None),
        grid_spec=pltpu.PrefetchScalarGridSpec(
            num_scalar_prefetch=1,
            grid=(steps,),
            in_specs=specs,
            out_specs=out_specs,
            scratch_shapes=scratch,
        ),
        out_shape=outs,
        cost_estimate=pl.CostEstimate(
            flops=6 * tokens * width * width,
            bytes_accessed=2 * (3 * width * width + 6 * tokens * width),
            transcendentals=0,
        ),
        compiler_params=pltpu.CompilerParams(vmem_limit_bytes=48 << 20),
        name="unproject%d" % (before is not None),
    )(which.reshape(1), *args)


def columns_of(matrix, start, width, axis=1):
    if isinstance(start, int) and start == 0 and width == matrix.shape[axis]:
        return matrix
    return lax.dynamic_slice_in_dim(matrix, start, width, axis)


def local(
    hidden,
    cotangent,
    levels,
    segments,
    live_frames,
    noise_table,
    mod_weight,
    mod_bias,
    qkv_weight,
    qkv_bias,
    out_weight,
    out_bias,
    up_weight,
    up_bias,
    down_weight,
    down_bias,
):
    seq_index = lax.axis_index("seq")
    seq_count = lax.axis_size("seq")
    tokens = hidden.shape[1]
    width = hidden.shape[2]
    per_device = tokens // PATCHES
    frames = segments.shape[1]
    heads = width // HEAD
    copies = seq_count // heads
    hidden_units = up_weight.shape[1]
    level_count = noise_table.shape[0]
    share = width // seq_count
    clip_ids = segments[0]
    live = live_frames[0]

    pack = lax.axis_index("pack")
    halves = halving_fits()
    frame_ids = jnp.arange(frames, dtype=jnp.int32)
    same_clip = clip_ids[:, None] == clip_ids[None, :]
    clip_starts = jnp.min(jnp.where(same_clip, frame_ids[None, :], frames), axis=1)
    frame_times = (frame_ids - clip_starts).astype(F32)
    own_cos, own_sin = rotary_tables(
        lax.dynamic_slice_in_dim(frame_times, seq_index * per_device, per_device)
    )

    embed = jnp.concatenate(
        [
            lax.dynamic_slice_in_dim(noise_table, levels[0, frame], 1, 0)
            for frame in range(per_device)
        ],
        axis=0,
    )
    cond = jax.nn.silu(embed).astype(BF16)
    modulation = jnp.dot(cond, mod_weight[:, : 2 * width], preferred_element_type=F32)
    attn_shift, attn_scale = jnp.split(modulation + mod_bias[: 2 * width], 2, axis=1)
    attn_in, sent = project(
        per_device, hidden[0], attn_shift, attn_scale, qkv_weight, qkv_bias, own_cos, own_sin
    )

    def to_heads(array):
        if copies > 1:
            array = jnp.concatenate([array] * copies, axis=0)
        return lax.all_to_all(array, "seq", 0, 0, tiled=True)

    def to_tokens(array):
        return lax.all_to_all(array, "seq", 0, 0, tiled=True)[:heads]

    x = to_heads(sent)
    late_modulation = jnp.dot(
        after(cond, attn_in), mod_weight[:, 2 * width :], preferred_element_type=F32
    )
    attn_gate, feed_shift, feed_scale, feed_gate = jnp.split(
        late_modulation + mod_bias[2 * width :], 4, axis=1
    )
    cos_all, sin_all = rotary_tables(after(frame_times, attn_in))
    grad_rows = cotangent[0].astype(F32).reshape(per_device, PATCHES, width)
    d_feed_out = (feed_gate[:, None, :] * grad_rows).reshape(tokens, width).astype(BF16)
    x, d_feed_out, cos_all, sin_all = lax.optimization_barrier((x, d_feed_out, cos_all, sin_all))
    mix, wide, lse, kv = attend(per_device, clip_ids, live, x)
    mix = to_tokens(mix)
    mixes = [mix[:, place].reshape(width, PATCHES) for place in range(per_device)]
    attn_rows = jnp.stack([dot_over(each, out_weight, 0, 0) for each in mixes]) + out_bias
    attn_mix = jnp.concatenate(mixes, axis=1)

    frame_rows = hidden[0].astype(F32).reshape(per_device, PATCHES, width)
    middle = frame_rows + attn_gate[:, None, :] * attn_rows
    feed_in = modulate_norm(middle, feed_shift, feed_scale).reshape(tokens, width).astype(BF16)
    feed_args = (feed_in, d_feed_out, up_weight, up_bias, down_weight)
    theirs = feed(1 - pack if halves else pack * 0 + 1, *feed_args, None)
    mine = feed(pack if halves else pack * 0, *feed_args, theirs[:2])
    small = 128

    def in_order(own, other):
        if halves:
            even, odd = jnp.where(pack == 0, own, other), jnp.where(pack == 0, other, own)
        else:
            even, odd = own, other
        rows = own.shape[0]
        return jnp.stack(
            [even.reshape(rows, -1, small), odd.reshape(rows, -1, small)], axis=2
        ).reshape(rows, -1)

    own_levels = levels[0]
    level_row = jnp.concatenate(
        [
            jnp.broadcast_to(part[frame], (width // (2 * per_device),))
            for frame in range(per_device)
            for part in (lax.div(own_levels, 32), lax.rem(own_levels, 32))
        ]
    ).astype(F32)[None]
    extra_rows = jnp.concatenate(
        [
            in_order(mine[4], theirs[4]).reshape(-1, width),
            level_row,
            jnp.zeros((1, width), F32),
        ],
        axis=0,
    )
    d_middle, d_attn_out, layer_out, blocks = middle_back(
        per_device,
        mine[1],
        middle.reshape(tokens, width),
        cotangent[0],
        attn_rows.reshape(tokens, width),
        mine[0],
        feed_scale,
        attn_gate,
        feed_gate,
        down_bias,
        extra_rows,
        out_weight,
    )
    layer_out = layer_out.reshape(1, tokens, width)
    d_mix = to_heads(blocks)

    def out_term(start, size):
        return dot_over(attn_mix, columns_of(d_attn_out, start, size), 1, 0).astype(BF16)

    sums = ()
    if halves:
        up_sum = RowSum(mine[2], exchange(theirs[2], "pack", 1), (2, 1, 4, 8))
        down_sum = RowSum(mine[3], exchange(theirs[3], "pack", 1), (1, 2, 4, 8))
        out_theirs = exchange(out_term((1 - pack) * (width // 2), width // 2), "pack", 1)
        out_sum = RowSum(out_term(pack * (width // 2), width // 2), out_theirs, (1, 2, 4, 8))
        sums = (down_sum, up_sum)
    def own_share(row):
        piece = row.shape[0] // seq_count
        return lax.dynamic_slice_in_dim(row, seq_index * piece, piece)

    chunks = width // PATCHES
    early_rows = d_mix[:, per_device].reshape(seq_count, chunks, 16, PATCHES)
    early_rows = early_rows.transpose(0, 2, 1, 3).reshape(seq_count, 16, width)
    early_sets = of_packs(early_rows)
    early_sum = functools.reduce(
        jnp.add, [jnp.sum(each.astype(F32), axis=0) for each in early_sets]
    )
    out_bias_grad = own_share(early_sum[8])
    down_bias_grad = own_share(early_sum[9])
    up_bias_grad = own_share(early_sum[10:14].reshape(hidden_units))

    def frames_of(rows, per_frame, kinds):
        return jnp.concatenate(
            [
                jnp.stack(
                    [rows[:, frame * per_frame + kind] for frame in range(per_device)], axis=1
                ).reshape(-1, width)
                for kind in range(kinds)
            ],
            axis=1,
        )

    own_table = lax.dynamic_slice_in_dim(noise_table, seq_index * share, share, 1)
    own_mod = lax.dynamic_slice_in_dim(mod_weight, seq_index * share, share, 0)
    stride = width // (2 * per_device)
    parts = []
    for rows in early_sets:
        coded = rows[:, 14, ::stride].astype(jnp.int32).reshape(-1, 2)
        set_levels = coded[:, 0] * 32 + coded[:, 1]
        picks = (set_levels[:, None] == jnp.arange(level_count, dtype=jnp.int32)[None, :]).astype(F32)
        embeds = jnp.dot(picks, own_table, precision=PRECISE, preferred_element_type=F32)
        set_cond = jax.nn.silu(embeds).astype(BF16)
        d_mod = frames_of(rows, 4, 4)
        parts.append(
            (
                picks,
                embeds,
                set_cond,
                dot_over(d_mod, own_mod[:, 2 * width :], 1, 1),
                dot_over(set_cond, d_mod, 0, 0),
            )
        )
    mod_grad_early = functools.reduce(jnp.add, [each[4] for each in parts])
    mod_sum_early = (early_sum[:4] + early_sum[4:8]).reshape(4 * width)
    orders = [each.stage() for each in sums]
    result = attend_back(
        per_device, clip_ids, live, x, kv, wide, lse, d_mix, cos_all, sin_all, orders
    )
    if halves:
        for each in sums:
            result = each.tie(result)
        result = out_sum.tie(result)
    back = to_tokens(result)
    orders = []
    if halves:
        for each in (up_sum, down_sum, out_sum):
            each.stage()
        orders = [each.stage() for each in (up_sum, down_sum, out_sum)]
    orders += [mod_grad_early] + [part[3] for part in parts]
    which = (1 - pack, pack) if halves else (pack * 0, pack * 0 + 1)
    d_in_theirs, qkv_theirs, bias_theirs = unproject(
        per_device, seq_count, which[0], attn_in, back, qkv_weight, orders
    )
    qkv_mine, hidden_grad, late = unproject(
        per_device,
        seq_count,
        which[1],
        attn_in,
        back,
        qkv_weight,
        (),
        d_in_theirs,
        (hidden[0], d_middle, attn_scale, bias_theirs),
    )
    hidden_grad = hidden_grad.reshape(1, tokens, width)
    late_rows = lax.all_to_all(late, "seq", 0, 0, tiled=True)

    def halves_in_order(own, other):
        if halves:
            return jnp.where(pack == 0, own, other), jnp.where(pack == 0, other, own)
        return other, own

    if halves:
        came = exchange(qkv_theirs, "pack", 1)
        split = width // 4
        qkv_sums = [
            RowSum(qkv_mine[..., :split], came[..., :split], (1, 2, 4, 8)),
            RowSum(qkv_mine[..., split:], came[..., split:], (2, 1, 4, 8)),
        ]
        for each in qkv_sums:
            each.stage((up_sum, down_sum, out_sum))
        up_weight_grad, down_weight_grad, out_weight_grad, qkv_weight_grad = settle(
            pack, *[each.finish() for each in (up_sum, down_sum, out_sum, *qkv_sums)]
        )
    else:
        up_weight_grad = row_sum_direct(in_order(mine[2], theirs[2]))
        pairs = [each[3].reshape(-1, small, width) for each in (mine, theirs)]
        down_weight_grad = row_sum_direct(jnp.stack(pairs, axis=1).reshape(hidden_units, width))
        out_weight_grad = row_sum_direct(out_term(0, width))
        qkv_term = jnp.concatenate(halves_in_order(qkv_mine, qkv_theirs), axis=-1)
        qkv_weight_grad = row_sum_direct(qkv_term.transpose(1, 0, 2).reshape(width, 3 * width))

    late_sets = of_packs(late_rows[:, :8])
    bias_at = 2 * per_device
    bias_sums = [
        jnp.sum(rows[:, bias_at : bias_at + 3].astype(F32), axis=0) for rows in late_sets
    ]
    if halves:
        ones, twos = bias_sums
        half = width // 2
        own_half = ones[:, :half] + twos[:, half:]
        other_half = ones[:, half:] + twos[:, :half]
    else:
        total = functools.reduce(jnp.add, bias_sums)
        own_half, other_half = total[:, : width // 2], total[:, width // 2 :]
    bias_total = jnp.concatenate(halves_in_order(own_half, other_half), axis=1)
    qkv_bias_grad = own_share(bias_total.reshape(3 * width))
    late_mods = [frames_of(rows, 2, 2) for rows in late_sets]
    mod_sum_late = functools.reduce(
        jnp.add, [jnp.sum(each.astype(F32), axis=0) for each in late_mods]
    )
    d_embeds = []
    for part, d_mod in zip(parts, late_mods):
        d_cond = part[3] + dot_over(d_mod, own_mod[:, : 2 * width], 1, 1)
        d_embeds.append(jax.vjp(jax.nn.silu, part[1])[1](d_cond)[0])
    table_grad = lax.dot_general(
        jnp.concatenate([part[0] for part in parts], axis=0),
        jnp.concatenate(d_embeds, axis=0),
        (((0,), (0,)), ((), ())),
        precision=PRECISE,
        preferred_element_type=F32,
    )
    mod_grad_late = functools.reduce(
        jnp.add, [dot_over(part[2], d_mod, 0, 0) for part, d_mod in zip(parts, late_mods)]
    )
    mod_weight_grad = jnp.concatenate([mod_grad_late, mod_grad_early], axis=1)
    mod_bias_grad = own_share(jnp.concatenate([mod_sum_late, mod_sum_early]))
    return (
        layer_out,
        hidden_grad,
        table_grad,
        mod_weight_grad,
        mod_bias_grad,
        qkv_weight_grad,
        qkv_bias_grad,
        out_weight_grad,
        out_bias_grad,
        up_weight_grad,
        up_bias_grad,
        down_weight_grad,
        down_bias_grad,
    )


def solution(mesh):
    in_specs = (
        P("pack", "seq", None),
        P("pack", "seq", None),
        P("pack", "seq"),
        P("pack", None),
        P("pack", None),
    ) + (P(),) * 11
    out_specs = (
        P("pack", "seq", None),
        P("pack", "seq", None),
        P(None, "seq"),
        P("seq", None),
        P("seq"),
        P("seq", None),
        P("seq"),
        P("seq", None),
        P("seq"),
        P("seq", None),
        P("seq"),
        P("seq", None),
        P("seq"),
    )
    return jax.shard_map(local, mesh=mesh, in_specs=in_specs, out_specs=out_specs, check_vma=False)
```

```python
import functools

import jax
import jax.numpy as jnp
from jax import lax
from jax.experimental import pallas as pl
from jax.experimental.pallas import tpu as pltpu
from jax.sharding import PartitionSpec as P

HEAD = 64
PATCHES = 256
SIDE = 16
EPSILON = 1e-06
PRECISE = lax.Precision.HIGHEST
HALF = HEAD // 2
F32 = jnp.float32
BF16 = jnp.bfloat16


def modulate_norm(rows, shift, scale):
    center = jnp.mean(rows, axis=-1, keepdims=True)
    centered = rows - center
    spread = jnp.mean(centered * centered, axis=-1, keepdims=True)
    normed = centered * lax.rsqrt(spread + EPSILON)
    return normed * (1.0 + scale[:, None, :]) + shift[:, None, :]


def gelu_tanh(values):
    return jax.nn.gelu(values, approximate=True)


def dot_over(first, second, first_dim, second_dim):
    return lax.dot_general(
        first, second, (((first_dim,), (second_dim,)), ((), ())), preferred_element_type=F32
    )


def spatial_angles():
    time_pairs = HALF // 4
    space_pairs = (HALF - time_pairs) // 2
    patch = jnp.arange(PATCHES, dtype=jnp.int32)
    row_pos = (patch // SIDE).astype(F32)
    col_pos = (patch % SIDE).astype(F32)
    time_freq = 10000.0 ** (-jnp.arange(time_pairs, dtype=F32) / time_pairs)
    space_freq = 10000.0 ** (-jnp.arange(space_pairs, dtype=F32) / space_pairs)
    space = jnp.concatenate(
        [space_freq[:, None] * row_pos[None, :], space_freq[:, None] * col_pos[None, :]], axis=0
    )
    return time_freq, space


def rotary_tables(time_frames):
    time_freq, space = spatial_angles()
    count = time_frames.shape[0]
    time_angle = time_frames[:, None] * time_freq[None, :]

    def whole(function):
        return jnp.concatenate(
            [
                jnp.broadcast_to(
                    function(time_angle)[:, :, None], (count, time_freq.shape[0], PATCHES)
                ),
                jnp.broadcast_to(function(space)[None], (count,) + space.shape),
            ],
            axis=1,
        )

    return whole(jnp.cos), whole(jnp.sin)


def walk_frames(frames, per_device, segments_ref, live_ref, list_ref, visit):
    def step(source, held):
        for place in range(per_device):
            frame = source * per_device + place
            before = jnp.maximum(frame - 1, 0)
            fresh = (frame == 0) | (segments_ref[frame] != segments_ref[before])
            held = jnp.where(fresh, 0, held)
            list_ref[held] = frame
            visit(source, place, frame, held + 1)
            held = held + jnp.where(live_ref[frame] == 1, 1, 0)
        return held

    lax.fori_loop(0, frames // per_device, step, jnp.int32(0))


def attend_kernel(per_device, segments_ref, live_ref, x_ref, mix_ref, wide_ref, lse_ref, kv_ref, list_ref):
    frames = kv_ref.shape[0]

    def turn(source, carry):
        for place in range(per_device):
            both = jnp.concatenate(
                [x_ref[source, place], x_ref[source, per_device + place]], axis=0
            )
            kv_ref[source * per_device + place] = both.T
        return carry

    lax.fori_loop(0, frames // per_device, turn, 0)

    def visit(source, place, frame, count):
        query = x_ref[source, 2 * per_device + place]
        query_side = jnp.concatenate([query, jnp.zeros_like(query)], axis=0)

        def scores_of(other):
            return jnp.dot(kv_ref[other], query_side, preferred_element_type=F32)

        def mixed(other, weights):
            value = x_ref[lax.div(other, per_device), per_device + lax.rem(other, per_device)]
            return jnp.dot(value, weights.astype(BF16), preferred_element_type=F32)

        def join(others, carry):
            scores = [scores_of(other) for other in others]
            tops = [jnp.max(score, axis=0, keepdims=True) for score in scores]
            new_top = functools.reduce(jnp.maximum, tops)
            if carry is not None:
                top, total, accum = carry
                new_top = jnp.maximum(top, new_top)
                shrink = jnp.exp(top - new_top)
                total = total * shrink
                accum = accum * shrink
            for index, score in enumerate(scores):
                weights = jnp.exp(score - new_top)
                added = jnp.sum(weights, axis=0, keepdims=True)
                product = mixed(others[index], weights)
                if carry is None and index == 0:
                    total, accum = added, product
                else:
                    total, accum = total + added, accum + product
            return new_top, total, accum

        others = count - 1
        carry = join([frame], None)
        carry = lax.fori_loop(
            0,
            lax.div(others, 4),
            lambda index, state: join([list_ref[4 * index + nth] for nth in range(4)], state),
            carry,
        )
        carry = lax.fori_loop(
            lax.div(others, 4) * 2,
            lax.div(others, 2),
            lambda index, state: join([list_ref[2 * index], list_ref[2 * index + 1]], state),
            carry,
        )
        top, total, accum = lax.fori_loop(
            0,
            lax.rem(others, 2),
            lambda unused, state: join([list_ref[others - 1]], state),
            carry,
        )
        result = accum * (1.0 / total)
        wide_ref[source, place] = result
        mix_ref[source, place] = result.astype(BF16)
        lse_ref[pl.ds(frame, 1), :] = top + jnp.log(total)

    walk_frames(frames, per_device, segments_ref, live_ref, list_ref, visit)


def corners(values):
    return [each.reshape(-1, each.shape[-1])[:1, :128] for each in values]


def unread_spec():
    return pl.BlockSpec(memory_space=pl.ANY)


def whole_spec():
    return pl.BlockSpec(memory_space=pltpu.VMEM)


def scalar_spec():
    return pl.BlockSpec(memory_space=pltpu.SMEM)


def attend(per_device, segments, live, x):
    sources = x.shape[0]
    frames = sources * per_device
    pairs = frames * 6
    outs = (
        jax.ShapeDtypeStruct((sources, per_device, HEAD, PATCHES), BF16),
        jax.ShapeDtypeStruct((sources, per_device, HEAD, PATCHES), F32),
        jax.ShapeDtypeStruct((frames, PATCHES), F32),
        jax.ShapeDtypeStruct((frames, PATCHES, 2 * HEAD), BF16),
    )
    return pl.pallas_call(
        functools.partial(attend_kernel, per_device),
        out_shape=outs,
        in_specs=[scalar_spec(), scalar_spec(), whole_spec()],
        out_specs=(whole_spec(),) * len(outs),
        scratch_shapes=[pltpu.SMEM((frames,), jnp.int32)],
        cost_estimate=pl.CostEstimate(
            flops=pairs * 4 * PATCHES * PATCHES * 256,
            bytes_accessed=x.size * 2 * 3,
            transcendentals=pairs * PATCHES * PATCHES,
        ),
        compiler_params=pltpu.CompilerParams(vmem_limit_bytes=40 << 20),
        name="attend",
    )(segments, live, x)


def attend_back_kernel(
    per_device,
    segments_ref,
    live_ref,
    x_ref,
    kv_ref,
    wide_ref,
    lse_ref,
    d_mix_ref,
    cos_ref,
    sin_ref,
    *refs
):
    out_ref, dkv_ref, list_ref = refs[-3:]
    frames = kv_ref.shape[0]

    def unturn(frame, values):
        lower = values[:HALF]
        upper = values[HALF:]
        cosine = cos_ref[frame]
        sine = sin_ref[frame]
        return jnp.concatenate([lower * cosine + upper * sine, upper * cosine - lower * sine], axis=0)

    def visit(source, place, frame, count):
        query = x_ref[source, 2 * per_device + place]
        d_mix = d_mix_ref[source, place]
        blank = jnp.zeros_like(query)
        query_side = jnp.concatenate([query, blank], axis=0)
        d_mix_side = jnp.concatenate([blank, d_mix], axis=0)
        turned = jnp.concatenate([query, d_mix], axis=0).T
        first = lax.broadcasted_iota(jnp.int32, turned.shape, 1) < HEAD
        nothing = jnp.zeros_like(turned)
        both = jnp.concatenate(
            [jnp.where(first, turned, nothing), jnp.where(first, nothing, turned)], axis=0
        )
        lse = lse_ref[pl.ds(frame, 1), :]
        delta = jnp.sum(d_mix.astype(F32) * wide_ref[source, place], axis=0, keepdims=True)

        def block(other, own=False):
            key_value = kv_ref[other]
            scores = jnp.dot(key_value, query_side, preferred_element_type=F32)
            d_weights = jnp.dot(key_value, d_mix_side, preferred_element_type=F32)
            weights = jnp.exp(scores - lse)
            d_scores = (weights * (d_weights - delta)).astype(BF16)
            sides = jnp.concatenate([d_scores, weights.astype(BF16)], axis=1)
            d_both = jnp.dot(sides, both, preferred_element_type=F32)
            if own:
                dkv_ref[other] = d_both
            else:
                dkv_ref[other] += d_both
            key = x_ref[lax.div(other, per_device), lax.rem(other, per_device)]
            return jnp.dot(key, d_scores, preferred_element_type=F32)

        others = count - 1
        d_query = block(frame, True)
        d_query = lax.fori_loop(
            0,
            lax.div(others, 2),
            lambda index, state: state
            + block(list_ref[2 * index])
            + block(list_ref[2 * index + 1]),
            d_query,
        )
        d_query = lax.fori_loop(
            0,
            lax.rem(others, 2),
            lambda unused, state: state + block(list_ref[others - 1]),
            d_query,
        )
        d_query = unturn(frame, d_query * (HEAD**-0.5)).astype(BF16)
        out_ref[source, 2 * per_device + place] = d_query

    walk_frames(frames, per_device, segments_ref, live_ref, list_ref, visit)

    def finish(source, carry):
        for place in range(per_device):
            frame = source * per_device + place
            both = dkv_ref[frame].T
            out_ref[source, place] = unturn(frame, both[:HEAD]).astype(BF16)
            out_ref[source, per_device + place] = both[HEAD:].astype(BF16)
        return carry

    lax.fori_loop(0, frames // per_device, finish, 0)


def attend_back(per_device, segments, live, x, kv, wide, lse, d_mix, cosine, sine, orders):
    sources = x.shape[0]
    frames = sources * per_device
    pairs = frames * 6
    args = [segments, live, x, kv, wide, lse, d_mix, cosine, sine]
    specs = [scalar_spec(), scalar_spec()] + [whole_spec()] * (len(args) - 2)
    orders = corners(orders)
    return pl.pallas_call(
        functools.partial(attend_back_kernel, per_device),
        out_shape=jax.ShapeDtypeStruct(x.shape, BF16),
        in_specs=specs + [unread_spec()] * len(orders),
        out_specs=whole_spec(),
        scratch_shapes=[
            pltpu.VMEM((frames, PATCHES, 2 * HEAD), F32),
            pltpu.SMEM((frames,), jnp.int32),
        ],
        cost_estimate=pl.CostEstimate(
            flops=pairs * 10 * PATCHES * PATCHES * 64,
            bytes_accessed=x.size * 2 * 5,
            transcendentals=pairs * PATCHES * PATCHES,
        ),
        compiler_params=pltpu.CompilerParams(vmem_limit_bytes=60 << 20),
        name="attend_back",
    )(*args, *orders)


def exchange(value, axis, bit):
    count = lax.axis_size(axis)
    return lax.ppermute(value, axis, [(source, source ^ bit) for source in range(count)])


def after(value, *earlier):
    return lax.optimization_barrier((value,) + earlier)[0]


def of_packs(value):
    values = [value]
    bit = lax.axis_size("pack") // 2
    while bit:
        values = values + [exchange(each, "pack", bit) for each in values]
        bit //= 2
    return values


def halving_fits():
    return lax.axis_size("pack") == 2 and lax.axis_size("seq") == 16


class RowSum:
    def __init__(self, mine, came, order):
        self.order = list(order)
        self.index = lax.axis_index("seq")
        rows = mine.shape[-2]
        self.tail = (rows // 16, mine.shape[-1])
        self.lead = mine.shape[:-2]
        shape = self.lead + (2, 2, 2, 2) + self.tail
        self.parts = [mine.reshape(shape), came.reshape(shape)]

    def pick(self, bit, which):
        axis = len(self.lead) + {8: 0, 4: 1, 2: 2, 1: 3}[bit]
        pieces = [lax.dynamic_slice_in_dim(part, which, 1, axis) for part in self.parts]
        return (pieces[0].astype(F32) + pieces[1].astype(F32)).astype(BF16)

    def stage(self, later=()):
        bit = self.order.pop(0)
        own_bit = lax.rem(lax.div(self.index, bit), 2)
        send = self.pick(bit, 1 - own_bit)
        for each in later:
            send = each.tie(send)
        came = exchange(send, "seq", bit)
        self.parts = [self.pick(bit, own_bit), came]
        return send

    def tie(self, value):
        value, *self.parts = lax.optimization_barrier((value, *self.parts))
        return value

    def finish(self):
        while self.order:
            self.stage()
        own = (self.parts[0].astype(F32) + self.parts[1].astype(F32)).astype(BF16)
        own = own.reshape(self.lead + self.tail)
        return own, exchange(own, "pack", 1)


def settle_kernel(pack_ref, *refs):
    ups, downs, outs, firsts, seconds = [refs[2 * nth : 2 * nth + 2] for nth in range(5)]
    up_ref, down_ref, out_ref, qkv_ref = refs[10:]
    own_first = pack_ref[0] == 0
    small = 128

    def of_pack(pack, pair, *index):
        one, two = pair[0][index].astype(F32), pair[1][index].astype(F32)
        return jnp.where(own_first, one, two) if pack == 0 else jnp.where(own_first, two, one)

    every = slice(None)
    for pack in range(2):
        for group in range(ups[0].shape[1] // small):
            at = (2 * group + pack) * small
            columns = slice(group * small, (group + 1) * small)
            up_ref[:, at : at + small] = of_pack(pack, ups, every, columns)
        rows = downs[0].shape[0]
        down_ref[pack * rows : (pack + 1) * rows, :] = of_pack(pack, downs, every, every)
        columns = outs[0].shape[1]
        out_ref[:, pack * columns : (pack + 1) * columns] = of_pack(pack, outs, every, every)
        for kind in range(3):
            for nth, pair in enumerate((firsts, seconds)):
                columns = pair[0].shape[2]
                at = (4 * kind + 2 * pack + nth) * columns
                qkv_ref[:, at : at + columns] = of_pack(pack, pair, kind, every, every)


def settle(pack, *pairs):
    up, down, out, qkv = pairs[0][0], pairs[1][0], pairs[2][0], pairs[3][0]
    shapes = (
        (up.shape[0], 2 * up.shape[1]),
        (2 * down.shape[0], down.shape[1]),
        (out.shape[0], 2 * out.shape[1]),
        (qkv.shape[1], 12 * qkv.shape[2]),
    )
    args = [each for pair in pairs for each in pair]
    return pl.pallas_call(
        settle_kernel,
        out_shape=tuple(jax.ShapeDtypeStruct(shape, F32) for shape in shapes),
        in_specs=[scalar_spec()] + [whole_spec()] * len(args),
        out_specs=(whole_spec(),) * 4,
        compiler_params=pltpu.CompilerParams(vmem_limit_bytes=32 << 20),
        name="settle",
    )(pack.reshape(1), *args)


def row_sum_direct(term):
    part = lax.psum_scatter(term.astype(BF16), "seq", scatter_dimension=0, tiled=True)
    return lax.psum(part, "pack").astype(F32)


def project_kernel(
    per_device,
    hidden_ref,
    shift_ref,
    scale_ref,
    wq_ref,
    wk_ref,
    wv_ref,
    bq_ref,
    bk_ref,
    bv_ref,
    cos_ref,
    sin_ref,
    in_ref,
    x_ref,
):
    @pl.when(pl.program_id(0) == 0)
    def _():
        for place in range(per_device):
            rows = pl.ds(place * PATCHES, PATCHES)
            values = hidden_ref[rows, :].astype(F32)
            centered = values - jnp.mean(values, axis=-1, keepdims=True)
            spread = jnp.mean(centered * centered, axis=-1, keepdims=True)
            normed = centered * lax.rsqrt(spread + EPSILON)
            scale = scale_ref[pl.ds(place, 1), :]
            in_ref[rows, :] = (normed * (1.0 + scale) + shift_ref[pl.ds(place, 1), :]).astype(BF16)

    rows = in_ref[...]
    group = wq_ref.shape[1] // HEAD

    def turned(values, place):
        lower = values[:HALF]
        upper = values[HALF:]
        cosine = cos_ref[place]
        sine = sin_ref[place]
        return jnp.concatenate([lower * cosine - upper * sine, upper * cosine + lower * sine], axis=0)

    for kind, (weight_ref, bias_ref) in enumerate(
        ((wq_ref, bq_ref), (wk_ref, bk_ref), (wv_ref, bv_ref))
    ):
        flat = jnp.dot(rows, weight_ref[...], preferred_element_type=F32) + bias_ref[...]
        for place in range(per_device):
            block = flat[place * PATCHES : (place + 1) * PATCHES].T
            for head in range(group):
                values = block[head * HEAD : (head + 1) * HEAD]
                if kind == 0:
                    values = turned(values, place) * (HEAD**-0.5)
                    x_ref[head, 2 * per_device + place] = values.astype(BF16)
                elif kind == 1:
                    x_ref[head, place] = turned(values, place).astype(BF16)
                else:
                    x_ref[head, per_device + place] = values.astype(BF16)


def project(per_device, hidden, shift, scale, weight, bias, cosine, sine):
    tokens, width = hidden.shape
    heads = width // HEAD
    group = 2
    lanes = group * HEAD
    steps = heads // group
    bias_row = bias[None, :]

    def whole(shape):
        return pl.BlockSpec(shape, lambda step: (0,) * len(shape))

    def part(kind, rows):
        return pl.BlockSpec((rows, lanes), lambda step: (0, kind * steps + step))

    blocks = (heads, 3 * per_device, HEAD, PATCHES)
    return pl.pallas_call(
        functools.partial(project_kernel, per_device),
        grid=(steps,),
        out_shape=(
            jax.ShapeDtypeStruct((tokens, width), BF16),
            jax.ShapeDtypeStruct(blocks, BF16),
        ),
        in_specs=[whole((tokens, width)), whole(shift.shape), whole(scale.shape)]
        + [part(kind, width) for kind in range(3)]
        + [part(kind, 1) for kind in range(3)]
        + [whole(cosine.shape), whole(sine.shape)],
        out_specs=(
            whole((tokens, width)),
            pl.BlockSpec((group,) + blocks[1:], lambda step: (step, 0, 0, 0)),
        ),
        cost_estimate=pl.CostEstimate(
            flops=2 * tokens * width * 3 * width,
            bytes_accessed=2 * (weight.size + 5 * tokens * width),
            transcendentals=0,
        ),
        compiler_params=pltpu.CompilerParams(vmem_limit_bytes=40 << 20),
        name="project",
    )(hidden, shift, scale, weight, weight, weight, bias_row, bias_row, bias_row, cosine, sine)


GELU_SLOPE = 0.7978845608028654
GELU_CUBE = 0.044715


def feed_kernel(
    carried,
    which_ref,
    in_ref,
    d_out_ref,
    up_a_ref,
    up_b_ref,
    bias_a_ref,
    bias_b_ref,
    down_a_ref,
    down_b_ref,
    *refs
):
    if carried:
        out_before_ref, d_in_before_ref = refs[:2]
        refs = refs[2:]
    out_ref, d_in_ref, d_up_ref, d_down_ref, d_bias_ref, turned_ref = refs

    @pl.when(pl.program_id(0) == 0)
    def _():
        turned_ref[...] = in_ref[...].astype(F32).T.astype(BF16)
        if carried:
            out_ref[...] = out_before_ref[...]
            d_in_ref[...] = d_in_before_ref[...]
        else:
            out_ref[...] = jnp.zeros_like(out_ref)
            d_in_ref[...] = jnp.zeros_like(d_in_ref)

    up = jnp.concatenate([up_a_ref[...], up_b_ref[...]], axis=1)
    down = jnp.concatenate([down_a_ref[...], down_b_ref[...]], axis=0)
    bias = jnp.concatenate([bias_a_ref[...], bias_b_ref[...]], axis=1)
    d_out = d_out_ref[...]
    pre = jnp.dot(in_ref[...], up, preferred_element_type=F32) + bias
    d_act = dot_over(d_out, down, 1, 1)
    square = pre * pre
    bend = jnp.tanh(GELU_SLOPE * pre * (1.0 + GELU_CUBE * square))
    half = 0.5 * (1.0 + bend)
    act = (pre * half).astype(BF16)
    slope = half + (0.5 * GELU_SLOPE) * pre * (1.0 - bend * bend) * (
        1.0 + (3.0 * GELU_CUBE) * square
    )
    d_pre = (d_act * slope).astype(BF16)
    out_ref[...] += jnp.dot(act, down, preferred_element_type=F32)
    d_in_ref[...] += dot_over(d_pre, up, 1, 1)
    d_up_ref[...] = jnp.dot(turned_ref[...], d_pre, preferred_element_type=F32).astype(BF16)
    d_down_ref[...] = jnp.dot(
        act.astype(F32).T.astype(BF16), d_out, preferred_element_type=F32
    ).astype(BF16)
    d_bias_ref[...] = jnp.sum(d_pre.astype(F32), axis=0, keepdims=True)


def feed(which, feed_in, d_feed_out, up_weight, up_bias, down_weight, before):
    tokens, width = feed_in.shape
    hidden_units = up_weight.shape[1]
    small = 128
    steps = hidden_units // (4 * small)
    own = hidden_units // 2

    def whole(shape):
        return pl.BlockSpec(shape, lambda step, which: (0,) * len(shape))

    def group(nth):
        return lambda step, which: 2 * (2 * step + nth) + which[0]

    def columns(nth, rows):
        return pl.BlockSpec((rows, small), lambda step, which: (0, group(nth)(step, which)))

    def rows_of(nth):
        return pl.BlockSpec((small, width), lambda step, which: (group(nth)(step, which), 0))

    args = [feed_in, d_feed_out, up_weight, up_weight, up_bias[None], up_bias[None]]
    args += [down_weight, down_weight]
    specs = [whole((tokens, width)), whole((tokens, width)), columns(0, width), columns(1, width)]
    specs += [columns(0, 1), columns(1, 1), rows_of(0), rows_of(1)]
    if before is not None:
        args += list(before)
        specs += [whole((tokens, width)), whole((tokens, width))]
    return pl.pallas_call(
        functools.partial(feed_kernel, before is not None),
        grid_spec=pltpu.PrefetchScalarGridSpec(
            num_scalar_prefetch=1,
            grid=(steps,),
            in_specs=specs,
            out_specs=(
                whole((tokens, width)),
                whole((tokens, width)),
                pl.BlockSpec((width, 2 * small), lambda step, which: (0, step)),
                pl.BlockSpec((2 * small, width), lambda step, which: (step, 0)),
                pl.BlockSpec((1, 2 * small), lambda step, which: (0, step)),
            ),
            scratch_shapes=[pltpu.VMEM((width, tokens), BF16)],
        ),
        out_shape=(
            jax.ShapeDtypeStruct((tokens, width), F32),
            jax.ShapeDtypeStruct((tokens, width), F32),
            jax.ShapeDtypeStruct((width, own), BF16),
            jax.ShapeDtypeStruct((own, width), BF16),
            jax.ShapeDtypeStruct((1, own), F32),
        ),
        cost_estimate=pl.CostEstimate(
            flops=12 * tokens * width * own,
            bytes_accessed=2 * (4 * own * width + 8 * tokens * width),
            transcendentals=tokens * own,
        ),
        compiler_params=pltpu.CompilerParams(vmem_limit_bytes=56 << 20),
        name="feed%d" % (before is not None),
    )(which.reshape(1), *args)


def norm_back(values, d_in, scale):
    centered = values - jnp.mean(values, axis=-1, keepdims=True)
    spread = jnp.mean(centered * centered, axis=-1, keepdims=True)
    inverse = lax.rsqrt(spread + EPSILON)
    normed = centered * inverse
    product = d_in * normed
    d_shift = jnp.sum(d_in, axis=0, keepdims=True)
    d_scale = jnp.sum(product, axis=0, keepdims=True)
    scaled = 1.0 + scale
    mean_d = jnp.mean(d_in * scaled, axis=-1, keepdims=True)
    mean_p = jnp.mean(product * scaled, axis=-1, keepdims=True)
    return (d_in * scaled - mean_d - normed * mean_p) * inverse, d_shift, d_scale


def middle_back_kernel(
    d_in_ref,
    middle_ref,
    grad_ref,
    attn_ref,
    feed_ref,
    scale_ref,
    gate_ref,
    feed_gate_ref,
    down_bias_ref,
    rows_ref,
    weight_ref,
    d_middle_ref,
    d_attn_ref,
    layer_ref,
    blocks_ref,
    sums_ref,
):
    frame = pl.program_id(0)
    per_device = pl.num_programs(0) - 1

    @pl.when(frame < per_device)
    def _():
        mine = pl.ds(frame, 1)
        middle = middle_ref[...]
        grads = grad_ref[...].astype(F32)
        back, d_shift, d_scale = norm_back(middle, d_in_ref[...], scale_ref[mine, :])
        d_middle = grads + back
        d_middle_ref[...] = d_middle
        d_attn = (d_middle * gate_ref[mine, :]).astype(BF16)
        d_attn_ref[...] = d_attn
        feed_rows = feed_ref[...] + down_bias_ref[...]
        feed_gate = feed_gate_ref[mine, :]
        layer_ref[...] = (middle + feed_gate * feed_rows).astype(BF16)
        d_feed_out = (feed_gate * grads).astype(BF16).astype(F32)
        sums_ref[frame] = jnp.concatenate(
            [
                jnp.sum(d_middle * attn_ref[...], axis=0, keepdims=True),
                d_shift,
                d_scale,
                jnp.sum(grads * feed_rows, axis=0, keepdims=True),
                jnp.sum(d_attn.astype(F32), axis=0, keepdims=True),
                jnp.sum(d_feed_out, axis=0, keepdims=True),
                jnp.zeros((2, d_shift.shape[1]), F32),
            ],
            axis=0,
        )
        d_mix = dot_over(weight_ref[...], d_attn, 1, 1).astype(BF16)
        for head in range(blocks_ref.shape[0]):
            blocks_ref[head, 0] = d_mix[head * HEAD : (head + 1) * HEAD]

    @pl.when(frame == per_device)
    def _():
        first = sums_ref[0]
        second = sums_ref[1]
        rows = jnp.concatenate(
            [first[:4], second[:4], first[4:6] + second[4:6], rows_ref[...]], axis=0
        ).astype(BF16)
        count = rows.shape[1] // PATCHES
        block = jnp.concatenate(
            [rows[:, nth * PATCHES : (nth + 1) * PATCHES] for nth in range(count)], axis=0
        )
        for head in range(blocks_ref.shape[0]):
            blocks_ref[head, 0] = block


def middle_back(
    per_device, d_in, middle, grads, attn_rows, feed_rows, scale, gate, feed_gate, down_bias, rows, weight
):
    tokens, width = d_in.shape
    heads = width // HEAD
    last = per_device - 1
    per_frame = pl.BlockSpec((PATCHES, width), lambda frame: (jnp.minimum(frame, last), 0))

    def whole(shape):
        return pl.BlockSpec(shape, lambda frame: (0,) * len(shape))

    small = whole((per_device, width))
    return pl.pallas_call(
        middle_back_kernel,
        grid=(per_device + 1,),
        out_shape=(
            jax.ShapeDtypeStruct((tokens, width), F32),
            jax.ShapeDtypeStruct((tokens, width), BF16),
            jax.ShapeDtypeStruct((tokens, width), BF16),
            jax.ShapeDtypeStruct((heads, per_device + 1, HEAD, PATCHES), BF16),
        ),
        in_specs=[per_frame] * 5
        + [small] * 3
        + [whole((1, width)), whole(rows.shape), whole(weight.shape)],
        out_specs=(
            per_frame,
            per_frame,
            per_frame,
            pl.BlockSpec((heads, 1, HEAD, PATCHES), lambda frame: (0, frame, 0, 0)),
        ),
        scratch_shapes=[pltpu.VMEM((per_device, 8, width), F32)],
        cost_estimate=pl.CostEstimate(
            flops=2 * tokens * width * width, bytes_accessed=24 * tokens * width, transcendentals=0
        ),
        compiler_params=pltpu.CompilerParams(vmem_limit_bytes=48 << 20),
        name="middle_back",
    )(
        d_in,
        middle,
        grads,
        attn_rows,
        feed_rows,
        scale,
        gate,
        feed_gate,
        down_bias[None],
        rows,
        weight,
    )


def unproject_kernel(
    per_device, carried, which_ref, in_ref, back_ref, wq_ref, wk_ref, wv_ref, *refs
):
    if not carried:
        refs = refs[-4:]
    if carried:
        before_ref, hidden_ref, d_middle_ref, scale_ref, bias_theirs_ref = refs[:5]
        d_weight_ref, grad_ref, rows_ref, d_in_ref, d_bias_ref, turned_ref = refs[5:]
    else:
        d_in_ref, d_weight_ref, d_bias_ref, turned_ref = refs

    @pl.when(pl.program_id(0) == 0)
    def _():
        turned_ref[...] = in_ref[...].astype(F32).T.astype(BF16)
        if carried:
            d_in_ref[...] = before_ref[...]
        else:
            d_in_ref[...] = jnp.zeros_like(d_in_ref)

    group = wq_ref.shape[1] // HEAD

    def token_major(block_of):
        rows = []
        for place in range(per_device):
            block = jnp.concatenate([block_of(head, place) for head in range(group)], axis=0)
            rows.append(block.astype(F32).T.astype(BF16))
        return jnp.concatenate(rows, axis=0)

    sides = jnp.concatenate(
        [
            token_major(lambda head, place: back_ref[head, 2 * per_device + place]),
            token_major(lambda head, place: back_ref[head, place]),
            token_major(lambda head, place: back_ref[head, per_device + place]),
        ],
        axis=1,
    )
    weights = jnp.concatenate([wq_ref[...], wk_ref[...], wv_ref[...]], axis=1)
    d_in_ref[...] += dot_over(sides, weights, 1, 1)
    d_weight = jnp.dot(turned_ref[...], sides, preferred_element_type=F32).astype(BF16)
    d_bias = jnp.sum(sides.astype(F32), axis=0, keepdims=True)
    lanes = group * HEAD
    for kind in range(3):
        d_weight_ref[kind] = d_weight[:, kind * lanes : (kind + 1) * lanes]
        part = d_bias[:, kind * lanes : (kind + 1) * lanes]
        if carried:
            start = pl.multiple_of(pl.program_id(0) * lanes, lanes)
            d_bias_ref[pl.ds(kind, 1), pl.ds(start, lanes)] = part
        else:
            d_bias_ref[kind] = part

    if carried:

        @pl.when(pl.program_id(0) == pl.num_programs(0) - 1)
        def _():
            sums = []
            for place in range(per_device):
                rows = pl.ds(place * PATCHES, PATCHES)
                mine = pl.ds(place, 1)
                back, d_shift, d_scale = norm_back(
                    hidden_ref[rows, :].astype(F32), d_in_ref[rows, :], scale_ref[mine, :]
                )
                grad_ref[rows, :] = (d_middle_ref[rows, :] + back).astype(BF16)
                sums += [d_shift, d_scale]
            for kind in range(3):
                sums.append(
                    jnp.concatenate([d_bias_ref[pl.ds(kind, 1), :], bias_theirs_ref[kind]], axis=1)
                )
            count = 16 - len(sums)
            late = jnp.concatenate(
                sums + [jnp.zeros((count, d_in_ref.shape[1]), F32)], axis=0
            ).astype(BF16)
            for target in range(rows_ref.shape[0]):
                rows_ref[target] = late


def unproject(per_device, targets, which, attn_in, back, weight, orders, before=None, norm_args=()):
    tokens, width = attn_in.shape
    heads = width // HEAD
    group = 2
    lanes = group * HEAD
    groups = heads // group
    steps = groups // 2

    def whole(shape):
        return pl.BlockSpec(shape, lambda step, which: (0,) * len(shape))

    def blocks(array):
        return pl.BlockSpec(
            (group,) + array.shape[1:], lambda step, which: (which[0] * steps + step, 0, 0, 0)
        )

    def part(kind):
        return pl.BlockSpec(
            (width, lanes), lambda step, which: (0, kind * groups + which[0] * steps + step)
        )

    args = [attn_in, back, weight, weight, weight]
    specs = [whole((tokens, width)), blocks(back), part(0), part(1), part(2)]
    weight_shape = (
        jax.ShapeDtypeStruct((3, width, width // 2), BF16),
        jax.ShapeDtypeStruct((3, 1, width // 2), F32),
    )
    weight_specs = (
        pl.BlockSpec((3, width, lanes), lambda step, which: (0, 0, step)),
        pl.BlockSpec((3, 1, lanes), lambda step, which: (0, 0, step)),
    )
    scratch = [pltpu.VMEM((width, tokens), BF16)]
    small = (per_device, width)
    if before is not None:
        args += [before] + list(norm_args)
        specs += [whole((tokens, width))] * 3 + [whole(small), whole((3, 1, width // 2))]
        late = (targets, 16, width)
        outs = weight_shape[:1] + (
            jax.ShapeDtypeStruct((tokens, width), BF16),
            jax.ShapeDtypeStruct(late, BF16),
        )
        out_specs = weight_specs[:1] + (whole((tokens, width)), whole(late))
        scratch = [pltpu.VMEM((tokens, width), F32), pltpu.VMEM((3, width // 2), F32)] + scratch
    else:
        outs = (jax.ShapeDtypeStruct((tokens, width), F32),) + weight_shape
        out_specs = (whole((tokens, width)),) + weight_specs
        orders = corners(orders)
        args += orders
        specs += [unread_spec()] * len(orders)
    return pl.pallas_call(
        functools.partial(unproject_kernel, per_device, before is not None),
        grid_spec=pltpu.PrefetchScalarGridSpec(
            num_scalar_prefetch=1,
            grid=(steps,),
            in_specs=specs,
            out_specs=out_specs,
            scratch_shapes=scratch,
        ),
        out_shape=outs,
        cost_estimate=pl.CostEstimate(
            flops=6 * tokens * width * width,
            bytes_accessed=2 * (3 * width * width + 6 * tokens * width),
            transcendentals=0,
        ),
        compiler_params=pltpu.CompilerParams(vmem_limit_bytes=48 << 20),
        name="unproject%d" % (before is not None),
    )(which.reshape(1), *args)


def columns_of(matrix, start, width, axis=1):
    if isinstance(start, int) and start == 0 and width == matrix.shape[axis]:
        return matrix
    return lax.dynamic_slice_in_dim(matrix, start, width, axis)


def local(
    hidden,
    cotangent,
    levels,
    segments,
    live_frames,
    noise_table,
    mod_weight,
    mod_bias,
    qkv_weight,
    qkv_bias,
    out_weight,
    out_bias,
    up_weight,
    up_bias,
    down_weight,
    down_bias,
):
    seq_index = lax.axis_index("seq")
    seq_count = lax.axis_size("seq")
    tokens = hidden.shape[1]
    width = hidden.shape[2]
    per_device = tokens // PATCHES
    frames = segments.shape[1]
    heads = width // HEAD
    copies = seq_count // heads
    hidden_units = up_weight.shape[1]
    level_count = noise_table.shape[0]
    share = width // seq_count
    clip_ids = segments[0]
    live = live_frames[0]

    pack = lax.axis_index("pack")
    halves = halving_fits()
    frame_ids = jnp.arange(frames, dtype=jnp.int32)
    same_clip = clip_ids[:, None] == clip_ids[None, :]
    clip_starts = jnp.min(jnp.where(same_clip, frame_ids[None, :], frames), axis=1)
    frame_times = (frame_ids - clip_starts).astype(F32)
    own_cos, own_sin = rotary_tables(
        lax.dynamic_slice_in_dim(frame_times, seq_index * per_device, per_device)
    )

    embed = jnp.concatenate(
        [
            lax.dynamic_slice_in_dim(noise_table, levels[0, frame], 1, 0)
            for frame in range(per_device)
        ],
        axis=0,
    )
    cond = jax.nn.silu(embed).astype(BF16)
    modulation = jnp.dot(cond, mod_weight[:, : 2 * width], preferred_element_type=F32)
    attn_shift, attn_scale = jnp.split(modulation + mod_bias[: 2 * width], 2, axis=1)
    attn_in, sent = project(
        per_device, hidden[0], attn_shift, attn_scale, qkv_weight, qkv_bias, own_cos, own_sin
    )

    def to_heads(array):
        if copies > 1:
            array = jnp.concatenate([array] * copies, axis=0)
        return lax.all_to_all(array, "seq", 0, 0, tiled=True)

    def to_tokens(array):
        return lax.all_to_all(array, "seq", 0, 0, tiled=True)[:heads]

    x = to_heads(sent)
    late_modulation = jnp.dot(
        after(cond, attn_in), mod_weight[:, 2 * width :], preferred_element_type=F32
    )
    attn_gate, feed_shift, feed_scale, feed_gate = jnp.split(
        late_modulation + mod_bias[2 * width :], 4, axis=1
    )
    cos_all, sin_all = rotary_tables(after(frame_times, attn_in))
    grad_rows = cotangent[0].astype(F32).reshape(per_device, PATCHES, width)
    d_feed_out = (feed_gate[:, None, :] * grad_rows).reshape(tokens, width).astype(BF16)
    x, d_feed_out, cos_all, sin_all = lax.optimization_barrier((x, d_feed_out, cos_all, sin_all))
    mix, wide, lse, kv = attend(per_device, clip_ids, live, x)
    mix = to_tokens(mix)
    mixes = [mix[:, place].reshape(width, PATCHES) for place in range(per_device)]
    attn_rows = jnp.stack([dot_over(each, out_weight, 0, 0) for each in mixes]) + out_bias
    attn_mix = jnp.concatenate(mixes, axis=1)

    frame_rows = hidden[0].astype(F32).reshape(per_device, PATCHES, width)
    middle = frame_rows + attn_gate[:, None, :] * attn_rows
    feed_in = modulate_norm(middle, feed_shift, feed_scale).reshape(tokens, width).astype(BF16)
    feed_args = (feed_in, d_feed_out, up_weight, up_bias, down_weight)
    theirs = feed(1 - pack if halves else pack * 0 + 1, *feed_args, None)
    mine = feed(pack if halves else pack * 0, *feed_args, theirs[:2])
    small = 128

    def in_order(own, other):
        if halves:
            even, odd = jnp.where(pack == 0, own, other), jnp.where(pack == 0, other, own)
        else:
            even, odd = own, other
        rows = own.shape[0]
        return jnp.stack(
            [even.reshape(rows, -1, small), odd.reshape(rows, -1, small)], axis=2
        ).reshape(rows, -1)

    own_levels = levels[0]
    level_row = jnp.concatenate(
        [
            jnp.broadcast_to(part[frame], (width // (2 * per_device),))
            for frame in range(per_device)
            for part in (lax.div(own_levels, 32), lax.rem(own_levels, 32))
        ]
    ).astype(F32)[None]
    extra_rows = jnp.concatenate(
        [
            in_order(mine[4], theirs[4]).reshape(-1, width),
            level_row,
            jnp.zeros((1, width), F32),
        ],
        axis=0,
    )
    d_middle, d_attn_out, layer_out, blocks = middle_back(
        per_device,
        mine[1],
        middle.reshape(tokens, width),
        cotangent[0],
        attn_rows.reshape(tokens, width),
        mine[0],
        feed_scale,
        attn_gate,
        feed_gate,
        down_bias,
        extra_rows,
        out_weight,
    )
    layer_out = layer_out.reshape(1, tokens, width)
    d_mix = to_heads(blocks)

    def out_term(start, size):
        return dot_over(attn_mix, columns_of(d_attn_out, start, size), 1, 0).astype(BF16)

    sums = ()
    if halves:
        up_sum = RowSum(mine[2], exchange(theirs[2], "pack", 1), (2, 1, 4, 8))
        down_sum = RowSum(mine[3], exchange(theirs[3], "pack", 1), (1, 2, 4, 8))
        out_theirs = exchange(out_term((1 - pack) * (width // 2), width // 2), "pack", 1)
        out_sum = RowSum(out_term(pack * (width // 2), width // 2), out_theirs, (1, 2, 4, 8))
        sums = (down_sum, up_sum)
    def own_share(row):
        piece = row.shape[0] // seq_count
        return lax.dynamic_slice_in_dim(row, seq_index * piece, piece)

    chunks = width // PATCHES
    early_rows = d_mix[:, per_device].reshape(seq_count, chunks, 16, PATCHES)
    early_rows = early_rows.transpose(0, 2, 1, 3).reshape(seq_count, 16, width)
    early_sets = of_packs(early_rows)
    early_sum = functools.reduce(
        jnp.add, [jnp.sum(each.astype(F32), axis=0) for each in early_sets]
    )
    out_bias_grad = own_share(early_sum[8])
    down_bias_grad = own_share(early_sum[9])
    up_bias_grad = own_share(early_sum[10:14].reshape(hidden_units))

    def frames_of(rows, per_frame, kinds):
        return jnp.concatenate(
            [
                jnp.stack(
                    [rows[:, frame * per_frame + kind] for frame in range(per_device)], axis=1
                ).reshape(-1, width)
                for kind in range(kinds)
            ],
            axis=1,
        )

    own_table = lax.dynamic_slice_in_dim(noise_table, seq_index * share, share, 1)
    own_mod = lax.dynamic_slice_in_dim(mod_weight, seq_index * share, share, 0)
    stride = width // (2 * per_device)
    parts = []
    for rows in early_sets:
        coded = rows[:, 14, ::stride].astype(jnp.int32).reshape(-1, 2)
        set_levels = coded[:, 0] * 32 + coded[:, 1]
        picks = (set_levels[:, None] == jnp.arange(level_count, dtype=jnp.int32)[None, :]).astype(F32)
        embeds = jnp.dot(picks, own_table, precision=PRECISE, preferred_element_type=F32)
        set_cond = jax.nn.silu(embeds).astype(BF16)
        d_mod = frames_of(rows, 4, 4)
        parts.append(
            (
                picks,
                embeds,
                set_cond,
                dot_over(d_mod, own_mod[:, 2 * width :], 1, 1),
                dot_over(set_cond, d_mod, 0, 0),
            )
        )
    mod_grad_early = functools.reduce(jnp.add, [each[4] for each in parts])
    mod_sum_early = (early_sum[:4] + early_sum[4:8]).reshape(4 * width)
    orders = [each.stage() for each in sums]
    result = attend_back(
        per_device, clip_ids, live, x, kv, wide, lse, d_mix, cos_all, sin_all, orders
    )
    if halves:
        for each in sums:
            result = each.tie(result)
        result = out_sum.tie(result)
    back = to_tokens(result)
    orders = []
    if halves:
        for each in (up_sum, down_sum, out_sum):
            each.stage()
        orders = [each.stage() for each in (up_sum, down_sum, out_sum)]
    orders += [mod_grad_early] + [part[3] for part in parts]
    which = (1 - pack, pack) if halves else (pack * 0, pack * 0 + 1)
    d_in_theirs, qkv_theirs, bias_theirs = unproject(
        per_device, seq_count, which[0], attn_in, back, qkv_weight, orders
    )
    qkv_mine, hidden_grad, late = unproject(
        per_device,
        seq_count,
        which[1],
        attn_in,
        back,
        qkv_weight,
        (),
        d_in_theirs,
        (hidden[0], d_middle, attn_scale, bias_theirs),
    )
    hidden_grad = hidden_grad.reshape(1, tokens, width)
    late_rows = lax.all_to_all(late, "seq", 0, 0, tiled=True)

    def halves_in_order(own, other):
        if halves:
            return jnp.where(pack == 0, own, other), jnp.where(pack == 0, other, own)
        return other, own

    if halves:
        came = exchange(qkv_theirs, "pack", 1)
        split = width // 4
        qkv_sums = [
            RowSum(qkv_mine[..., :split], came[..., :split], (1, 2, 4, 8)),
            RowSum(qkv_mine[..., split:], came[..., split:], (2, 1, 4, 8)),
        ]
        for each in qkv_sums:
            each.stage((up_sum, down_sum, out_sum))
        up_weight_grad, down_weight_grad, out_weight_grad, qkv_weight_grad = settle(
            pack, *[each.finish() for each in (up_sum, down_sum, out_sum, *qkv_sums)]
        )
    else:
        up_weight_grad = row_sum_direct(in_order(mine[2], theirs[2]))
        pairs = [each[3].reshape(-1, small, width) for each in (mine, theirs)]
        down_weight_grad = row_sum_direct(jnp.stack(pairs, axis=1).reshape(hidden_units, width))
        out_weight_grad = row_sum_direct(out_term(0, width))
        qkv_term = jnp.concatenate(halves_in_order(qkv_mine, qkv_theirs), axis=-1)
        qkv_weight_grad = row_sum_direct(qkv_term.transpose(1, 0, 2).reshape(width, 3 * width))

    late_sets = of_packs(late_rows[:, :8])
    bias_at = 2 * per_device
    bias_sums = [
        jnp.sum(rows[:, bias_at : bias_at + 3].astype(F32), axis=0) for rows in late_sets
    ]
    if halves:
        ones, twos = bias_sums
        half = width // 2
        own_half = ones[:, :half] + twos[:, half:]
        other_half = ones[:, half:] + twos[:, :half]
    else:
        total = functools.reduce(jnp.add, bias_sums)
        own_half, other_half = total[:, : width // 2], total[:, width // 2 :]
    bias_total = jnp.concatenate(halves_in_order(own_half, other_half), axis=1)
    qkv_bias_grad = own_share(bias_total.reshape(3 * width))
    late_mods = [frames_of(rows, 2, 2) for rows in late_sets]
    mod_sum_late = functools.reduce(
        jnp.add, [jnp.sum(each.astype(F32), axis=0) for each in late_mods]
    )
    d_embeds = []
    for part, d_mod in zip(parts, late_mods):
        d_cond = part[3] + dot_over(d_mod, own_mod[:, : 2 * width], 1, 1)
        d_embeds.append(jax.vjp(jax.nn.silu, part[1])[1](d_cond)[0])
    table_grad = lax.dot_general(
        jnp.concatenate([part[0] for part in parts], axis=0),
        jnp.concatenate(d_embeds, axis=0),
        (((0,), (0,)), ((), ())),
        precision=PRECISE,
        preferred_element_type=F32,
    )
    mod_grad_late = functools.reduce(
        jnp.add, [dot_over(part[2], d_mod, 0, 0) for part, d_mod in zip(parts, late_mods)]
    )
    mod_weight_grad = jnp.concatenate([mod_grad_late, mod_grad_early], axis=1)
    mod_bias_grad = own_share(jnp.concatenate([mod_sum_late, mod_sum_early]))
    return (
        layer_out,
        hidden_grad,
        table_grad,
        mod_weight_grad,
        mod_bias_grad,
        qkv_weight_grad,
        qkv_bias_grad,
        out_weight_grad,
        out_bias_grad,
        up_weight_grad,
        up_bias_grad,
        down_weight_grad,
        down_bias_grad,
    )


def solution(mesh):
    in_specs = (
        P("pack", "seq", None),
        P("pack", "seq", None),
        P("pack", "seq"),
        P("pack", None),
        P("pack", None),
    ) + (P(),) * 11
    out_specs = (
        P("pack", "seq", None),
        P("pack", "seq", None),
        P(None, "seq"),
        P("seq", None),
        P("seq"),
        P("seq", None),
        P("seq"),
        P("seq", None),
        P("seq"),
        P("seq", None),
        P("seq"),
        P("seq", None),
        P("seq"),
    )
    return jax.shard_map(local, mesh=mesh, in_specs=in_specs, out_specs=out_specs, check_vma=False)
```

```python
import functools

import jax
import jax.numpy as jnp
from jax import lax
from jax.experimental import pallas as pl
from jax.experimental.pallas import tpu as pltpu
from jax.sharding import PartitionSpec as P

HEAD = 64
PATCHES = 256
SIDE = 16
EPSILON = 1e-06
PRECISE = lax.Precision.HIGHEST
HALF = HEAD // 2
F32 = jnp.float32
BF16 = jnp.bfloat16


def modulate_norm(rows, shift, scale):
    center = jnp.mean(rows, axis=-1, keepdims=True)
    centered = rows - center
    spread = jnp.mean(centered * centered, axis=-1, keepdims=True)
    normed = centered * lax.rsqrt(spread + EPSILON)
    return normed * (1.0 + scale[:, None, :]) + shift[:, None, :]


def gelu_tanh(values):
    return jax.nn.gelu(values, approximate=True)


def dot_over(first, second, first_dim, second_dim):
    return lax.dot_general(
        first, second, (((first_dim,), (second_dim,)), ((), ())), preferred_element_type=F32
    )


def spatial_angles():
    time_pairs = HALF // 4
    space_pairs = (HALF - time_pairs) // 2
    patch = jnp.arange(PATCHES, dtype=jnp.int32)
    row_pos = (patch // SIDE).astype(F32)
    col_pos = (patch % SIDE).astype(F32)
    time_freq = 10000.0 ** (-jnp.arange(time_pairs, dtype=F32) / time_pairs)
    space_freq = 10000.0 ** (-jnp.arange(space_pairs, dtype=F32) / space_pairs)
    space = jnp.concatenate(
        [space_freq[:, None] * row_pos[None, :], space_freq[:, None] * col_pos[None, :]], axis=0
    )
    return time_freq, space


def rotary_tables(time_frames):
    time_freq, space = spatial_angles()
    count = time_frames.shape[0]
    time_angle = time_frames[:, None] * time_freq[None, :]

    def whole(function):
        return jnp.concatenate(
            [
                jnp.broadcast_to(
                    function(time_angle)[:, :, None], (count, time_freq.shape[0], PATCHES)
                ),
                jnp.broadcast_to(function(space)[None], (count,) + space.shape),
            ],
            axis=1,
        )

    return whole(jnp.cos), whole(jnp.sin)


def walk_frames(frames, per_device, parts, segments_ref, live_ref, list_ref, visit):
    def step(source, held):
        for place in range(per_device):
            frame = source * per_device + place
            before = jnp.maximum(frame - 1, 0)
            fresh = (frame == 0) | (segments_ref[frame] != segments_ref[before])
            held = jnp.where(fresh, 0, held)
            list_ref[held] = frame
            if place in parts:
                visit(source, place, frame, held + 1)
            held = held + jnp.where(live_ref[frame] == 1, 1, 0)
        return held

    lax.fori_loop(0, frames // per_device, step, jnp.int32(0))


def attend_kernel(per_device, segments_ref, live_ref, x_ref, mix_ref, wide_ref, lse_ref, kv_ref, list_ref):
    frames = kv_ref.shape[0]

    def turn(source, carry):
        for place in range(per_device):
            both = jnp.concatenate(
                [x_ref[source, place], x_ref[source, per_device + place]], axis=0
            )
            kv_ref[source * per_device + place] = both.T
        return carry

    lax.fori_loop(0, frames // per_device, turn, 0)

    def visit(source, place, frame, count):
        query = x_ref[source, 2 * per_device + place]
        query_side = jnp.concatenate([query, jnp.zeros_like(query)], axis=0)

        def scores_of(other):
            return jnp.dot(kv_ref[other], query_side, preferred_element_type=F32)

        def mixed(other, weights):
            value = x_ref[lax.div(other, per_device), per_device + lax.rem(other, per_device)]
            return jnp.dot(value, weights.astype(BF16), preferred_element_type=F32)

        def join(others, carry):
            scores = [scores_of(other) for other in others]
            tops = [jnp.max(score, axis=0, keepdims=True) for score in scores]
            new_top = functools.reduce(jnp.maximum, tops)
            if carry is not None:
                top, total, accum = carry
                new_top = jnp.maximum(top, new_top)
                shrink = jnp.exp(top - new_top)
                total = total * shrink
                accum = accum * shrink
            for index, score in enumerate(scores):
                weights = jnp.exp(score - new_top)
                added = jnp.sum(weights, axis=0, keepdims=True)
                product = mixed(others[index], weights)
                if carry is None and index == 0:
                    total, accum = added, product
                else:
                    total, accum = total + added, accum + product
            return new_top, total, accum

        others = count - 1
        carry = join([frame], None)
        carry = lax.fori_loop(
            0,
            lax.div(others, 4),
            lambda index, state: join([list_ref[4 * index + nth] for nth in range(4)], state),
            carry,
        )
        carry = lax.fori_loop(
            lax.div(others, 4) * 2,
            lax.div(others, 2),
            lambda index, state: join([list_ref[2 * index], list_ref[2 * index + 1]], state),
            carry,
        )
        top, total, accum = lax.fori_loop(
            0,
            lax.rem(others, 2),
            lambda unused, state: join([list_ref[others - 1]], state),
            carry,
        )
        result = accum * (1.0 / total)
        wide_ref[source, place] = result
        mix_ref[source, place] = result.astype(BF16)
        lse_ref[pl.ds(frame, 1), :] = top + jnp.log(total)

    walk_frames(frames, per_device, range(per_device), segments_ref, live_ref, list_ref, visit)


def corners(values):
    return [each.reshape(-1, each.shape[-1])[:1, :128] for each in values]


def unread_spec():
    return pl.BlockSpec(memory_space=pl.ANY)


def whole_spec():
    return pl.BlockSpec(memory_space=pltpu.VMEM)


def scalar_spec():
    return pl.BlockSpec(memory_space=pltpu.SMEM)


def attend(per_device, segments, live, x):
    sources = x.shape[0]
    frames = sources * per_device
    pairs = frames * 6
    outs = (
        jax.ShapeDtypeStruct((sources, per_device, HEAD, PATCHES), BF16),
        jax.ShapeDtypeStruct((sources, per_device, HEAD, PATCHES), F32),
        jax.ShapeDtypeStruct((frames, PATCHES), F32),
        jax.ShapeDtypeStruct((frames, PATCHES, 2 * HEAD), BF16),
    )
    return pl.pallas_call(
        functools.partial(attend_kernel, per_device),
        out_shape=outs,
        in_specs=[scalar_spec(), scalar_spec(), whole_spec()],
        out_specs=(whole_spec(),) * len(outs),
        scratch_shapes=[pltpu.SMEM((frames,), jnp.int32)],
        cost_estimate=pl.CostEstimate(
            flops=pairs * 4 * PATCHES * PATCHES * 256,
            bytes_accessed=x.size * 2 * 3,
            transcendentals=pairs * PATCHES * PATCHES,
        ),
        compiler_params=pltpu.CompilerParams(vmem_limit_bytes=40 << 20),
        name="attend",
    )(segments, live, x)


def attend_back_kernel(
    per_device,
    part,
    last,
    segments_ref,
    live_ref,
    x_ref,
    kv_ref,
    wide_ref,
    lse_ref,
    d_mix_ref,
    cos_ref,
    sin_ref,
    *refs
):
    if last:
        before_ref, d_query_ref = refs[:2]
    out_ref, dkv_ref, list_ref = refs[-3:]
    frames = kv_ref.shape[0]

    def clear(source, carry):
        for place in range(per_device):
            if place != part:
                dkv_ref[source * per_device + place] = jnp.zeros((PATCHES, 2 * HEAD), F32)
        return carry

    lax.fori_loop(0, frames // per_device, clear, 0)

    def unturn(frame, values):
        lower = values[:HALF]
        upper = values[HALF:]
        cosine = cos_ref[frame]
        sine = sin_ref[frame]
        return jnp.concatenate([lower * cosine + upper * sine, upper * cosine - lower * sine], axis=0)

    def visit(source, place, frame, count):
        query = x_ref[source, 2 * per_device + place]
        d_mix = d_mix_ref[source, place]
        blank = jnp.zeros_like(query)
        query_side = jnp.concatenate([query, blank], axis=0)
        d_mix_side = jnp.concatenate([blank, d_mix], axis=0)
        turned = jnp.concatenate([query, d_mix], axis=0).T
        first = lax.broadcasted_iota(jnp.int32, turned.shape, 1) < HEAD
        nothing = jnp.zeros_like(turned)
        both = jnp.concatenate(
            [jnp.where(first, turned, nothing), jnp.where(first, nothing, turned)], axis=0
        )
        lse = lse_ref[pl.ds(frame, 1), :]
        delta = jnp.sum(d_mix.astype(F32) * wide_ref[source, place], axis=0, keepdims=True)

        def block(other, own=False):
            key_value = kv_ref[other]
            scores = jnp.dot(key_value, query_side, preferred_element_type=F32)
            d_weights = jnp.dot(key_value, d_mix_side, preferred_element_type=F32)
            weights = jnp.exp(scores - lse)
            d_scores = (weights * (d_weights - delta)).astype(BF16)
            sides = jnp.concatenate([d_scores, weights.astype(BF16)], axis=1)
            d_both = jnp.dot(sides, both, preferred_element_type=F32)
            if own:
                dkv_ref[other] = d_both
            else:
                dkv_ref[other] += d_both
            key = x_ref[lax.div(other, per_device), lax.rem(other, per_device)]
            return jnp.dot(key, d_scores, preferred_element_type=F32)

        others = count - 1
        d_query = block(frame, True)
        d_query = lax.fori_loop(
            0,
            lax.div(others, 2),
            lambda index, state: state
            + block(list_ref[2 * index])
            + block(list_ref[2 * index + 1]),
            d_query,
        )
        d_query = lax.fori_loop(
            0,
            lax.rem(others, 2),
            lambda unused, state: state + block(list_ref[others - 1]),
            d_query,
        )
        d_query = unturn(frame, d_query * (HEAD**-0.5)).astype(BF16)
        if last:
            out_ref[source, 2 * per_device + place] = d_query
        else:
            out_ref[source] = d_query

    walk_frames(frames, per_device, (part,), segments_ref, live_ref, list_ref, visit)

    def finish(source, carry):
        for place in range(per_device):
            frame = source * per_device + place
            both = (dkv_ref[frame] + before_ref[frame]).T
            out_ref[source, place] = unturn(frame, both[:HEAD]).astype(BF16)
            out_ref[source, per_device + place] = both[HEAD:].astype(BF16)
        for place in range(part):
            out_ref[source, 2 * per_device + place] = d_query_ref[source]
        return carry

    if last:
        lax.fori_loop(0, frames // per_device, finish, 0)


def attend_back(
    part, per_device, segments, live, x, kv, wide, lse, d_mix, cosine, sine, before, orders
):
    sources = x.shape[0]
    frames = sources * per_device
    pairs = sources * 6
    last = part == per_device - 1
    args = [segments, live, x, kv, wide, lse, d_mix, cosine, sine]
    dkv = (frames, PATCHES, 2 * HEAD)
    lists = pltpu.SMEM((frames,), jnp.int32)
    if last:
        args += [before[1], before[0]]
        outs = jax.ShapeDtypeStruct(x.shape, BF16)
        out_specs = whole_spec()
        scratch = [pltpu.VMEM(dkv, F32), lists]
    else:
        outs = (
            jax.ShapeDtypeStruct((sources, HEAD, PATCHES), BF16),
            jax.ShapeDtypeStruct(dkv, F32),
        )
        out_specs = (whole_spec(), whole_spec())
        scratch = [lists]
    specs = [scalar_spec(), scalar_spec()] + [whole_spec()] * (len(args) - 2)
    orders = corners(orders)
    return pl.pallas_call(
        functools.partial(attend_back_kernel, per_device, part, last),
        out_shape=outs,
        in_specs=specs + [unread_spec()] * len(orders),
        out_specs=out_specs,
        scratch_shapes=scratch,
        cost_estimate=pl.CostEstimate(
            flops=pairs * 10 * PATCHES * PATCHES * 64,
            bytes_accessed=x.size * 2 * 5,
            transcendentals=pairs * PATCHES * PATCHES,
        ),
        compiler_params=pltpu.CompilerParams(vmem_limit_bytes=60 << 20),
        name="attend_back%d" % part,
    )(*args, *orders)


def exchange(value, axis, bit):
    count = lax.axis_size(axis)
    return lax.ppermute(value, axis, [(source, source ^ bit) for source in range(count)])


def after(value, *earlier):
    return lax.optimization_barrier((value,) + earlier)[0]


def of_packs(value):
    values = [value]
    bit = lax.axis_size("pack") // 2
    while bit:
        values = values + [exchange(each, "pack", bit) for each in values]
        bit //= 2
    return values


def halving_fits():
    return lax.axis_size("pack") == 2 and lax.axis_size("seq") == 16


class RowSum:
    def __init__(self, mine, came, order):
        self.order = list(order)
        self.index = lax.axis_index("seq")
        rows = mine.shape[-2]
        self.tail = (rows // 16, mine.shape[-1])
        self.lead = mine.shape[:-2]
        shape = self.lead + (2, 2, 2, 2) + self.tail
        self.parts = [mine.reshape(shape), came.reshape(shape)]

    def pick(self, bit, which):
        axis = len(self.lead) + {8: 0, 4: 1, 2: 2, 1: 3}[bit]
        pieces = [lax.dynamic_slice_in_dim(part, which, 1, axis) for part in self.parts]
        return (pieces[0].astype(F32) + pieces[1].astype(F32)).astype(BF16)

    def tie_kept(self, value):
        value, self.parts[0] = lax.optimization_barrier((value, self.parts[0]))
        return value

    def stage(self, later=()):
        bit = self.order.pop(0)
        own_bit = lax.rem(lax.div(self.index, bit), 2)
        send = self.pick(bit, 1 - own_bit)
        for each in later:
            send = each.tie_kept(send)
        came = exchange(send, "seq", bit)
        self.parts = [self.pick(bit, own_bit), came]
        return send

    def tie(self, value):
        value, *self.parts = lax.optimization_barrier((value, *self.parts))
        return value

    def finish(self):
        while self.order:
            self.stage()
        own = (self.parts[0].astype(F32) + self.parts[1].astype(F32)).astype(BF16)
        own = own.reshape(self.lead + self.tail)
        return own, exchange(own, "pack", 1)


def settle_kernel(pack_ref, *refs):
    ups, downs, outs, firsts, seconds = [refs[2 * nth : 2 * nth + 2] for nth in range(5)]
    up_ref, down_ref, out_ref, qkv_ref = refs[10:]
    own_first = pack_ref[0] == 0
    small = 128

    def of_pack(pack, pair, *index):
        one, two = pair[0][index].astype(F32), pair[1][index].astype(F32)
        return jnp.where(own_first, one, two) if pack == 0 else jnp.where(own_first, two, one)

    every = slice(None)
    for pack in range(2):
        for group in range(ups[0].shape[1] // small):
            at = (2 * group + pack) * small
            columns = slice(group * small, (group + 1) * small)
            up_ref[:, at : at + small] = of_pack(pack, ups, every, columns)
        rows = downs[0].shape[0]
        down_ref[pack * rows : (pack + 1) * rows, :] = of_pack(pack, downs, every, every)
        columns = outs[0].shape[1]
        out_ref[:, pack * columns : (pack + 1) * columns] = of_pack(pack, outs, every, every)
        for kind in range(3):
            for nth, pair in enumerate((firsts, seconds)):
                columns = pair[0].shape[2]
                at = (4 * kind + 2 * pack + nth) * columns
                qkv_ref[:, at : at + columns] = of_pack(pack, pair, kind, every, every)


def settle(pack, *pairs):
    up, down, out, qkv = pairs[0][0], pairs[1][0], pairs[2][0], pairs[3][0]
    shapes = (
        (up.shape[0], 2 * up.shape[1]),
        (2 * down.shape[0], down.shape[1]),
        (out.shape[0], 2 * out.shape[1]),
        (qkv.shape[1], 12 * qkv.shape[2]),
    )
    args = [each for pair in pairs for each in pair]
    return pl.pallas_call(
        settle_kernel,
        out_shape=tuple(jax.ShapeDtypeStruct(shape, F32) for shape in shapes),
        in_specs=[scalar_spec()] + [whole_spec()] * len(args),
        out_specs=(whole_spec(),) * 4,
        compiler_params=pltpu.CompilerParams(vmem_limit_bytes=32 << 20),
        name="settle",
    )(pack.reshape(1), *args)


def row_sum_direct(term):
    part = lax.psum_scatter(term.astype(BF16), "seq", scatter_dimension=0, tiled=True)
    return lax.psum(part, "pack").astype(F32)


def project_kernel(
    per_device,
    hidden_ref,
    shift_ref,
    scale_ref,
    wq_ref,
    wk_ref,
    wv_ref,
    bq_ref,
    bk_ref,
    bv_ref,
    cos_ref,
    sin_ref,
    in_ref,
    x_ref,
):
    @pl.when(pl.program_id(0) == 0)
    def _():
        for place in range(per_device):
            rows = pl.ds(place * PATCHES, PATCHES)
            values = hidden_ref[rows, :].astype(F32)
            centered = values - jnp.mean(values, axis=-1, keepdims=True)
            spread = jnp.mean(centered * centered, axis=-1, keepdims=True)
            normed = centered * lax.rsqrt(spread + EPSILON)
            scale = scale_ref[pl.ds(place, 1), :]
            in_ref[rows, :] = (normed * (1.0 + scale) + shift_ref[pl.ds(place, 1), :]).astype(BF16)

    rows = in_ref[...]
    group = wq_ref.shape[1] // HEAD

    def turned(values, place):
        lower = values[:HALF]
        upper = values[HALF:]
        cosine = cos_ref[place]
        sine = sin_ref[place]
        return jnp.concatenate([lower * cosine - upper * sine, upper * cosine + lower * sine], axis=0)

    for kind, (weight_ref, bias_ref) in enumerate(
        ((wq_ref, bq_ref), (wk_ref, bk_ref), (wv_ref, bv_ref))
    ):
        flat = jnp.dot(rows, weight_ref[...], preferred_element_type=F32) + bias_ref[...]
        for place in range(per_device):
            block = flat[place * PATCHES : (place + 1) * PATCHES].T
            for head in range(group):
                values = block[head * HEAD : (head + 1) * HEAD]
                if kind == 0:
                    values = turned(values, place) * (HEAD**-0.5)
                    x_ref[head, 2 * per_device + place] = values.astype(BF16)
                elif kind == 1:
                    x_ref[head, place] = turned(values, place).astype(BF16)
                else:
                    x_ref[head, per_device + place] = values.astype(BF16)


def project(per_device, hidden, shift, scale, weight, bias, cosine, sine):
    tokens, width = hidden.shape
    heads = width // HEAD
    group = 2
    lanes = group * HEAD
    steps = heads // group
    bias_row = bias[None, :]

    def whole(shape):
        return pl.BlockSpec(shape, lambda step: (0,) * len(shape))

    def part(kind, rows):
        return pl.BlockSpec((rows, lanes), lambda step: (0, kind * steps + step))

    blocks = (heads, 3 * per_device, HEAD, PATCHES)
    return pl.pallas_call(
        functools.partial(project_kernel, per_device),
        grid=(steps,),
        out_shape=(
            jax.ShapeDtypeStruct((tokens, width), BF16),
            jax.ShapeDtypeStruct(blocks, BF16),
        ),
        in_specs=[whole((tokens, width)), whole(shift.shape), whole(scale.shape)]
        + [part(kind, width) for kind in range(3)]
        + [part(kind, 1) for kind in range(3)]
        + [whole(cosine.shape), whole(sine.shape)],
        out_specs=(
            whole((tokens, width)),
            pl.BlockSpec((group,) + blocks[1:], lambda step: (step, 0, 0, 0)),
        ),
        cost_estimate=pl.CostEstimate(
            flops=2 * tokens * width * 3 * width,
            bytes_accessed=2 * (weight.size + 5 * tokens * width),
            transcendentals=0,
        ),
        compiler_params=pltpu.CompilerParams(vmem_limit_bytes=40 << 20),
        name="project",
    )(hidden, shift, scale, weight, weight, weight, bias_row, bias_row, bias_row, cosine, sine)


GELU_SLOPE = 0.7978845608028654
GELU_CUBE = 0.044715


def feed_kernel(
    carried,
    which_ref,
    in_ref,
    d_out_ref,
    up_a_ref,
    up_b_ref,
    bias_a_ref,
    bias_b_ref,
    down_a_ref,
    down_b_ref,
    *refs
):
    if carried:
        out_before_ref, d_in_before_ref = refs[:2]
        refs = refs[2:]
    out_ref, d_in_ref, d_up_ref, d_down_ref, d_bias_ref, turned_ref = refs

    @pl.when(pl.program_id(0) == 0)
    def _():
        turned_ref[...] = in_ref[...].astype(F32).T.astype(BF16)
        if carried:
            out_ref[...] = out_before_ref[...]
            d_in_ref[...] = d_in_before_ref[...]
        else:
            out_ref[...] = jnp.zeros_like(out_ref)
            d_in_ref[...] = jnp.zeros_like(d_in_ref)

    up = jnp.concatenate([up_a_ref[...], up_b_ref[...]], axis=1)
    down = jnp.concatenate([down_a_ref[...], down_b_ref[...]], axis=0)
    bias = jnp.concatenate([bias_a_ref[...], bias_b_ref[...]], axis=1)
    d_out = d_out_ref[...]
    pre = jnp.dot(in_ref[...], up, preferred_element_type=F32) + bias
    d_act = dot_over(d_out, down, 1, 1)
    square = pre * pre
    bend = jnp.tanh(GELU_SLOPE * pre * (1.0 + GELU_CUBE * square))
    half = 0.5 * (1.0 + bend)
    act = (pre * half).astype(BF16)
    slope = half + (0.5 * GELU_SLOPE) * pre * (1.0 - bend * bend) * (
        1.0 + (3.0 * GELU_CUBE) * square
    )
    d_pre = (d_act * slope).astype(BF16)
    out_ref[...] += jnp.dot(act, down, preferred_element_type=F32)
    d_in_ref[...] += dot_over(d_pre, up, 1, 1)
    d_up_ref[...] = jnp.dot(turned_ref[...], d_pre, preferred_element_type=F32).astype(BF16)
    d_down_ref[...] = jnp.dot(
        act.astype(F32).T.astype(BF16), d_out, preferred_element_type=F32
    ).astype(BF16)
    d_bias_ref[...] = jnp.sum(d_pre.astype(F32), axis=0, keepdims=True)


def feed(which, feed_in, d_feed_out, up_weight, up_bias, down_weight, before):
    tokens, width = feed_in.shape
    hidden_units = up_weight.shape[1]
    small = 128
    steps = hidden_units // (4 * small)
    own = hidden_units // 2

    def whole(shape):
        return pl.BlockSpec(shape, lambda step, which: (0,) * len(shape))

    def group(nth):
        return lambda step, which: 2 * (2 * step + nth) + which[0]

    def columns(nth, rows):
        return pl.BlockSpec((rows, small), lambda step, which: (0, group(nth)(step, which)))

    def rows_of(nth):
        return pl.BlockSpec((small, width), lambda step, which: (group(nth)(step, which), 0))

    args = [feed_in, d_feed_out, up_weight, up_weight, up_bias[None], up_bias[None]]
    args += [down_weight, down_weight]
    specs = [whole((tokens, width)), whole((tokens, width)), columns(0, width), columns(1, width)]
    specs += [columns(0, 1), columns(1, 1), rows_of(0), rows_of(1)]
    if before is not None:
        args += list(before)
        specs += [whole((tokens, width)), whole((tokens, width))]
    return pl.pallas_call(
        functools.partial(feed_kernel, before is not None),
        grid_spec=pltpu.PrefetchScalarGridSpec(
            num_scalar_prefetch=1,
            grid=(steps,),
            in_specs=specs,
            out_specs=(
                whole((tokens, width)),
                whole((tokens, width)),
                pl.BlockSpec((width, 2 * small), lambda step, which: (0, step)),
                pl.BlockSpec((2 * small, width), lambda step, which: (step, 0)),
                pl.BlockSpec((1, 2 * small), lambda step, which: (0, step)),
            ),
            scratch_shapes=[pltpu.VMEM((width, tokens), BF16)],
        ),
        out_shape=(
            jax.ShapeDtypeStruct((tokens, width), F32),
            jax.ShapeDtypeStruct((tokens, width), F32),
            jax.ShapeDtypeStruct((width, own), BF16),
            jax.ShapeDtypeStruct((own, width), BF16),
            jax.ShapeDtypeStruct((1, own), F32),
        ),
        cost_estimate=pl.CostEstimate(
            flops=12 * tokens * width * own,
            bytes_accessed=2 * (4 * own * width + 8 * tokens * width),
            transcendentals=tokens * own,
        ),
        compiler_params=pltpu.CompilerParams(vmem_limit_bytes=56 << 20),
        name="feed%d" % (before is not None),
    )(which.reshape(1), *args)


def norm_back(values, d_in, scale):
    centered = values - jnp.mean(values, axis=-1, keepdims=True)
    spread = jnp.mean(centered * centered, axis=-1, keepdims=True)
    inverse = lax.rsqrt(spread + EPSILON)
    normed = centered * inverse
    product = d_in * normed
    d_shift = jnp.sum(d_in, axis=0, keepdims=True)
    d_scale = jnp.sum(product, axis=0, keepdims=True)
    scaled = 1.0 + scale
    mean_d = jnp.mean(d_in * scaled, axis=-1, keepdims=True)
    mean_p = jnp.mean(product * scaled, axis=-1, keepdims=True)
    return (d_in * scaled - mean_d - normed * mean_p) * inverse, d_shift, d_scale


def middle_back_kernel(
    d_in_ref,
    middle_ref,
    grad_ref,
    attn_ref,
    feed_ref,
    scale_ref,
    gate_ref,
    feed_gate_ref,
    down_bias_ref,
    rows_ref,
    weight_ref,
    d_middle_ref,
    d_attn_ref,
    layer_ref,
    blocks_ref,
    sums_ref,
):
    frame = pl.program_id(0)
    per_device = pl.num_programs(0) - 1

    @pl.when(frame < per_device)
    def _():
        mine = pl.ds(frame, 1)
        middle = middle_ref[...]
        grads = grad_ref[...].astype(F32)
        back, d_shift, d_scale = norm_back(middle, d_in_ref[...], scale_ref[mine, :])
        d_middle = grads + back
        d_middle_ref[...] = d_middle
        d_attn = (d_middle * gate_ref[mine, :]).astype(BF16)
        d_attn_ref[...] = d_attn
        feed_rows = feed_ref[...] + down_bias_ref[...]
        feed_gate = feed_gate_ref[mine, :]
        layer_ref[...] = (middle + feed_gate * feed_rows).astype(BF16)
        d_feed_out = (feed_gate * grads).astype(BF16).astype(F32)
        sums_ref[frame] = jnp.concatenate(
            [
                jnp.sum(d_middle * attn_ref[...], axis=0, keepdims=True),
                d_shift,
                d_scale,
                jnp.sum(grads * feed_rows, axis=0, keepdims=True),
                jnp.sum(d_attn.astype(F32), axis=0, keepdims=True),
                jnp.sum(d_feed_out, axis=0, keepdims=True),
                jnp.zeros((2, d_shift.shape[1]), F32),
            ],
            axis=0,
        )
        d_mix = dot_over(weight_ref[...], d_attn, 1, 1).astype(BF16)
        for head in range(blocks_ref.shape[0]):
            blocks_ref[head, 0] = d_mix[head * HEAD : (head + 1) * HEAD]

    @pl.when(frame == per_device)
    def _():
        first = sums_ref[0]
        second = sums_ref[1]
        rows = jnp.concatenate(
            [first[:4], second[:4], first[4:6] + second[4:6], rows_ref[...]], axis=0
        ).astype(BF16)
        count = rows.shape[1] // PATCHES
        block = jnp.concatenate(
            [rows[:, nth * PATCHES : (nth + 1) * PATCHES] for nth in range(count)], axis=0
        )
        for head in range(blocks_ref.shape[0]):
            blocks_ref[head, 0] = block


def middle_back(
    per_device, d_in, middle, grads, attn_rows, feed_rows, scale, gate, feed_gate, down_bias, rows, weight
):
    tokens, width = d_in.shape
    heads = width // HEAD
    last = per_device - 1
    per_frame = pl.BlockSpec((PATCHES, width), lambda frame: (jnp.minimum(frame, last), 0))

    def whole(shape):
        return pl.BlockSpec(shape, lambda frame: (0,) * len(shape))

    small = whole((per_device, width))
    return pl.pallas_call(
        middle_back_kernel,
        grid=(per_device + 1,),
        out_shape=(
            jax.ShapeDtypeStruct((tokens, width), F32),
            jax.ShapeDtypeStruct((tokens, width), BF16),
            jax.ShapeDtypeStruct((tokens, width), BF16),
            jax.ShapeDtypeStruct((heads, per_device + 1, HEAD, PATCHES), BF16),
        ),
        in_specs=[per_frame] * 5
        + [small] * 3
        + [whole((1, width)), whole(rows.shape), whole(weight.shape)],
        out_specs=(
            per_frame,
            per_frame,
            per_frame,
            pl.BlockSpec((heads, 1, HEAD, PATCHES), lambda frame: (0, frame, 0, 0)),
        ),
        scratch_shapes=[pltpu.VMEM((per_device, 8, width), F32)],
        cost_estimate=pl.CostEstimate(
            flops=2 * tokens * width * width, bytes_accessed=24 * tokens * width, transcendentals=0
        ),
        compiler_params=pltpu.CompilerParams(vmem_limit_bytes=48 << 20),
        name="middle_back",
    )(
        d_in,
        middle,
        grads,
        attn_rows,
        feed_rows,
        scale,
        gate,
        feed_gate,
        down_bias[None],
        rows,
        weight,
    )


def unproject_kernel(
    per_device, carried, which_ref, in_ref, back_ref, wq_ref, wk_ref, wv_ref, *refs
):
    if not carried:
        refs = refs[-4:]
    if carried:
        before_ref, hidden_ref, d_middle_ref, scale_ref, bias_theirs_ref = refs[:5]
        d_weight_ref, grad_ref, rows_ref, d_in_ref, d_bias_ref, turned_ref = refs[5:]
    else:
        d_in_ref, d_weight_ref, d_bias_ref, turned_ref = refs

    @pl.when(pl.program_id(0) == 0)
    def _():
        turned_ref[...] = in_ref[...].astype(F32).T.astype(BF16)
        if carried:
            d_in_ref[...] = before_ref[...]
        else:
            d_in_ref[...] = jnp.zeros_like(d_in_ref)

    group = wq_ref.shape[1] // HEAD

    def token_major(block_of):
        rows = []
        for place in range(per_device):
            block = jnp.concatenate([block_of(head, place) for head in range(group)], axis=0)
            rows.append(block.astype(F32).T.astype(BF16))
        return jnp.concatenate(rows, axis=0)

    sides = jnp.concatenate(
        [
            token_major(lambda head, place: back_ref[head, 2 * per_device + place]),
            token_major(lambda head, place: back_ref[head, place]),
            token_major(lambda head, place: back_ref[head, per_device + place]),
        ],
        axis=1,
    )
    weights = jnp.concatenate([wq_ref[...], wk_ref[...], wv_ref[...]], axis=1)
    d_in_ref[...] += dot_over(sides, weights, 1, 1)
    d_weight = jnp.dot(turned_ref[...], sides, preferred_element_type=F32).astype(BF16)
    d_bias = jnp.sum(sides.astype(F32), axis=0, keepdims=True)
    lanes = group * HEAD
    for kind in range(3):
        d_weight_ref[kind] = d_weight[:, kind * lanes : (kind + 1) * lanes]
        part = d_bias[:, kind * lanes : (kind + 1) * lanes]
        if carried:
            start = pl.multiple_of(pl.program_id(0) * lanes, lanes)
            d_bias_ref[pl.ds(kind, 1), pl.ds(start, lanes)] = part
        else:
            d_bias_ref[kind] = part

    if carried:

        @pl.when(pl.program_id(0) == pl.num_programs(0) - 1)
        def _():
            sums = []
            for place in range(per_device):
                rows = pl.ds(place * PATCHES, PATCHES)
                mine = pl.ds(place, 1)
                back, d_shift, d_scale = norm_back(
                    hidden_ref[rows, :].astype(F32), d_in_ref[rows, :], scale_ref[mine, :]
                )
                grad_ref[rows, :] = (d_middle_ref[rows, :] + back).astype(BF16)
                sums += [d_shift, d_scale]
            for kind in range(3):
                sums.append(
                    jnp.concatenate([d_bias_ref[pl.ds(kind, 1), :], bias_theirs_ref[kind]], axis=1)
                )
            count = 16 - len(sums)
            late = jnp.concatenate(
                sums + [jnp.zeros((count, d_in_ref.shape[1]), F32)], axis=0
            ).astype(BF16)
            for target in range(rows_ref.shape[0]):
                rows_ref[target] = late


def unproject(per_device, targets, which, attn_in, back, weight, orders, before=None, norm_args=()):
    tokens, width = attn_in.shape
    heads = width // HEAD
    group = 2
    lanes = group * HEAD
    groups = heads // group
    steps = groups // 2

    def whole(shape):
        return pl.BlockSpec(shape, lambda step, which: (0,) * len(shape))

    def blocks(array):
        return pl.BlockSpec(
            (group,) + array.shape[1:], lambda step, which: (which[0] * steps + step, 0, 0, 0)
        )

    def part(kind):
        return pl.BlockSpec(
            (width, lanes), lambda step, which: (0, kind * groups + which[0] * steps + step)
        )

    args = [attn_in, back, weight, weight, weight]
    specs = [whole((tokens, width)), blocks(back), part(0), part(1), part(2)]
    weight_shape = (
        jax.ShapeDtypeStruct((3, width, width // 2), BF16),
        jax.ShapeDtypeStruct((3, 1, width // 2), F32),
    )
    weight_specs = (
        pl.BlockSpec((3, width, lanes), lambda step, which: (0, 0, step)),
        pl.BlockSpec((3, 1, lanes), lambda step, which: (0, 0, step)),
    )
    scratch = [pltpu.VMEM((width, tokens), BF16)]
    small = (per_device, width)
    if before is not None:
        args += [before] + list(norm_args)
        specs += [whole((tokens, width))] * 3 + [whole(small), whole((3, 1, width // 2))]
        late = (targets, 16, width)
        outs = weight_shape[:1] + (
            jax.ShapeDtypeStruct((tokens, width), BF16),
            jax.ShapeDtypeStruct(late, BF16),
        )
        out_specs = weight_specs[:1] + (whole((tokens, width)), whole(late))
        scratch = [pltpu.VMEM((tokens, width), F32), pltpu.VMEM((3, width // 2), F32)] + scratch
    else:
        outs = (jax.ShapeDtypeStruct((tokens, width), F32),) + weight_shape
        out_specs = (whole((tokens, width)),) + weight_specs
        orders = corners(orders)
        args += orders
        specs += [unread_spec()] * len(orders)
    return pl.pallas_call(
        functools.partial(unproject_kernel, per_device, before is not None),
        grid_spec=pltpu.PrefetchScalarGridSpec(
            num_scalar_prefetch=1,
            grid=(steps,),
            in_specs=specs,
            out_specs=out_specs,
            scratch_shapes=scratch,
        ),
        out_shape=outs,
        cost_estimate=pl.CostEstimate(
            flops=6 * tokens * width * width,
            bytes_accessed=2 * (3 * width * width + 6 * tokens * width),
            transcendentals=0,
        ),
        compiler_params=pltpu.CompilerParams(vmem_limit_bytes=48 << 20),
        name="unproject%d" % (before is not None),
    )(which.reshape(1), *args)


def columns_of(matrix, start, width, axis=1):
    if isinstance(start, int) and start == 0 and width == matrix.shape[axis]:
        return matrix
    return lax.dynamic_slice_in_dim(matrix, start, width, axis)


def local(
    hidden,
    cotangent,
    levels,
    segments,
    live_frames,
    noise_table,
    mod_weight,
    mod_bias,
    qkv_weight,
    qkv_bias,
    out_weight,
    out_bias,
    up_weight,
    up_bias,
    down_weight,
    down_bias,
):
    seq_index = lax.axis_index("seq")
    seq_count = lax.axis_size("seq")
    tokens = hidden.shape[1]
    width = hidden.shape[2]
    per_device = tokens // PATCHES
    frames = segments.shape[1]
    heads = width // HEAD
    copies = seq_count // heads
    hidden_units = up_weight.shape[1]
    level_count = noise_table.shape[0]
    share = width // seq_count
    clip_ids = segments[0]
    live = live_frames[0]

    pack = lax.axis_index("pack")
    halves = halving_fits()
    frame_ids = jnp.arange(frames, dtype=jnp.int32)
    same_clip = clip_ids[:, None] == clip_ids[None, :]
    clip_starts = jnp.min(jnp.where(same_clip, frame_ids[None, :], frames), axis=1)
    frame_times = (frame_ids - clip_starts).astype(F32)
    own_cos, own_sin = rotary_tables(
        lax.dynamic_slice_in_dim(frame_times, seq_index * per_device, per_device)
    )

    embed = jnp.concatenate(
        [
            lax.dynamic_slice_in_dim(noise_table, levels[0, frame], 1, 0)
            for frame in range(per_device)
        ],
        axis=0,
    )
    cond = jax.nn.silu(embed).astype(BF16)
    modulation = jnp.dot(cond, mod_weight[:, : 2 * width], preferred_element_type=F32)
    attn_shift, attn_scale = jnp.split(modulation + mod_bias[: 2 * width], 2, axis=1)
    attn_in, sent = project(
        per_device, hidden[0], attn_shift, attn_scale, qkv_weight, qkv_bias, own_cos, own_sin
    )

    def to_heads(array):
        if copies > 1:
            array = jnp.concatenate([array] * copies, axis=0)
        return lax.all_to_all(array, "seq", 0, 0, tiled=True)

    def to_tokens(array):
        return lax.all_to_all(array, "seq", 0, 0, tiled=True)[:heads]

    x = to_heads(sent)
    late_modulation = jnp.dot(
        after(cond, attn_in), mod_weight[:, 2 * width :], preferred_element_type=F32
    )
    attn_gate, feed_shift, feed_scale, feed_gate = jnp.split(
        late_modulation + mod_bias[2 * width :], 4, axis=1
    )
    cos_all, sin_all = rotary_tables(after(frame_times, attn_in))
    grad_rows = cotangent[0].astype(F32).reshape(per_device, PATCHES, width)
    d_feed_out = (feed_gate[:, None, :] * grad_rows).reshape(tokens, width).astype(BF16)
    x, d_feed_out, cos_all, sin_all = lax.optimization_barrier((x, d_feed_out, cos_all, sin_all))
    mix, wide, lse, kv = attend(per_device, clip_ids, live, x)
    mix = to_tokens(mix)
    mixes = [mix[:, place].reshape(width, PATCHES) for place in range(per_device)]
    attn_rows = jnp.stack([dot_over(each, out_weight, 0, 0) for each in mixes]) + out_bias
    attn_mix = jnp.concatenate(mixes, axis=1)

    frame_rows = hidden[0].astype(F32).reshape(per_device, PATCHES, width)
    middle = frame_rows + attn_gate[:, None, :] * attn_rows
    feed_in = modulate_norm(middle, feed_shift, feed_scale).reshape(tokens, width).astype(BF16)
    feed_args = (feed_in, d_feed_out, up_weight, up_bias, down_weight)
    theirs = feed(1 - pack if halves else pack * 0 + 1, *feed_args, None)
    mine = feed(pack if halves else pack * 0, *feed_args, theirs[:2])
    small = 128

    def in_order(own, other):
        if halves:
            even, odd = jnp.where(pack == 0, own, other), jnp.where(pack == 0, other, own)
        else:
            even, odd = own, other
        rows = own.shape[0]
        return jnp.stack(
            [even.reshape(rows, -1, small), odd.reshape(rows, -1, small)], axis=2
        ).reshape(rows, -1)

    own_levels = levels[0]
    level_row = jnp.concatenate(
        [
            jnp.broadcast_to(part[frame], (width // (2 * per_device),))
            for frame in range(per_device)
            for part in (lax.div(own_levels, 32), lax.rem(own_levels, 32))
        ]
    ).astype(F32)[None]
    extra_rows = jnp.concatenate(
        [
            in_order(mine[4], theirs[4]).reshape(-1, width),
            level_row,
            jnp.zeros((1, width), F32),
        ],
        axis=0,
    )
    d_middle, d_attn_out, layer_out, blocks = middle_back(
        per_device,
        mine[1],
        middle.reshape(tokens, width),
        cotangent[0],
        attn_rows.reshape(tokens, width),
        mine[0],
        feed_scale,
        attn_gate,
        feed_gate,
        down_bias,
        extra_rows,
        out_weight,
    )
    layer_out = layer_out.reshape(1, tokens, width)
    d_mix = to_heads(blocks)

    def out_term(start, size):
        return dot_over(attn_mix, columns_of(d_attn_out, start, size), 1, 0).astype(BF16)

    sums = ()
    if halves:
        up_sum = RowSum(mine[2], exchange(theirs[2], "pack", 1), (2, 1, 4, 8))
        down_sum = RowSum(mine[3], exchange(theirs[3], "pack", 1), (1, 2, 4, 8))
        out_theirs = exchange(out_term((1 - pack) * (width // 2), width // 2), "pack", 1)
        out_sum = RowSum(out_term(pack * (width // 2), width // 2), out_theirs, (1, 2, 4, 8))
        sums = (down_sum, up_sum)
    def own_share(row):
        piece = row.shape[0] // seq_count
        return lax.dynamic_slice_in_dim(row, seq_index * piece, piece)

    chunks = width // PATCHES
    early_rows = d_mix[:, per_device].reshape(seq_count, chunks, 16, PATCHES)
    early_rows = early_rows.transpose(0, 2, 1, 3).reshape(seq_count, 16, width)
    early_sets = of_packs(early_rows)
    early_sum = functools.reduce(
        jnp.add, [jnp.sum(each.astype(F32), axis=0) for each in early_sets]
    )
    out_bias_grad = own_share(early_sum[8])
    down_bias_grad = own_share(early_sum[9])
    up_bias_grad = own_share(early_sum[10:14].reshape(hidden_units))

    def frames_of(rows, per_frame, kinds):
        return jnp.concatenate(
            [
                jnp.stack(
                    [rows[:, frame * per_frame + kind] for frame in range(per_device)], axis=1
                ).reshape(-1, width)
                for kind in range(kinds)
            ],
            axis=1,
        )

    own_table = lax.dynamic_slice_in_dim(noise_table, seq_index * share, share, 1)
    own_mod = lax.dynamic_slice_in_dim(mod_weight, seq_index * share, share, 0)
    stride = width // (2 * per_device)
    parts = []
    for rows in early_sets:
        coded = rows[:, 14, ::stride].astype(jnp.int32).reshape(-1, 2)
        set_levels = coded[:, 0] * 32 + coded[:, 1]
        picks = (set_levels[:, None] == jnp.arange(level_count, dtype=jnp.int32)[None, :]).astype(F32)
        embeds = jnp.dot(picks, own_table, precision=PRECISE, preferred_element_type=F32)
        set_cond = jax.nn.silu(embeds).astype(BF16)
        d_mod = frames_of(rows, 4, 4)
        parts.append(
            (
                picks,
                embeds,
                set_cond,
                dot_over(d_mod, own_mod[:, 2 * width :], 1, 1),
                dot_over(set_cond, d_mod, 0, 0),
            )
        )
    mod_grad_early = functools.reduce(jnp.add, [each[4] for each in parts])
    mod_sum_early = (early_sum[:4] + early_sum[4:8]).reshape(4 * width)
    before = None
    for part in range(per_device):
        if halves and part:
            for each in (up_sum, down_sum, out_sum):
                before = (each.tie(before[0]), before[1])
        orders = [each.stage() for each in sums]
        if halves and part:
            orders.append(out_sum.stage())
        before = attend_back(
            part,
            per_device,
            clip_ids,
            live,
            x,
            kv,
            wide,
            lse,
            d_mix,
            cos_all,
            sin_all,
            before,
            orders,
        )
    for each in sums:
        before = each.tie(before)
    back = to_tokens(before)
    orders = []
    if halves:
        out_sum.stage()
        for each in (up_sum, down_sum, out_sum):
            each.stage()
            orders.append(each.parts[1])
    orders += [mod_grad_early] + [part[3] for part in parts]
    which = (1 - pack, pack) if halves else (pack * 0, pack * 0 + 1)
    d_in_theirs, qkv_theirs, bias_theirs = unproject(
        per_device, seq_count, which[0], attn_in, back, qkv_weight, orders
    )
    qkv_mine, hidden_grad, late = unproject(
        per_device,
        seq_count,
        which[1],
        attn_in,
        back,
        qkv_weight,
        (),
        d_in_theirs,
        (hidden[0], d_middle, attn_scale, bias_theirs),
    )
    hidden_grad = hidden_grad.reshape(1, tokens, width)
    late_rows = lax.all_to_all(late, "seq", 0, 0, tiled=True)

    def halves_in_order(own, other):
        if halves:
            return jnp.where(pack == 0, own, other), jnp.where(pack == 0, other, own)
        return other, own

    if halves:
        came = exchange(qkv_theirs, "pack", 1)
        split = width // 4
        qkv_sums = [
            RowSum(qkv_mine[..., :split], came[..., :split], (1, 2, 4, 8)),
            RowSum(qkv_mine[..., split:], came[..., split:], (2, 1, 4, 8)),
        ]
        for each in qkv_sums:
            each.stage((up_sum, down_sum, out_sum))
        for each in (up_sum, down_sum, out_sum):
            each.stage(qkv_sums)
        up_weight_grad, down_weight_grad, out_weight_grad, qkv_weight_grad = settle(
            pack, *[each.finish() for each in (up_sum, down_sum, out_sum, *qkv_sums)]
        )
    else:
        up_weight_grad = row_sum_direct(in_order(mine[2], theirs[2]))
        pairs = [each[3].reshape(-1, small, width) for each in (mine, theirs)]
        down_weight_grad = row_sum_direct(jnp.stack(pairs, axis=1).reshape(hidden_units, width))
        out_weight_grad = row_sum_direct(out_term(0, width))
        qkv_term = jnp.concatenate(halves_in_order(qkv_mine, qkv_theirs), axis=-1)
        qkv_weight_grad = row_sum_direct(qkv_term.transpose(1, 0, 2).reshape(width, 3 * width))

    late_sets = of_packs(late_rows[:, :8])
    bias_at = 2 * per_device
    bias_sums = [
        jnp.sum(rows[:, bias_at : bias_at + 3].astype(F32), axis=0) for rows in late_sets
    ]
    if halves:
        ones, twos = bias_sums
        half = width // 2
        own_half = ones[:, :half] + twos[:, half:]
        other_half = ones[:, half:] + twos[:, :half]
    else:
        total = functools.reduce(jnp.add, bias_sums)
        own_half, other_half = total[:, : width // 2], total[:, width // 2 :]
    bias_total = jnp.concatenate(halves_in_order(own_half, other_half), axis=1)
    qkv_bias_grad = own_share(bias_total.reshape(3 * width))
    late_mods = [frames_of(rows, 2, 2) for rows in late_sets]
    mod_sum_late = functools.reduce(
        jnp.add, [jnp.sum(each.astype(F32), axis=0) for each in late_mods]
    )
    d_embeds = []
    for part, d_mod in zip(parts, late_mods):
        d_cond = part[3] + dot_over(d_mod, own_mod[:, : 2 * width], 1, 1)
        d_embeds.append(jax.vjp(jax.nn.silu, part[1])[1](d_cond)[0])
    table_grad = lax.dot_general(
        jnp.concatenate([part[0] for part in parts], axis=0),
        jnp.concatenate(d_embeds, axis=0),
        (((0,), (0,)), ((), ())),
        precision=PRECISE,
        preferred_element_type=F32,
    )
    mod_grad_late = functools.reduce(
        jnp.add, [dot_over(part[2], d_mod, 0, 0) for part, d_mod in zip(parts, late_mods)]
    )
    mod_weight_grad = jnp.concatenate([mod_grad_late, mod_grad_early], axis=1)
    mod_bias_grad = own_share(jnp.concatenate([mod_sum_late, mod_sum_early]))
    return (
        layer_out,
        hidden_grad,
        table_grad,
        mod_weight_grad,
        mod_bias_grad,
        qkv_weight_grad,
        qkv_bias_grad,
        out_weight_grad,
        out_bias_grad,
        up_weight_grad,
        up_bias_grad,
        down_weight_grad,
        down_bias_grad,
    )


def solution(mesh):
    in_specs = (
        P("pack", "seq", None),
        P("pack", "seq", None),
        P("pack", "seq"),
        P("pack", None),
        P("pack", None),
    ) + (P(),) * 11
    out_specs = (
        P("pack", "seq", None),
        P("pack", "seq", None),
        P(None, "seq"),
        P("seq", None),
        P("seq"),
        P("seq", None),
        P("seq"),
        P("seq", None),
        P("seq"),
        P("seq", None),
        P("seq"),
        P("seq", None),
        P("seq"),
    )
    return jax.shard_map(local, mesh=mesh, in_specs=in_specs, out_specs=out_specs, check_vma=False)
```

```python
import functools

import jax
import jax.numpy as jnp
from jax import lax
from jax.experimental import pallas as pl
from jax.experimental.pallas import tpu as pltpu
from jax.sharding import PartitionSpec as P

HEAD = 64
PATCHES = 256
SIDE = 16
EPSILON = 1e-06
PRECISE = lax.Precision.HIGHEST
HALF = HEAD // 2
F32 = jnp.float32
BF16 = jnp.bfloat16


def modulate_norm(rows, shift, scale):
    center = jnp.mean(rows, axis=-1, keepdims=True)
    centered = rows - center
    spread = jnp.mean(centered * centered, axis=-1, keepdims=True)
    normed = centered * lax.rsqrt(spread + EPSILON)
    return normed * (1.0 + scale[:, None, :]) + shift[:, None, :]


def gelu_tanh(values):
    return jax.nn.gelu(values, approximate=True)


def dot_over(first, second, first_dim, second_dim):
    return lax.dot_general(
        first, second, (((first_dim,), (second_dim,)), ((), ())), preferred_element_type=F32
    )


def spatial_angles():
    time_pairs = HALF // 4
    space_pairs = (HALF - time_pairs) // 2
    patch = jnp.arange(PATCHES, dtype=jnp.int32)
    row_pos = (patch // SIDE).astype(F32)
    col_pos = (patch % SIDE).astype(F32)
    time_freq = 10000.0 ** (-jnp.arange(time_pairs, dtype=F32) / time_pairs)
    space_freq = 10000.0 ** (-jnp.arange(space_pairs, dtype=F32) / space_pairs)
    space = jnp.concatenate(
        [space_freq[:, None] * row_pos[None, :], space_freq[:, None] * col_pos[None, :]], axis=0
    )
    return time_freq, space


def rotary_tables(time_frames):
    time_freq, space = spatial_angles()
    count = time_frames.shape[0]
    time_angle = time_frames[:, None] * time_freq[None, :]

    def whole(function):
        return jnp.concatenate(
            [
                jnp.broadcast_to(
                    function(time_angle)[:, :, None], (count, time_freq.shape[0], PATCHES)
                ),
                jnp.broadcast_to(function(space)[None], (count,) + space.shape),
            ],
            axis=1,
        )

    return whole(jnp.cos), whole(jnp.sin)


def walk_frames(frames, per_device, segments_ref, live_ref, list_ref, visit):
    def step(source, held):
        for place in range(per_device):
            frame = source * per_device + place
            before = jnp.maximum(frame - 1, 0)
            fresh = (frame == 0) | (segments_ref[frame] != segments_ref[before])
            held = jnp.where(fresh, 0, held)
            list_ref[held] = frame
            visit(source, place, frame, held + 1)
            held = held + jnp.where(live_ref[frame] == 1, 1, 0)
        return held

    lax.fori_loop(0, frames // per_device, step, jnp.int32(0))


def attend_kernel(per_device, segments_ref, live_ref, x_ref, mix_ref, wide_ref, lse_ref, kv_ref, list_ref):
    frames = kv_ref.shape[0]

    def turn(source, carry):
        for place in range(per_device):
            both = jnp.concatenate(
                [x_ref[source, place], x_ref[source, per_device + place]], axis=0
            )
            kv_ref[source * per_device + place] = both.T
        return carry

    lax.fori_loop(0, frames // per_device, turn, 0)

    def visit(source, place, frame, count):
        query = x_ref[source, 2 * per_device + place]
        query_side = jnp.concatenate([query, jnp.zeros_like(query)], axis=0)

        def scores_of(other):
            return jnp.dot(kv_ref[other], query_side, preferred_element_type=F32)

        def mixed(other, weights):
            value = x_ref[lax.div(other, per_device), per_device + lax.rem(other, per_device)]
            return jnp.dot(value, weights.astype(BF16), preferred_element_type=F32)

        def join(others, carry):
            scores = [scores_of(other) for other in others]
            tops = [jnp.max(score, axis=0, keepdims=True) for score in scores]
            new_top = functools.reduce(jnp.maximum, tops)
            if carry is not None:
                top, total, accum = carry
                new_top = jnp.maximum(top, new_top)
                shrink = jnp.exp(top - new_top)
                total = total * shrink
                accum = accum * shrink
            for index, score in enumerate(scores):
                weights = jnp.exp(score - new_top)
                added = jnp.sum(weights, axis=0, keepdims=True)
                product = mixed(others[index], weights)
                if carry is None and index == 0:
                    total, accum = added, product
                else:
                    total, accum = total + added, accum + product
            return new_top, total, accum

        others = count - 1
        carry = join([frame], None)
        carry = lax.fori_loop(
            0,
            lax.div(others, 4),
            lambda index, state: join([list_ref[4 * index + nth] for nth in range(4)], state),
            carry,
        )
        carry = lax.fori_loop(
            lax.div(others, 4) * 2,
            lax.div(others, 2),
            lambda index, state: join([list_ref[2 * index], list_ref[2 * index + 1]], state),
            carry,
        )
        top, total, accum = lax.fori_loop(
            0,
            lax.rem(others, 2),
            lambda unused, state: join([list_ref[others - 1]], state),
            carry,
        )
        result = accum * (1.0 / total)
        wide_ref[source, place] = result
        mix_ref[source, place] = result.astype(BF16)
        lse_ref[pl.ds(frame, 1), :] = top + jnp.log(total)

    walk_frames(frames, per_device, segments_ref, live_ref, list_ref, visit)


def corners(values):
    return [each.reshape(-1, each.shape[-1])[:1, :128] for each in values]


def unread_spec():
    return pl.BlockSpec(memory_space=pl.ANY)


def whole_spec():
    return pl.BlockSpec(memory_space=pltpu.VMEM)


def scalar_spec():
    return pl.BlockSpec(memory_space=pltpu.SMEM)


def attend(per_device, segments, live, x):
    sources = x.shape[0]
    frames = sources * per_device
    pairs = frames * 6
    outs = (
        jax.ShapeDtypeStruct((sources, per_device, HEAD, PATCHES), BF16),
        jax.ShapeDtypeStruct((sources, per_device, HEAD, PATCHES), F32),
        jax.ShapeDtypeStruct((frames, PATCHES), F32),
        jax.ShapeDtypeStruct((frames, PATCHES, 2 * HEAD), BF16),
    )
    return pl.pallas_call(
        functools.partial(attend_kernel, per_device),
        out_shape=outs,
        in_specs=[scalar_spec(), scalar_spec(), whole_spec()],
        out_specs=(whole_spec(),) * len(outs),
        scratch_shapes=[pltpu.SMEM((frames,), jnp.int32)],
        cost_estimate=pl.CostEstimate(
            flops=pairs * 4 * PATCHES * PATCHES * 256,
            bytes_accessed=x.size * 2 * 3,
            transcendentals=pairs * PATCHES * PATCHES,
        ),
        compiler_params=pltpu.CompilerParams(vmem_limit_bytes=40 << 20),
        name="attend",
    )(segments, live, x)


def attend_back_kernel(
    per_device,
    segments_ref,
    live_ref,
    x_ref,
    kv_ref,
    wide_ref,
    lse_ref,
    d_mix_ref,
    cos_ref,
    sin_ref,
    *refs
):
    out_ref, dkv_ref, list_ref = refs[-3:]
    frames = kv_ref.shape[0]

    def unturn(frame, values):
        lower = values[:HALF]
        upper = values[HALF:]
        cosine = cos_ref[frame]
        sine = sin_ref[frame]
        return jnp.concatenate([lower * cosine + upper * sine, upper * cosine - lower * sine], axis=0)

    def visit(source, place, frame, count):
        query = x_ref[source, 2 * per_device + place]
        d_mix = d_mix_ref[source, place]
        blank = jnp.zeros_like(query)
        query_side = jnp.concatenate([query, blank], axis=0)
        d_mix_side = jnp.concatenate([blank, d_mix], axis=0)
        turned = jnp.concatenate([query, d_mix], axis=0).T
        first = lax.broadcasted_iota(jnp.int32, turned.shape, 1) < HEAD
        nothing = jnp.zeros_like(turned)
        both = jnp.concatenate(
            [jnp.where(first, turned, nothing), jnp.where(first, nothing, turned)], axis=0
        )
        lse = lse_ref[pl.ds(frame, 1), :]
        delta = jnp.sum(d_mix.astype(F32) * wide_ref[source, place], axis=0, keepdims=True)

        def block(other, own=False):
            key_value = kv_ref[other]
            scores = jnp.dot(key_value, query_side, preferred_element_type=F32)
            d_weights = jnp.dot(key_value, d_mix_side, preferred_element_type=F32)
            weights = jnp.exp(scores - lse)
            d_scores = (weights * (d_weights - delta)).astype(BF16)
            sides = jnp.concatenate([d_scores, weights.astype(BF16)], axis=1)
            d_both = jnp.dot(sides, both, preferred_element_type=F32)
            if own:
                dkv_ref[other] = d_both
            else:
                dkv_ref[other] += d_both
            key = x_ref[lax.div(other, per_device), lax.rem(other, per_device)]
            return jnp.dot(key, d_scores, preferred_element_type=F32)

        others = count - 1
        d_query = block(frame, True)
        d_query = lax.fori_loop(
            0,
            lax.div(others, 2),
            lambda index, state: state
            + block(list_ref[2 * index])
            + block(list_ref[2 * index + 1]),
            d_query,
        )
        d_query = lax.fori_loop(
            0,
            lax.rem(others, 2),
            lambda unused, state: state + block(list_ref[others - 1]),
            d_query,
        )
        d_query = unturn(frame, d_query * (HEAD**-0.5)).astype(BF16)
        out_ref[source, 2 * per_device + place] = d_query

    walk_frames(frames, per_device, segments_ref, live_ref, list_ref, visit)

    def finish(source, carry):
        for place in range(per_device):
            frame = source * per_device + place
            both = dkv_ref[frame].T
            out_ref[source, place] = unturn(frame, both[:HEAD]).astype(BF16)
            out_ref[source, per_device + place] = both[HEAD:].astype(BF16)
        return carry

    lax.fori_loop(0, frames // per_device, finish, 0)


def attend_back(per_device, segments, live, x, kv, wide, lse, d_mix, cosine, sine, orders):
    sources = x.shape[0]
    frames = sources * per_device
    pairs = frames * 6
    args = [segments, live, x, kv, wide, lse, d_mix, cosine, sine]
    specs = [scalar_spec(), scalar_spec()] + [whole_spec()] * (len(args) - 2)
    orders = corners(orders)
    return pl.pallas_call(
        functools.partial(attend_back_kernel, per_device),
        out_shape=jax.ShapeDtypeStruct(x.shape, BF16),
        in_specs=specs + [unread_spec()] * len(orders),
        out_specs=whole_spec(),
        scratch_shapes=[
            pltpu.VMEM((frames, PATCHES, 2 * HEAD), F32),
            pltpu.SMEM((frames,), jnp.int32),
        ],
        cost_estimate=pl.CostEstimate(
            flops=pairs * 10 * PATCHES * PATCHES * 64,
            bytes_accessed=x.size * 2 * 5,
            transcendentals=pairs * PATCHES * PATCHES,
        ),
        compiler_params=pltpu.CompilerParams(vmem_limit_bytes=60 << 20),
        name="attend_back",
    )(*args, *orders)


def exchange(value, axis, bit):
    count = lax.axis_size(axis)
    return lax.ppermute(value, axis, [(source, source ^ bit) for source in range(count)])


def after(value, *earlier):
    return lax.optimization_barrier((value,) + earlier)[0]


def of_packs(value):
    values = [value]
    bit = lax.axis_size("pack") // 2
    while bit:
        values = values + [exchange(each, "pack", bit) for each in values]
        bit //= 2
    return values


def halving_fits():
    return lax.axis_size("pack") == 2 and lax.axis_size("seq") == 16


class RowSum:
    def __init__(self, mine, came, order):
        self.order = list(order)
        self.index = lax.axis_index("seq")
        rows = mine.shape[-2]
        self.tail = (rows // 16, mine.shape[-1])
        self.lead = mine.shape[:-2]
        shape = self.lead + (2, 2, 2, 2) + self.tail
        self.parts = [mine.reshape(shape), came.reshape(shape)]

    def pick(self, bit, which):
        axis = len(self.lead) + {8: 0, 4: 1, 2: 2, 1: 3}[bit]
        pieces = [lax.dynamic_slice_in_dim(part, which, 1, axis) for part in self.parts]
        return (pieces[0].astype(F32) + pieces[1].astype(F32)).astype(BF16)

    def tie_kept(self, value):
        value, self.parts[0] = lax.optimization_barrier((value, self.parts[0]))
        return value

    def stage(self, later=(), value=None):
        bit = self.order.pop(0)
        own_bit = lax.rem(lax.div(self.index, bit), 2)
        send = self.pick(bit, 1 - own_bit)
        for each in later:
            send = each.tie_kept(send)
        if value is not None:
            send, value = lax.optimization_barrier((send, value))
        came = exchange(send, "seq", bit)
        self.parts = [self.pick(bit, own_bit), came]
        return send if value is None else value

    def tie(self, value):
        value, *self.parts = lax.optimization_barrier((value, *self.parts))
        return value

    def finish(self):
        while self.order:
            self.stage()
        own = (self.parts[0].astype(F32) + self.parts[1].astype(F32)).astype(BF16)
        own = own.reshape(self.lead + self.tail)
        return own, exchange(own, "pack", 1)


def settle_kernel(pack_ref, *refs):
    ups, downs, outs, firsts, seconds = [refs[2 * nth : 2 * nth + 2] for nth in range(5)]
    up_ref, down_ref, out_ref, qkv_ref = refs[10:]
    own_first = pack_ref[0] == 0
    small = 128

    def of_pack(pack, pair, *index):
        one, two = pair[0][index].astype(F32), pair[1][index].astype(F32)
        return jnp.where(own_first, one, two) if pack == 0 else jnp.where(own_first, two, one)

    every = slice(None)
    for pack in range(2):
        for group in range(ups[0].shape[1] // small):
            at = (2 * group + pack) * small
            columns = slice(group * small, (group + 1) * small)
            up_ref[:, at : at + small] = of_pack(pack, ups, every, columns)
        rows = downs[0].shape[0]
        down_ref[pack * rows : (pack + 1) * rows, :] = of_pack(pack, downs, every, every)
        columns = outs[0].shape[1]
        out_ref[:, pack * columns : (pack + 1) * columns] = of_pack(pack, outs, every, every)
        for kind in range(3):
            for nth, pair in enumerate((firsts, seconds)):
                columns = pair[0].shape[2]
                at = (4 * kind + 2 * pack + nth) * columns
                qkv_ref[:, at : at + columns] = of_pack(pack, pair, kind, every, every)


def settle(pack, *pairs):
    up, down, out, qkv = pairs[0][0], pairs[1][0], pairs[2][0], pairs[3][0]
    shapes = (
        (up.shape[0], 2 * up.shape[1]),
        (2 * down.shape[0], down.shape[1]),
        (out.shape[0], 2 * out.shape[1]),
        (qkv.shape[1], 12 * qkv.shape[2]),
    )
    args = [each for pair in pairs for each in pair]
    return pl.pallas_call(
        settle_kernel,
        out_shape=tuple(jax.ShapeDtypeStruct(shape, F32) for shape in shapes),
        in_specs=[scalar_spec()] + [whole_spec()] * len(args),
        out_specs=(whole_spec(),) * 4,
        compiler_params=pltpu.CompilerParams(vmem_limit_bytes=32 << 20),
        name="settle",
    )(pack.reshape(1), *args)


def row_sum_direct(term):
    part = lax.psum_scatter(term.astype(BF16), "seq", scatter_dimension=0, tiled=True)
    return lax.psum(part, "pack").astype(F32)


def project_kernel(
    per_device,
    hidden_ref,
    shift_ref,
    scale_ref,
    wq_ref,
    wk_ref,
    wv_ref,
    bq_ref,
    bk_ref,
    bv_ref,
    cos_ref,
    sin_ref,
    in_ref,
    x_ref,
):
    @pl.when(pl.program_id(0) == 0)
    def _():
        for place in range(per_device):
            rows = pl.ds(place * PATCHES, PATCHES)
            values = hidden_ref[rows, :].astype(F32)
            centered = values - jnp.mean(values, axis=-1, keepdims=True)
            spread = jnp.mean(centered * centered, axis=-1, keepdims=True)
            normed = centered * lax.rsqrt(spread + EPSILON)
            scale = scale_ref[pl.ds(place, 1), :]
            in_ref[rows, :] = (normed * (1.0 + scale) + shift_ref[pl.ds(place, 1), :]).astype(BF16)

    rows = in_ref[...]
    group = wq_ref.shape[1] // HEAD

    def turned(values, place):
        lower = values[:HALF]
        upper = values[HALF:]
        cosine = cos_ref[place]
        sine = sin_ref[place]
        return jnp.concatenate([lower * cosine - upper * sine, upper * cosine + lower * sine], axis=0)

    for kind, (weight_ref, bias_ref) in enumerate(
        ((wq_ref, bq_ref), (wk_ref, bk_ref), (wv_ref, bv_ref))
    ):
        flat = jnp.dot(rows, weight_ref[...], preferred_element_type=F32) + bias_ref[...]
        for place in range(per_device):
            block = flat[place * PATCHES : (place + 1) * PATCHES].T
            for head in range(group):
                values = block[head * HEAD : (head + 1) * HEAD]
                if kind == 0:
                    values = turned(values, place) * (HEAD**-0.5)
                    x_ref[head, 2 * per_device + place] = values.astype(BF16)
                elif kind == 1:
                    x_ref[head, place] = turned(values, place).astype(BF16)
                else:
                    x_ref[head, per_device + place] = values.astype(BF16)


def project(per_device, hidden, shift, scale, weight, bias, cosine, sine):
    tokens, width = hidden.shape
    heads = width // HEAD
    group = 2
    lanes = group * HEAD
    steps = heads // group
    bias_row = bias[None, :]

    def whole(shape):
        return pl.BlockSpec(shape, lambda step: (0,) * len(shape))

    def part(kind, rows):
        return pl.BlockSpec((rows, lanes), lambda step: (0, kind * steps + step))

    blocks = (heads, 3 * per_device, HEAD, PATCHES)
    return pl.pallas_call(
        functools.partial(project_kernel, per_device),
        grid=(steps,),
        out_shape=(
            jax.ShapeDtypeStruct((tokens, width), BF16),
            jax.ShapeDtypeStruct(blocks, BF16),
        ),
        in_specs=[whole((tokens, width)), whole(shift.shape), whole(scale.shape)]
        + [part(kind, width) for kind in range(3)]
        + [part(kind, 1) for kind in range(3)]
        + [whole(cosine.shape), whole(sine.shape)],
        out_specs=(
            whole((tokens, width)),
            pl.BlockSpec((group,) + blocks[1:], lambda step: (step, 0, 0, 0)),
        ),
        cost_estimate=pl.CostEstimate(
            flops=2 * tokens * width * 3 * width,
            bytes_accessed=2 * (weight.size + 5 * tokens * width),
            transcendentals=0,
        ),
        compiler_params=pltpu.CompilerParams(vmem_limit_bytes=40 << 20),
        name="project",
    )(hidden, shift, scale, weight, weight, weight, bias_row, bias_row, bias_row, cosine, sine)


GELU_SLOPE = 0.7978845608028654
GELU_CUBE = 0.044715


def feed_kernel(
    carried,
    which_ref,
    in_ref,
    d_out_ref,
    up_a_ref,
    up_b_ref,
    bias_a_ref,
    bias_b_ref,
    down_a_ref,
    down_b_ref,
    *refs
):
    if carried:
        out_before_ref, d_in_before_ref = refs[:2]
        refs = refs[2:]
    out_ref, d_in_ref, d_up_ref, d_down_ref, d_bias_ref, turned_ref = refs

    @pl.when(pl.program_id(0) == 0)
    def _():
        turned_ref[...] = in_ref[...].astype(F32).T.astype(BF16)
        if carried:
            out_ref[...] = out_before_ref[...]
            d_in_ref[...] = d_in_before_ref[...]
        else:
            out_ref[...] = jnp.zeros_like(out_ref)
            d_in_ref[...] = jnp.zeros_like(d_in_ref)

    up = jnp.concatenate([up_a_ref[...], up_b_ref[...]], axis=1)
    down = jnp.concatenate([down_a_ref[...], down_b_ref[...]], axis=0)
    bias = jnp.concatenate([bias_a_ref[...], bias_b_ref[...]], axis=1)
    d_out = d_out_ref[...]
    pre = jnp.dot(in_ref[...], up, preferred_element_type=F32) + bias
    d_act = dot_over(d_out, down, 1, 1)
    square = pre * pre
    bend = jnp.tanh(GELU_SLOPE * pre * (1.0 + GELU_CUBE * square))
    half = 0.5 * (1.0 + bend)
    act = (pre * half).astype(BF16)
    slope = half + (0.5 * GELU_SLOPE) * pre * (1.0 - bend * bend) * (
        1.0 + (3.0 * GELU_CUBE) * square
    )
    d_pre = (d_act * slope).astype(BF16)
    out_ref[...] += jnp.dot(act, down, preferred_element_type=F32)
    d_in_ref[...] += dot_over(d_pre, up, 1, 1)
    d_up_ref[...] = jnp.dot(turned_ref[...], d_pre, preferred_element_type=F32).astype(BF16)
    d_down_ref[...] = jnp.dot(
        act.astype(F32).T.astype(BF16), d_out, preferred_element_type=F32
    ).astype(BF16)
    d_bias_ref[...] = jnp.sum(d_pre.astype(F32), axis=0, keepdims=True)


def feed(which, feed_in, d_feed_out, up_weight, up_bias, down_weight, before):
    tokens, width = feed_in.shape
    hidden_units = up_weight.shape[1]
    small = 128
    steps = hidden_units // (4 * small)
    own = hidden_units // 2

    def whole(shape):
        return pl.BlockSpec(shape, lambda step, which: (0,) * len(shape))

    def group(nth):
        return lambda step, which: 2 * (2 * step + nth) + which[0]

    def columns(nth, rows):
        return pl.BlockSpec((rows, small), lambda step, which: (0, group(nth)(step, which)))

    def rows_of(nth):
        return pl.BlockSpec((small, width), lambda step, which: (group(nth)(step, which), 0))

    args = [feed_in, d_feed_out, up_weight, up_weight, up_bias[None], up_bias[None]]
    args += [down_weight, down_weight]
    specs = [whole((tokens, width)), whole((tokens, width)), columns(0, width), columns(1, width)]
    specs += [columns(0, 1), columns(1, 1), rows_of(0), rows_of(1)]
    if before is not None:
        args += list(before)
        specs += [whole((tokens, width)), whole((tokens, width))]
    return pl.pallas_call(
        functools.partial(feed_kernel, before is not None),
        grid_spec=pltpu.PrefetchScalarGridSpec(
            num_scalar_prefetch=1,
            grid=(steps,),
            in_specs=specs,
            out_specs=(
                whole((tokens, width)),
                whole((tokens, width)),
                pl.BlockSpec((width, 2 * small), lambda step, which: (0, step)),
                pl.BlockSpec((2 * small, width), lambda step, which: (step, 0)),
                pl.BlockSpec((1, 2 * small), lambda step, which: (0, step)),
            ),
            scratch_shapes=[pltpu.VMEM((width, tokens), BF16)],
        ),
        out_shape=(
            jax.ShapeDtypeStruct((tokens, width), F32),
            jax.ShapeDtypeStruct((tokens, width), F32),
            jax.ShapeDtypeStruct((width, own), BF16),
            jax.ShapeDtypeStruct((own, width), BF16),
            jax.ShapeDtypeStruct((1, own), F32),
        ),
        cost_estimate=pl.CostEstimate(
            flops=12 * tokens * width * own,
            bytes_accessed=2 * (4 * own * width + 8 * tokens * width),
            transcendentals=tokens * own,
        ),
        compiler_params=pltpu.CompilerParams(vmem_limit_bytes=56 << 20),
        name="feed%d" % (before is not None),
    )(which.reshape(1), *args)


def norm_back(values, d_in, scale):
    centered = values - jnp.mean(values, axis=-1, keepdims=True)
    spread = jnp.mean(centered * centered, axis=-1, keepdims=True)
    inverse = lax.rsqrt(spread + EPSILON)
    normed = centered * inverse
    product = d_in * normed
    d_shift = jnp.sum(d_in, axis=0, keepdims=True)
    d_scale = jnp.sum(product, axis=0, keepdims=True)
    scaled = 1.0 + scale
    mean_d = jnp.mean(d_in * scaled, axis=-1, keepdims=True)
    mean_p = jnp.mean(product * scaled, axis=-1, keepdims=True)
    return (d_in * scaled - mean_d - normed * mean_p) * inverse, d_shift, d_scale


def middle_back_kernel(
    d_in_ref,
    middle_ref,
    grad_ref,
    attn_ref,
    feed_ref,
    scale_ref,
    gate_ref,
    feed_gate_ref,
    down_bias_ref,
    rows_ref,
    weight_ref,
    d_middle_ref,
    d_attn_ref,
    layer_ref,
    blocks_ref,
    sums_ref,
):
    frame = pl.program_id(0)
    per_device = pl.num_programs(0) - 1

    @pl.when(frame < per_device)
    def _():
        mine = pl.ds(frame, 1)
        middle = middle_ref[...]
        grads = grad_ref[...].astype(F32)
        back, d_shift, d_scale = norm_back(middle, d_in_ref[...], scale_ref[mine, :])
        d_middle = grads + back
        d_middle_ref[...] = d_middle
        d_attn = (d_middle * gate_ref[mine, :]).astype(BF16)
        d_attn_ref[...] = d_attn
        feed_rows = feed_ref[...] + down_bias_ref[...]
        feed_gate = feed_gate_ref[mine, :]
        layer_ref[...] = (middle + feed_gate * feed_rows).astype(BF16)
        d_feed_out = (feed_gate * grads).astype(BF16).astype(F32)
        sums_ref[frame] = jnp.concatenate(
            [
                jnp.sum(d_middle * attn_ref[...], axis=0, keepdims=True),
                d_shift,
                d_scale,
                jnp.sum(grads * feed_rows, axis=0, keepdims=True),
                jnp.sum(d_attn.astype(F32), axis=0, keepdims=True),
                jnp.sum(d_feed_out, axis=0, keepdims=True),
                jnp.zeros((2, d_shift.shape[1]), F32),
            ],
            axis=0,
        )
        d_mix = dot_over(weight_ref[...], d_attn, 1, 1).astype(BF16)
        for head in range(blocks_ref.shape[0]):
            blocks_ref[head, 0] = d_mix[head * HEAD : (head + 1) * HEAD]

    @pl.when(frame == per_device)
    def _():
        first = sums_ref[0]
        second = sums_ref[1]
        rows = jnp.concatenate(
            [first[:4], second[:4], first[4:6] + second[4:6], rows_ref[...]], axis=0
        ).astype(BF16)
        count = rows.shape[1] // PATCHES
        block = jnp.concatenate(
            [rows[:, nth * PATCHES : (nth + 1) * PATCHES] for nth in range(count)], axis=0
        )
        for head in range(blocks_ref.shape[0]):
            blocks_ref[head, 0] = block


def middle_back(
    per_device, d_in, middle, grads, attn_rows, feed_rows, scale, gate, feed_gate, down_bias, rows, weight
):
    tokens, width = d_in.shape
    heads = width // HEAD
    last = per_device - 1
    per_frame = pl.BlockSpec((PATCHES, width), lambda frame: (jnp.minimum(frame, last), 0))

    def whole(shape):
        return pl.BlockSpec(shape, lambda frame: (0,) * len(shape))

    small = whole((per_device, width))
    return pl.pallas_call(
        middle_back_kernel,
        grid=(per_device + 1,),
        out_shape=(
            jax.ShapeDtypeStruct((tokens, width), F32),
            jax.ShapeDtypeStruct((tokens, width), BF16),
            jax.ShapeDtypeStruct((tokens, width), BF16),
            jax.ShapeDtypeStruct((heads, per_device + 1, HEAD, PATCHES), BF16),
        ),
        in_specs=[per_frame] * 5
        + [small] * 3
        + [whole((1, width)), whole(rows.shape), whole(weight.shape)],
        out_specs=(
            per_frame,
            per_frame,
            per_frame,
            pl.BlockSpec((heads, 1, HEAD, PATCHES), lambda frame: (0, frame, 0, 0)),
        ),
        scratch_shapes=[pltpu.VMEM((per_device, 8, width), F32)],
        cost_estimate=pl.CostEstimate(
            flops=2 * tokens * width * width, bytes_accessed=24 * tokens * width, transcendentals=0
        ),
        compiler_params=pltpu.CompilerParams(vmem_limit_bytes=48 << 20),
        name="middle_back",
    )(
        d_in,
        middle,
        grads,
        attn_rows,
        feed_rows,
        scale,
        gate,
        feed_gate,
        down_bias[None],
        rows,
        weight,
    )


def unproject_kernel(
    per_device, carried, which_ref, in_ref, back_ref, wq_ref, wk_ref, wv_ref, *refs
):
    if not carried:
        refs = refs[-4:]
    if carried:
        before_ref, hidden_ref, d_middle_ref, scale_ref, bias_theirs_ref = refs[:5]
        d_weight_ref, grad_ref, rows_ref, d_in_ref, d_bias_ref, turned_ref = refs[5:]
    else:
        d_in_ref, d_weight_ref, d_bias_ref, turned_ref = refs

    @pl.when(pl.program_id(0) == 0)
    def _():
        turned_ref[...] = in_ref[...].astype(F32).T.astype(BF16)
        if carried:
            d_in_ref[...] = before_ref[...]
        else:
            d_in_ref[...] = jnp.zeros_like(d_in_ref)

    group = wq_ref.shape[1] // HEAD

    def token_major(block_of):
        rows = []
        for place in range(per_device):
            block = jnp.concatenate([block_of(head, place) for head in range(group)], axis=0)
            rows.append(block.astype(F32).T.astype(BF16))
        return jnp.concatenate(rows, axis=0)

    sides = jnp.concatenate(
        [
            token_major(lambda head, place: back_ref[head, 2 * per_device + place]),
            token_major(lambda head, place: back_ref[head, place]),
            token_major(lambda head, place: back_ref[head, per_device + place]),
        ],
        axis=1,
    )
    weights = jnp.concatenate([wq_ref[...], wk_ref[...], wv_ref[...]], axis=1)
    d_in_ref[...] += dot_over(sides, weights, 1, 1)
    d_weight = jnp.dot(turned_ref[...], sides, preferred_element_type=F32).astype(BF16)
    d_bias = jnp.sum(sides.astype(F32), axis=0, keepdims=True)
    lanes = group * HEAD
    for kind in range(3):
        d_weight_ref[kind] = d_weight[:, kind * lanes : (kind + 1) * lanes]
        part = d_bias[:, kind * lanes : (kind + 1) * lanes]
        if carried:
            start = pl.multiple_of(pl.program_id(0) * lanes, lanes)
            d_bias_ref[pl.ds(kind, 1), pl.ds(start, lanes)] = part
        else:
            d_bias_ref[kind] = part

    if carried:

        @pl.when(pl.program_id(0) == pl.num_programs(0) - 1)
        def _():
            sums = []
            for place in range(per_device):
                rows = pl.ds(place * PATCHES, PATCHES)
                mine = pl.ds(place, 1)
                back, d_shift, d_scale = norm_back(
                    hidden_ref[rows, :].astype(F32), d_in_ref[rows, :], scale_ref[mine, :]
                )
                grad_ref[rows, :] = (d_middle_ref[rows, :] + back).astype(BF16)
                sums += [d_shift, d_scale]
            for kind in range(3):
                sums.append(
                    jnp.concatenate([d_bias_ref[pl.ds(kind, 1), :], bias_theirs_ref[kind]], axis=1)
                )
            count = 16 - len(sums)
            late = jnp.concatenate(
                sums + [jnp.zeros((count, d_in_ref.shape[1]), F32)], axis=0
            ).astype(BF16)
            for target in range(rows_ref.shape[0]):
                rows_ref[target] = late


def unproject(per_device, targets, which, attn_in, back, weight, orders, before=None, norm_args=()):
    tokens, width = attn_in.shape
    heads = width // HEAD
    group = 2
    lanes = group * HEAD
    groups = heads // group
    steps = groups // 2

    def whole(shape):
        return pl.BlockSpec(shape, lambda step, which: (0,) * len(shape))

    def blocks(array):
        return pl.BlockSpec(
            (group,) + array.shape[1:], lambda step, which: (which[0] * steps + step, 0, 0, 0)
        )

    def part(kind):
        return pl.BlockSpec(
            (width, lanes), lambda step, which: (0, kind * groups + which[0] * steps + step)
        )

    args = [attn_in, back, weight, weight, weight]
    specs = [whole((tokens, width)), blocks(back), part(0), part(1), part(2)]
    weight_shape = (
        jax.ShapeDtypeStruct((3, width, width // 2), BF16),
        jax.ShapeDtypeStruct((3, 1, width // 2), F32),
    )
    weight_specs = (
        pl.BlockSpec((3, width, lanes), lambda step, which: (0, 0, step)),
        pl.BlockSpec((3, 1, lanes), lambda step, which: (0, 0, step)),
    )
    scratch = [pltpu.VMEM((width, tokens), BF16)]
    small = (per_device, width)
    if before is not None:
        args += [before] + list(norm_args)
        specs += [whole((tokens, width))] * 3 + [whole(small), whole((3, 1, width // 2))]
        late = (targets, 16, width)
        outs = weight_shape[:1] + (
            jax.ShapeDtypeStruct((tokens, width), BF16),
            jax.ShapeDtypeStruct(late, BF16),
        )
        out_specs = weight_specs[:1] + (whole((tokens, width)), whole(late))
        scratch = [pltpu.VMEM((tokens, width), F32), pltpu.VMEM((3, width // 2), F32)] + scratch
    else:
        outs = (jax.ShapeDtypeStruct((tokens, width), F32),) + weight_shape
        out_specs = (whole((tokens, width)),) + weight_specs
        orders = corners(orders)
        args += orders
        specs += [unread_spec()] * len(orders)
    return pl.pallas_call(
        functools.partial(unproject_kernel, per_device, before is not None),
        grid_spec=pltpu.PrefetchScalarGridSpec(
            num_scalar_prefetch=1,
            grid=(steps,),
            in_specs=specs,
            out_specs=out_specs,
            scratch_shapes=scratch,
        ),
        out_shape=outs,
        cost_estimate=pl.CostEstimate(
            flops=6 * tokens * width * width,
            bytes_accessed=2 * (3 * width * width + 6 * tokens * width),
            transcendentals=0,
        ),
        compiler_params=pltpu.CompilerParams(vmem_limit_bytes=48 << 20),
        name="unproject%d" % (before is not None),
    )(which.reshape(1), *args)


def columns_of(matrix, start, width, axis=1):
    if isinstance(start, int) and start == 0 and width == matrix.shape[axis]:
        return matrix
    return lax.dynamic_slice_in_dim(matrix, start, width, axis)


def local(
    hidden,
    cotangent,
    levels,
    segments,
    live_frames,
    noise_table,
    mod_weight,
    mod_bias,
    qkv_weight,
    qkv_bias,
    out_weight,
    out_bias,
    up_weight,
    up_bias,
    down_weight,
    down_bias,
):
    seq_index = lax.axis_index("seq")
    seq_count = lax.axis_size("seq")
    tokens = hidden.shape[1]
    width = hidden.shape[2]
    per_device = tokens // PATCHES
    frames = segments.shape[1]
    heads = width // HEAD
    copies = seq_count // heads
    hidden_units = up_weight.shape[1]
    level_count = noise_table.shape[0]
    share = width // seq_count
    clip_ids = segments[0]
    live = live_frames[0]

    pack = lax.axis_index("pack")
    halves = halving_fits()
    frame_ids = jnp.arange(frames, dtype=jnp.int32)
    same_clip = clip_ids[:, None] == clip_ids[None, :]
    clip_starts = jnp.min(jnp.where(same_clip, frame_ids[None, :], frames), axis=1)
    frame_times = (frame_ids - clip_starts).astype(F32)
    own_cos, own_sin = rotary_tables(
        lax.dynamic_slice_in_dim(frame_times, seq_index * per_device, per_device)
    )

    embed = jnp.concatenate(
        [
            lax.dynamic_slice_in_dim(noise_table, levels[0, frame], 1, 0)
            for frame in range(per_device)
        ],
        axis=0,
    )
    cond = jax.nn.silu(embed).astype(BF16)
    modulation = jnp.dot(cond, mod_weight[:, : 2 * width], preferred_element_type=F32)
    attn_shift, attn_scale = jnp.split(modulation + mod_bias[: 2 * width], 2, axis=1)
    attn_in, sent = project(
        per_device, hidden[0], attn_shift, attn_scale, qkv_weight, qkv_bias, own_cos, own_sin
    )

    def to_heads(array):
        if copies > 1:
            array = jnp.concatenate([array] * copies, axis=0)
        return lax.all_to_all(array, "seq", 0, 0, tiled=True)

    def to_tokens(array):
        return lax.all_to_all(array, "seq", 0, 0, tiled=True)[:heads]

    x = to_heads(sent)
    late_modulation = jnp.dot(
        after(cond, attn_in), mod_weight[:, 2 * width :], preferred_element_type=F32
    )
    attn_gate, feed_shift, feed_scale, feed_gate = jnp.split(
        late_modulation + mod_bias[2 * width :], 4, axis=1
    )
    cos_all, sin_all = rotary_tables(after(frame_times, attn_in))
    grad_rows = cotangent[0].astype(F32).reshape(per_device, PATCHES, width)
    d_feed_out = (feed_gate[:, None, :] * grad_rows).reshape(tokens, width).astype(BF16)
    x, d_feed_out, cos_all, sin_all = lax.optimization_barrier((x, d_feed_out, cos_all, sin_all))
    mix, wide, lse, kv = attend(per_device, clip_ids, live, x)
    mix = to_tokens(mix)
    mixes = [mix[:, place].reshape(width, PATCHES) for place in range(per_device)]
    attn_rows = jnp.stack([dot_over(each, out_weight, 0, 0) for each in mixes]) + out_bias
    attn_mix = jnp.concatenate(mixes, axis=1)

    frame_rows = hidden[0].astype(F32).reshape(per_device, PATCHES, width)
    middle = frame_rows + attn_gate[:, None, :] * attn_rows
    feed_in = modulate_norm(middle, feed_shift, feed_scale).reshape(tokens, width).astype(BF16)
    feed_args = (feed_in, d_feed_out, up_weight, up_bias, down_weight)
    theirs = feed(1 - pack if halves else pack * 0 + 1, *feed_args, None)
    mine = feed(pack if halves else pack * 0, *feed_args, theirs[:2])
    small = 128

    def in_order(own, other):
        if halves:
            even, odd = jnp.where(pack == 0, own, other), jnp.where(pack == 0, other, own)
        else:
            even, odd = own, other
        rows = own.shape[0]
        return jnp.stack(
            [even.reshape(rows, -1, small), odd.reshape(rows, -1, small)], axis=2
        ).reshape(rows, -1)

    own_levels = levels[0]
    level_row = jnp.concatenate(
        [
            jnp.broadcast_to(part[frame], (width // (2 * per_device),))
            for frame in range(per_device)
            for part in (lax.div(own_levels, 32), lax.rem(own_levels, 32))
        ]
    ).astype(F32)[None]
    extra_rows = jnp.concatenate(
        [
            in_order(mine[4], theirs[4]).reshape(-1, width),
            level_row,
            jnp.zeros((1, width), F32),
        ],
        axis=0,
    )
    d_middle, d_attn_out, layer_out, blocks = middle_back(
        per_device,
        mine[1],
        middle.reshape(tokens, width),
        cotangent[0],
        attn_rows.reshape(tokens, width),
        mine[0],
        feed_scale,
        attn_gate,
        feed_gate,
        down_bias,
        extra_rows,
        out_weight,
    )
    layer_out = layer_out.reshape(1, tokens, width)
    d_mix = to_heads(blocks)

    def out_term(start, size):
        return dot_over(attn_mix, columns_of(d_attn_out, start, size), 1, 0).astype(BF16)

    sums = ()
    if halves:
        up_sum = RowSum(mine[2], exchange(theirs[2], "pack", 1), (2, 1, 4, 8))
        down_sum = RowSum(mine[3], exchange(theirs[3], "pack", 1), (1, 2, 4, 8))
        out_theirs = exchange(out_term((1 - pack) * (width // 2), width // 2), "pack", 1)
        out_sum = RowSum(out_term(pack * (width // 2), width // 2), out_theirs, (1, 2, 4, 8))
        sums = (down_sum, up_sum)
    def own_share(row):
        piece = row.shape[0] // seq_count
        return lax.dynamic_slice_in_dim(row, seq_index * piece, piece)

    chunks = width // PATCHES
    early_rows = d_mix[:, per_device].reshape(seq_count, chunks, 16, PATCHES)
    early_rows = early_rows.transpose(0, 2, 1, 3).reshape(seq_count, 16, width)
    early_sets = of_packs(early_rows)
    early_sum = functools.reduce(
        jnp.add, [jnp.sum(each.astype(F32), axis=0) for each in early_sets]
    )
    out_bias_grad = own_share(early_sum[8])
    down_bias_grad = own_share(early_sum[9])
    up_bias_grad = own_share(early_sum[10:14].reshape(hidden_units))

    def frames_of(rows, per_frame, kinds):
        return jnp.concatenate(
            [
                jnp.stack(
                    [rows[:, frame * per_frame + kind] for frame in range(per_device)], axis=1
                ).reshape(-1, width)
                for kind in range(kinds)
            ],
            axis=1,
        )

    own_table = lax.dynamic_slice_in_dim(noise_table, seq_index * share, share, 1)
    own_mod = lax.dynamic_slice_in_dim(mod_weight, seq_index * share, share, 0)
    stride = width // (2 * per_device)
    parts = []
    for rows in early_sets:
        coded = rows[:, 14, ::stride].astype(jnp.int32).reshape(-1, 2)
        set_levels = coded[:, 0] * 32 + coded[:, 1]
        picks = (set_levels[:, None] == jnp.arange(level_count, dtype=jnp.int32)[None, :]).astype(F32)
        embeds = jnp.dot(picks, own_table, precision=PRECISE, preferred_element_type=F32)
        set_cond = jax.nn.silu(embeds).astype(BF16)
        d_mod = frames_of(rows, 4, 4)
        parts.append(
            (
                picks,
                embeds,
                set_cond,
                dot_over(d_mod, own_mod[:, 2 * width :], 1, 1),
                dot_over(set_cond, d_mod, 0, 0),
            )
        )
    mod_grad_early = functools.reduce(jnp.add, [each[4] for each in parts])
    mod_sum_early = (early_sum[:4] + early_sum[4:8]).reshape(4 * width)
    orders = [each.stage() for each in sums]
    result = attend_back(
        per_device, clip_ids, live, x, kv, wide, lse, d_mix, cos_all, sin_all, orders
    )
    if halves:
        for each in sums:
            result = each.tie(result)
        result = out_sum.tie(result)
    back = to_tokens(result)
    orders = []
    if halves:
        for each in (up_sum, down_sum, out_sum):
            each.stage()
        orders = [each.stage() for each in (up_sum, down_sum, out_sum)]
    orders += [mod_grad_early] + [part[3] for part in parts]
    which = (1 - pack, pack) if halves else (pack * 0, pack * 0 + 1)
    d_in_theirs, qkv_theirs, bias_theirs = unproject(
        per_device, seq_count, which[0], attn_in, back, qkv_weight, orders
    )
    qkv_mine, hidden_grad, late = unproject(
        per_device,
        seq_count,
        which[1],
        attn_in,
        back,
        qkv_weight,
        (),
        d_in_theirs,
        (hidden[0], d_middle, attn_scale, bias_theirs),
    )
    hidden_grad = hidden_grad.reshape(1, tokens, width)
    if halves:
        came = exchange(qkv_theirs, "pack", 1)
        split = width // 4
        qkv_sums = [
            RowSum(qkv_mine[..., :split], came[..., :split], (1, 2, 4, 8)),
            RowSum(qkv_mine[..., split:], came[..., split:], (2, 1, 4, 8)),
        ]
        for each in qkv_sums:
            late = each.stage((up_sum, down_sum, out_sum), late)
    late_rows = lax.all_to_all(late, "seq", 0, 0, tiled=True)

    def halves_in_order(own, other):
        if halves:
            return jnp.where(pack == 0, own, other), jnp.where(pack == 0, other, own)
        return other, own

    if halves:
        up_weight_grad, down_weight_grad, out_weight_grad, qkv_weight_grad = settle(
            pack, *[each.finish() for each in (up_sum, down_sum, out_sum, *qkv_sums)]
        )
    else:
        up_weight_grad = row_sum_direct(in_order(mine[2], theirs[2]))
        pairs = [each[3].reshape(-1, small, width) for each in (mine, theirs)]
        down_weight_grad = row_sum_direct(jnp.stack(pairs, axis=1).reshape(hidden_units, width))
        out_weight_grad = row_sum_direct(out_term(0, width))
        qkv_term = jnp.concatenate(halves_in_order(qkv_mine, qkv_theirs), axis=-1)
        qkv_weight_grad = row_sum_direct(qkv_term.transpose(1, 0, 2).reshape(width, 3 * width))

    late_sets = of_packs(late_rows[:, :8])
    bias_at = 2 * per_device
    bias_sums = [
        jnp.sum(rows[:, bias_at : bias_at + 3].astype(F32), axis=0) for rows in late_sets
    ]
    if halves:
        ones, twos = bias_sums
        half = width // 2
        own_half = ones[:, :half] + twos[:, half:]
        other_half = ones[:, half:] + twos[:, :half]
    else:
        total = functools.reduce(jnp.add, bias_sums)
        own_half, other_half = total[:, : width // 2], total[:, width // 2 :]
    bias_total = jnp.concatenate(halves_in_order(own_half, other_half), axis=1)
    qkv_bias_grad = own_share(bias_total.reshape(3 * width))
    late_mods = [frames_of(rows, 2, 2) for rows in late_sets]
    mod_sum_late = functools.reduce(
        jnp.add, [jnp.sum(each.astype(F32), axis=0) for each in late_mods]
    )
    d_embeds = []
    for part, d_mod in zip(parts, late_mods):
        d_cond = part[3] + dot_over(d_mod, own_mod[:, : 2 * width], 1, 1)
        d_embeds.append(jax.vjp(jax.nn.silu, part[1])[1](d_cond)[0])
    table_grad = lax.dot_general(
        jnp.concatenate([part[0] for part in parts], axis=0),
        jnp.concatenate(d_embeds, axis=0),
        (((0,), (0,)), ((), ())),
        precision=PRECISE,
        preferred_element_type=F32,
    )
    mod_grad_late = functools.reduce(
        jnp.add, [dot_over(part[2], d_mod, 0, 0) for part, d_mod in zip(parts, late_mods)]
    )
    mod_weight_grad = jnp.concatenate([mod_grad_late, mod_grad_early], axis=1)
    mod_bias_grad = own_share(jnp.concatenate([mod_sum_late, mod_sum_early]))
    return (
        layer_out,
        hidden_grad,
        table_grad,
        mod_weight_grad,
        mod_bias_grad,
        qkv_weight_grad,
        qkv_bias_grad,
        out_weight_grad,
        out_bias_grad,
        up_weight_grad,
        up_bias_grad,
        down_weight_grad,
        down_bias_grad,
    )


def solution(mesh):
    in_specs = (
        P("pack", "seq", None),
        P("pack", "seq", None),
        P("pack", "seq"),
        P("pack", None),
        P("pack", None),
    ) + (P(),) * 11
    out_specs = (
        P("pack", "seq", None),
        P("pack", "seq", None),
        P(None, "seq"),
        P("seq", None),
        P("seq"),
        P("seq", None),
        P("seq"),
        P("seq", None),
        P("seq"),
        P("seq", None),
        P("seq"),
        P("seq", None),
        P("seq"),
    )
    return jax.shard_map(local, mesh=mesh, in_specs=in_specs, out_specs=out_specs, check_vma=False)
```

```python
import functools

import jax
import jax.numpy as jnp
from jax import lax
from jax.experimental import pallas as pl
from jax.experimental.pallas import tpu as pltpu
from jax.sharding import PartitionSpec as P

HEAD = 64
PATCHES = 256
SIDE = 16
EPSILON = 1e-06
PRECISE = lax.Precision.HIGHEST
HALF = HEAD // 2
F32 = jnp.float32
BF16 = jnp.bfloat16


def modulate_norm(rows, shift, scale):
    center = jnp.mean(rows, axis=-1, keepdims=True)
    centered = rows - center
    spread = jnp.mean(centered * centered, axis=-1, keepdims=True)
    normed = centered * lax.rsqrt(spread + EPSILON)
    return normed * (1.0 + scale[:, None, :]) + shift[:, None, :]


def gelu_tanh(values):
    return jax.nn.gelu(values, approximate=True)


def dot_over(first, second, first_dim, second_dim):
    return lax.dot_general(
        first, second, (((first_dim,), (second_dim,)), ((), ())), preferred_element_type=F32
    )


def spatial_angles():
    time_pairs = HALF // 4
    space_pairs = (HALF - time_pairs) // 2
    patch = jnp.arange(PATCHES, dtype=jnp.int32)
    row_pos = (patch // SIDE).astype(F32)
    col_pos = (patch % SIDE).astype(F32)
    time_freq = 10000.0 ** (-jnp.arange(time_pairs, dtype=F32) / time_pairs)
    space_freq = 10000.0 ** (-jnp.arange(space_pairs, dtype=F32) / space_pairs)
    space = jnp.concatenate(
        [space_freq[:, None] * row_pos[None, :], space_freq[:, None] * col_pos[None, :]], axis=0
    )
    return time_freq, space


def rotary_tables(time_frames):
    time_freq, space = spatial_angles()
    count = time_frames.shape[0]
    time_angle = time_frames[:, None] * time_freq[None, :]

    def whole(function):
        return jnp.concatenate(
            [
                jnp.broadcast_to(
                    function(time_angle)[:, :, None], (count, time_freq.shape[0], PATCHES)
                ),
                jnp.broadcast_to(function(space)[None], (count,) + space.shape),
            ],
            axis=1,
        )

    return whole(jnp.cos), whole(jnp.sin)


def walk_frames(frames, per_device, segments_ref, live_ref, list_ref, visit):
    def step(source, held):
        for place in range(per_device):
            frame = source * per_device + place
            before = jnp.maximum(frame - 1, 0)
            fresh = (frame == 0) | (segments_ref[frame] != segments_ref[before])
            held = jnp.where(fresh, 0, held)
            list_ref[held] = frame
            visit(source, place, frame, held + 1)
            held = held + jnp.where(live_ref[frame] == 1, 1, 0)
        return held

    lax.fori_loop(0, frames // per_device, step, jnp.int32(0))


def attend_kernel(per_device, segments_ref, live_ref, x_ref, mix_ref, wide_ref, lse_ref, kv_ref, list_ref):
    frames = kv_ref.shape[0]

    def turn(source, carry):
        for place in range(per_device):
            both = jnp.concatenate(
                [x_ref[source, place], x_ref[source, per_device + place]], axis=0
            )
            kv_ref[source * per_device + place] = both.T
        return carry

    lax.fori_loop(0, frames // per_device, turn, 0)

    def visit(source, place, frame, count):
        query = x_ref[source, 2 * per_device + place]
        query_side = jnp.concatenate([query, jnp.zeros_like(query)], axis=0)

        def scores_of(other):
            return jnp.dot(kv_ref[other], query_side, preferred_element_type=F32)

        def mixed(other, weights):
            value = x_ref[lax.div(other, per_device), per_device + lax.rem(other, per_device)]
            return jnp.dot(value, weights.astype(BF16), preferred_element_type=F32)

        def join(others, carry):
            scores = [scores_of(other) for other in others]
            tops = [jnp.max(score, axis=0, keepdims=True) for score in scores]
            new_top = functools.reduce(jnp.maximum, tops)
            if carry is not None:
                top, total, accum = carry
                new_top = jnp.maximum(top, new_top)
                shrink = jnp.exp(top - new_top)
                total = total * shrink
                accum = accum * shrink
            for index, score in enumerate(scores):
                weights = jnp.exp(score - new_top)
                added = jnp.sum(weights, axis=0, keepdims=True)
                product = mixed(others[index], weights)
                if carry is None and index == 0:
                    total, accum = added, product
                else:
                    total, accum = total + added, accum + product
            return new_top, total, accum

        others = count - 1
        carry = join([frame], None)
        carry = lax.fori_loop(
            0,
            lax.div(others, 4),
            lambda index, state: join([list_ref[4 * index + nth] for nth in range(4)], state),
            carry,
        )
        carry = lax.fori_loop(
            lax.div(others, 4) * 2,
            lax.div(others, 2),
            lambda index, state: join([list_ref[2 * index], list_ref[2 * index + 1]], state),
            carry,
        )
        top, total, accum = lax.fori_loop(
            0,
            lax.rem(others, 2),
            lambda unused, state: join([list_ref[others - 1]], state),
            carry,
        )
        result = accum * (1.0 / total)
        wide_ref[source, place] = result
        mix_ref[source, place] = result.astype(BF16)
        lse_ref[pl.ds(frame, 1), :] = top + jnp.log(total)

    walk_frames(frames, per_device, segments_ref, live_ref, list_ref, visit)


def corners(values):
    return [each.reshape(-1, each.shape[-1])[:1, :128] for each in values]


def unread_spec():
    return pl.BlockSpec(memory_space=pl.ANY)


def whole_spec():
    return pl.BlockSpec(memory_space=pltpu.VMEM)


def scalar_spec():
    return pl.BlockSpec(memory_space=pltpu.SMEM)


def attend(per_device, segments, live, x):
    sources = x.shape[0]
    frames = sources * per_device
    pairs = frames * 6
    outs = (
        jax.ShapeDtypeStruct((sources, per_device, HEAD, PATCHES), BF16),
        jax.ShapeDtypeStruct((sources, per_device, HEAD, PATCHES), F32),
        jax.ShapeDtypeStruct((frames, PATCHES), F32),
        jax.ShapeDtypeStruct((frames, PATCHES, 2 * HEAD), BF16),
    )
    return pl.pallas_call(
        functools.partial(attend_kernel, per_device),
        out_shape=outs,
        in_specs=[scalar_spec(), scalar_spec(), whole_spec()],
        out_specs=(whole_spec(),) * len(outs),
        scratch_shapes=[pltpu.SMEM((frames,), jnp.int32)],
        cost_estimate=pl.CostEstimate(
            flops=pairs * 4 * PATCHES * PATCHES * 256,
            bytes_accessed=x.size * 2 * 3,
            transcendentals=pairs * PATCHES * PATCHES,
        ),
        compiler_params=pltpu.CompilerParams(vmem_limit_bytes=40 << 20),
        name="attend",
    )(segments, live, x)


def attend_back_kernel(
    per_device,
    segments_ref,
    live_ref,
    x_ref,
    kv_ref,
    wide_ref,
    lse_ref,
    d_mix_ref,
    cos_ref,
    sin_ref,
    *refs
):
    out_ref, dkv_ref, list_ref = refs[-3:]
    frames = kv_ref.shape[0]

    def unturn(frame, values):
        lower = values[:HALF]
        upper = values[HALF:]
        cosine = cos_ref[frame]
        sine = sin_ref[frame]
        return jnp.concatenate([lower * cosine + upper * sine, upper * cosine - lower * sine], axis=0)

    def visit(source, place, frame, count):
        query = x_ref[source, 2 * per_device + place]
        d_mix = d_mix_ref[source, place]
        blank = jnp.zeros_like(query)
        query_side = jnp.concatenate([query, blank], axis=0)
        d_mix_side = jnp.concatenate([blank, d_mix], axis=0)
        turned = jnp.concatenate([query, d_mix], axis=0).T
        first = lax.broadcasted_iota(jnp.int32, turned.shape, 1) < HEAD
        nothing = jnp.zeros_like(turned)
        both = jnp.concatenate(
            [jnp.where(first, turned, nothing), jnp.where(first, nothing, turned)], axis=0
        )
        lse = lse_ref[pl.ds(frame, 1), :]
        delta = jnp.sum(d_mix.astype(F32) * wide_ref[source, place], axis=0, keepdims=True)

        def block(other, own=False):
            key_value = kv_ref[other]
            scores = jnp.dot(key_value, query_side, preferred_element_type=F32)
            d_weights = jnp.dot(key_value, d_mix_side, preferred_element_type=F32)
            weights = jnp.exp(scores - lse)
            d_scores = (weights * (d_weights - delta)).astype(BF16)
            sides = jnp.concatenate([d_scores, weights.astype(BF16)], axis=1)
            d_both = jnp.dot(sides, both, preferred_element_type=F32)
            if own:
                dkv_ref[other] = d_both
            else:
                dkv_ref[other] += d_both
            key = x_ref[lax.div(other, per_device), lax.rem(other, per_device)]
            return jnp.dot(key, d_scores, preferred_element_type=F32)

        others = count - 1
        d_query = block(frame, True)
        d_query = lax.fori_loop(
            0,
            lax.div(others, 2),
            lambda index, state: state
            + block(list_ref[2 * index])
            + block(list_ref[2 * index + 1]),
            d_query,
        )
        d_query = lax.fori_loop(
            0,
            lax.rem(others, 2),
            lambda unused, state: state + block(list_ref[others - 1]),
            d_query,
        )
        d_query = unturn(frame, d_query * (HEAD**-0.5)).astype(BF16)
        out_ref[source, 2 * per_device + place] = d_query

    walk_frames(frames, per_device, segments_ref, live_ref, list_ref, visit)

    def finish(source, carry):
        for place in range(per_device):
            frame = source * per_device + place
            both = dkv_ref[frame].T
            out_ref[source, place] = unturn(frame, both[:HEAD]).astype(BF16)
            out_ref[source, per_device + place] = both[HEAD:].astype(BF16)
        return carry

    lax.fori_loop(0, frames // per_device, finish, 0)


def attend_back(per_device, segments, live, x, kv, wide, lse, d_mix, cosine, sine, orders):
    sources = x.shape[0]
    frames = sources * per_device
    pairs = frames * 6
    args = [segments, live, x, kv, wide, lse, d_mix, cosine, sine]
    specs = [scalar_spec(), scalar_spec()] + [whole_spec()] * (len(args) - 2)
    orders = corners(orders)
    return pl.pallas_call(
        functools.partial(attend_back_kernel, per_device),
        out_shape=jax.ShapeDtypeStruct(x.shape, BF16),
        in_specs=specs + [unread_spec()] * len(orders),
        out_specs=whole_spec(),
        scratch_shapes=[
            pltpu.VMEM((frames, PATCHES, 2 * HEAD), F32),
            pltpu.SMEM((frames,), jnp.int32),
        ],
        cost_estimate=pl.CostEstimate(
            flops=pairs * 10 * PATCHES * PATCHES * 64,
            bytes_accessed=x.size * 2 * 5,
            transcendentals=pairs * PATCHES * PATCHES,
        ),
        compiler_params=pltpu.CompilerParams(vmem_limit_bytes=60 << 20),
        name="attend_back",
    )(*args, *orders)


def exchange(value, axis, bit):
    count = lax.axis_size(axis)
    return lax.ppermute(value, axis, [(source, source ^ bit) for source in range(count)])


def after(value, *earlier):
    return lax.optimization_barrier((value,) + earlier)[0]


def of_packs(value):
    values = [value]
    bit = lax.axis_size("pack") // 2
    while bit:
        values = values + [exchange(each, "pack", bit) for each in values]
        bit //= 2
    return values


def halving_fits():
    return lax.axis_size("pack") == 2 and lax.axis_size("seq") == 16


class RowSum:
    def __init__(self, mine, came, order):
        self.order = list(order)
        self.index = lax.axis_index("seq")
        rows = mine.shape[-2]
        self.tail = (rows // 16, mine.shape[-1])
        self.lead = mine.shape[:-2]
        shape = self.lead + (2, 2, 2, 2) + self.tail
        self.parts = [mine.reshape(shape), came.reshape(shape)]

    def pick(self, bit, which):
        axis = len(self.lead) + {8: 0, 4: 1, 2: 2, 1: 3}[bit]
        pieces = [lax.dynamic_slice_in_dim(part, which, 1, axis) for part in self.parts]
        return (pieces[0].astype(F32) + pieces[1].astype(F32)).astype(BF16)

    def tie_kept(self, value):
        value, self.parts[0] = lax.optimization_barrier((value, self.parts[0]))
        return value

    def stage(self, later=()):
        bit = self.order.pop(0)
        own_bit = lax.rem(lax.div(self.index, bit), 2)
        send = self.pick(bit, 1 - own_bit)
        for each in later:
            send = each.tie_kept(send)
        came = exchange(send, "seq", bit)
        self.parts = [self.pick(bit, own_bit), came]
        return send

    def tie(self, value):
        value, *self.parts = lax.optimization_barrier((value, *self.parts))
        return value

    def finish(self):
        while self.order:
            self.stage()
        own = (self.parts[0].astype(F32) + self.parts[1].astype(F32)).astype(BF16)
        own = own.reshape(self.lead + self.tail)
        return own, exchange(own, "pack", 1)


def settle_kernel(pack_ref, *refs):
    ups, downs, outs, firsts, seconds = [refs[2 * nth : 2 * nth + 2] for nth in range(5)]
    up_ref, down_ref, out_ref, qkv_ref = refs[10:]
    own_first = pack_ref[0] == 0
    small = 128

    def of_pack(pack, pair, *index):
        one, two = pair[0][index].astype(F32), pair[1][index].astype(F32)
        return jnp.where(own_first, one, two) if pack == 0 else jnp.where(own_first, two, one)

    every = slice(None)
    for pack in range(2):
        for group in range(ups[0].shape[1] // small):
            at = (2 * group + pack) * small
            columns = slice(group * small, (group + 1) * small)
            up_ref[:, at : at + small] = of_pack(pack, ups, every, columns)
        rows = downs[0].shape[0]
        down_ref[pack * rows : (pack + 1) * rows, :] = of_pack(pack, downs, every, every)
        columns = outs[0].shape[1]
        out_ref[:, pack * columns : (pack + 1) * columns] = of_pack(pack, outs, every, every)
        for kind in range(3):
            for nth, pair in enumerate((firsts, seconds)):
                columns = pair[0].shape[2]
                at = (4 * kind + 2 * pack + nth) * columns
                qkv_ref[:, at : at + columns] = of_pack(pack, pair, kind, every, every)


def settle(pack, *pairs):
    up, down, out, qkv = pairs[0][0], pairs[1][0], pairs[2][0], pairs[3][0]
    shapes = (
        (up.shape[0], 2 * up.shape[1]),
        (2 * down.shape[0], down.shape[1]),
        (out.shape[0], 2 * out.shape[1]),
        (qkv.shape[1], 12 * qkv.shape[2]),
    )
    args = [each for pair in pairs for each in pair]
    return pl.pallas_call(
        settle_kernel,
        out_shape=tuple(jax.ShapeDtypeStruct(shape, F32) for shape in shapes),
        in_specs=[scalar_spec()] + [whole_spec()] * len(args),
        out_specs=(whole_spec(),) * 4,
        compiler_params=pltpu.CompilerParams(vmem_limit_bytes=32 << 20),
        name="settle",
    )(pack.reshape(1), *args)


def row_sum_direct(term):
    part = lax.psum_scatter(term.astype(BF16), "seq", scatter_dimension=0, tiled=True)
    return lax.psum(part, "pack").astype(F32)


def project_kernel(
    per_device,
    hidden_ref,
    shift_ref,
    scale_ref,
    wq_ref,
    wk_ref,
    wv_ref,
    bq_ref,
    bk_ref,
    bv_ref,
    cos_ref,
    sin_ref,
    in_ref,
    x_ref,
):
    @pl.when(pl.program_id(0) == 0)
    def _():
        for place in range(per_device):
            rows = pl.ds(place * PATCHES, PATCHES)
            values = hidden_ref[rows, :].astype(F32)
            centered = values - jnp.mean(values, axis=-1, keepdims=True)
            spread = jnp.mean(centered * centered, axis=-1, keepdims=True)
            normed = centered * lax.rsqrt(spread + EPSILON)
            scale = scale_ref[pl.ds(place, 1), :]
            in_ref[rows, :] = (normed * (1.0 + scale) + shift_ref[pl.ds(place, 1), :]).astype(BF16)

    rows = in_ref[...]
    group = wq_ref.shape[1] // HEAD

    def turned(values, place):
        lower = values[:HALF]
        upper = values[HALF:]
        cosine = cos_ref[place]
        sine = sin_ref[place]
        return jnp.concatenate([lower * cosine - upper * sine, upper * cosine + lower * sine], axis=0)

    for kind, (weight_ref, bias_ref) in enumerate(
        ((wq_ref, bq_ref), (wk_ref, bk_ref), (wv_ref, bv_ref))
    ):
        flat = jnp.dot(rows, weight_ref[...], preferred_element_type=F32) + bias_ref[...]
        for place in range(per_device):
            block = flat[place * PATCHES : (place + 1) * PATCHES].T
            for head in range(group):
                values = block[head * HEAD : (head + 1) * HEAD]
                if kind == 0:
                    values = turned(values, place) * (HEAD**-0.5)
                    x_ref[head, 2 * per_device + place] = values.astype(BF16)
                elif kind == 1:
                    x_ref[head, place] = turned(values, place).astype(BF16)
                else:
                    x_ref[head, per_device + place] = values.astype(BF16)


def project(per_device, hidden, shift, scale, weight, bias, cosine, sine):
    tokens, width = hidden.shape
    heads = width // HEAD
    group = 2
    lanes = group * HEAD
    steps = heads // group
    bias_row = bias[None, :]

    def whole(shape):
        return pl.BlockSpec(shape, lambda step: (0,) * len(shape))

    def part(kind, rows):
        return pl.BlockSpec((rows, lanes), lambda step: (0, kind * steps + step))

    blocks = (heads, 3 * per_device, HEAD, PATCHES)
    return pl.pallas_call(
        functools.partial(project_kernel, per_device),
        grid=(steps,),
        out_shape=(
            jax.ShapeDtypeStruct((tokens, width), BF16),
            jax.ShapeDtypeStruct(blocks, BF16),
        ),
        in_specs=[whole((tokens, width)), whole(shift.shape), whole(scale.shape)]
        + [part(kind, width) for kind in range(3)]
        + [part(kind, 1) for kind in range(3)]
        + [whole(cosine.shape), whole(sine.shape)],
        out_specs=(
            whole((tokens, width)),
            pl.BlockSpec((group,) + blocks[1:], lambda step: (step, 0, 0, 0)),
        ),
        cost_estimate=pl.CostEstimate(
            flops=2 * tokens * width * 3 * width,
            bytes_accessed=2 * (weight.size + 5 * tokens * width),
            transcendentals=0,
        ),
        compiler_params=pltpu.CompilerParams(vmem_limit_bytes=40 << 20),
        name="project",
    )(hidden, shift, scale, weight, weight, weight, bias_row, bias_row, bias_row, cosine, sine)


GELU_SLOPE = 0.7978845608028654
GELU_CUBE = 0.044715


def feed_kernel(
    carried,
    which_ref,
    in_ref,
    d_out_ref,
    up_a_ref,
    up_b_ref,
    bias_a_ref,
    bias_b_ref,
    down_a_ref,
    down_b_ref,
    *refs
):
    if carried:
        out_before_ref, d_in_before_ref = refs[:2]
        refs = refs[2:]
    out_ref, d_in_ref, d_up_ref, d_down_ref, d_bias_ref, turned_ref = refs

    @pl.when(pl.program_id(0) == 0)
    def _():
        turned_ref[...] = in_ref[...].astype(F32).T.astype(BF16)
        if carried:
            out_ref[...] = out_before_ref[...]
            d_in_ref[...] = d_in_before_ref[...]
        else:
            out_ref[...] = jnp.zeros_like(out_ref)
            d_in_ref[...] = jnp.zeros_like(d_in_ref)

    up = jnp.concatenate([up_a_ref[...], up_b_ref[...]], axis=1)
    down = jnp.concatenate([down_a_ref[...], down_b_ref[...]], axis=0)
    bias = jnp.concatenate([bias_a_ref[...], bias_b_ref[...]], axis=1)
    d_out = d_out_ref[...]
    pre = jnp.dot(in_ref[...], up, preferred_element_type=F32) + bias
    d_act = dot_over(d_out, down, 1, 1)
    square = pre * pre
    bend = jnp.tanh(GELU_SLOPE * pre * (1.0 + GELU_CUBE * square))
    half = 0.5 * (1.0 + bend)
    act = (pre * half).astype(BF16)
    slope = half + (0.5 * GELU_SLOPE) * pre * (1.0 - bend * bend) * (
        1.0 + (3.0 * GELU_CUBE) * square
    )
    d_pre = (d_act * slope).astype(BF16)
    out_ref[...] += jnp.dot(act, down, preferred_element_type=F32)
    d_in_ref[...] += dot_over(d_pre, up, 1, 1)
    d_up_ref[...] = jnp.dot(turned_ref[...], d_pre, preferred_element_type=F32).astype(BF16)
    d_down_ref[...] = jnp.dot(
        act.astype(F32).T.astype(BF16), d_out, preferred_element_type=F32
    ).astype(BF16)
    d_bias_ref[...] = jnp.sum(d_pre.astype(F32), axis=0, keepdims=True)


def feed(which, feed_in, d_feed_out, up_weight, up_bias, down_weight, before):
    tokens, width = feed_in.shape
    hidden_units = up_weight.shape[1]
    small = 128
    steps = hidden_units // (4 * small)
    own = hidden_units // 2

    def whole(shape):
        return pl.BlockSpec(shape, lambda step, which: (0,) * len(shape))

    def group(nth):
        return lambda step, which: 2 * (2 * step + nth) + which[0]

    def columns(nth, rows):
        return pl.BlockSpec((rows, small), lambda step, which: (0, group(nth)(step, which)))

    def rows_of(nth):
        return pl.BlockSpec((small, width), lambda step, which: (group(nth)(step, which), 0))

    args = [feed_in, d_feed_out, up_weight, up_weight, up_bias[None], up_bias[None]]
    args += [down_weight, down_weight]
    specs = [whole((tokens, width)), whole((tokens, width)), columns(0, width), columns(1, width)]
    specs += [columns(0, 1), columns(1, 1), rows_of(0), rows_of(1)]
    if before is not None:
        args += list(before)
        specs += [whole((tokens, width)), whole((tokens, width))]
    return pl.pallas_call(
        functools.partial(feed_kernel, before is not None),
        grid_spec=pltpu.PrefetchScalarGridSpec(
            num_scalar_prefetch=1,
            grid=(steps,),
            in_specs=specs,
            out_specs=(
                whole((tokens, width)),
                whole((tokens, width)),
                pl.BlockSpec((width, 2 * small), lambda step, which: (0, step)),
                pl.BlockSpec((2 * small, width), lambda step, which: (step, 0)),
                pl.BlockSpec((1, 2 * small), lambda step, which: (0, step)),
            ),
            scratch_shapes=[pltpu.VMEM((width, tokens), BF16)],
        ),
        out_shape=(
            jax.ShapeDtypeStruct((tokens, width), F32),
            jax.ShapeDtypeStruct((tokens, width), F32),
            jax.ShapeDtypeStruct((width, own), BF16),
            jax.ShapeDtypeStruct((own, width), BF16),
            jax.ShapeDtypeStruct((1, own), F32),
        ),
        cost_estimate=pl.CostEstimate(
            flops=12 * tokens * width * own,
            bytes_accessed=2 * (4 * own * width + 8 * tokens * width),
            transcendentals=tokens * own,
        ),
        compiler_params=pltpu.CompilerParams(vmem_limit_bytes=56 << 20),
        name="feed%d" % (before is not None),
    )(which.reshape(1), *args)


def norm_back(values, d_in, scale):
    centered = values - jnp.mean(values, axis=-1, keepdims=True)
    spread = jnp.mean(centered * centered, axis=-1, keepdims=True)
    inverse = lax.rsqrt(spread + EPSILON)
    normed = centered * inverse
    product = d_in * normed
    d_shift = jnp.sum(d_in, axis=0, keepdims=True)
    d_scale = jnp.sum(product, axis=0, keepdims=True)
    scaled = 1.0 + scale
    mean_d = jnp.mean(d_in * scaled, axis=-1, keepdims=True)
    mean_p = jnp.mean(product * scaled, axis=-1, keepdims=True)
    return (d_in * scaled - mean_d - normed * mean_p) * inverse, d_shift, d_scale


def middle_back_kernel(
    d_in_ref,
    middle_ref,
    grad_ref,
    attn_ref,
    feed_ref,
    scale_ref,
    gate_ref,
    feed_gate_ref,
    down_bias_ref,
    rows_ref,
    weight_ref,
    d_middle_ref,
    d_attn_ref,
    layer_ref,
    blocks_ref,
    sums_ref,
):
    frame = pl.program_id(0)
    per_device = pl.num_programs(0) - 1

    @pl.when(frame < per_device)
    def _():
        mine = pl.ds(frame, 1)
        middle = middle_ref[...]
        grads = grad_ref[...].astype(F32)
        back, d_shift, d_scale = norm_back(middle, d_in_ref[...], scale_ref[mine, :])
        d_middle = grads + back
        d_middle_ref[...] = d_middle
        d_attn = (d_middle * gate_ref[mine, :]).astype(BF16)
        d_attn_ref[...] = d_attn
        feed_rows = feed_ref[...] + down_bias_ref[...]
        feed_gate = feed_gate_ref[mine, :]
        layer_ref[...] = (middle + feed_gate * feed_rows).astype(BF16)
        d_feed_out = (feed_gate * grads).astype(BF16).astype(F32)
        sums_ref[frame] = jnp.concatenate(
            [
                jnp.sum(d_middle * attn_ref[...], axis=0, keepdims=True),
                d_shift,
                d_scale,
                jnp.sum(grads * feed_rows, axis=0, keepdims=True),
                jnp.sum(d_attn.astype(F32), axis=0, keepdims=True),
                jnp.sum(d_feed_out, axis=0, keepdims=True),
                jnp.zeros((2, d_shift.shape[1]), F32),
            ],
            axis=0,
        )
        d_mix = dot_over(weight_ref[...], d_attn, 1, 1).astype(BF16)
        for head in range(blocks_ref.shape[0]):
            blocks_ref[head, 0] = d_mix[head * HEAD : (head + 1) * HEAD]

    @pl.when(frame == per_device)
    def _():
        first = sums_ref[0]
        second = sums_ref[1]
        rows = jnp.concatenate(
            [first[:4], second[:4], first[4:6] + second[4:6], rows_ref[...]], axis=0
        ).astype(BF16)
        count = rows.shape[1] // PATCHES
        block = jnp.concatenate(
            [rows[:, nth * PATCHES : (nth + 1) * PATCHES] for nth in range(count)], axis=0
        )
        for head in range(blocks_ref.shape[0]):
            blocks_ref[head, 0] = block


def middle_back(
    per_device, d_in, middle, grads, attn_rows, feed_rows, scale, gate, feed_gate, down_bias, rows, weight
):
    tokens, width = d_in.shape
    heads = width // HEAD
    last = per_device - 1
    per_frame = pl.BlockSpec((PATCHES, width), lambda frame: (jnp.minimum(frame, last), 0))

    def whole(shape):
        return pl.BlockSpec(shape, lambda frame: (0,) * len(shape))

    small = whole((per_device, width))
    return pl.pallas_call(
        middle_back_kernel,
        grid=(per_device + 1,),
        out_shape=(
            jax.ShapeDtypeStruct((tokens, width), F32),
            jax.ShapeDtypeStruct((tokens, width), BF16),
            jax.ShapeDtypeStruct((tokens, width), BF16),
            jax.ShapeDtypeStruct((heads, per_device + 1, HEAD, PATCHES), BF16),
        ),
        in_specs=[per_frame] * 5
        + [small] * 3
        + [whole((1, width)), whole(rows.shape), whole(weight.shape)],
        out_specs=(
            per_frame,
            per_frame,
            per_frame,
            pl.BlockSpec((heads, 1, HEAD, PATCHES), lambda frame: (0, frame, 0, 0)),
        ),
        scratch_shapes=[pltpu.VMEM((per_device, 8, width), F32)],
        cost_estimate=pl.CostEstimate(
            flops=2 * tokens * width * width, bytes_accessed=24 * tokens * width, transcendentals=0
        ),
        compiler_params=pltpu.CompilerParams(vmem_limit_bytes=48 << 20),
        name="middle_back",
    )(
        d_in,
        middle,
        grads,
        attn_rows,
        feed_rows,
        scale,
        gate,
        feed_gate,
        down_bias[None],
        rows,
        weight,
    )


def unproject_kernel(
    per_device, carried, which_ref, in_ref, back_ref, wq_ref, wk_ref, wv_ref, *refs
):
    if not carried:
        refs = refs[-4:]
    if carried:
        before_ref, hidden_ref, d_middle_ref, scale_ref, bias_theirs_ref = refs[:5]
        d_weight_ref, grad_ref, rows_ref, d_in_ref, d_bias_ref, turned_ref = refs[5:]
    else:
        d_in_ref, d_weight_ref, d_bias_ref, turned_ref = refs

    @pl.when(pl.program_id(0) == 0)
    def _():
        turned_ref[...] = in_ref[...].astype(F32).T.astype(BF16)
        if carried:
            d_in_ref[...] = before_ref[...]
        else:
            d_in_ref[...] = jnp.zeros_like(d_in_ref)

    group = wq_ref.shape[1] // HEAD

    def token_major(block_of):
        rows = []
        for place in range(per_device):
            block = jnp.concatenate([block_of(head, place) for head in range(group)], axis=0)
            rows.append(block.astype(F32).T.astype(BF16))
        return jnp.concatenate(rows, axis=0)

    sides = jnp.concatenate(
        [
            token_major(lambda head, place: back_ref[head, 2 * per_device + place]),
            token_major(lambda head, place: back_ref[head, place]),
            token_major(lambda head, place: back_ref[head, per_device + place]),
        ],
        axis=1,
    )
    weights = jnp.concatenate([wq_ref[...], wk_ref[...], wv_ref[...]], axis=1)
    d_in_ref[...] += dot_over(sides, weights, 1, 1)
    d_weight = jnp.dot(turned_ref[...], sides, preferred_element_type=F32).astype(BF16)
    d_bias = jnp.sum(sides.astype(F32), axis=0, keepdims=True)
    lanes = group * HEAD
    for kind in range(3):
        d_weight_ref[kind] = d_weight[:, kind * lanes : (kind + 1) * lanes]
        part = d_bias[:, kind * lanes : (kind + 1) * lanes]
        if carried:
            start = pl.multiple_of(pl.program_id(0) * lanes, lanes)
            d_bias_ref[pl.ds(kind, 1), pl.ds(start, lanes)] = part
        else:
            d_bias_ref[kind] = part

    if carried:

        @pl.when(pl.program_id(0) == pl.num_programs(0) - 1)
        def _():
            sums = []
            for place in range(per_device):
                rows = pl.ds(place * PATCHES, PATCHES)
                mine = pl.ds(place, 1)
                back, d_shift, d_scale = norm_back(
                    hidden_ref[rows, :].astype(F32), d_in_ref[rows, :], scale_ref[mine, :]
                )
                grad_ref[rows, :] = (d_middle_ref[rows, :] + back).astype(BF16)
                sums += [d_shift, d_scale]
            for kind in range(3):
                sums.append(
                    jnp.concatenate([d_bias_ref[pl.ds(kind, 1), :], bias_theirs_ref[kind]], axis=1)
                )
            count = 16 - len(sums)
            late = jnp.concatenate(
                sums + [jnp.zeros((count, d_in_ref.shape[1]), F32)], axis=0
            ).astype(BF16)
            for target in range(rows_ref.shape[0]):
                rows_ref[target] = late


def unproject(per_device, targets, which, attn_in, back, weight, orders, before=None, norm_args=()):
    tokens, width = attn_in.shape
    heads = width // HEAD
    group = 2
    lanes = group * HEAD
    groups = heads // group
    steps = groups // 2

    def whole(shape):
        return pl.BlockSpec(shape, lambda step, which: (0,) * len(shape))

    def blocks(array):
        return pl.BlockSpec(
            (group,) + array.shape[1:], lambda step, which: (which[0] * steps + step, 0, 0, 0)
        )

    def part(kind):
        return pl.BlockSpec(
            (width, lanes), lambda step, which: (0, kind * groups + which[0] * steps + step)
        )

    args = [attn_in, back, weight, weight, weight]
    specs = [whole((tokens, width)), blocks(back), part(0), part(1), part(2)]
    weight_shape = (
        jax.ShapeDtypeStruct((3, width, width // 2), BF16),
        jax.ShapeDtypeStruct((3, 1, width // 2), F32),
    )
    weight_specs = (
        pl.BlockSpec((3, width, lanes), lambda step, which: (0, 0, step)),
        pl.BlockSpec((3, 1, lanes), lambda step, which: (0, 0, step)),
    )
    scratch = [pltpu.VMEM((width, tokens), BF16)]
    small = (per_device, width)
    if before is not None:
        args += [before] + list(norm_args)
        specs += [whole((tokens, width))] * 3 + [whole(small), whole((3, 1, width // 2))]
        late = (targets, 16, width)
        outs = weight_shape[:1] + (
            jax.ShapeDtypeStruct((tokens, width), BF16),
            jax.ShapeDtypeStruct(late, BF16),
        )
        out_specs = weight_specs[:1] + (whole((tokens, width)), whole(late))
        scratch = [pltpu.VMEM((tokens, width), F32), pltpu.VMEM((3, width // 2), F32)] + scratch
    else:
        outs = (jax.ShapeDtypeStruct((tokens, width), F32),) + weight_shape
        out_specs = (whole((tokens, width)),) + weight_specs
        orders = corners(orders)
        args += orders
        specs += [unread_spec()] * len(orders)
    return pl.pallas_call(
        functools.partial(unproject_kernel, per_device, before is not None),
        grid_spec=pltpu.PrefetchScalarGridSpec(
            num_scalar_prefetch=1,
            grid=(steps,),
            in_specs=specs,
            out_specs=out_specs,
            scratch_shapes=scratch,
        ),
        out_shape=outs,
        cost_estimate=pl.CostEstimate(
            flops=6 * tokens * width * width,
            bytes_accessed=2 * (3 * width * width + 6 * tokens * width),
            transcendentals=0,
        ),
        compiler_params=pltpu.CompilerParams(vmem_limit_bytes=48 << 20),
        name="unproject%d" % (before is not None),
    )(which.reshape(1), *args)


def columns_of(matrix, start, width, axis=1):
    if isinstance(start, int) and start == 0 and width == matrix.shape[axis]:
        return matrix
    return lax.dynamic_slice_in_dim(matrix, start, width, axis)


def local(
    hidden,
    cotangent,
    levels,
    segments,
    live_frames,
    noise_table,
    mod_weight,
    mod_bias,
    qkv_weight,
    qkv_bias,
    out_weight,
    out_bias,
    up_weight,
    up_bias,
    down_weight,
    down_bias,
):
    seq_index = lax.axis_index("seq")
    seq_count = lax.axis_size("seq")
    tokens = hidden.shape[1]
    width = hidden.shape[2]
    per_device = tokens // PATCHES
    frames = segments.shape[1]
    heads = width // HEAD
    copies = seq_count // heads
    hidden_units = up_weight.shape[1]
    level_count = noise_table.shape[0]
    share = width // seq_count
    clip_ids = segments[0]
    live = live_frames[0]

    pack = lax.axis_index("pack")
    halves = halving_fits()
    frame_ids = jnp.arange(frames, dtype=jnp.int32)
    same_clip = clip_ids[:, None] == clip_ids[None, :]
    clip_starts = jnp.min(jnp.where(same_clip, frame_ids[None, :], frames), axis=1)
    frame_times = (frame_ids - clip_starts).astype(F32)
    own_cos, own_sin = rotary_tables(
        lax.dynamic_slice_in_dim(frame_times, seq_index * per_device, per_device)
    )

    embed = jnp.concatenate(
        [
            lax.dynamic_slice_in_dim(noise_table, levels[0, frame], 1, 0)
            for frame in range(per_device)
        ],
        axis=0,
    )
    cond = jax.nn.silu(embed).astype(BF16)
    modulation = jnp.dot(cond, mod_weight[:, : 2 * width], preferred_element_type=F32)
    attn_shift, attn_scale = jnp.split(modulation + mod_bias[: 2 * width], 2, axis=1)
    attn_in, sent = project(
        per_device, hidden[0], attn_shift, attn_scale, qkv_weight, qkv_bias, own_cos, own_sin
    )

    def to_heads(array):
        if copies > 1:
            array = jnp.concatenate([array] * copies, axis=0)
        return lax.all_to_all(array, "seq", 0, 0, tiled=True)

    def to_tokens(array):
        return lax.all_to_all(array, "seq", 0, 0, tiled=True)[:heads]

    x = to_heads(sent)
    late_modulation = jnp.dot(
        after(cond, attn_in), mod_weight[:, 2 * width :], preferred_element_type=F32
    )
    attn_gate, feed_shift, feed_scale, feed_gate = jnp.split(
        late_modulation + mod_bias[2 * width :], 4, axis=1
    )
    cos_all, sin_all = rotary_tables(after(frame_times, attn_in))
    grad_rows = cotangent[0].astype(F32).reshape(per_device, PATCHES, width)
    d_feed_out = (feed_gate[:, None, :] * grad_rows).reshape(tokens, width).astype(BF16)
    x, d_feed_out, cos_all, sin_all = lax.optimization_barrier((x, d_feed_out, cos_all, sin_all))
    mix, wide, lse, kv = attend(per_device, clip_ids, live, x)
    mix = to_tokens(mix)
    mixes = [mix[:, place].reshape(width, PATCHES) for place in range(per_device)]
    attn_rows = jnp.stack([dot_over(each, out_weight, 0, 0) for each in mixes]) + out_bias
    attn_mix = jnp.concatenate(mixes, axis=1)

    frame_rows = hidden[0].astype(F32).reshape(per_device, PATCHES, width)
    middle = frame_rows + attn_gate[:, None, :] * attn_rows
    feed_in = modulate_norm(middle, feed_shift, feed_scale).reshape(tokens, width).astype(BF16)
    feed_args = (feed_in, d_feed_out, up_weight, up_bias, down_weight)
    theirs = feed(1 - pack if halves else pack * 0 + 1, *feed_args, None)
    mine = feed(pack if halves else pack * 0, *feed_args, theirs[:2])
    small = 128

    def in_order(own, other):
        if halves:
            even, odd = jnp.where(pack == 0, own, other), jnp.where(pack == 0, other, own)
        else:
            even, odd = own, other
        rows = own.shape[0]
        return jnp.stack(
            [even.reshape(rows, -1, small), odd.reshape(rows, -1, small)], axis=2
        ).reshape(rows, -1)

    own_levels = levels[0]
    level_row = jnp.concatenate(
        [
            jnp.broadcast_to(part[frame], (width // (2 * per_device),))
            for frame in range(per_device)
            for part in (lax.div(own_levels, 32), lax.rem(own_levels, 32))
        ]
    ).astype(F32)[None]
    extra_rows = jnp.concatenate(
        [
            in_order(mine[4], theirs[4]).reshape(-1, width),
            level_row,
            jnp.zeros((1, width), F32),
        ],
        axis=0,
    )
    d_middle, d_attn_out, layer_out, blocks = middle_back(
        per_device,
        mine[1],
        middle.reshape(tokens, width),
        cotangent[0],
        attn_rows.reshape(tokens, width),
        mine[0],
        feed_scale,
        attn_gate,
        feed_gate,
        down_bias,
        extra_rows,
        out_weight,
    )
    layer_out = layer_out.reshape(1, tokens, width)
    d_mix = to_heads(blocks)

    def out_term(start, size):
        return dot_over(attn_mix, columns_of(d_attn_out, start, size), 1, 0).astype(BF16)

    sums = ()
    if halves:
        up_sum = RowSum(mine[2], exchange(theirs[2], "pack", 1), (2, 1, 4, 8))
        down_sum = RowSum(mine[3], exchange(theirs[3], "pack", 1), (1, 2, 4, 8))
        out_theirs = exchange(out_term((1 - pack) * (width // 2), width // 2), "pack", 1)
        out_sum = RowSum(out_term(pack * (width // 2), width // 2), out_theirs, (1, 2, 4, 8))
        sums = (down_sum, up_sum)
    def own_share(row):
        piece = row.shape[0] // seq_count
        return lax.dynamic_slice_in_dim(row, seq_index * piece, piece)

    chunks = width // PATCHES
    early_rows = d_mix[:, per_device].reshape(seq_count, chunks, 16, PATCHES)
    early_rows = early_rows.transpose(0, 2, 1, 3).reshape(seq_count, 16, width)
    early_sets = of_packs(early_rows)
    early_sum = functools.reduce(
        jnp.add, [jnp.sum(each.astype(F32), axis=0) for each in early_sets]
    )
    out_bias_grad = own_share(early_sum[8])
    down_bias_grad = own_share(early_sum[9])
    up_bias_grad = own_share(early_sum[10:14].reshape(hidden_units))

    def frames_of(rows, per_frame, kinds):
        return jnp.concatenate(
            [
                jnp.stack(
                    [rows[:, frame * per_frame + kind] for frame in range(per_device)], axis=1
                ).reshape(-1, width)
                for kind in range(kinds)
            ],
            axis=1,
        )

    own_table = lax.dynamic_slice_in_dim(noise_table, seq_index * share, share, 1)
    own_mod = lax.dynamic_slice_in_dim(mod_weight, seq_index * share, share, 0)
    stride = width // (2 * per_device)
    parts = []
    for rows in early_sets:
        coded = rows[:, 14, ::stride].astype(jnp.int32).reshape(-1, 2)
        set_levels = coded[:, 0] * 32 + coded[:, 1]
        picks = (set_levels[:, None] == jnp.arange(level_count, dtype=jnp.int32)[None, :]).astype(F32)
        embeds = jnp.dot(picks, own_table, precision=PRECISE, preferred_element_type=F32)
        set_cond = jax.nn.silu(embeds).astype(BF16)
        d_mod = frames_of(rows, 4, 4)
        parts.append(
            (
                picks,
                embeds,
                set_cond,
                dot_over(d_mod, own_mod[:, 2 * width :], 1, 1),
                dot_over(set_cond, d_mod, 0, 0),
            )
        )
    mod_grad_early = functools.reduce(jnp.add, [each[4] for each in parts])
    mod_sum_early = (early_sum[:4] + early_sum[4:8]).reshape(4 * width)
    orders = [each.stage() for each in sums]
    result = attend_back(
        per_device, clip_ids, live, x, kv, wide, lse, d_mix, cos_all, sin_all, orders
    )
    if halves:
        for each in sums:
            result = each.tie(result)
        result = out_sum.tie(result)
    back = to_tokens(result)
    orders = []
    if halves:
        for each in (up_sum, down_sum, out_sum):
            each.stage()
        orders = [each.stage() for each in (up_sum, down_sum, out_sum)]
    orders += [mod_grad_early] + [part[3] for part in parts]
    which = (1 - pack, pack) if halves else (pack * 0, pack * 0 + 1)
    d_in_theirs, qkv_theirs, bias_theirs = unproject(
        per_device, seq_count, which[0], attn_in, back, qkv_weight, orders
    )
    qkv_mine, hidden_grad, late = unproject(
        per_device,
        seq_count,
        which[1],
        attn_in,
        back,
        qkv_weight,
        (),
        d_in_theirs,
        (hidden[0], d_middle, attn_scale, bias_theirs),
    )
    hidden_grad = hidden_grad.reshape(1, tokens, width)
    late_rows = lax.all_to_all(late, "seq", 0, 0, tiled=True)

    def halves_in_order(own, other):
        if halves:
            return jnp.where(pack == 0, own, other), jnp.where(pack == 0, other, own)
        return other, own

    if halves:
        came = exchange(qkv_theirs, "pack", 1)
        split = width // 4
        qkv_sums = [
            RowSum(qkv_mine[..., :split], came[..., :split], (1, 2, 4, 8)),
            RowSum(qkv_mine[..., split:], came[..., split:], (2, 1, 4, 8)),
        ]
        for each in qkv_sums:
            each.stage((up_sum, down_sum, out_sum))
        up_weight_grad, down_weight_grad, out_weight_grad, qkv_weight_grad = settle(
            pack, *[each.finish() for each in (up_sum, down_sum, out_sum, *qkv_sums)]
        )
    else:
        up_weight_grad = row_sum_direct(in_order(mine[2], theirs[2]))
        pairs = [each[3].reshape(-1, small, width) for each in (mine, theirs)]
        down_weight_grad = row_sum_direct(jnp.stack(pairs, axis=1).reshape(hidden_units, width))
        out_weight_grad = row_sum_direct(out_term(0, width))
        qkv_term = jnp.concatenate(halves_in_order(qkv_mine, qkv_theirs), axis=-1)
        qkv_weight_grad = row_sum_direct(qkv_term.transpose(1, 0, 2).reshape(width, 3 * width))

    late_sets = of_packs(late_rows[:, :8])
    bias_at = 2 * per_device
    bias_sums = [
        jnp.sum(rows[:, bias_at : bias_at + 3].astype(F32), axis=0) for rows in late_sets
    ]
    if halves:
        ones, twos = bias_sums
        half = width // 2
        own_half = ones[:, :half] + twos[:, half:]
        other_half = ones[:, half:] + twos[:, :half]
    else:
        total = functools.reduce(jnp.add, bias_sums)
        own_half, other_half = total[:, : width // 2], total[:, width // 2 :]
    bias_total = jnp.concatenate(halves_in_order(own_half, other_half), axis=1)
    qkv_bias_grad = own_share(bias_total.reshape(3 * width))
    late_mods = [frames_of(rows, 2, 2) for rows in late_sets]
    mod_sum_late = functools.reduce(
        jnp.add, [jnp.sum(each.astype(F32), axis=0) for each in late_mods]
    )
    d_embeds = []
    for part, d_mod in zip(parts, late_mods):
        d_cond = part[3] + dot_over(d_mod, own_mod[:, : 2 * width], 1, 1)
        d_embeds.append(jax.vjp(jax.nn.silu, part[1])[1](d_cond)[0])
    table_grad = lax.dot_general(
        jnp.concatenate([part[0] for part in parts], axis=0),
        jnp.concatenate(d_embeds, axis=0),
        (((0,), (0,)), ((), ())),
        precision=PRECISE,
        preferred_element_type=F32,
    )
    mod_grad_late = functools.reduce(
        jnp.add, [dot_over(part[2], d_mod, 0, 0) for part, d_mod in zip(parts, late_mods)]
    )
    mod_weight_grad = jnp.concatenate([mod_grad_late, mod_grad_early], axis=1)
    mod_bias_grad = own_share(jnp.concatenate([mod_sum_late, mod_sum_early]))
    return (
        layer_out,
        hidden_grad,
        table_grad,
        mod_weight_grad,
        mod_bias_grad,
        qkv_weight_grad,
        qkv_bias_grad,
        out_weight_grad,
        out_bias_grad,
        up_weight_grad,
        up_bias_grad,
        down_weight_grad,
        down_bias_grad,
    )


def solution(mesh):
    in_specs = (
        P("pack", "seq", None),
        P("pack", "seq", None),
        P("pack", "seq"),
        P("pack", None),
        P("pack", None),
    ) + (P(),) * 11
    out_specs = (
        P("pack", "seq", None),
        P("pack", "seq", None),
        P(None, "seq"),
        P("seq", None),
        P("seq"),
        P("seq", None),
        P("seq"),
        P("seq", None),
        P("seq"),
        P("seq", None),
        P("seq"),
        P("seq", None),
        P("seq"),
    )
    return jax.shard_map(local, mesh=mesh, in_specs=in_specs, out_specs=out_specs, check_vma=False)
```

```python
import functools

import jax
import jax.numpy as jnp
from jax import lax
from jax.experimental import pallas as pl
from jax.experimental.pallas import tpu as pltpu
from jax.sharding import PartitionSpec as P

HEAD = 64
PATCHES = 256
SIDE = 16
EPSILON = 1e-06
PRECISE = lax.Precision.HIGHEST
HALF = HEAD // 2
F32 = jnp.float32
BF16 = jnp.bfloat16


def modulate_norm(rows, shift, scale):
    center = jnp.mean(rows, axis=-1, keepdims=True)
    centered = rows - center
    spread = jnp.mean(centered * centered, axis=-1, keepdims=True)
    normed = centered * lax.rsqrt(spread + EPSILON)
    return normed * (1.0 + scale[:, None, :]) + shift[:, None, :]


def gelu_tanh(values):
    return jax.nn.gelu(values, approximate=True)


def dot_over(first, second, first_dim, second_dim):
    return lax.dot_general(
        first, second, (((first_dim,), (second_dim,)), ((), ())), preferred_element_type=F32
    )


def spatial_angles():
    time_pairs = HALF // 4
    space_pairs = (HALF - time_pairs) // 2
    patch = jnp.arange(PATCHES, dtype=jnp.int32)
    row_pos = (patch // SIDE).astype(F32)
    col_pos = (patch % SIDE).astype(F32)
    time_freq = 10000.0 ** (-jnp.arange(time_pairs, dtype=F32) / time_pairs)
    space_freq = 10000.0 ** (-jnp.arange(space_pairs, dtype=F32) / space_pairs)
    space = jnp.concatenate(
        [space_freq[:, None] * row_pos[None, :], space_freq[:, None] * col_pos[None, :]], axis=0
    )
    return time_freq, space


def rotary_tables(time_frames):
    time_freq, space = spatial_angles()
    count = time_frames.shape[0]
    time_angle = time_frames[:, None] * time_freq[None, :]

    def whole(function):
        return jnp.concatenate(
            [
                jnp.broadcast_to(
                    function(time_angle)[:, :, None], (count, time_freq.shape[0], PATCHES)
                ),
                jnp.broadcast_to(function(space)[None], (count,) + space.shape),
            ],
            axis=1,
        )

    return whole(jnp.cos), whole(jnp.sin)


def walk_frames(frames, per_device, segments_ref, live_ref, list_ref, visit):
    def step(source, held):
        for place in range(per_device):
            frame = source * per_device + place
            before = jnp.maximum(frame - 1, 0)
            fresh = (frame == 0) | (segments_ref[frame] != segments_ref[before])
            held = jnp.where(fresh, 0, held)
            list_ref[held] = frame
            visit(source, place, frame, held + 1)
            held = held + jnp.where(live_ref[frame] == 1, 1, 0)
        return held

    lax.fori_loop(0, frames // per_device, step, jnp.int32(0))


def attend_kernel(per_device, segments_ref, live_ref, x_ref, mix_ref, wide_ref, lse_ref, kv_ref, list_ref):
    frames = kv_ref.shape[0]

    def turn(source, carry):
        for place in range(per_device):
            both = jnp.concatenate(
                [x_ref[source, place], x_ref[source, per_device + place]], axis=0
            )
            kv_ref[source * per_device + place] = both.T
        return carry

    lax.fori_loop(0, frames // per_device, turn, 0)

    def visit(source, place, frame, count):
        query = x_ref[source, 2 * per_device + place]
        query_side = jnp.concatenate([query, jnp.zeros_like(query)], axis=0)

        def scores_of(other):
            return jnp.dot(kv_ref[other], query_side, preferred_element_type=F32)

        def mixed(other, weights):
            value = x_ref[lax.div(other, per_device), per_device + lax.rem(other, per_device)]
            return jnp.dot(value, weights.astype(BF16), preferred_element_type=F32)

        def join(others, carry):
            scores = [scores_of(other) for other in others]
            tops = [jnp.max(score, axis=0, keepdims=True) for score in scores]
            new_top = functools.reduce(jnp.maximum, tops)
            if carry is not None:
                top, total, accum = carry
                new_top = jnp.maximum(top, new_top)
                shrink = jnp.exp(top - new_top)
                total = total * shrink
                accum = accum * shrink
            for index, score in enumerate(scores):
                weights = jnp.exp(score - new_top)
                added = jnp.sum(weights, axis=0, keepdims=True)
                product = mixed(others[index], weights)
                if carry is None and index == 0:
                    total, accum = added, product
                else:
                    total, accum = total + added, accum + product
            return new_top, total, accum

        others = count - 1
        carry = join([frame], None)
        carry = lax.fori_loop(
            0,
            lax.div(others, 4),
            lambda index, state: join([list_ref[4 * index + nth] for nth in range(4)], state),
            carry,
        )
        carry = lax.fori_loop(
            lax.div(others, 4) * 2,
            lax.div(others, 2),
            lambda index, state: join([list_ref[2 * index], list_ref[2 * index + 1]], state),
            carry,
        )
        top, total, accum = lax.fori_loop(
            0,
            lax.rem(others, 2),
            lambda unused, state: join([list_ref[others - 1]], state),
            carry,
        )
        result = accum * (1.0 / total)
        wide_ref[source, place] = result
        mix_ref[source, place] = result.astype(BF16)
        lse_ref[pl.ds(frame, 1), :] = top + jnp.log(total)

    walk_frames(frames, per_device, segments_ref, live_ref, list_ref, visit)


def corners(values):
    return [each.reshape(-1, each.shape[-1])[:1, :128] for each in values]


def unread_spec():
    return pl.BlockSpec(memory_space=pl.ANY)


def whole_spec():
    return pl.BlockSpec(memory_space=pltpu.VMEM)


def scalar_spec():
    return pl.BlockSpec(memory_space=pltpu.SMEM)


def attend(per_device, segments, live, x):
    sources = x.shape[0]
    frames = sources * per_device
    pairs = frames * 6
    outs = (
        jax.ShapeDtypeStruct((sources, per_device, HEAD, PATCHES), BF16),
        jax.ShapeDtypeStruct((sources, per_device, HEAD, PATCHES), F32),
        jax.ShapeDtypeStruct((frames, PATCHES), F32),
        jax.ShapeDtypeStruct((frames, PATCHES, 2 * HEAD), BF16),
    )
    return pl.pallas_call(
        functools.partial(attend_kernel, per_device),
        out_shape=outs,
        in_specs=[scalar_spec(), scalar_spec(), whole_spec()],
        out_specs=(whole_spec(),) * len(outs),
        scratch_shapes=[pltpu.SMEM((frames,), jnp.int32)],
        cost_estimate=pl.CostEstimate(
            flops=pairs * 4 * PATCHES * PATCHES * 256,
            bytes_accessed=x.size * 2 * 3,
            transcendentals=pairs * PATCHES * PATCHES,
        ),
        compiler_params=pltpu.CompilerParams(vmem_limit_bytes=40 << 20),
        name="attend",
    )(segments, live, x)


def attend_back_kernel(
    per_device,
    segments_ref,
    live_ref,
    x_ref,
    kv_ref,
    wide_ref,
    lse_ref,
    d_mix_ref,
    cos_ref,
    sin_ref,
    *refs
):
    out_ref, dkv_ref, list_ref = refs[-3:]
    frames = kv_ref.shape[0]

    def unturn(frame, values):
        lower = values[:HALF]
        upper = values[HALF:]
        cosine = cos_ref[frame]
        sine = sin_ref[frame]
        return jnp.concatenate([lower * cosine + upper * sine, upper * cosine - lower * sine], axis=0)

    def visit(source, place, frame, count):
        query = x_ref[source, 2 * per_device + place]
        d_mix = d_mix_ref[source, place]
        blank = jnp.zeros_like(query)
        query_side = jnp.concatenate([query, blank], axis=0)
        d_mix_side = jnp.concatenate([blank, d_mix], axis=0)
        turned = jnp.concatenate([query, d_mix], axis=0).T
        first = lax.broadcasted_iota(jnp.int32, turned.shape, 1) < HEAD
        nothing = jnp.zeros_like(turned)
        both = jnp.concatenate(
            [jnp.where(first, turned, nothing), jnp.where(first, nothing, turned)], axis=0
        )
        lse = lse_ref[pl.ds(frame, 1), :]
        delta = jnp.sum(d_mix.astype(F32) * wide_ref[source, place], axis=0, keepdims=True)

        def block(other, own=False):
            key_value = kv_ref[other]
            scores = jnp.dot(key_value, query_side, preferred_element_type=F32)
            d_weights = jnp.dot(key_value, d_mix_side, preferred_element_type=F32)
            weights = jnp.exp(scores - lse)
            d_scores = (weights * (d_weights - delta)).astype(BF16)
            sides = jnp.concatenate([d_scores, weights.astype(BF16)], axis=1)
            d_both = jnp.dot(sides, both, preferred_element_type=F32)
            if own:
                dkv_ref[other] = d_both
            else:
                dkv_ref[other] += d_both
            key = x_ref[lax.div(other, per_device), lax.rem(other, per_device)]
            return jnp.dot(key, d_scores, preferred_element_type=F32)

        others = count - 1
        d_query = block(frame, True)
        d_query = lax.fori_loop(
            0,
            lax.div(others, 2),
            lambda index, state: state
            + block(list_ref[2 * index])
            + block(list_ref[2 * index + 1]),
            d_query,
        )
        d_query = lax.fori_loop(
            0,
            lax.rem(others, 2),
            lambda unused, state: state + block(list_ref[others - 1]),
            d_query,
        )
        d_query = unturn(frame, d_query * (HEAD**-0.5)).astype(BF16)
        out_ref[source, 2 * per_device + place] = d_query

    walk_frames(frames, per_device, segments_ref, live_ref, list_ref, visit)

    def finish(source, carry):
        for place in range(per_device):
            frame = source * per_device + place
            both = dkv_ref[frame].T
            out_ref[source, place] = unturn(frame, both[:HEAD]).astype(BF16)
            out_ref[source, per_device + place] = both[HEAD:].astype(BF16)
        return carry

    lax.fori_loop(0, frames // per_device, finish, 0)


def attend_back(per_device, segments, live, x, kv, wide, lse, d_mix, cosine, sine, orders):
    sources = x.shape[0]
    frames = sources * per_device
    pairs = frames * 6
    args = [segments, live, x, kv, wide, lse, d_mix, cosine, sine]
    specs = [scalar_spec(), scalar_spec()] + [whole_spec()] * (len(args) - 2)
    orders = corners(orders)
    return pl.pallas_call(
        functools.partial(attend_back_kernel, per_device),
        out_shape=jax.ShapeDtypeStruct(x.shape, BF16),
        in_specs=specs + [unread_spec()] * len(orders),
        out_specs=whole_spec(),
        scratch_shapes=[
            pltpu.VMEM((frames, PATCHES, 2 * HEAD), F32),
            pltpu.SMEM((frames,), jnp.int32),
        ],
        cost_estimate=pl.CostEstimate(
            flops=pairs * 10 * PATCHES * PATCHES * 64,
            bytes_accessed=x.size * 2 * 5,
            transcendentals=pairs * PATCHES * PATCHES,
        ),
        compiler_params=pltpu.CompilerParams(vmem_limit_bytes=60 << 20),
        name="attend_back",
    )(*args, *orders)


def exchange(value, axis, bit):
    count = lax.axis_size(axis)
    return lax.ppermute(value, axis, [(source, source ^ bit) for source in range(count)])


def after(value, *earlier):
    return lax.optimization_barrier((value,) + earlier)[0]


def of_packs(value):
    values = [value]
    bit = lax.axis_size("pack") // 2
    while bit:
        values = values + [exchange(each, "pack", bit) for each in values]
        bit //= 2
    return values


def halving_fits():
    return lax.axis_size("pack") == 2 and lax.axis_size("seq") == 16


class RowSum:
    def __init__(self, mine, came, order):
        self.order = list(order)
        self.index = lax.axis_index("seq")
        rows = mine.shape[-2]
        self.tail = (rows // 16, mine.shape[-1])
        self.lead = mine.shape[:-2]
        shape = self.lead + (2, 2, 2, 2) + self.tail
        self.parts = [mine.reshape(shape), came.reshape(shape)]

    def pick(self, bit, which):
        axis = len(self.lead) + {8: 0, 4: 1, 2: 2, 1: 3}[bit]
        pieces = [lax.dynamic_slice_in_dim(part, which, 1, axis) for part in self.parts]
        return (pieces[0].astype(F32) + pieces[1].astype(F32)).astype(BF16)

    def tie_kept(self, value):
        value, self.parts[0] = lax.optimization_barrier((value, self.parts[0]))
        return value

    def stage(self, later=()):
        bit = self.order.pop(0)
        own_bit = lax.rem(lax.div(self.index, bit), 2)
        send = self.pick(bit, 1 - own_bit)
        for each in later:
            send = each.tie_kept(send)
        came = exchange(send, "seq", bit)
        self.parts = [self.pick(bit, own_bit), came]
        return send

    def tie(self, value):
        value, *self.parts = lax.optimization_barrier((value, *self.parts))
        return value

    def finish(self):
        while self.order:
            self.stage()
        own = (self.parts[0].astype(F32) + self.parts[1].astype(F32)).astype(BF16)
        own = own.reshape(self.lead + self.tail)
        return own, exchange(own, "pack", 1)


def settle_kernel(pack_ref, *refs):
    ups, downs, outs, firsts, seconds = [refs[2 * nth : 2 * nth + 2] for nth in range(5)]
    up_ref, down_ref, out_ref, qkv_ref = refs[10:]
    own_first = pack_ref[0] == 0
    small = 128

    def of_pack(pack, pair, *index):
        one, two = pair[0][index].astype(F32), pair[1][index].astype(F32)
        return jnp.where(own_first, one, two) if pack == 0 else jnp.where(own_first, two, one)

    every = slice(None)
    for pack in range(2):
        for group in range(ups[0].shape[1] // small):
            at = (2 * group + pack) * small
            columns = slice(group * small, (group + 1) * small)
            up_ref[:, at : at + small] = of_pack(pack, ups, every, columns)
        rows = downs[0].shape[0]
        down_ref[pack * rows : (pack + 1) * rows, :] = of_pack(pack, downs, every, every)
        columns = outs[0].shape[1]
        out_ref[:, pack * columns : (pack + 1) * columns] = of_pack(pack, outs, every, every)
        for kind in range(3):
            for nth, pair in enumerate((firsts, seconds)):
                columns = pair[0].shape[2]
                at = (4 * kind + 2 * pack + nth) * columns
                qkv_ref[:, at : at + columns] = of_pack(pack, pair, kind, every, every)


def settle(pack, *pairs):
    up, down, out, qkv = pairs[0][0], pairs[1][0], pairs[2][0], pairs[3][0]
    shapes = (
        (up.shape[0], 2 * up.shape[1]),
        (2 * down.shape[0], down.shape[1]),
        (out.shape[0], 2 * out.shape[1]),
        (qkv.shape[1], 12 * qkv.shape[2]),
    )
    args = [each for pair in pairs for each in pair]
    return pl.pallas_call(
        settle_kernel,
        out_shape=tuple(jax.ShapeDtypeStruct(shape, F32) for shape in shapes),
        in_specs=[scalar_spec()] + [whole_spec()] * len(args),
        out_specs=(whole_spec(),) * 4,
        compiler_params=pltpu.CompilerParams(vmem_limit_bytes=32 << 20),
        name="settle",
    )(pack.reshape(1), *args)


def row_sum_direct(term):
    part = lax.psum_scatter(term.astype(BF16), "seq", scatter_dimension=0, tiled=True)
    return lax.psum(part, "pack").astype(F32)


def project_kernel(
    per_device,
    hidden_ref,
    shift_ref,
    scale_ref,
    wq_ref,
    wk_ref,
    wv_ref,
    bq_ref,
    bk_ref,
    bv_ref,
    cos_ref,
    sin_ref,
    in_ref,
    x_ref,
):
    @pl.when(pl.program_id(0) == 0)
    def _():
        for place in range(per_device):
            rows = pl.ds(place * PATCHES, PATCHES)
            values = hidden_ref[rows, :].astype(F32)
            centered = values - jnp.mean(values, axis=-1, keepdims=True)
            spread = jnp.mean(centered * centered, axis=-1, keepdims=True)
            normed = centered * lax.rsqrt(spread + EPSILON)
            scale = scale_ref[pl.ds(place, 1), :]
            in_ref[rows, :] = (normed * (1.0 + scale) + shift_ref[pl.ds(place, 1), :]).astype(BF16)

    rows = in_ref[...]
    group = wq_ref.shape[1] // HEAD

    def turned(values, place):
        lower = values[:HALF]
        upper = values[HALF:]
        cosine = cos_ref[place]
        sine = sin_ref[place]
        return jnp.concatenate([lower * cosine - upper * sine, upper * cosine + lower * sine], axis=0)

    for kind, (weight_ref, bias_ref) in enumerate(
        ((wq_ref, bq_ref), (wk_ref, bk_ref), (wv_ref, bv_ref))
    ):
        flat = jnp.dot(rows, weight_ref[...], preferred_element_type=F32) + bias_ref[...]
        for place in range(per_device):
            block = flat[place * PATCHES : (place + 1) * PATCHES].T
            for head in range(group):
                values = block[head * HEAD : (head + 1) * HEAD]
                if kind == 0:
                    values = turned(values, place) * (HEAD**-0.5)
                    x_ref[head, 2 * per_device + place] = values.astype(BF16)
                elif kind == 1:
                    x_ref[head, place] = turned(values, place).astype(BF16)
                else:
                    x_ref[head, per_device + place] = values.astype(BF16)


def project(per_device, hidden, shift, scale, weight, bias, cosine, sine):
    tokens, width = hidden.shape
    heads = width // HEAD
    group = 2
    lanes = group * HEAD
    steps = heads // group
    bias_row = bias[None, :]

    def whole(shape):
        return pl.BlockSpec(shape, lambda step: (0,) * len(shape))

    def part(kind, rows):
        return pl.BlockSpec((rows, lanes), lambda step: (0, kind * steps + step))

    blocks = (heads, 3 * per_device, HEAD, PATCHES)
    return pl.pallas_call(
        functools.partial(project_kernel, per_device),
        grid=(steps,),
        out_shape=(
            jax.ShapeDtypeStruct((tokens, width), BF16),
            jax.ShapeDtypeStruct(blocks, BF16),
        ),
        in_specs=[whole((tokens, width)), whole(shift.shape), whole(scale.shape)]
        + [part(kind, width) for kind in range(3)]
        + [part(kind, 1) for kind in range(3)]
        + [whole(cosine.shape), whole(sine.shape)],
        out_specs=(
            whole((tokens, width)),
            pl.BlockSpec((group,) + blocks[1:], lambda step: (step, 0, 0, 0)),
        ),
        cost_estimate=pl.CostEstimate(
            flops=2 * tokens * width * 3 * width,
            bytes_accessed=2 * (weight.size + 5 * tokens * width),
            transcendentals=0,
        ),
        compiler_params=pltpu.CompilerParams(vmem_limit_bytes=40 << 20),
        name="project",
    )(hidden, shift, scale, weight, weight, weight, bias_row, bias_row, bias_row, cosine, sine)


GELU_SLOPE = 0.7978845608028654
GELU_CUBE = 0.044715


def feed_kernel(
    carried,
    which_ref,
    in_ref,
    d_out_ref,
    up_a_ref,
    up_b_ref,
    bias_a_ref,
    bias_b_ref,
    down_a_ref,
    down_b_ref,
    *refs
):
    if carried:
        out_before_ref, d_in_before_ref = refs[:2]
        refs = refs[2:]
    out_ref, d_in_ref, d_up_ref, d_down_ref, d_bias_ref, turned_ref = refs

    @pl.when(pl.program_id(0) == 0)
    def _():
        turned_ref[...] = in_ref[...].astype(F32).T.astype(BF16)
        if carried:
            out_ref[...] = out_before_ref[...]
            d_in_ref[...] = d_in_before_ref[...]
        else:
            out_ref[...] = jnp.zeros_like(out_ref)
            d_in_ref[...] = jnp.zeros_like(d_in_ref)

    up = jnp.concatenate([up_a_ref[...], up_b_ref[...]], axis=1)
    down = jnp.concatenate([down_a_ref[...], down_b_ref[...]], axis=0)
    bias = jnp.concatenate([bias_a_ref[...], bias_b_ref[...]], axis=1)
    d_out = d_out_ref[...]
    pre = jnp.dot(in_ref[...], up, preferred_element_type=F32) + bias
    d_act = dot_over(d_out, down, 1, 1)
    square = pre * pre
    bend = jnp.tanh(GELU_SLOPE * pre * (1.0 + GELU_CUBE * square))
    half = 0.5 * (1.0 + bend)
    act = (pre * half).astype(BF16)
    slope = half + (0.5 * GELU_SLOPE) * pre * (1.0 - bend * bend) * (
        1.0 + (3.0 * GELU_CUBE) * square
    )
    d_pre = (d_act * slope).astype(BF16)
    out_ref[...] += jnp.dot(act, down, preferred_element_type=F32)
    d_in_ref[...] += dot_over(d_pre, up, 1, 1)
    d_up_ref[...] = jnp.dot(turned_ref[...], d_pre, preferred_element_type=F32).astype(BF16)
    d_down_ref[...] = jnp.dot(
        act.astype(F32).T.astype(BF16), d_out, preferred_element_type=F32
    ).astype(BF16)
    d_bias_ref[...] = jnp.sum(d_pre.astype(F32), axis=0, keepdims=True)


def feed(which, feed_in, d_feed_out, up_weight, up_bias, down_weight, before):
    tokens, width = feed_in.shape
    hidden_units = up_weight.shape[1]
    small = 128
    steps = hidden_units // (4 * small)
    own = hidden_units // 2

    def whole(shape):
        return pl.BlockSpec(shape, lambda step, which: (0,) * len(shape))

    def group(nth):
        return lambda step, which: 2 * (2 * step + nth) + which[0]

    def columns(nth, rows):
        return pl.BlockSpec((rows, small), lambda step, which: (0, group(nth)(step, which)))

    def rows_of(nth):
        return pl.BlockSpec((small, width), lambda step, which: (group(nth)(step, which), 0))

    args = [feed_in, d_feed_out, up_weight, up_weight, up_bias[None], up_bias[None]]
    args += [down_weight, down_weight]
    specs = [whole((tokens, width)), whole((tokens, width)), columns(0, width), columns(1, width)]
    specs += [columns(0, 1), columns(1, 1), rows_of(0), rows_of(1)]
    if before is not None:
        args += list(before)
        specs += [whole((tokens, width)), whole((tokens, width))]
    return pl.pallas_call(
        functools.partial(feed_kernel, before is not None),
        grid_spec=pltpu.PrefetchScalarGridSpec(
            num_scalar_prefetch=1,
            grid=(steps,),
            in_specs=specs,
            out_specs=(
                whole((tokens, width)),
                whole((tokens, width)),
                pl.BlockSpec((width, 2 * small), lambda step, which: (0, step)),
                pl.BlockSpec((2 * small, width), lambda step, which: (step, 0)),
                pl.BlockSpec((1, 2 * small), lambda step, which: (0, step)),
            ),
            scratch_shapes=[pltpu.VMEM((width, tokens), BF16)],
        ),
        out_shape=(
            jax.ShapeDtypeStruct((tokens, width), F32),
            jax.ShapeDtypeStruct((tokens, width), F32),
            jax.ShapeDtypeStruct((width, own), BF16),
            jax.ShapeDtypeStruct((own, width), BF16),
            jax.ShapeDtypeStruct((1, own), F32),
        ),
        cost_estimate=pl.CostEstimate(
            flops=12 * tokens * width * own,
            bytes_accessed=2 * (4 * own * width + 8 * tokens * width),
            transcendentals=tokens * own,
        ),
        compiler_params=pltpu.CompilerParams(vmem_limit_bytes=56 << 20),
        name="feed%d" % (before is not None),
    )(which.reshape(1), *args)


def norm_back(values, d_in, scale):
    centered = values - jnp.mean(values, axis=-1, keepdims=True)
    spread = jnp.mean(centered * centered, axis=-1, keepdims=True)
    inverse = lax.rsqrt(spread + EPSILON)
    normed = centered * inverse
    product = d_in * normed
    d_shift = jnp.sum(d_in, axis=0, keepdims=True)
    d_scale = jnp.sum(product, axis=0, keepdims=True)
    scaled = 1.0 + scale
    mean_d = jnp.mean(d_in * scaled, axis=-1, keepdims=True)
    mean_p = jnp.mean(product * scaled, axis=-1, keepdims=True)
    return (d_in * scaled - mean_d - normed * mean_p) * inverse, d_shift, d_scale


def middle_back_kernel(
    d_in_ref,
    middle_ref,
    grad_ref,
    attn_ref,
    feed_ref,
    scale_ref,
    gate_ref,
    feed_gate_ref,
    down_bias_ref,
    rows_ref,
    weight_ref,
    d_middle_ref,
    d_attn_ref,
    layer_ref,
    blocks_ref,
    sums_ref,
):
    frame = pl.program_id(0)
    per_device = pl.num_programs(0) - 1

    @pl.when(frame < per_device)
    def _():
        mine = pl.ds(frame, 1)
        middle = middle_ref[...]
        grads = grad_ref[...].astype(F32)
        back, d_shift, d_scale = norm_back(middle, d_in_ref[...], scale_ref[mine, :])
        d_middle = grads + back
        d_middle_ref[...] = d_middle
        d_attn = (d_middle * gate_ref[mine, :]).astype(BF16)
        d_attn_ref[...] = d_attn
        feed_rows = feed_ref[...] + down_bias_ref[...]
        feed_gate = feed_gate_ref[mine, :]
        layer_ref[...] = (middle + feed_gate * feed_rows).astype(BF16)
        d_feed_out = (feed_gate * grads).astype(BF16).astype(F32)
        sums_ref[frame] = jnp.concatenate(
            [
                jnp.sum(d_middle * attn_ref[...], axis=0, keepdims=True),
                d_shift,
                d_scale,
                jnp.sum(grads * feed_rows, axis=0, keepdims=True),
                jnp.sum(d_attn.astype(F32), axis=0, keepdims=True),
                jnp.sum(d_feed_out, axis=0, keepdims=True),
                jnp.zeros((2, d_shift.shape[1]), F32),
            ],
            axis=0,
        )
        d_mix = dot_over(weight_ref[...], d_attn, 1, 1).astype(BF16)
        for head in range(blocks_ref.shape[0]):
            blocks_ref[head, 0] = d_mix[head * HEAD : (head + 1) * HEAD]

    @pl.when(frame == per_device)
    def _():
        first = sums_ref[0]
        second = sums_ref[1]
        rows = jnp.concatenate(
            [first[:4], second[:4], first[4:6] + second[4:6], rows_ref[...]], axis=0
        ).astype(BF16)
        count = rows.shape[1] // PATCHES
        block = jnp.concatenate(
            [rows[:, nth * PATCHES : (nth + 1) * PATCHES] for nth in range(count)], axis=0
        )
        for head in range(blocks_ref.shape[0]):
            blocks_ref[head, 0] = block


def middle_back(
    per_device, d_in, middle, grads, attn_rows, feed_rows, scale, gate, feed_gate, down_bias, rows, weight
):
    tokens, width = d_in.shape
    heads = width // HEAD
    last = per_device - 1
    per_frame = pl.BlockSpec((PATCHES, width), lambda frame: (jnp.minimum(frame, last), 0))

    def whole(shape):
        return pl.BlockSpec(shape, lambda frame: (0,) * len(shape))

    small = whole((per_device, width))
    return pl.pallas_call(
        middle_back_kernel,
        grid=(per_device + 1,),
        out_shape=(
            jax.ShapeDtypeStruct((tokens, width), F32),
            jax.ShapeDtypeStruct((tokens, width), BF16),
            jax.ShapeDtypeStruct((tokens, width), BF16),
            jax.ShapeDtypeStruct((heads, per_device + 1, HEAD, PATCHES), BF16),
        ),
        in_specs=[per_frame] * 5
        + [small] * 3
        + [whole((1, width)), whole(rows.shape), whole(weight.shape)],
        out_specs=(
            per_frame,
            per_frame,
            per_frame,
            pl.BlockSpec((heads, 1, HEAD, PATCHES), lambda frame: (0, frame, 0, 0)),
        ),
        scratch_shapes=[pltpu.VMEM((per_device, 8, width), F32)],
        cost_estimate=pl.CostEstimate(
            flops=2 * tokens * width * width, bytes_accessed=24 * tokens * width, transcendentals=0
        ),
        compiler_params=pltpu.CompilerParams(vmem_limit_bytes=48 << 20),
        name="middle_back",
    )(
        d_in,
        middle,
        grads,
        attn_rows,
        feed_rows,
        scale,
        gate,
        feed_gate,
        down_bias[None],
        rows,
        weight,
    )


def unproject_kernel(
    per_device, carried, which_ref, in_ref, back_ref, wq_ref, wk_ref, wv_ref, *refs
):
    if not carried:
        refs = refs[-4:]
    if carried:
        before_ref, hidden_ref, d_middle_ref, scale_ref, bias_theirs_ref = refs[:5]
        d_weight_ref, grad_ref, rows_ref, d_in_ref, d_bias_ref, turned_ref = refs[5:]
    else:
        d_in_ref, d_weight_ref, d_bias_ref, turned_ref = refs

    @pl.when(pl.program_id(0) == 0)
    def _():
        turned_ref[...] = in_ref[...].astype(F32).T.astype(BF16)
        if carried:
            d_in_ref[...] = before_ref[...]
        else:
            d_in_ref[...] = jnp.zeros_like(d_in_ref)

    group = wq_ref.shape[1] // HEAD

    def token_major(block_of):
        rows = []
        for place in range(per_device):
            block = jnp.concatenate([block_of(head, place) for head in range(group)], axis=0)
            rows.append(block.astype(F32).T.astype(BF16))
        return jnp.concatenate(rows, axis=0)

    sides = jnp.concatenate(
        [
            token_major(lambda head, place: back_ref[head, 2 * per_device + place]),
            token_major(lambda head, place: back_ref[head, place]),
            token_major(lambda head, place: back_ref[head, per_device + place]),
        ],
        axis=1,
    )
    weights = jnp.concatenate([wq_ref[...], wk_ref[...], wv_ref[...]], axis=1)
    d_in_ref[...] += dot_over(sides, weights, 1, 1)
    d_weight = jnp.dot(turned_ref[...], sides, preferred_element_type=F32).astype(BF16)
    d_bias = jnp.sum(sides.astype(F32), axis=0, keepdims=True)
    lanes = group * HEAD
    for kind in range(3):
        d_weight_ref[kind] = d_weight[:, kind * lanes : (kind + 1) * lanes]
        part = d_bias[:, kind * lanes : (kind + 1) * lanes]
        if carried:
            start = pl.multiple_of(pl.program_id(0) * lanes, lanes)
            d_bias_ref[pl.ds(kind, 1), pl.ds(start, lanes)] = part
        else:
            d_bias_ref[kind] = part

    if carried:

        @pl.when(pl.program_id(0) == pl.num_programs(0) - 1)
        def _():
            sums = []
            for place in range(per_device):
                rows = pl.ds(place * PATCHES, PATCHES)
                mine = pl.ds(place, 1)
                back, d_shift, d_scale = norm_back(
                    hidden_ref[rows, :].astype(F32), d_in_ref[rows, :], scale_ref[mine, :]
                )
                grad_ref[rows, :] = (d_middle_ref[rows, :] + back).astype(BF16)
                sums += [d_shift, d_scale]
            for kind in range(3):
                sums.append(
                    jnp.concatenate([d_bias_ref[pl.ds(kind, 1), :], bias_theirs_ref[kind]], axis=1)
                )
            count = 16 - len(sums)
            late = jnp.concatenate(
                sums + [jnp.zeros((count, d_in_ref.shape[1]), F32)], axis=0
            ).astype(BF16)
            for target in range(rows_ref.shape[0]):
                rows_ref[target] = late


def unproject(per_device, targets, which, attn_in, back, weight, orders, before=None, norm_args=()):
    tokens, width = attn_in.shape
    heads = width // HEAD
    group = 2
    lanes = group * HEAD
    groups = heads // group
    steps = groups // 2

    def whole(shape):
        return pl.BlockSpec(shape, lambda step, which: (0,) * len(shape))

    def blocks(array):
        return pl.BlockSpec(
            (group,) + array.shape[1:], lambda step, which: (which[0] * steps + step, 0, 0, 0)
        )

    def part(kind):
        return pl.BlockSpec(
            (width, lanes), lambda step, which: (0, kind * groups + which[0] * steps + step)
        )

    args = [attn_in, back, weight, weight, weight]
    specs = [whole((tokens, width)), blocks(back), part(0), part(1), part(2)]
    weight_shape = (
        jax.ShapeDtypeStruct((3, width, width // 2), BF16),
        jax.ShapeDtypeStruct((3, 1, width // 2), F32),
    )
    weight_specs = (
        pl.BlockSpec((3, width, lanes), lambda step, which: (0, 0, step)),
        pl.BlockSpec((3, 1, lanes), lambda step, which: (0, 0, step)),
    )
    scratch = [pltpu.VMEM((width, tokens), BF16)]
    small = (per_device, width)
    if before is not None:
        args += [before] + list(norm_args)
        specs += [whole((tokens, width))] * 3 + [whole(small), whole((3, 1, width // 2))]
        late = (targets, 16, width)
        outs = weight_shape[:1] + (
            jax.ShapeDtypeStruct((tokens, width), BF16),
            jax.ShapeDtypeStruct(late, BF16),
        )
        out_specs = weight_specs[:1] + (whole((tokens, width)), whole(late))
        scratch = [pltpu.VMEM((tokens, width), F32), pltpu.VMEM((3, width // 2), F32)] + scratch
    else:
        outs = (jax.ShapeDtypeStruct((tokens, width), F32),) + weight_shape
        out_specs = (whole((tokens, width)),) + weight_specs
        orders = corners(orders)
        args += orders
        specs += [unread_spec()] * len(orders)
    return pl.pallas_call(
        functools.partial(unproject_kernel, per_device, before is not None),
        grid_spec=pltpu.PrefetchScalarGridSpec(
            num_scalar_prefetch=1,
            grid=(steps,),
            in_specs=specs,
            out_specs=out_specs,
            scratch_shapes=scratch,
        ),
        out_shape=outs,
        cost_estimate=pl.CostEstimate(
            flops=6 * tokens * width * width,
            bytes_accessed=2 * (3 * width * width + 6 * tokens * width),
            transcendentals=0,
        ),
        compiler_params=pltpu.CompilerParams(vmem_limit_bytes=48 << 20),
        name="unproject%d" % (before is not None),
    )(which.reshape(1), *args)


def columns_of(matrix, start, width, axis=1):
    if isinstance(start, int) and start == 0 and width == matrix.shape[axis]:
        return matrix
    return lax.dynamic_slice_in_dim(matrix, start, width, axis)


def local(
    hidden,
    cotangent,
    levels,
    segments,
    live_frames,
    noise_table,
    mod_weight,
    mod_bias,
    qkv_weight,
    qkv_bias,
    out_weight,
    out_bias,
    up_weight,
    up_bias,
    down_weight,
    down_bias,
):
    seq_index = lax.axis_index("seq")
    seq_count = lax.axis_size("seq")
    tokens = hidden.shape[1]
    width = hidden.shape[2]
    per_device = tokens // PATCHES
    frames = segments.shape[1]
    heads = width // HEAD
    copies = seq_count // heads
    hidden_units = up_weight.shape[1]
    level_count = noise_table.shape[0]
    share = width // seq_count
    clip_ids = segments[0]
    live = live_frames[0]

    pack = lax.axis_index("pack")
    halves = halving_fits()
    frame_ids = jnp.arange(frames, dtype=jnp.int32)
    same_clip = clip_ids[:, None] == clip_ids[None, :]
    clip_starts = jnp.min(jnp.where(same_clip, frame_ids[None, :], frames), axis=1)
    frame_times = (frame_ids - clip_starts).astype(F32)
    own_cos, own_sin = rotary_tables(
        lax.dynamic_slice_in_dim(frame_times, seq_index * per_device, per_device)
    )

    embed = jnp.concatenate(
        [
            lax.dynamic_slice_in_dim(noise_table, levels[0, frame], 1, 0)
            for frame in range(per_device)
        ],
        axis=0,
    )
    cond = jax.nn.silu(embed).astype(BF16)
    modulation = jnp.dot(cond, mod_weight[:, : 2 * width], preferred_element_type=F32)
    attn_shift, attn_scale = jnp.split(modulation + mod_bias[: 2 * width], 2, axis=1)
    attn_in, sent = project(
        per_device, hidden[0], attn_shift, attn_scale, qkv_weight, qkv_bias, own_cos, own_sin
    )

    def to_heads(array):
        if copies > 1:
            array = jnp.concatenate([array] * copies, axis=0)
        return lax.all_to_all(array, "seq", 0, 0, tiled=True)

    def to_tokens(array):
        return lax.all_to_all(array, "seq", 0, 0, tiled=True)[:heads]

    x = to_heads(sent)
    late_modulation = jnp.dot(
        after(cond, attn_in), mod_weight[:, 2 * width :], preferred_element_type=F32
    )
    attn_gate, feed_shift, feed_scale, feed_gate = jnp.split(
        late_modulation + mod_bias[2 * width :], 4, axis=1
    )
    cos_all, sin_all = rotary_tables(after(frame_times, attn_in))
    grad_rows = cotangent[0].astype(F32).reshape(per_device, PATCHES, width)
    d_feed_out = (feed_gate[:, None, :] * grad_rows).reshape(tokens, width).astype(BF16)
    x, d_feed_out, cos_all, sin_all = lax.optimization_barrier((x, d_feed_out, cos_all, sin_all))
    mix, wide, lse, kv = attend(per_device, clip_ids, live, x)
    mix = to_tokens(mix)
    mixes = [mix[:, place].reshape(width, PATCHES) for place in range(per_device)]
    attn_rows = jnp.stack([dot_over(each, out_weight, 0, 0) for each in mixes]) + out_bias
    attn_mix = jnp.concatenate(mixes, axis=1)

    frame_rows = hidden[0].astype(F32).reshape(per_device, PATCHES, width)
    middle = frame_rows + attn_gate[:, None, :] * attn_rows
    feed_in = modulate_norm(middle, feed_shift, feed_scale).reshape(tokens, width).astype(BF16)
    feed_args = (feed_in, d_feed_out, up_weight, up_bias, down_weight)
    theirs = feed(1 - pack if halves else pack * 0 + 1, *feed_args, None)
    mine = feed(pack if halves else pack * 0, *feed_args, theirs[:2])
    small = 128

    def in_order(own, other):
        if halves:
            even, odd = jnp.where(pack == 0, own, other), jnp.where(pack == 0, other, own)
        else:
            even, odd = own, other
        rows = own.shape[0]
        return jnp.stack(
            [even.reshape(rows, -1, small), odd.reshape(rows, -1, small)], axis=2
        ).reshape(rows, -1)

    own_levels = levels[0]
    level_row = jnp.concatenate(
        [
            jnp.broadcast_to(part[frame], (width // (2 * per_device),))
            for frame in range(per_device)
            for part in (lax.div(own_levels, 32), lax.rem(own_levels, 32))
        ]
    ).astype(F32)[None]
    extra_rows = jnp.concatenate(
        [
            in_order(mine[4], theirs[4]).reshape(-1, width),
            level_row,
            jnp.zeros((1, width), F32),
        ],
        axis=0,
    )
    d_middle, d_attn_out, layer_out, blocks = middle_back(
        per_device,
        mine[1],
        middle.reshape(tokens, width),
        cotangent[0],
        attn_rows.reshape(tokens, width),
        mine[0],
        feed_scale,
        attn_gate,
        feed_gate,
        down_bias,
        extra_rows,
        out_weight,
    )
    layer_out = layer_out.reshape(1, tokens, width)
    d_mix = to_heads(blocks)

    def out_term(start, size):
        return dot_over(attn_mix, columns_of(d_attn_out, start, size), 1, 0).astype(BF16)

    sums = ()
    if halves:
        up_sum = RowSum(mine[2], exchange(theirs[2], "pack", 1), (2, 1, 4, 8))
        down_sum = RowSum(mine[3], exchange(theirs[3], "pack", 1), (1, 2, 4, 8))
        out_theirs = exchange(out_term((1 - pack) * (width // 2), width // 2), "pack", 1)
        out_sum = RowSum(out_term(pack * (width // 2), width // 2), out_theirs, (1, 2, 4, 8))
        sums = (down_sum, up_sum)
    def own_share(row):
        piece = row.shape[0] // seq_count
        return lax.dynamic_slice_in_dim(row, seq_index * piece, piece)

    chunks = width // PATCHES
    early_rows = d_mix[:, per_device].reshape(seq_count, chunks, 16, PATCHES)
    early_rows = early_rows.transpose(0, 2, 1, 3).reshape(seq_count, 16, width)
    early_sets = of_packs(early_rows)
    early_sum = functools.reduce(
        jnp.add, [jnp.sum(each.astype(F32), axis=0) for each in early_sets]
    )
    out_bias_grad = own_share(early_sum[8])
    down_bias_grad = own_share(early_sum[9])
    up_bias_grad = own_share(early_sum[10:14].reshape(hidden_units))

    def frames_of(rows, per_frame, kinds):
        return jnp.concatenate(
            [
                jnp.stack(
                    [rows[:, frame * per_frame + kind] for frame in range(per_device)], axis=1
                ).reshape(-1, width)
                for kind in range(kinds)
            ],
            axis=1,
        )

    own_table = lax.dynamic_slice_in_dim(noise_table, seq_index * share, share, 1)
    own_mod = lax.dynamic_slice_in_dim(mod_weight, seq_index * share, share, 0)
    stride = width // (2 * per_device)
    parts = []
    for rows in early_sets:
        coded = rows[:, 14, ::stride].astype(jnp.int32).reshape(-1, 2)
        set_levels = coded[:, 0] * 32 + coded[:, 1]
        picks = (set_levels[:, None] == jnp.arange(level_count, dtype=jnp.int32)[None, :]).astype(F32)
        embeds = jnp.dot(picks, own_table, precision=PRECISE, preferred_element_type=F32)
        set_cond = jax.nn.silu(embeds).astype(BF16)
        d_mod = frames_of(rows, 4, 4)
        parts.append(
            (
                picks,
                embeds,
                set_cond,
                dot_over(d_mod, own_mod[:, 2 * width :], 1, 1),
                dot_over(set_cond, d_mod, 0, 0),
            )
        )
    mod_grad_early = functools.reduce(jnp.add, [each[4] for each in parts])
    mod_sum_early = (early_sum[:4] + early_sum[4:8]).reshape(4 * width)
    orders = [each.stage() for each in sums]
    result = attend_back(
        per_device, clip_ids, live, x, kv, wide, lse, d_mix, cos_all, sin_all, orders
    )
    if halves:
        for each in sums:
            result = each.tie(result)
        result = out_sum.tie(result)
    back = to_tokens(result)
    orders = []
    if halves:
        for each in (up_sum, down_sum, out_sum):
            each.stage()
        orders = [each.stage() for each in (up_sum, down_sum)]
        out_sum.stage()
    orders += [mod_grad_early] + [part[3] for part in parts]
    which = (1 - pack, pack) if halves else (pack * 0, pack * 0 + 1)
    d_in_theirs, qkv_theirs, bias_theirs = unproject(
        per_device, seq_count, which[0], attn_in, back, qkv_weight, orders
    )
    qkv_mine, hidden_grad, late = unproject(
        per_device,
        seq_count,
        which[1],
        attn_in,
        back,
        qkv_weight,
        (),
        d_in_theirs,
        (hidden[0], d_middle, attn_scale, bias_theirs),
    )
    hidden_grad = hidden_grad.reshape(1, tokens, width)
    late_rows = lax.all_to_all(late, "seq", 0, 0, tiled=True)

    def halves_in_order(own, other):
        if halves:
            return jnp.where(pack == 0, own, other), jnp.where(pack == 0, other, own)
        return other, own

    if halves:
        came = exchange(qkv_theirs, "pack", 1)
        split = width // 4
        qkv_sums = [
            RowSum(qkv_mine[..., :split], came[..., :split], (1, 2, 4, 8)),
            RowSum(qkv_mine[..., split:], came[..., split:], (2, 1, 4, 8)),
        ]
        for each in qkv_sums:
            each.stage((up_sum, down_sum, out_sum))
        up_weight_grad, down_weight_grad, out_weight_grad, qkv_weight_grad = settle(
            pack, *[each.finish() for each in (up_sum, down_sum, out_sum, *qkv_sums)]
        )
    else:
        up_weight_grad = row_sum_direct(in_order(mine[2], theirs[2]))
        pairs = [each[3].reshape(-1, small, width) for each in (mine, theirs)]
        down_weight_grad = row_sum_direct(jnp.stack(pairs, axis=1).reshape(hidden_units, width))
        out_weight_grad = row_sum_direct(out_term(0, width))
        qkv_term = jnp.concatenate(halves_in_order(qkv_mine, qkv_theirs), axis=-1)
        qkv_weight_grad = row_sum_direct(qkv_term.transpose(1, 0, 2).reshape(width, 3 * width))

    late_sets = of_packs(late_rows[:, :8])
    bias_at = 2 * per_device
    bias_sums = [
        jnp.sum(rows[:, bias_at : bias_at + 3].astype(F32), axis=0) for rows in late_sets
    ]
    if halves:
        ones, twos = bias_sums
        half = width // 2
        own_half = ones[:, :half] + twos[:, half:]
        other_half = ones[:, half:] + twos[:, :half]
    else:
        total = functools.reduce(jnp.add, bias_sums)
        own_half, other_half = total[:, : width // 2], total[:, width // 2 :]
    bias_total = jnp.concatenate(halves_in_order(own_half, other_half), axis=1)
    qkv_bias_grad = own_share(bias_total.reshape(3 * width))
    late_mods = [frames_of(rows, 2, 2) for rows in late_sets]
    mod_sum_late = functools.reduce(
        jnp.add, [jnp.sum(each.astype(F32), axis=0) for each in late_mods]
    )
    d_embeds = []
    for part, d_mod in zip(parts, late_mods):
        d_cond = part[3] + dot_over(d_mod, own_mod[:, : 2 * width], 1, 1)
        d_embeds.append(jax.vjp(jax.nn.silu, part[1])[1](d_cond)[0])
    table_grad = lax.dot_general(
        jnp.concatenate([part[0] for part in parts], axis=0),
        jnp.concatenate(d_embeds, axis=0),
        (((0,), (0,)), ((), ())),
        precision=PRECISE,
        preferred_element_type=F32,
    )
    mod_grad_late = functools.reduce(
        jnp.add, [dot_over(part[2], d_mod, 0, 0) for part, d_mod in zip(parts, late_mods)]
    )
    mod_weight_grad = jnp.concatenate([mod_grad_late, mod_grad_early], axis=1)
    mod_bias_grad = own_share(jnp.concatenate([mod_sum_late, mod_sum_early]))
    return (
        layer_out,
        hidden_grad,
        table_grad,
        mod_weight_grad,
        mod_bias_grad,
        qkv_weight_grad,
        qkv_bias_grad,
        out_weight_grad,
        out_bias_grad,
        up_weight_grad,
        up_bias_grad,
        down_weight_grad,
        down_bias_grad,
    )


def solution(mesh):
    in_specs = (
        P("pack", "seq", None),
        P("pack", "seq", None),
        P("pack", "seq"),
        P("pack", None),
        P("pack", None),
    ) + (P(),) * 11
    out_specs = (
        P("pack", "seq", None),
        P("pack", "seq", None),
        P(None, "seq"),
        P("seq", None),
        P("seq"),
        P("seq", None),
        P("seq"),
        P("seq", None),
        P("seq"),
        P("seq", None),
        P("seq"),
        P("seq", None),
        P("seq"),
    )
    return jax.shard_map(local, mesh=mesh, in_specs=in_specs, out_specs=out_specs, check_vma=False)
```
